32 devices in a mesh: dp: 2 (over y), row: 4 (over x, core), col: 4 (over z).
Axes of the slice: x: 2, y: 2, z: 4, core: 2. Of those that a mesh axis runs over, the one named last changes fastest.
Arguments:
- hidden_in: bfloat16 [8192, 1024], P(('dp', 'col'), 'row'), may hold values from -6 to 6
- norm_gain: bfloat16 [1024], P('row'), may hold values from 0.5 to 1.5
- w_qkv: bfloat16 [1024, 8, 256], P('row', 'col'), may hold values from -0.1875 to 0.1875
- w_out: bfloat16 [8, 128, 1024], P('col', None, 'row'), may hold values from -1.5 to 1.5
- ffn_gain: bfloat16 [1024], P('row'), may hold values from 0.5 to 1.5
- router: bfloat16 [1024, 32], P('row'), may hold values from -0.09375 to 0.09375
- w_gate: bfloat16 [32, 1024, 512], P(('dp', 'row')), may hold values from -0.1875 to 0.1875
- w_up: bfloat16 [32, 1024, 512], P(('dp', 'row')), may hold values from -0.1875 to 0.1875
- w_down: bfloat16 [32, 512, 1024], P(('dp', 'row')), may hold values from -1 to 1
- cotangent: bfloat16 [8192, 1024], P(('dp', 'col'), 'row'), may hold values from -6 to 6
- segment_ids: int32 [8, 1024], P(('dp', 'row')), may hold values from 0 to 3, never falling along the last dimension, each value on 1 to 512 neighbouring positions
- expert_ids: int32 [8192, 8], P(('dp', 'col')), may hold values from 0 to 31, all different within a row
- pair_order: int32 [8192, 8], P(('dp', 'col')), may hold values from 0 to 8191, as said below
Outputs:
- layer_out: bfloat16 [8192, 1024], P(('dp', 'col'), 'row')
- grad_in: float32 [8192, 1024], P(('dp', 'col'), 'row')
- grad_norm_gain: float32 [1024], P('row')
- grad_qkv: float32 [1024, 8, 256], P('row', 'col')
- grad_out: float32 [8, 128, 1024], P('col', None, 'row')
- grad_ffn_gain: float32 [1024], P('row')
- grad_router: float32 [1024, 32], P('row')
- grad_gate: float32 [32, 1024, 512], P(('dp', 'row'))
- grad_up: float32 [32, 1024, 512], P(('dp', 'row'))
- grad_down: float32 [32, 512, 1024], P(('dp', 'row'))
The draws below stay inside these ranges and needn't reach their ends.
Inputs may be any that keep to these rules, and one draw needn't show every extreme that they name: Within each block of 1024 consecutive tokens, read row by row, pair_order holds every number of 0 to 8191 once.
All inputs are finite; a program needn't handle non-finite values.
Results may differ from the reference program's by a relative error of at most 0.024.
Values may be sent and summed in bfloat16 or wider, within the bound.
A program may use at most 192 MiB of HBM per device.

```python
import math
import jax
import jax.numpy as jnp
import numpy as np
from jax import lax

D = 1024
HQ = 16
HK = 8
HD = 64
FF = 512
EXPERTS = 32
TOP = 8
LEN = 1024
DOCS = 4
TOK_DEV = 1024
TOKENS = 8192
SEQS = 8
CAP = 256


def draw_pair_order(key, part):
    block_total = TOKENS // TOK_DEV
    pair_count = TOK_DEV * TOP
    block_keys = jax.random.split(key, block_total)

    def one_block(block_key):
        return jax.random.permutation(block_key, pair_count)
    orders = jax.vmap(one_block)(block_keys)
    return orders.astype(jnp.int32).reshape(TOKENS, TOP)


def block_levels(stream_key, dims, shards, smallest, top_value):
    factor_of, own = 1.0, jax.random.fold_in(stream_key, 6)
    for dim, parts in shards:
        steps = jnp.exp(jax.random.uniform(jax.random.fold_in(own, dim), (parts,), jnp.float32, smallest / len(shards), top_value / len(shards)))
        factor_of = factor_of * jnp.repeat(steps, dims[dim] // parts).reshape([-1 if axis == dim else 1 for axis in range(len(dims))])
    return factor_of


def different_ones(rng, rows, number_of, top, lift):
    ranking = jax.random.permutation(jax.random.fold_in(rng, 1), number_of)
    favour = ranking
    for power in range(3):
        favour = favour * favour // number_of
    favour = favour * lift // number_of
    tickets = jax.random.randint(jax.random.fold_in(rng, 2), (rows, number_of), 0, 4096) + favour
    sure = jax.random.permutation(jax.random.fold_in(rng, 3), rows)[jnp.arange(number_of) % rows]
    tickets = jnp.where(jnp.arange(rows)[:, None] == sure[None, :], 1 << 14, tickets)
    score = tickets * number_of + jnp.arange(number_of)
    return lax.top_k(score.astype(jnp.int32), top)[1].astype(jnp.int32)


def split_up(number_of, total, limit, skew):
    weights = [(1 << 20) // math.isqrt(standing ** skew) + 1 for standing in range(2, number_of + 1)]
    surplus, given = total - limit - (number_of - 1), [1] * (number_of - 1)
    while surplus > 0:
        movable = [i for i in range(number_of - 1) if given[i] < limit]
        pool, left = sum([weights[i] for i in movable]), surplus
        for i in movable:
            extra = min(limit - given[i], max(1, left * weights[i] // pool), surplus)
            given[i] = given[i] + extra
            surplus = surplus - extra
    return np.array([limit] + given)


def ragged(stream_key, amount, total, bound, skew):
    if amount == 2:
        one = jax.random.randint(stream_key, (), max(1, total - bound), min(bound, total - 1) + 1)
        return jnp.stack([one, total - one])
    tallies = jnp.asarray(split_up(amount, total, bound, skew), jnp.int32)
    twos = (amount - 1) // 2
    donor, taker = tallies[1:1 + 2 * twos:2], tallies[2:2 + 2 * twos:2]
    room = jnp.minimum(donor - 1, bound - taker)
    passed = jax.random.randint(jax.random.fold_in(stream_key, 1), (twos,), 0, 1 << 20) % (room + 1)
    tallies = tallies.at[1:1 + 2 * twos:2].set(donor - passed).at[2:2 + 2 * twos:2].set(taker + passed)
    return tallies[jax.random.permutation(jax.random.fold_in(stream_key, 2), amount)]


def scatter_about(rng, shape, scale, limit, pieces=(), kind=jnp.bfloat16):
    level = block_levels(rng, shape, pieces, -0.22, 0.18) if pieces else 1.0
    values = jax.random.normal(rng, shape, jnp.float32) * scale * level
    return jnp.minimum(jnp.maximum(values, -limit), limit).astype(kind)


def setup_inputs(seed: int = 0) -> dict:
    seeds = jax.random.split(jax.random.key(seed), 14)
    hidden_in = scatter_about(seeds[0], (TOKENS, D), 1.0, 6.0, ((0, 8), (1, 4)))
    norm_gain = jnp.clip(1.0 + 0.1 * jax.random.normal(seeds[1], (D,), jnp.float32), 0.5, 1.5).astype(jnp.bfloat16)
    w_qkv = scatter_about(seeds[2], (D, HK, (HQ // HK + 2) * HD), D ** -0.5, 0.1875, ((0, 4), (1, 4)))
    w_out = scatter_about(seeds[3], (HK, HQ // HK * HD, D), (HQ * HD // 64) ** -0.5, 1.5, ((0, 4), (2, 4)))
    ffn_gain = jnp.clip(1.0 + 0.1 * jax.random.normal(seeds[4], (D,), jnp.float32), 0.5, 1.5).astype(jnp.bfloat16)
    router = scatter_about(seeds[5], (D, EXPERTS), (4 * D) ** -0.5, 0.09375, ((0, 4),))
    w_gate = scatter_about(seeds[6], (EXPERTS, D, FF), D ** -0.5, 0.1875, ((0, 8),))
    w_up = scatter_about(seeds[7], (EXPERTS, D, FF), D ** -0.5, 0.1875, ((0, 8),))
    w_down = scatter_about(seeds[8], (EXPERTS, FF, D), (FF // 16) ** -0.5, 1.0, ((0, 8),))
    cotangent = scatter_about(seeds[9], (TOKENS, D), 1.0, 6.0, ((0, 8), (1, 4)))
    segment_ids = jax.vmap(lambda own: jnp.searchsorted(jnp.cumsum(ragged(own, DOCS, LEN, LEN // 2, 2)), jnp.arange(LEN), side="right"))(jax.random.split(seeds[10], SEQS)).reshape((SEQS, LEN)).astype(jnp.int32)
    expert_ids = different_ones(seeds[11], TOKENS, EXPERTS, TOP, 2048)
    pair_order = draw_pair_order(jax.random.fold_in(seeds[13], 71), 0)
    return {"hidden_in": hidden_in, "norm_gain": norm_gain, "w_qkv": w_qkv, "w_out": w_out, "ffn_gain": ffn_gain, "router": router, "w_gate": w_gate, "w_up": w_up, "w_down": w_down, "cotangent": cotangent, "segment_ids": segment_ids, "expert_ids": expert_ids, "pair_order": pair_order}


@jax.custom_vjp
def low(v):
    return lax.optimization_barrier(v.astype(jnp.bfloat16)).astype(jnp.float32)

@jax.custom_vjp
def low_back(v):
    return v

def low_keep(v):
    return (low(v), None)

def low_pass(kept, grad):
    return (grad,)

def back_keep(v):
    return (v, None)

def back_low(kept, grad):
    return (low(grad),)
low.defvjp(low_keep, low_pass)
low_back.defvjp(back_keep, back_low)
EPSILON = 1e-06
ROPE_BASE = 10000.0
NEG_LARGE = -1e+30
HIGHEST = lax.Precision.HIGHEST

def rotate(values, cosine, sine_table):
    half_size = values.shape[-1] // 2
    lower_half = values[..., :half_size]
    upper_half = values[..., half_size:]
    return jnp.concatenate([lower_half * cosine - upper_half * sine_table, upper_half * cosine + lower_half * sine_table], axis=-1)

def rope_tables(length, head_size):
    positions = jnp.arange(length, dtype=jnp.float32)
    frequency = ROPE_BASE ** (-2.0 * jnp.arange(head_size // 2, dtype=jnp.float32) / head_size)
    angles = positions[:, None] * frequency[None, :]
    return (jnp.cos(angles), jnp.sin(angles))

def visible(segment_row):
    positions = jnp.arange(segment_row.shape[-1], dtype=jnp.int32)
    causal = positions[:, None] >= positions[None, :]
    return causal & (segment_row[..., :, None] == segment_row[..., None, :])

def pair_ranks(expert_ids, pair_order, block_rows):
    experts_flat = expert_ids.reshape(-1, block_rows * TOP)
    order_flat = pair_order.reshape(-1, block_rows * TOP)

    def one_block(experts_row, order_row):
        pair_count = experts_row.shape[0]
        by_order = jnp.zeros((pair_count,), jnp.int32).at[order_row].set(jnp.arange(pair_count, dtype=jnp.int32))
        sorted_experts = experts_row[by_order]
        onehot = (sorted_experts[:, None] == jnp.arange(EXPERTS, dtype=jnp.int32)[None, :]).astype(jnp.int32)
        before = (jnp.cumsum(onehot, axis=0) - onehot).astype(jnp.int32)
        sorted_rank = lax.optimization_barrier(jnp.sum(before * onehot, axis=1)).astype(jnp.int32)
        return sorted_rank[order_row]
    return jax.vmap(one_block)(experts_flat, order_flat).reshape(expert_ids.shape).astype(jnp.int32)

def attend_group(pack):
    qkv_seq, segment_seq = pack
    seq_count = qkv_seq.shape[0]
    group_size = HQ // HK
    cosine, sine_table = rope_tables(LEN, HD)
    queries = qkv_seq[..., :group_size * HD].reshape(seq_count, LEN, HK, group_size, HD)
    queries = low(rotate(queries, cosine[None, :, None, None, :], sine_table[None, :, None, None, :]))
    key_rot = low(rotate(qkv_seq[..., group_size * HD:(group_size + 1) * HD], cosine[None, :, None, :], sine_table[None, :, None, :]))
    value_low = low(qkv_seq[..., (group_size + 1) * HD:])
    scores = low_back(jnp.einsum('pqhgd,pkhd->phgqk', queries, key_rot, precision=HIGHEST) * HD ** (-0.5))
    allowed = visible(segment_seq)[:, None, None]
    scores = jnp.where(allowed, scores, NEG_LARGE)
    weights = jax.nn.softmax(scores, axis=-1)
    mixed_heads = jnp.einsum('phgqk,pkhd->pqhgd', low(weights), value_low, precision=HIGHEST)
    return low(low_back(mixed_heads)).reshape(seq_count, LEN, HK, group_size * HD)

def expert_apply(pack):
    expert_rows, gate_matrix, up_matrix, down_matrix = pack
    gate_pre = low_back(jnp.dot(expert_rows, gate_matrix, precision=HIGHEST))
    up_pre = low_back(jnp.dot(expert_rows, up_matrix, precision=HIGHEST))
    hidden = low(jax.nn.silu(gate_pre) * up_pre)
    return low(low_back(jnp.dot(hidden, down_matrix, precision=HIGHEST)))

def reference(hidden_in, norm_gain, w_qkv, w_out, ffn_gain, router, w_gate, w_up, w_down, cotangent, segment_ids, expert_ids, pair_order):
    block_count = TOKENS // TOK_DEV
    slot_rows = block_count * CAP
    total_slots = EXPERTS * slot_rows
    pair_rank = pair_ranks(expert_ids, pair_order, TOK_DEV)
    token_index = jnp.arange(TOKENS, dtype=jnp.int32)
    block_index = (token_index // TOK_DEV).astype(jnp.int32)
    pair_slot = jnp.where(pair_rank < CAP, expert_ids * slot_rows + block_index[:, None] * CAP + pair_rank, total_slots).astype(jnp.int32)
    slot_token = jnp.full((total_slots + 1,), TOKENS, jnp.int32).at[pair_slot.reshape(-1)].set(jnp.repeat(token_index, TOP))[:total_slots]
    pack_size = math.gcd(SEQS, max(1, 4096 // LEN))

    def forward(hidden, gain_one, qkv_weight, out_weight, gain_two, router_weight, gate_weight, up_weight, down_weight):
        rstd_one = lax.rsqrt(lax.optimization_barrier(jnp.mean(hidden * hidden, axis=1, keepdims=True)) + EPSILON)
        normed_one = low(hidden * rstd_one * gain_one)
        qkv = low_back(jnp.dot(normed_one, qkv_weight.reshape(D, -1), precision=HIGHEST))
        grouped = qkv.reshape(SEQS // pack_size, pack_size, LEN, HK, qkv_weight.shape[2])
        segments = segment_ids.reshape(SEQS // pack_size, pack_size, LEN)
        mixed_heads = lax.map(jax.checkpoint(attend_group), (grouped, segments)).reshape(TOKENS, HQ * HD)
        branch = low_back(jnp.dot(mixed_heads, out_weight.reshape(HQ * HD, D), precision=HIGHEST))
        resid = hidden + branch
        rstd_two = lax.rsqrt(lax.optimization_barrier(jnp.mean(resid * resid, axis=1, keepdims=True)) + EPSILON)
        normed_float = resid * rstd_two * gain_two
        logits = jnp.dot(normed_float, router_weight, precision=HIGHEST)
        gate_weights = jax.nn.softmax(jnp.take_along_axis(logits, expert_ids, axis=1), axis=1)
        normed_two = low(normed_float)
        padded = jnp.concatenate([normed_two, jnp.zeros((1, D), jnp.float32)], axis=0)
        expert_rows = low_back(padded[slot_token]).reshape(EXPERTS, slot_rows, D)
        expert_out = lax.map(jax.checkpoint(expert_apply), (expert_rows, gate_weight, up_weight, down_weight))
        slot_table = jnp.concatenate([expert_out.reshape(total_slots, D), jnp.zeros((1, D), jnp.float32)], axis=0)
        layer_sum = resid
        for column in range(TOP):
            layer_sum = layer_sum + gate_weights[:, column:column + 1] * slot_table[pair_slot[:, column]]
        return layer_sum
    layer_sum, pullback = jax.vjp(forward, hidden_in.astype(jnp.float32), norm_gain.astype(jnp.float32), w_qkv.astype(jnp.float32), w_out.astype(jnp.float32), ffn_gain.astype(jnp.float32), router.astype(jnp.float32), w_gate.astype(jnp.float32), w_up.astype(jnp.float32), w_down.astype(jnp.float32))
    grads = pullback(cotangent.astype(jnp.float32))
    return (layer_sum.astype(jnp.bfloat16), grads[0], grads[1], grads[2], grads[3], grads[4], grads[5], grads[6], grads[7], grads[8])
```

```python
import functools

import jax
import jax.numpy as jnp
import numpy as np
from jax import lax
from jax.experimental import pallas as pl
from jax.experimental.pallas import tpu as pltpu
from jax.sharding import PartitionSpec as P

D = 1024
HQ = 16
HK = 8
HD = 64
EXPERTS = 32
TOP = 8


EPSILON = 1e-06
ROPE_BASE = 10000.0
NEG_LARGE = -1e30
HIGHEST = lax.Precision.HIGHEST


def rotate(values, cosine, sine_table):
    half_size = values.shape[-1] // 2
    lower_half = values[..., :half_size]
    upper_half = values[..., half_size:]
    return jnp.concatenate(
        [
            lower_half * cosine - upper_half * sine_table,
            upper_half * cosine + lower_half * sine_table,
        ],
        axis=-1,
    )


def rotate_back(values, cosine, sine_table):
    half_size = values.shape[-1] // 2
    lower_half = values[..., :half_size]
    upper_half = values[..., half_size:]
    return jnp.concatenate(
        [
            lower_half * cosine + upper_half * sine_table,
            upper_half * cosine - lower_half * sine_table,
        ],
        axis=-1,
    )


def rope_tables(length, head_size):
    positions = jnp.arange(length, dtype=jnp.float32)
    frequency = ROPE_BASE ** (-2.0 * jnp.arange(head_size // 2, dtype=jnp.float32) / head_size)
    angles = positions[:, None] * frequency[None, :]
    return (jnp.cos(angles), jnp.sin(angles))


def visible(segment_row):
    positions = jnp.arange(segment_row.shape[-1], dtype=jnp.int32)
    causal = positions[:, None] >= positions[None, :]
    return causal & (segment_row[..., :, None] == segment_row[..., None, :])


def pair_ranks(expert_ids, pair_order, block_rows):
    experts_flat = expert_ids.reshape(-1, block_rows * TOP)
    order_flat = pair_order.reshape(-1, block_rows * TOP)

    def one_block(experts_row, order_row):
        pair_count = experts_row.shape[0]
        by_order = (
            jnp.zeros((pair_count,), jnp.int32)
            .at[order_row]
            .set(jnp.arange(pair_count, dtype=jnp.int32))
        )
        sorted_experts = experts_row[by_order]
        onehot = (sorted_experts[:, None] == jnp.arange(EXPERTS, dtype=jnp.int32)[None, :]).astype(
            jnp.int32
        )
        before = jnp.cumsum(onehot, axis=0) - onehot
        sorted_rank = jnp.sum(before * onehot, axis=1)
        return sorted_rank[order_row]

    return jax.vmap(one_block)(experts_flat, order_flat).reshape(expert_ids.shape)


def feature_total(values):
    return lax.psum(values, "row")


def tokens_by_col(values):
    return lax.all_gather(values, "col", axis=0, tiled=True)


def tokens_by_row(values):
    return lax.all_gather(values, "row", axis=0, tiled=True)


def col_scatter(term_fn, keep_rows):
    return lax.psum_scatter(
        term_fn(jnp.int32(0), keep_rows * lax.axis_size("col")),
        "col",
        scatter_dimension=0,
        tiled=True,
    )


def to_experts(outgoing):
    arrived = lax.all_to_all(outgoing, ("dp", "row"), split_axis=0, concat_axis=0, tiled=True)
    return arrived


def from_experts(outgoing):
    arrived = lax.all_to_all(outgoing, ("dp", "row"), split_axis=0, concat_axis=0, tiled=True)
    return arrived


def owner_layout(incoming, dp_count, row_count, exp_local):
    capacity = incoming.shape[1] // exp_local
    part_width = incoming.shape[2]
    sectioned = incoming.reshape(dp_count, row_count, exp_local, capacity, part_width)
    return sectioned.transpose(2, 0, 3, 1, 4).reshape(
        exp_local, dp_count * capacity, row_count * part_width
    )


def source_layout(owner_rows, dp_count, row_count):
    exp_local, slot_rows, full_width = owner_rows.shape
    capacity = slot_rows // dp_count
    part_width = full_width // row_count
    sectioned = owner_rows.reshape(exp_local, dp_count, capacity, row_count, part_width)
    return sectioned.transpose(1, 3, 0, 2, 4).reshape(
        dp_count * row_count, exp_local * capacity, part_width
    )


def attend_forward(pack):
    query_seq, key_seq, value_seq, segment_seq = pack
    score_scale = query_seq.shape[-1] ** (-0.5)
    scores = (
        jnp.einsum("qhgd,khd->hgqk", query_seq, key_seq, preferred_element_type=jnp.float32)
        * score_scale
    )
    scores = jnp.where(visible(segment_seq), scores, NEG_LARGE)
    row_max = jnp.max(scores, axis=-1, keepdims=True)
    weights = jnp.exp(scores - row_max)
    row_total = jnp.sum(weights, axis=-1, keepdims=True)
    weights_low = (weights / row_total).astype(jnp.bfloat16)
    mixed_seq = jnp.einsum(
        "hgqk,khd->qhgd", weights_low, value_seq, preferred_element_type=jnp.float32
    )
    return (mixed_seq.astype(jnp.bfloat16), row_max + jnp.log(row_total))


def attend_backward(pack):
    query_seq, key_seq, value_seq, segment_seq, log_total, grad_seq = pack
    score_scale = query_seq.shape[-1] ** (-0.5)
    scores = (
        jnp.einsum("qhgd,khd->hgqk", query_seq, key_seq, preferred_element_type=jnp.float32)
        * score_scale
    )
    scores = jnp.where(visible(segment_seq), scores, NEG_LARGE)
    weights = jnp.exp(scores - log_total)
    grad_weights = jnp.einsum(
        "qhgd,khd->hgqk", grad_seq, value_seq, preferred_element_type=jnp.float32
    )
    inner_sum = jnp.sum(weights * grad_weights, axis=-1, keepdims=True)
    grad_scores = (weights * (grad_weights - inner_sum)).astype(jnp.bfloat16)
    grad_values = jnp.einsum(
        "hgqk,qhgd->khd", weights.astype(jnp.bfloat16), grad_seq, preferred_element_type=jnp.float32
    )
    grad_query = (
        jnp.einsum("hgqk,khd->qhgd", grad_scores, key_seq, preferred_element_type=jnp.float32)
        * score_scale
    )
    grad_key = (
        jnp.einsum("hgqk,qhgd->khd", grad_scores, query_seq, preferred_element_type=jnp.float32)
        * score_scale
    )
    return (grad_query, grad_key, grad_values)


def on_device(
    hidden_in,
    norm_gain,
    w_qkv,
    w_out,
    ffn_gain,
    router,
    w_gate,
    w_up,
    w_down,
    cotangent,
    segment_ids,
    expert_ids,
    pair_order,
):
    dp_count = lax.axis_size("dp")
    row_count = lax.axis_size("row")
    owners = dp_count * row_count
    tok_rows, part_width = hidden_in.shape
    seq_count, length = segment_ids.shape
    att_rows = seq_count * length
    kv_local = w_qkv.shape[1]
    group_size = HQ // HK
    exp_local = w_gate.shape[0]
    capacity = tok_rows * TOP // EXPERTS
    total_slots = EXPERTS * capacity
    resid_in = hidden_in.astype(jnp.float32)
    gain_one = norm_gain.astype(jnp.float32)
    rstd_one = lax.rsqrt(feature_total(jnp.sum(resid_in * resid_in, axis=1)) / D + EPSILON)
    normed_one = (resid_in * rstd_one[:, None] * gain_one).astype(jnp.bfloat16)
    group_rows = tokens_by_col(normed_one)
    qkv_flat = w_qkv.reshape(part_width, -1)
    picked = group_rows
    qkv_local = lax.psum_scatter(
        jnp.dot(picked, qkv_flat, preferred_element_type=jnp.float32),
        "row",
        scatter_dimension=0,
        tiled=True,
    )
    qkv_local = qkv_local.reshape(seq_count, length, kv_local, -1)
    cosine, sine_table = rope_tables(length, HD)
    queries = qkv_local[..., : group_size * HD].reshape(seq_count, length, kv_local, group_size, HD)
    query_rot = rotate(
        queries, cosine[None, :, None, None, :], sine_table[None, :, None, None, :]
    ).astype(jnp.bfloat16)
    key_rot = rotate(
        qkv_local[..., group_size * HD : (group_size + 1) * HD],
        cosine[None, :, None, :],
        sine_table[None, :, None, :],
    ).astype(jnp.bfloat16)
    value_low = qkv_local[..., (group_size + 1) * HD :].astype(jnp.bfloat16)
    mixed_heads, log_total = lax.map(attend_forward, (query_rot, key_rot, value_low, segment_ids))
    mixed_rows = tokens_by_row(mixed_heads.reshape(att_rows, -1))
    out_flat = w_out.reshape(-1, part_width)

    def out_term(first_row, block_rows):
        return jnp.dot(mixed_rows, out_flat, preferred_element_type=jnp.float32)

    resid_mid = resid_in + col_scatter(out_term, tok_rows)
    gain_two = ffn_gain.astype(jnp.float32)
    router_float = router.astype(jnp.float32)
    square_two, logit_part = (
        lax.psum(jnp.sum(resid_mid * resid_mid, axis=1).astype(jnp.bfloat16), "row").astype(
            jnp.float32
        ),
        lax.psum(
            jnp.dot(resid_mid * gain_two, router_float, precision=HIGHEST).astype(jnp.bfloat16),
            "row",
        ).astype(jnp.float32),
    )
    rstd_two = lax.rsqrt(square_two / D + EPSILON)
    logits = logit_part * rstd_two[:, None]
    normed_float = resid_mid * rstd_two[:, None] * gain_two
    normed_two = normed_float.astype(jnp.bfloat16)
    choose = (expert_ids[:, :, None] == jnp.arange(EXPERTS, dtype=jnp.int32)[None, None, :]).astype(
        jnp.float32
    )
    gate_weights = jax.nn.softmax(jnp.sum(choose * logits[:, None, :], axis=2), axis=1)
    pair_rank = pair_ranks(expert_ids, pair_order, tok_rows)
    pair_slot = jnp.where(pair_rank < capacity, expert_ids * capacity + pair_rank, total_slots)
    pair_index = jnp.arange(tok_rows * TOP, dtype=jnp.int32)
    slot_pair = (
        jnp.full((total_slots + 1,), tok_rows * TOP, jnp.int32)
        .at[pair_slot.reshape(-1)]
        .set(pair_index)[:total_slots]
    )
    padded_two = jnp.concatenate([normed_two, jnp.zeros((1, part_width), jnp.bfloat16)], axis=0)
    outgoing = padded_two[slot_pair // TOP].reshape(owners, exp_local * capacity, part_width)
    expert_rows = owner_layout(to_experts(outgoing), dp_count, row_count, exp_local)
    gate_pre = jnp.einsum("erd,edf->erf", expert_rows, w_gate, preferred_element_type=jnp.float32)
    up_pre = jnp.einsum("erd,edf->erf", expert_rows, w_up, preferred_element_type=jnp.float32)
    hidden = (jax.nn.silu(gate_pre) * up_pre).astype(jnp.bfloat16)
    expert_out = jnp.einsum(
        "erf,efd->erd", hidden, w_down, preferred_element_type=jnp.float32
    ).astype(jnp.bfloat16)
    returned = from_experts(source_layout(expert_out, dp_count, row_count))
    slot_table = jnp.concatenate(
        [returned.reshape(total_slots, part_width), jnp.zeros((1, part_width), jnp.bfloat16)],
        axis=0,
    )
    pair_rows = slot_table[pair_slot].astype(jnp.float32)
    layer_sum = resid_mid + jnp.einsum("tk,tkd->td", gate_weights, pair_rows, precision=HIGHEST)
    grad_top = cotangent.astype(jnp.float32)
    grad_gates = lax.psum(jnp.einsum("td,tkd->tk", grad_top, pair_rows, precision=HIGHEST), "row")
    pair_grad = (gate_weights[:, :, None] * grad_top[:, None, :]).astype(jnp.bfloat16)
    grad_padded = jnp.concatenate(
        [pair_grad.reshape(tok_rows * TOP, part_width), jnp.zeros((1, part_width), jnp.bfloat16)],
        axis=0,
    )
    outgoing_grad = grad_padded[slot_pair].reshape(owners, exp_local * capacity, part_width)
    grad_rows = owner_layout(to_experts(outgoing_grad), dp_count, row_count, exp_local)
    grad_hidden = jnp.einsum("erd,efd->erf", grad_rows, w_down, preferred_element_type=jnp.float32)
    sigmoid_gate = jax.nn.sigmoid(gate_pre)
    grad_gate_pre = (
        grad_hidden * up_pre * sigmoid_gate * (1.0 + gate_pre * (1.0 - sigmoid_gate))
    ).astype(jnp.bfloat16)
    grad_up_pre = (grad_hidden * gate_pre * sigmoid_gate).astype(jnp.bfloat16)
    grad_down_local = jnp.einsum(
        "erf,erd->efd", hidden, grad_rows, preferred_element_type=jnp.float32
    )
    grad_gate_local = jnp.einsum(
        "erd,erf->edf", expert_rows, grad_gate_pre, preferred_element_type=jnp.float32
    )
    grad_up_local = jnp.einsum(
        "erd,erf->edf", expert_rows, grad_up_pre, preferred_element_type=jnp.float32
    )
    rows_back = jnp.einsum(
        "erf,edf->erd", grad_gate_pre, w_gate, preferred_element_type=jnp.float32
    )
    rows_back = (
        rows_back
        + jnp.einsum("erf,edf->erd", grad_up_pre, w_up, preferred_element_type=jnp.float32)
    ).astype(jnp.bfloat16)
    returned_grad = from_experts(source_layout(rows_back, dp_count, row_count))
    grad_table = jnp.concatenate(
        [returned_grad.reshape(total_slots, part_width), jnp.zeros((1, part_width), jnp.bfloat16)],
        axis=0,
    )
    inner_gate = jnp.sum(gate_weights * grad_gates, axis=1, keepdims=True)
    grad_chosen = gate_weights * (grad_gates - inner_gate)
    grad_logits = jnp.einsum("tk,tke->te", grad_chosen, choose, precision=HIGHEST)
    grad_router_part = jnp.einsum("td,te->de", normed_float, grad_logits, precision=HIGHEST)
    grad_normed = jnp.sum(grad_table[pair_slot].astype(jnp.float32), axis=1)
    grad_normed = grad_normed + jnp.einsum(
        "te,de->td", grad_logits, router_float, precision=HIGHEST
    )
    grad_gain_two_part = jnp.sum(grad_normed * resid_mid * rstd_two[:, None], axis=0)
    scaled_two = grad_normed * gain_two
    inner_two = feature_total(jnp.sum(scaled_two * resid_mid, axis=1))
    grad_resid = (
        grad_top
        + rstd_two[:, None] * scaled_two
        - resid_mid * (rstd_two * rstd_two * rstd_two * inner_two / D)[:, None]
    )
    branch_rows = tokens_by_col(grad_resid.astype(jnp.bfloat16))
    grad_out_local = jnp.einsum(
        "tc,td->cd", mixed_rows, branch_rows, preferred_element_type=jnp.float32
    ).reshape(w_out.shape)
    picked = branch_rows
    grad_mixed = lax.psum_scatter(
        jnp.einsum("td,cd->tc", picked, out_flat, preferred_element_type=jnp.float32).astype(
            jnp.bfloat16
        ),
        "row",
        scatter_dimension=0,
        tiled=True,
    ).astype(jnp.float32)
    grad_mixed = grad_mixed.astype(jnp.bfloat16).reshape(
        seq_count, length, kv_local, group_size, HD
    )
    grad_query, grad_key, grad_values = lax.map(
        attend_backward, (query_rot, key_rot, value_low, segment_ids, log_total, grad_mixed)
    )
    grad_query = rotate_back(
        grad_query, cosine[None, :, None, None, :], sine_table[None, :, None, None, :]
    )
    grad_key = rotate_back(grad_key, cosine[None, :, None, :], sine_table[None, :, None, :])
    grad_qkv_pre = jnp.concatenate(
        [grad_query.reshape(seq_count, length, kv_local, group_size * HD), grad_key, grad_values],
        axis=-1,
    )
    grad_qkv_pre = grad_qkv_pre.astype(jnp.bfloat16).reshape(att_rows, -1)
    qkv_rows = tokens_by_row(grad_qkv_pre)
    grad_qkv_local = jnp.einsum(
        "td,tc->dc", group_rows, qkv_rows, preferred_element_type=jnp.float32
    ).reshape(w_qkv.shape)

    def normed_term(first_row, block_rows):
        return jnp.einsum("tc,dc->td", qkv_rows, qkv_flat, preferred_element_type=jnp.float32)

    grad_normed_one = col_scatter(normed_term, tok_rows)
    grad_gain_one_part = jnp.sum(grad_normed_one * resid_in * rstd_one[:, None], axis=0)
    scaled_one = grad_normed_one * gain_one
    inner_one = feature_total(jnp.sum(scaled_one * resid_in, axis=1))
    grad_in = (
        grad_resid
        + rstd_one[:, None] * scaled_one
        - resid_in * (rstd_one * rstd_one * rstd_one * inner_one / D)[:, None]
    )
    col_sums = (
        lax.psum(grad_gate_local.astype(jnp.bfloat16), "col").astype(jnp.float32),
        lax.psum(grad_up_local.astype(jnp.bfloat16), "col").astype(jnp.float32),
        lax.psum(grad_down_local.astype(jnp.bfloat16), "col").astype(jnp.float32),
        lax.psum(grad_router_part.astype(jnp.bfloat16), "col").astype(jnp.float32),
        lax.psum(grad_gain_one_part.astype(jnp.bfloat16), "col").astype(jnp.float32),
        lax.psum(grad_gain_two_part.astype(jnp.bfloat16), "col").astype(jnp.float32),
    )
    dp_sums = (
        lax.psum(grad_qkv_local.astype(jnp.bfloat16), "dp").astype(jnp.float32),
        lax.psum(grad_out_local.astype(jnp.bfloat16), "dp").astype(jnp.float32),
        lax.psum(col_sums[3].astype(jnp.bfloat16), "dp").astype(jnp.float32),
        lax.psum(col_sums[4].astype(jnp.bfloat16), "dp").astype(jnp.float32),
        lax.psum(col_sums[5].astype(jnp.bfloat16), "dp").astype(jnp.float32),
    )
    return (
        layer_sum.astype(jnp.bfloat16),
        grad_in,
        dp_sums[3],
        dp_sums[0],
        dp_sums[1],
        dp_sums[4],
        dp_sums[2],
        col_sums[0],
        col_sums[1],
        col_sums[2],
    )

WINDOW = 512
BLOCK_Q = 256
LANES = 128
F32 = jnp.float32
LOW = jnp.bfloat16
VMEM_BYTES = 67_000_000


def dot_nn(a, b):
    return jnp.dot(a, b, preferred_element_type=F32)


def dot_nt(a, b):
    return lax.dot_general(a, b, (((1,), (1,)), ((), ())), preferred_element_type=F32)


def dot_tn(a, b):
    return lax.dot_general(a, b, (((0,), (0,)), ((), ())), preferred_element_type=F32)


def rope_lanes(length):
    positions = np.arange(length, dtype=np.float32)
    frequency = (ROPE_BASE ** (-2.0 * np.arange(HD // 2, dtype=np.float32) / HD)).astype(np.float32)
    angles = (positions[:, None] * frequency[None, :]).astype(np.float32)
    cosine, sine = np.cos(angles), np.sin(angles)
    signed = np.concatenate([-sine, sine], axis=1)
    double = np.concatenate([cosine, cosine], axis=1)
    ones, zeros = np.ones_like(double), np.zeros_like(double)
    return np.stack(
        [
            np.concatenate([double, double], axis=1),
            np.concatenate([signed, signed], axis=1),
            np.concatenate([double, ones], axis=1),
            np.concatenate([signed, zeros], axis=1),
        ]
    ).astype(np.float32)


def swap_halves(values):
    half = HD // 2
    lane = lax.broadcasted_iota(jnp.int32, values.shape, 1)
    ahead = pltpu.roll(values, LANES - half, 1)
    behind = pltpu.roll(values, half, 1)
    return jnp.where(lane % HD < half, ahead, behind)


def window_mask(seg_col, seg_row, q_start, k_start):
    shape = (seg_col.shape[0], seg_row.shape[1])
    q_at = lax.broadcasted_iota(jnp.int32, shape, 0) + q_start
    k_at = lax.broadcasted_iota(jnp.int32, shape, 1) + k_start
    return (q_at >= k_at) & (seg_col == seg_row)


def attend_forward_kernel(
    h_ref, gain_ref, w_ref, seg_col_ref, seg_row_ref, tab_ref,
    mixed_ref, normed_ref, q_ref, k_ref, v_ref, lse_ref,
):
    parts, length, width = h_ref.shape
    kv_heads = k_ref.shape[0]
    features = parts * width

    @pl.loop(0, length // BLOCK_Q)
    def _(chunk):
        rows = pl.ds(pl.multiple_of(chunk * BLOCK_Q, BLOCK_Q), BLOCK_Q)
        total = jnp.zeros((BLOCK_Q, 1), F32)
        for part in range(parts):
            piece = h_ref[part, rows, :].astype(F32)
            total = total + jnp.sum(piece * piece, axis=1, keepdims=True)
        rstd = lax.rsqrt(total / features + EPSILON)
        for part in range(parts):
            piece = h_ref[part, rows, :].astype(F32)
            normed_ref[rows, part * width : (part + 1) * width] = (
                piece * rstd * gain_ref[part]
            ).astype(LOW)
        qkv = dot_nn(normed_ref[rows, :], w_ref[...])
        for head in range(kv_heads):
            base = head * 4 * HD
            queries = qkv[:, base : base + LANES]
            queries = queries * tab_ref[0, rows, :] + swap_halves(queries) * tab_ref[1, rows, :]
            others = qkv[:, base + LANES : base + 2 * LANES]
            others = others * tab_ref[2, rows, :] + swap_halves(others) * tab_ref[3, rows, :]
            q_ref[2 * head, rows, :] = queries[:, :HD].astype(LOW)
            q_ref[2 * head + 1, rows, :] = queries[:, HD:].astype(LOW)
            k_ref[head, rows, :] = others[:, :HD].astype(LOW)
            v_ref[head, rows, :] = others[:, HD:].astype(LOW)

    scale = HD**-0.5
    lane = lax.broadcasted_iota(jnp.int32, (BLOCK_Q, LANES), 1)
    for block in range(length // BLOCK_Q):
        q_start = block * BLOCK_Q
        k_start = max(0, q_start - WINDOW)
        q_rows, k_rows = slice(q_start, q_start + BLOCK_Q), slice(k_start, q_start + BLOCK_Q)
        mask = window_mask(seg_col_ref[q_rows, :], seg_row_ref[:, k_rows], q_start, k_start)
        logs = jnp.zeros((BLOCK_Q, LANES), F32)
        for head in range(2 * kv_heads):
            scores = dot_nt(q_ref[head, q_rows, :], k_ref[head // 2, k_rows, :]) * scale
            scores = jnp.where(mask, scores, NEG_LARGE)
            top = jnp.max(scores, axis=1, keepdims=True)
            weights = jnp.exp(scores - top)
            total = jnp.sum(weights, axis=1, keepdims=True)
            out = dot_nn(weights.astype(LOW), v_ref[head // 2, k_rows, :]) / total
            mixed_ref[q_rows, head * HD : (head + 1) * HD] = out.astype(LOW)
            logs = jnp.where(lane == head, top + jnp.log(total), logs)
        lse_ref[q_rows, :] = logs


def attend_backward_kernel(
    gb_ref, wo_ref, wq_ref, normed_ref, mixed_ref, q_ref, k_ref, v_ref, lse_ref, seg_col_ref, seg_row_ref, tab_ref,
    back_ref, grads_ref,
    gm_ref, dqkv_ref, dk_ref, dv_ref, low_ref,
):
    parts, length, width = gb_ref.shape
    kv_heads = k_ref.shape[0]
    scale = HD**-0.5
    dk_ref[...] = jnp.zeros_like(dk_ref)
    dv_ref[...] = jnp.zeros_like(dv_ref)

    @pl.loop(0, length // BLOCK_Q)
    def _(chunk):
        rows = pl.ds(pl.multiple_of(chunk * BLOCK_Q, BLOCK_Q), BLOCK_Q)
        total = dot_nt(gb_ref[0, rows, :], wo_ref[0])
        for part in range(1, parts):
            total = total + dot_nt(gb_ref[part, rows, :], wo_ref[part])
        for head in range(2 * kv_heads):
            gm_ref[head, rows, :] = total[:, head * HD : (head + 1) * HD].astype(LOW)

    for block in range(length // BLOCK_Q):
        q_start = block * BLOCK_Q
        k_start = max(0, q_start - WINDOW)
        q_rows, k_rows = slice(q_start, q_start + BLOCK_Q), slice(k_start, q_start + BLOCK_Q)
        mask = window_mask(seg_col_ref[q_rows, :], seg_row_ref[:, k_rows], q_start, k_start)
        logs = lse_ref[q_rows, :]
        for kv in range(kv_heads):
            keys, vals = k_ref[kv, k_rows, :], v_ref[kv, k_rows, :]
            for head in (2 * kv, 2 * kv + 1):
                queries, grad = q_ref[head, q_rows, :], gm_ref[head, q_rows, :]
                scores = dot_nt(queries, keys) * scale
                weights = jnp.where(mask, jnp.exp(scores - logs[:, head : head + 1]), 0.0)
                grad_weights = dot_nt(grad, vals)
                inner = jnp.sum(weights * grad_weights, axis=1, keepdims=True)
                grad_scores = (weights * (grad_weights - inner)).astype(LOW)
                dv_ref[kv, k_rows, :] += dot_tn(weights.astype(LOW), grad)
                dk_ref[kv, k_rows, :] += dot_tn(grad_scores, queries)
                lanes = kv * 4 * HD + (head % 2) * HD
                dqkv_ref[q_rows, lanes : lanes + HD] = dot_nn(grad_scores, keys) * scale

    @pl.loop(0, length // BLOCK_Q)
    def _(chunk):
        rows = pl.ds(pl.multiple_of(chunk * BLOCK_Q, BLOCK_Q), BLOCK_Q)
        for kv in range(kv_heads):
            base = kv * 4 * HD
            queries = dqkv_ref[rows, base : base + LANES]
            queries = queries * tab_ref[0, rows, :] - swap_halves(queries) * tab_ref[1, rows, :]
            others = jnp.concatenate([dk_ref[kv, rows, :] * scale, dv_ref[kv, rows, :]], axis=1)
            others = others * tab_ref[2, rows, :] - swap_halves(others) * tab_ref[3, rows, :]
            low_ref[rows, base : base + LANES] = queries.astype(LOW)
            low_ref[rows, base + LANES : base + 2 * LANES] = others.astype(LOW)
        for part in range(parts):
            back_ref[part, rows, :] = dot_nt(low_ref[rows, :], wq_ref[part]).astype(LOW)

    columns = low_ref.shape[1]
    for part in range(parts):
        grads_ref[part, :, :columns] = dot_tn(
            normed_ref[:, part * width : (part + 1) * width], low_ref[...]
        ).astype(LOW)
        grads_ref[part, :, columns:] = dot_tn(mixed_ref[...], gb_ref[part]).astype(LOW)


def moe_kernel(
    counts, res_hbm, cot_hbm, rk_ref, gain_ref, router_ref, wg_ref, wu_ref, wd_ref,
    y_hbm, pb_hbm, gg_ref, gates_out_ref, logits_out_ref, dg_ref, du_ref, dd_ref,
    res_ref, cot_ref, x_ref, gate_ref, pick_ref, eo_ref, back_ref, stage_ref, sems, out_sem,
):
    dp_count, row_count, col_count = counts
    blocks = dp_count * col_count
    my_dp, my_row, my_col = lax.axis_index("dp"), lax.axis_index("row"), lax.axis_index("col")
    experts, features, hidden_width = wg_ref.shape
    _, parts, length, width = res_hbm.shape
    capacity = pick_ref.shape[0] // experts
    first_expert = (my_dp * row_count + my_row) * experts

    def block_of(step):
        other = step - dp_count
        far = dp_count <= step
        dp_at = jnp.where(far, other // (col_count - 1), step)
        col_at = jnp.where(far, lax.rem(my_col + 1 + lax.rem(other, col_count - 1), col_count), my_col)
        return dp_at * col_count + col_at

    def fetch(step):
        b = block_of(step)
        slot = lax.rem(step, 2)
        return (
            pltpu.make_async_copy(res_hbm.at[b], res_ref, sems.at[0]),
            pltpu.make_async_copy(cot_hbm.at[b], cot_ref.at[slot], sems.at[1 + slot]),
        )

    for copy in fetch(0):
        copy.start()
    dg_ref[...] = jnp.zeros_like(dg_ref)
    du_ref[...] = jnp.zeros_like(du_ref)
    dd_ref[...] = jnp.zeros_like(dd_ref)

    @pl.loop(0, blocks)
    def _(step):
        b = block_of(step)
        slot = lax.rem(step, 2)
        for copy in fetch(step):
            copy.wait()

        @pl.loop(0, length // BLOCK_Q)
        def _(chunk):
            rows = pl.ds(pl.multiple_of(chunk * BLOCK_Q, BLOCK_Q), BLOCK_Q)
            total = jnp.zeros((BLOCK_Q, 1), F32)
            for part in range(parts):
                piece = res_ref[part, rows, :].astype(F32)
                total = total + jnp.sum(piece * piece, axis=1, keepdims=True)
            rstd = lax.rsqrt(total / features + EPSILON)
            for part in range(parts):
                piece = res_ref[part, rows, :].astype(F32)
                x_ref[rows, part * width : (part + 1) * width] = (
                    piece * rstd * gain_ref[part]
                ).astype(LOW)

        @pl.when(step + 1 < blocks)
        def _():
            for copy in fetch(step + 1):
                copy.start()

        logits = dot_nt(router_ref[...], x_ref[...])
        chosen = rk_ref[b] >= 0.0
        shown = jnp.where(chosen, logits, NEG_LARGE)
        weights = jnp.where(chosen, jnp.exp(shown - jnp.max(shown, axis=0, keepdims=True)), 0.0)
        gates = weights / jnp.sum(weights, axis=0, keepdims=True)
        gate_ref[...] = gates

        @pl.when(step < dp_count)
        def _():
            gates_out_ref[step] = gates
            logits_out_ref[step] = logits

        @pl.loop(0, experts)
        def _(e):
            rank_row = rk_ref[b, pl.ds(first_expert + e, 1), :]
            gate_row = gate_ref[pl.ds(first_expert + e, 1), :]
            at = lax.broadcasted_iota(jnp.int32, (capacity, length), 0).astype(F32)
            here = at == rank_row
            pick = here.astype(F32).astype(LOW)
            gate_slot = jnp.sum(jnp.where(here, gate_row, 0.0), axis=1, keepdims=True)
            x = dot_nn(pick, x_ref[...]).astype(LOW)
            g = jnp.concatenate([dot_nn(pick, cot_ref[slot, part]) for part in range(parts)], axis=1)
            pair_grad = (g * gate_slot).astype(LOW)
            gate_pre = dot_nn(x, wg_ref[e])
            up_pre = dot_nn(x, wu_ref[e])
            sig = 1.0 / (1.0 + jnp.exp(-gate_pre))
            silu = gate_pre * sig
            hidden = (silu * up_pre).astype(LOW)
            grad_hidden = dot_nt(pair_grad, wd_ref[e])
            grad_gate = (grad_hidden * up_pre * (sig * (1.0 + gate_pre * (1.0 - sig)))).astype(LOW)
            grad_up = (grad_hidden * silu).astype(LOW)

            @pl.when(step < dp_count)
            def _():
                slots = pl.ds(pl.multiple_of(e * capacity, capacity), capacity)
                out = dot_nn(hidden, wd_ref[e]).astype(LOW).astype(F32)
                along = jnp.sum(g * out, axis=1, keepdims=True)
                gg_ref[step, pl.ds(e, 1), :] = jnp.sum(
                    jnp.where(here, along, 0.0), axis=0, keepdims=True
                )
                pick_ref[slots, :] = pick
                eo_ref[slots, :] = (out * gate_slot).astype(LOW)
                back_ref[slots, :] = (
                    dot_nt(grad_gate, wg_ref[e]) + dot_nt(grad_up, wu_ref[e])
                ).astype(LOW)

            dd_ref[e] += dot_tn(hidden, pair_grad)
            dg_ref[e] += dot_tn(x, grad_gate)
            du_ref[e] += dot_tn(x, grad_up)

        @pl.when(step < dp_count)
        def _():
            for source, target in ((back_ref, pb_hbm), (eo_ref, y_hbm)):
                for part in range(parts):
                    cols = slice(part * width, (part + 1) * width)
                    stage_ref[part] = dot_tn(pick_ref[...], source[:, cols]).astype(LOW)
                copy = pltpu.make_async_copy(stage_ref, target.at[step], out_sem)
                copy.start()
                copy.wait()


def fast_device(
    hidden_in, norm_gain, w_qkv, w_out, ffn_gain, router, w_gate, w_up, w_down, cotangent,
    segment_ids, expert_ids, pair_order,
):
    dp_count, row_count, col_count = (lax.axis_size(name) for name in ("dp", "row", "col"))
    my_dp, my_row, my_col = (lax.axis_index(name) for name in ("dp", "row", "col"))
    length, width = hidden_in.shape
    kv_local = w_qkv.shape[1]
    head_width = kv_local * (HQ // HK) * HD
    qkv_width = kv_local * (HQ // HK + 2) * HD
    exp_local, _, hidden_width = w_gate.shape
    capacity = length * TOP // EXPERTS
    blocks = dp_count * col_count
    vmem = pl.BlockSpec(memory_space=pltpu.VMEM)
    hbm = pl.BlockSpec(memory_space=pl.ANY)
    params = pltpu.CompilerParams(vmem_limit_bytes=VMEM_BYTES)

    ids_t, order_t = expert_ids.T, pair_order.T
    experts_here = EXPERTS // row_count
    mine = my_row * experts_here + jnp.arange(experts_here, dtype=jnp.int32)
    match = ids_t[None, :, :] == mine[:, None, None]
    chosen = jnp.any(match, axis=1)
    orders = jnp.sum(jnp.where(match, order_t[None], 0), axis=1)
    orders = jnp.where(chosen, orders, length * TOP)
    ranks = jnp.sum((orders[:, :, None] < orders[:, None, :]).astype(jnp.int32), axis=1)
    ranks = jnp.where(chosen, jnp.minimum(ranks, capacity), -1).astype(F32)
    rank_all = lax.all_gather(ranks, ("dp", "row", "col"), axis=0)
    rank_all = (
        rank_all.reshape(dp_count, row_count, col_count, experts_here, length)
        .transpose(0, 2, 1, 3, 4)
        .reshape(blocks, EXPERTS, length)
    )
    cot_all = lax.all_gather(cotangent, ("dp", "col", "row"), axis=0).reshape(
        blocks, row_count, length, width
    )

    own = jnp.concatenate([w_qkv.reshape(width, qkv_width), w_out.reshape(head_width, width)], axis=1)
    own_cols = lax.all_gather(own, "col", axis=0)
    own_rows = lax.all_to_all(own_cols, "row", split_axis=0, concat_axis=0, tiled=True)
    wq_rows = own_rows[:, :, :qkv_width]
    wo_rows = own_rows[:, :, qkv_width:]
    wo_cols = own_cols[:, :, qkv_width:]
    gains = lax.all_gather(
        jnp.concatenate([norm_gain[None], ffn_gain[None], router.T], axis=0), "row", axis=0
    ).astype(F32)
    gain_one, gain_two = gains[:, 0:1], gains[:, 1:2]
    router_t = gains[:, 2:].transpose(1, 0, 2).reshape(EXPERTS, -1).astype(LOW)
    segments = lax.dynamic_index_in_dim(
        lax.all_gather(segment_ids, "row", axis=0), my_col, axis=0, keepdims=False
    )
    seg_row, seg_col = segments.reshape(1, length), segments.reshape(length, 1)
    tables = jnp.asarray(rope_lanes(length))

    hidden_all = lax.all_gather(hidden_in, "row", axis=0)
    mixed, normed_one, query_rot, key_rot, value_low, logs = pl.pallas_call(
        attend_forward_kernel,
        out_shape=(
            jax.ShapeDtypeStruct((length, head_width), LOW),
            jax.ShapeDtypeStruct((length, D), LOW),
            jax.ShapeDtypeStruct((2 * kv_local, length, HD), LOW),
            jax.ShapeDtypeStruct((kv_local, length, HD), LOW),
            jax.ShapeDtypeStruct((kv_local, length, HD), LOW),
            jax.ShapeDtypeStruct((length, LANES), F32),
        ),
        in_specs=[vmem] * 6,
        out_specs=[vmem] * 6,
        compiler_params=params,
        name="attend_forward",
    )(hidden_all, gain_one, wq_rows.reshape(D, qkv_width), seg_col, seg_row, tables)

    mixed_all = lax.all_gather(mixed, "row", axis=0)
    resid_in = hidden_in.astype(F32)
    branch = jnp.einsum("rtc,rcd->td", mixed_all, wo_cols, preferred_element_type=F32)
    resid_mid = resid_in + branch
    resid_low = resid_mid.astype(LOW)
    resid_all = lax.all_gather(resid_low, ("dp", "col", "row"), axis=0).reshape(
        blocks, row_count, length, width
    )

    y_part, pb_part, gg_part, gates_plane, logits_plane, grad_gate, grad_up, grad_down = pl.pallas_call(
        functools.partial(moe_kernel, (dp_count, row_count, col_count)),
        out_shape=(
            jax.ShapeDtypeStruct((dp_count, row_count, length, width), LOW),
            jax.ShapeDtypeStruct((dp_count, row_count, length, width), LOW),
            jax.ShapeDtypeStruct((dp_count, exp_local, length), F32),
            jax.ShapeDtypeStruct((dp_count, EXPERTS, length), F32),
            jax.ShapeDtypeStruct((dp_count, EXPERTS, length), F32),
            jax.ShapeDtypeStruct(w_gate.shape, F32),
            jax.ShapeDtypeStruct(w_up.shape, F32),
            jax.ShapeDtypeStruct(w_down.shape, F32),
        ),
        in_specs=[hbm, hbm] + [vmem] * 6,
        out_specs=[hbm, hbm] + [vmem] * 6,
        scratch_shapes=[
            pltpu.VMEM((row_count, length, width), LOW),
            pltpu.VMEM((2, row_count, length, width), LOW),
            pltpu.VMEM((length, D), LOW),
            pltpu.VMEM((EXPERTS, length), F32),
            pltpu.VMEM((exp_local * capacity, length), LOW),
            pltpu.VMEM((exp_local * capacity, D), LOW),
            pltpu.VMEM((exp_local * capacity, D), LOW),
            pltpu.VMEM((row_count, length, width), LOW),
            pltpu.SemaphoreType.DMA((3,)),
            pltpu.SemaphoreType.DMA,
        ],
        compiler_params=params,
        name="experts",
    )(resid_all, cot_all, rank_all, gain_two, router_t, w_gate, w_up, w_down)

    grad_expert = lax.psum_scatter(
        pb_part.reshape(-1, width), ("dp", "row"), scatter_dimension=0, tiled=True
    ).astype(F32)
    mixture = lax.psum_scatter(
        y_part.reshape(-1, width), ("dp", "row"), scatter_dimension=0, tiled=True
    ).astype(F32)
    layer_out = (resid_mid + mixture).astype(LOW)

    gg_all = lax.all_gather(gg_part, ("dp", "row"), axis=0)
    gg = lax.dynamic_index_in_dim(gg_all, my_dp, axis=1, keepdims=False).reshape(EXPERTS, length)
    gates = lax.dynamic_index_in_dim(gates_plane, my_dp, axis=0, keepdims=False)
    inner_gate = jnp.sum(gates * gg, axis=0, keepdims=True)
    grad_logits = gates * (gg - inner_gate)

    gain_float = ffn_gain.astype(F32)
    router_float = router.astype(F32)
    block_all = lax.dynamic_index_in_dim(
        resid_all, my_dp * col_count + my_col, axis=0, keepdims=False
    ).astype(F32)
    rstd_two = lax.rsqrt(jnp.sum(block_all * block_all, axis=(0, 2)) / D + EPSILON)[:, None]
    grad_top = cotangent.astype(F32)
    grad_normed = grad_expert + jnp.einsum("et,de->td", grad_logits, router_float)
    normed_float = resid_mid * rstd_two * gain_float
    grad_router = jnp.einsum("td,et->de", normed_float, grad_logits)
    grad_gain_two = jnp.sum(grad_normed * resid_mid * rstd_two, axis=0)
    scaled_two = grad_normed * gain_float
    inner_two = lax.psum(jnp.sum(scaled_two * resid_mid, axis=1), "row")[:, None]
    grad_resid = (
        grad_top + rstd_two * scaled_two - resid_mid * (rstd_two * rstd_two * rstd_two * inner_two / D)
    )
    branch_all = lax.all_gather(grad_resid.astype(LOW), "row", axis=0)

    back_part, grads_part = pl.pallas_call(
        attend_backward_kernel,
        out_shape=(
            jax.ShapeDtypeStruct((row_count, length, width), LOW),
            jax.ShapeDtypeStruct((row_count, width, qkv_width + width), LOW),
        ),
        in_specs=[vmem] * 12,
        out_specs=[vmem] * 2,
        scratch_shapes=[
            pltpu.VMEM((2 * kv_local, length, HD), LOW),
            pltpu.VMEM((length, qkv_width), F32),
            pltpu.VMEM((kv_local, length, HD), F32),
            pltpu.VMEM((kv_local, length, HD), F32),
            pltpu.VMEM((length, qkv_width), LOW),
        ],
        compiler_params=params,
        name="attend_backward",
    )(
        branch_all, wo_rows, wq_rows, normed_one, mixed, query_rot, key_rot, value_low, logs,
        seg_col, seg_row, tables,
    )
    grad_normed_one = lax.psum_scatter(
        back_part.reshape(-1, width), "row", scatter_dimension=0, tiled=True
    ).astype(F32)
    grads_own = lax.psum_scatter(
        grads_part.reshape(row_count * width, -1), "col", scatter_dimension=0, tiled=True
    )
    swap = [(a * col_count + b, b * col_count + a) for a in range(row_count) for b in range(col_count)]
    grads_own = lax.psum(lax.ppermute(grads_own, ("row", "col"), swap), "dp").astype(F32)
    grad_qkv = grads_own[:, :qkv_width].reshape(w_qkv.shape)
    grad_out = grads_own[:, qkv_width:].reshape(w_out.shape)

    gain_first = norm_gain.astype(F32)
    hid_float = hidden_all.astype(F32)
    rstd_one = lax.rsqrt(jnp.sum(hid_float * hid_float, axis=(0, 2)) / D + EPSILON)[:, None]
    grad_gain_one = jnp.sum(grad_normed_one * resid_in * rstd_one, axis=0)
    scaled_one = grad_normed_one * gain_first
    inner_one = lax.psum(jnp.sum(scaled_one * resid_in, axis=1), "row")[:, None]
    grad_in = (
        grad_resid + rstd_one * scaled_one - resid_in * (rstd_one * rstd_one * rstd_one * inner_one / D)
    )
    small = jnp.concatenate([grad_router.T, grad_gain_one[None], grad_gain_two[None]], axis=0)
    small = lax.psum(small, ("dp", "col"))
    return (
        layer_out,
        grad_in,
        small[EXPERTS],
        grad_qkv,
        grad_out,
        small[EXPERTS + 1],
        small[:EXPERTS].T,
        grad_gate,
        grad_up,
        grad_down,
    )


def solution(mesh):
    token = P(("dp", "col"), "row")
    routed = P(("dp", "col"), None)
    expert = P(("dp", "row"), None, None)
    wide, tall = P("row", "col", None), P("col", None, "row")
    row = P("row")
    square = P("row", None)

    def step(*arrays):
        length = arrays[10].shape[1]
        tokens_here = arrays[0].shape[0] // (mesh.shape["dp"] * mesh.shape["col"])
        whole_sequence = tokens_here == length and mesh.shape["row"] == mesh.shape["col"]
        return jax.shard_map(
            fast_device if whole_sequence else on_device,
            mesh=mesh,
            in_specs=(
                token, row, wide, tall, row, square, expert, expert, expert, token,
                P(("dp", "row"), None), routed, routed,
            ),
            out_specs=(token, token, row, wide, tall, row, square, expert, expert, expert),
            check_vma=False,
        )(*arrays)

    return step
```

```python
import functools

import jax
import jax.numpy as jnp
import numpy as np
from jax import lax
from jax.experimental import pallas as pl
from jax.experimental.pallas import tpu as pltpu
from jax.sharding import PartitionSpec as P

D = 1024
HQ = 16
HK = 8
HD = 64
EXPERTS = 32
TOP = 8


EPSILON = 1e-06
ROPE_BASE = 10000.0
NEG_LARGE = -1e30
HIGHEST = lax.Precision.HIGHEST


def rotate(values, cosine, sine_table):
    half_size = values.shape[-1] // 2
    lower_half = values[..., :half_size]
    upper_half = values[..., half_size:]
    return jnp.concatenate(
        [
            lower_half * cosine - upper_half * sine_table,
            upper_half * cosine + lower_half * sine_table,
        ],
        axis=-1,
    )


def rotate_back(values, cosine, sine_table):
    half_size = values.shape[-1] // 2
    lower_half = values[..., :half_size]
    upper_half = values[..., half_size:]
    return jnp.concatenate(
        [
            lower_half * cosine + upper_half * sine_table,
            upper_half * cosine - lower_half * sine_table,
        ],
        axis=-1,
    )


def rope_tables(length, head_size):
    positions = jnp.arange(length, dtype=jnp.float32)
    frequency = ROPE_BASE ** (-2.0 * jnp.arange(head_size // 2, dtype=jnp.float32) / head_size)
    angles = positions[:, None] * frequency[None, :]
    return (jnp.cos(angles), jnp.sin(angles))


def visible(segment_row):
    positions = jnp.arange(segment_row.shape[-1], dtype=jnp.int32)
    causal = positions[:, None] >= positions[None, :]
    return causal & (segment_row[..., :, None] == segment_row[..., None, :])


def pair_ranks(expert_ids, pair_order, block_rows):
    experts_flat = expert_ids.reshape(-1, block_rows * TOP)
    order_flat = pair_order.reshape(-1, block_rows * TOP)

    def one_block(experts_row, order_row):
        pair_count = experts_row.shape[0]
        by_order = (
            jnp.zeros((pair_count,), jnp.int32)
            .at[order_row]
            .set(jnp.arange(pair_count, dtype=jnp.int32))
        )
        sorted_experts = experts_row[by_order]
        onehot = (sorted_experts[:, None] == jnp.arange(EXPERTS, dtype=jnp.int32)[None, :]).astype(
            jnp.int32
        )
        before = jnp.cumsum(onehot, axis=0) - onehot
        sorted_rank = jnp.sum(before * onehot, axis=1)
        return sorted_rank[order_row]

    return jax.vmap(one_block)(experts_flat, order_flat).reshape(expert_ids.shape)


def feature_total(values):
    return lax.psum(values, "row")


def tokens_by_col(values):
    return lax.all_gather(values, "col", axis=0, tiled=True)


def tokens_by_row(values):
    return lax.all_gather(values, "row", axis=0, tiled=True)


def col_scatter(term_fn, keep_rows):
    return lax.psum_scatter(
        term_fn(jnp.int32(0), keep_rows * lax.axis_size("col")),
        "col",
        scatter_dimension=0,
        tiled=True,
    )


def to_experts(outgoing):
    arrived = lax.all_to_all(outgoing, ("dp", "row"), split_axis=0, concat_axis=0, tiled=True)
    return arrived


def from_experts(outgoing):
    arrived = lax.all_to_all(outgoing, ("dp", "row"), split_axis=0, concat_axis=0, tiled=True)
    return arrived


def owner_layout(incoming, dp_count, row_count, exp_local):
    capacity = incoming.shape[1] // exp_local
    part_width = incoming.shape[2]
    sectioned = incoming.reshape(dp_count, row_count, exp_local, capacity, part_width)
    return sectioned.transpose(2, 0, 3, 1, 4).reshape(
        exp_local, dp_count * capacity, row_count * part_width
    )


def source_layout(owner_rows, dp_count, row_count):
    exp_local, slot_rows, full_width = owner_rows.shape
    capacity = slot_rows // dp_count
    part_width = full_width // row_count
    sectioned = owner_rows.reshape(exp_local, dp_count, capacity, row_count, part_width)
    return sectioned.transpose(1, 3, 0, 2, 4).reshape(
        dp_count * row_count, exp_local * capacity, part_width
    )


def attend_forward(pack):
    query_seq, key_seq, value_seq, segment_seq = pack
    score_scale = query_seq.shape[-1] ** (-0.5)
    scores = (
        jnp.einsum("qhgd,khd->hgqk", query_seq, key_seq, preferred_element_type=jnp.float32)
        * score_scale
    )
    scores = jnp.where(visible(segment_seq), scores, NEG_LARGE)
    row_max = jnp.max(scores, axis=-1, keepdims=True)
    weights = jnp.exp(scores - row_max)
    row_total = jnp.sum(weights, axis=-1, keepdims=True)
    weights_low = (weights / row_total).astype(jnp.bfloat16)
    mixed_seq = jnp.einsum(
        "hgqk,khd->qhgd", weights_low, value_seq, preferred_element_type=jnp.float32
    )
    return (mixed_seq.astype(jnp.bfloat16), row_max + jnp.log(row_total))


def attend_backward(pack):
    query_seq, key_seq, value_seq, segment_seq, log_total, grad_seq = pack
    score_scale = query_seq.shape[-1] ** (-0.5)
    scores = (
        jnp.einsum("qhgd,khd->hgqk", query_seq, key_seq, preferred_element_type=jnp.float32)
        * score_scale
    )
    scores = jnp.where(visible(segment_seq), scores, NEG_LARGE)
    weights = jnp.exp(scores - log_total)
    grad_weights = jnp.einsum(
        "qhgd,khd->hgqk", grad_seq, value_seq, preferred_element_type=jnp.float32
    )
    inner_sum = jnp.sum(weights * grad_weights, axis=-1, keepdims=True)
    grad_scores = (weights * (grad_weights - inner_sum)).astype(jnp.bfloat16)
    grad_values = jnp.einsum(
        "hgqk,qhgd->khd", weights.astype(jnp.bfloat16), grad_seq, preferred_element_type=jnp.float32
    )
    grad_query = (
        jnp.einsum("hgqk,khd->qhgd", grad_scores, key_seq, preferred_element_type=jnp.float32)
        * score_scale
    )
    grad_key = (
        jnp.einsum("hgqk,qhgd->khd", grad_scores, query_seq, preferred_element_type=jnp.float32)
        * score_scale
    )
    return (grad_query, grad_key, grad_values)


def on_device(
    hidden_in,
    norm_gain,
    w_qkv,
    w_out,
    ffn_gain,
    router,
    w_gate,
    w_up,
    w_down,
    cotangent,
    segment_ids,
    expert_ids,
    pair_order,
):
    dp_count = lax.axis_size("dp")
    row_count = lax.axis_size("row")
    owners = dp_count * row_count
    tok_rows, part_width = hidden_in.shape
    seq_count, length = segment_ids.shape
    att_rows = seq_count * length
    kv_local = w_qkv.shape[1]
    group_size = HQ // HK
    exp_local = w_gate.shape[0]
    capacity = tok_rows * TOP // EXPERTS
    total_slots = EXPERTS * capacity
    resid_in = hidden_in.astype(jnp.float32)
    gain_one = norm_gain.astype(jnp.float32)
    rstd_one = lax.rsqrt(feature_total(jnp.sum(resid_in * resid_in, axis=1)) / D + EPSILON)
    normed_one = (resid_in * rstd_one[:, None] * gain_one).astype(jnp.bfloat16)
    group_rows = tokens_by_col(normed_one)
    qkv_flat = w_qkv.reshape(part_width, -1)
    picked = group_rows
    qkv_local = lax.psum_scatter(
        jnp.dot(picked, qkv_flat, preferred_element_type=jnp.float32),
        "row",
        scatter_dimension=0,
        tiled=True,
    )
    qkv_local = qkv_local.reshape(seq_count, length, kv_local, -1)
    cosine, sine_table = rope_tables(length, HD)
    queries = qkv_local[..., : group_size * HD].reshape(seq_count, length, kv_local, group_size, HD)
    query_rot = rotate(
        queries, cosine[None, :, None, None, :], sine_table[None, :, None, None, :]
    ).astype(jnp.bfloat16)
    key_rot = rotate(
        qkv_local[..., group_size * HD : (group_size + 1) * HD],
        cosine[None, :, None, :],
        sine_table[None, :, None, :],
    ).astype(jnp.bfloat16)
    value_low = qkv_local[..., (group_size + 1) * HD :].astype(jnp.bfloat16)
    mixed_heads, log_total = lax.map(attend_forward, (query_rot, key_rot, value_low, segment_ids))
    mixed_rows = tokens_by_row(mixed_heads.reshape(att_rows, -1))
    out_flat = w_out.reshape(-1, part_width)

    def out_term(first_row, block_rows):
        return jnp.dot(mixed_rows, out_flat, preferred_element_type=jnp.float32)

    resid_mid = resid_in + col_scatter(out_term, tok_rows)
    gain_two = ffn_gain.astype(jnp.float32)
    router_float = router.astype(jnp.float32)
    square_two, logit_part = (
        lax.psum(jnp.sum(resid_mid * resid_mid, axis=1).astype(jnp.bfloat16), "row").astype(
            jnp.float32
        ),
        lax.psum(
            jnp.dot(resid_mid * gain_two, router_float, precision=HIGHEST).astype(jnp.bfloat16),
            "row",
        ).astype(jnp.float32),
    )
    rstd_two = lax.rsqrt(square_two / D + EPSILON)
    logits = logit_part * rstd_two[:, None]
    normed_float = resid_mid * rstd_two[:, None] * gain_two
    normed_two = normed_float.astype(jnp.bfloat16)
    choose = (expert_ids[:, :, None] == jnp.arange(EXPERTS, dtype=jnp.int32)[None, None, :]).astype(
        jnp.float32
    )
    gate_weights = jax.nn.softmax(jnp.sum(choose * logits[:, None, :], axis=2), axis=1)
    pair_rank = pair_ranks(expert_ids, pair_order, tok_rows)
    pair_slot = jnp.where(pair_rank < capacity, expert_ids * capacity + pair_rank, total_slots)
    pair_index = jnp.arange(tok_rows * TOP, dtype=jnp.int32)
    slot_pair = (
        jnp.full((total_slots + 1,), tok_rows * TOP, jnp.int32)
        .at[pair_slot.reshape(-1)]
        .set(pair_index)[:total_slots]
    )
    padded_two = jnp.concatenate([normed_two, jnp.zeros((1, part_width), jnp.bfloat16)], axis=0)
    outgoing = padded_two[slot_pair // TOP].reshape(owners, exp_local * capacity, part_width)
    expert_rows = owner_layout(to_experts(outgoing), dp_count, row_count, exp_local)
    gate_pre = jnp.einsum("erd,edf->erf", expert_rows, w_gate, preferred_element_type=jnp.float32)
    up_pre = jnp.einsum("erd,edf->erf", expert_rows, w_up, preferred_element_type=jnp.float32)
    hidden = (jax.nn.silu(gate_pre) * up_pre).astype(jnp.bfloat16)
    expert_out = jnp.einsum(
        "erf,efd->erd", hidden, w_down, preferred_element_type=jnp.float32
    ).astype(jnp.bfloat16)
    returned = from_experts(source_layout(expert_out, dp_count, row_count))
    slot_table = jnp.concatenate(
        [returned.reshape(total_slots, part_width), jnp.zeros((1, part_width), jnp.bfloat16)],
        axis=0,
    )
    pair_rows = slot_table[pair_slot].astype(jnp.float32)
    layer_sum = resid_mid + jnp.einsum("tk,tkd->td", gate_weights, pair_rows, precision=HIGHEST)
    grad_top = cotangent.astype(jnp.float32)
    grad_gates = lax.psum(jnp.einsum("td,tkd->tk", grad_top, pair_rows, precision=HIGHEST), "row")
    pair_grad = (gate_weights[:, :, None] * grad_top[:, None, :]).astype(jnp.bfloat16)
    grad_padded = jnp.concatenate(
        [pair_grad.reshape(tok_rows * TOP, part_width), jnp.zeros((1, part_width), jnp.bfloat16)],
        axis=0,
    )
    outgoing_grad = grad_padded[slot_pair].reshape(owners, exp_local * capacity, part_width)
    grad_rows = owner_layout(to_experts(outgoing_grad), dp_count, row_count, exp_local)
    grad_hidden = jnp.einsum("erd,efd->erf", grad_rows, w_down, preferred_element_type=jnp.float32)
    sigmoid_gate = jax.nn.sigmoid(gate_pre)
    grad_gate_pre = (
        grad_hidden * up_pre * sigmoid_gate * (1.0 + gate_pre * (1.0 - sigmoid_gate))
    ).astype(jnp.bfloat16)
    grad_up_pre = (grad_hidden * gate_pre * sigmoid_gate).astype(jnp.bfloat16)
    grad_down_local = jnp.einsum(
        "erf,erd->efd", hidden, grad_rows, preferred_element_type=jnp.float32
    )
    grad_gate_local = jnp.einsum(
        "erd,erf->edf", expert_rows, grad_gate_pre, preferred_element_type=jnp.float32
    )
    grad_up_local = jnp.einsum(
        "erd,erf->edf", expert_rows, grad_up_pre, preferred_element_type=jnp.float32
    )
    rows_back = jnp.einsum(
        "erf,edf->erd", grad_gate_pre, w_gate, preferred_element_type=jnp.float32
    )
    rows_back = (
        rows_back
        + jnp.einsum("erf,edf->erd", grad_up_pre, w_up, preferred_element_type=jnp.float32)
    ).astype(jnp.bfloat16)
    returned_grad = from_experts(source_layout(rows_back, dp_count, row_count))
    grad_table = jnp.concatenate(
        [returned_grad.reshape(total_slots, part_width), jnp.zeros((1, part_width), jnp.bfloat16)],
        axis=0,
    )
    inner_gate = jnp.sum(gate_weights * grad_gates, axis=1, keepdims=True)
    grad_chosen = gate_weights * (grad_gates - inner_gate)
    grad_logits = jnp.einsum("tk,tke->te", grad_chosen, choose, precision=HIGHEST)
    grad_router_part = jnp.einsum("td,te->de", normed_float, grad_logits, precision=HIGHEST)
    grad_normed = jnp.sum(grad_table[pair_slot].astype(jnp.float32), axis=1)
    grad_normed = grad_normed + jnp.einsum(
        "te,de->td", grad_logits, router_float, precision=HIGHEST
    )
    grad_gain_two_part = jnp.sum(grad_normed * resid_mid * rstd_two[:, None], axis=0)
    scaled_two = grad_normed * gain_two
    inner_two = feature_total(jnp.sum(scaled_two * resid_mid, axis=1))
    grad_resid = (
        grad_top
        + rstd_two[:, None] * scaled_two
        - resid_mid * (rstd_two * rstd_two * rstd_two * inner_two / D)[:, None]
    )
    branch_rows = tokens_by_col(grad_resid.astype(jnp.bfloat16))
    grad_out_local = jnp.einsum(
        "tc,td->cd", mixed_rows, branch_rows, preferred_element_type=jnp.float32
    ).reshape(w_out.shape)
    picked = branch_rows
    grad_mixed = lax.psum_scatter(
        jnp.einsum("td,cd->tc", picked, out_flat, preferred_element_type=jnp.float32).astype(
            jnp.bfloat16
        ),
        "row",
        scatter_dimension=0,
        tiled=True,
    ).astype(jnp.float32)
    grad_mixed = grad_mixed.astype(jnp.bfloat16).reshape(
        seq_count, length, kv_local, group_size, HD
    )
    grad_query, grad_key, grad_values = lax.map(
        attend_backward, (query_rot, key_rot, value_low, segment_ids, log_total, grad_mixed)
    )
    grad_query = rotate_back(
        grad_query, cosine[None, :, None, None, :], sine_table[None, :, None, None, :]
    )
    grad_key = rotate_back(grad_key, cosine[None, :, None, :], sine_table[None, :, None, :])
    grad_qkv_pre = jnp.concatenate(
        [grad_query.reshape(seq_count, length, kv_local, group_size * HD), grad_key, grad_values],
        axis=-1,
    )
    grad_qkv_pre = grad_qkv_pre.astype(jnp.bfloat16).reshape(att_rows, -1)
    qkv_rows = tokens_by_row(grad_qkv_pre)
    grad_qkv_local = jnp.einsum(
        "td,tc->dc", group_rows, qkv_rows, preferred_element_type=jnp.float32
    ).reshape(w_qkv.shape)

    def normed_term(first_row, block_rows):
        return jnp.einsum("tc,dc->td", qkv_rows, qkv_flat, preferred_element_type=jnp.float32)

    grad_normed_one = col_scatter(normed_term, tok_rows)
    grad_gain_one_part = jnp.sum(grad_normed_one * resid_in * rstd_one[:, None], axis=0)
    scaled_one = grad_normed_one * gain_one
    inner_one = feature_total(jnp.sum(scaled_one * resid_in, axis=1))
    grad_in = (
        grad_resid
        + rstd_one[:, None] * scaled_one
        - resid_in * (rstd_one * rstd_one * rstd_one * inner_one / D)[:, None]
    )
    col_sums = (
        lax.psum(grad_gate_local.astype(jnp.bfloat16), "col").astype(jnp.float32),
        lax.psum(grad_up_local.astype(jnp.bfloat16), "col").astype(jnp.float32),
        lax.psum(grad_down_local.astype(jnp.bfloat16), "col").astype(jnp.float32),
        lax.psum(grad_router_part.astype(jnp.bfloat16), "col").astype(jnp.float32),
        lax.psum(grad_gain_one_part.astype(jnp.bfloat16), "col").astype(jnp.float32),
        lax.psum(grad_gain_two_part.astype(jnp.bfloat16), "col").astype(jnp.float32),
    )
    dp_sums = (
        lax.psum(grad_qkv_local.astype(jnp.bfloat16), "dp").astype(jnp.float32),
        lax.psum(grad_out_local.astype(jnp.bfloat16), "dp").astype(jnp.float32),
        lax.psum(col_sums[3].astype(jnp.bfloat16), "dp").astype(jnp.float32),
        lax.psum(col_sums[4].astype(jnp.bfloat16), "dp").astype(jnp.float32),
        lax.psum(col_sums[5].astype(jnp.bfloat16), "dp").astype(jnp.float32),
    )
    return (
        layer_sum.astype(jnp.bfloat16),
        grad_in,
        dp_sums[3],
        dp_sums[0],
        dp_sums[1],
        dp_sums[4],
        dp_sums[2],
        col_sums[0],
        col_sums[1],
        col_sums[2],
    )

WINDOW = 512
BLOCK_Q = 256
LANES = 128
SMALL_ROWS = 48
GAIN_ONE = EXPERTS
GAIN_TWO = EXPERTS + 1
RSTD_LANE = LANES - 1
RSTD_ROW = 8
F32 = jnp.float32
LOW = jnp.bfloat16
VMEM_BYTES = 67_000_000


def dot_nn(a, b):
    return jnp.dot(a, b, preferred_element_type=F32)


def dot_nt(a, b):
    return lax.dot_general(a, b, (((1,), (1,)), ((), ())), preferred_element_type=F32)


def dot_tn(a, b):
    return lax.dot_general(a, b, (((0,), (0,)), ((), ())), preferred_element_type=F32)


def rope_lanes(length):
    positions = np.arange(length, dtype=np.float32)
    frequency = (ROPE_BASE ** (-2.0 * np.arange(HD // 2, dtype=np.float32) / HD)).astype(np.float32)
    angles = (positions[:, None] * frequency[None, :]).astype(np.float32)
    cosine, sine = np.cos(angles), np.sin(angles)
    signed = np.concatenate([-sine, sine], axis=1)
    double = np.concatenate([cosine, cosine], axis=1)
    ones, zeros = np.ones_like(double), np.zeros_like(double)
    return np.stack(
        [
            np.concatenate([double, double], axis=1),
            np.concatenate([signed, signed], axis=1),
            np.concatenate([double, ones], axis=1),
            np.concatenate([signed, zeros], axis=1),
        ]
    ).astype(np.float32)


def swap_halves(values):
    half = HD // 2
    lane = lax.broadcasted_iota(jnp.int32, values.shape, 1)
    ahead = pltpu.roll(values, LANES - half, 1)
    behind = pltpu.roll(values, half, 1)
    return jnp.where(lane % HD < half, ahead, behind)


def window_mask(seg_col, seg_row, q_start, k_start):
    shape = (seg_col.shape[0], seg_row.shape[1])
    q_at = lax.broadcasted_iota(jnp.int32, shape, 0) + q_start
    k_at = lax.broadcasted_iota(jnp.int32, shape, 1) + k_start
    return (q_at >= k_at) & (seg_col == seg_row)


def remote(src, dst, send_sem, recv_sem, where):
    return pltpu.make_async_remote_copy(
        src_ref=src, dst_ref=dst, send_sem=send_sem, recv_sem=recv_sem,
        device_id=where, device_id_type=pl.DeviceIdType.MESH,
    )


class Copies:
    def __init__(self, send_sems, recv_sems):
        self.send_sems, self.recv_sems = send_sems, recv_sems
        self.sends = self.recvs = 0
        self.open = []

    def receivers(self, number=1):
        first = self.recvs
        self.recvs += number
        return first

    def send(self, src, dst, receiver, where, when=None):
        at = self.sends
        self.sends += 1
        copy = remote(src, dst, self.send_sems.at[at], self.recv_sems.at[receiver], where)
        if when is None:
            copy.start()
        else:
            pl.when(when)(copy.start)
        self.open.append((copy, when))

    def local(self, src, dst, when=None):
        at = self.sends
        self.sends += 1
        copy = pltpu.make_async_copy(src, dst, self.send_sems.at[at])
        if when is None:
            copy.start()
        else:
            pl.when(when)(copy.start)
        return copy

    def arrived(self, dst, receiver, where):
        remote(dst, dst, self.recv_sems.at[receiver], self.recv_sems.at[receiver], where).wait_recv()

    def finish(self):
        for copy, when in self.open:
            if when is None:
                copy.wait_send()
            else:
                pl.when(when)(copy.wait_send)


class Place:
    def __init__(self, counts):
        self.dp_count, self.row_count, self.col_count = counts
        self.dp, self.row, self.col = (lax.axis_index(name) for name in ("dp", "row", "col"))
        self.pair_row = self.row + 1 - 2 * lax.rem(self.row, 2)
        self.far_row = lax.rem(self.row + 2, self.row_count)
        self.cross_row = lax.rem(self.pair_row + 2, self.row_count)
        self.other_dp = self.dp_count - 1 - self.dp
        self.here = (self.dp, self.row, self.col)
        self.pair = (self.dp, self.pair_row, self.col)
        self.far = (self.dp, self.far_row, self.col)
        self.over = (self.other_dp, self.row, self.col)
        self.over_far = (self.other_dp, self.far_row, self.col)

    def row_at(self, step):
        return lax.rem(self.row + step + self.row_count, self.row_count)

    def col_at(self, step):
        return lax.rem(self.col + step + self.col_count, self.col_count)

    def plane(self):
        peers = [(self.dp, self.row_at(k), self.col) for k in range(1, self.row_count)]
        return peers + [(self.other_dp, self.row_at(k), self.col) for k in range(self.row_count)]

    def column(self):
        return [(self.dp, self.row, self.col_at(k)) for k in range(1, self.col_count)]


def greet(peers):
    barrier = pltpu.get_barrier_semaphore()
    for peer in peers:
        pl.semaphore_signal(barrier, inc=1, device_id=peer, device_id_type=pl.DeviceIdType.MESH)
    pl.semaphore_wait(barrier, len(peers))


def attend_forward_kernel(
    counts, hidden_hbm, own_q_hbm, own_o_hbm, small_hbm, seg_hbm, cot_hbm, tab_ref,
    resid_ref, low_ref, mix_ref, normed_ref, q_ref, k_ref, v_ref, lse_ref, wq_ref, zo_ref, small_ref, seg_ref, cot_plane,
    h_ref, zq_ref, own_ref, column_ref, send_sems, recv_sems,
):
    place = Place(counts)
    row_count, col_count = place.row_count, place.col_count
    copies = Copies(send_sems, recv_sems)
    parts, length, width = h_ref.shape
    kv_heads = k_ref.shape[0]
    features = parts * width
    chunks = length // BLOCK_Q
    greet(place.plane() + place.column())

    h_pair, h_far, h_cross = (copies.receivers() for _ in range(3))
    copies.send(hidden_hbm, h_ref.at[place.row], h_far, place.far)
    copies.send(hidden_hbm, h_ref.at[place.row], h_pair, place.pair)
    h_own = copies.local(hidden_hbm, h_ref.at[place.row])
    zq_own = copies.local(own_q_hbm, zq_ref.at[place.col])
    zo_own = copies.local(own_o_hbm, zo_ref.at[place.col])
    small_own = copies.local(small_hbm, small_ref.at[place.row])
    seg_own = copies.local(seg_hbm, seg_ref.at[place.row])
    zq_in = copies.receivers(col_count)
    zo_in = copies.receivers(col_count)
    for k in range(1, col_count):
        copies.send(own_q_hbm, zq_ref.at[place.col], zq_in + k, (place.dp, place.row, place.col_at(k)))
    small_in, seg_in = copies.receivers(row_count), copies.receivers(row_count)
    for k in range(1, row_count):
        copies.send(small_hbm, small_ref.at[place.row], small_in + k, (place.dp, place.row_at(k), place.col))
        copies.send(seg_hbm, seg_ref.at[place.row], seg_in + k, (place.dp, place.row_at(k), place.col))
    cot_own = copies.local(cot_hbm, own_ref)
    cot_pair, cot_in, cot_back = copies.receivers(), copies.receivers(3), copies.receivers(3)
    own_cot = cot_plane.at[place.dp, place.row]
    copies.send(cot_hbm, own_cot, cot_in + 1, place.over)
    copies.send(cot_hbm, own_cot, cot_pair, place.pair)

    def share_blocks(landing, result, landed, first, own):
        waits = []
        for k in range(col_count):
            source = place.col_at(-k)
            if k == 0:
                own.wait()
            else:
                copies.arrived(landing.at[source], landed + k, place.here)
            mine = source == place.row
            step = lax.rem(source - place.row + row_count, row_count)
            copies.send(
                landing.at[source], result.at[place.row], first + step, (place.dp, source, place.col), source != place.row
            )
            waits.append((copies.local(landing.at[source], result.at[place.row], mine), mine))
        return waits

    def blocks_shared(result, first, waits):
        for copy, mine in waits:
            pl.when(mine)(copy.wait)
        for k in range(1, row_count):
            copies.arrived(result.at[place.row_at(-k)], first + k, place.here)

    copies.arrived(h_ref.at[place.far_row], h_far, place.far)
    copies.send(h_ref.at[place.far_row], h_ref.at[place.far_row], h_cross, place.pair)
    wq_in = copies.receivers(row_count)
    wq_waits = share_blocks(zq_ref, wq_ref, zq_in, wq_in, zq_own)

    for k in range(1, col_count):
        copies.send(own_o_hbm, zo_ref.at[place.col], zo_in + k, (place.dp, place.row, place.col_at(k)))
    copies.send(cot_hbm, own_cot, cot_in, place.far)
    h_own.wait()
    copies.arrived(h_ref.at[place.pair_row], h_pair, place.pair)
    copies.arrived(h_ref.at[place.cross_row], h_cross, place.pair)
    small_own.wait()
    for k in range(1, row_count):
        copies.arrived(small_ref.at[place.row_at(-k)], small_in + k, place.here)

    @pl.loop(0, chunks)
    def _(chunk):
        rows = pl.ds(pl.multiple_of(chunk * BLOCK_Q, BLOCK_Q), BLOCK_Q)
        total = jnp.zeros((BLOCK_Q, 1), F32)
        for part in range(parts):
            piece = h_ref[part, rows, :].astype(F32)
            total = total + jnp.sum(piece * piece, axis=1, keepdims=True)
        rstd = lax.rsqrt(total / features + EPSILON)
        lse_ref[rows, :] = jnp.broadcast_to(rstd, (BLOCK_Q, LANES))
        for part in range(parts):
            piece = h_ref[part, rows, :].astype(F32)
            gain = small_ref[part, GAIN_ONE : GAIN_ONE + 1, :].astype(F32)
            normed_ref[rows, part * width : (part + 1) * width] = (piece * rstd * gain).astype(LOW)

    seg_own.wait()
    for k in range(1, row_count):
        copies.arrived(seg_ref.at[place.row_at(-k)], seg_in + k, place.here)
    segments = seg_ref[place.col]
    for start in range(0, length, LANES):
        column_ref[start : start + LANES, :] = jnp.broadcast_to(
            segments[0:1, start : start + LANES], (LANES, LANES)
        ).T

    cot_own.wait()
    cot_kept = copies.local(own_ref, cot_plane.at[place.dp, place.row])

    blocks_shared(wq_ref, wq_in, wq_waits)

    @pl.loop(0, chunks)
    def _(chunk):
        rows = pl.ds(pl.multiple_of(chunk * BLOCK_Q, BLOCK_Q), BLOCK_Q)
        qkv = dot_nn(normed_ref[rows, :], wq_ref[...].reshape(features, -1))
        for head in range(kv_heads):
            base = head * 4 * HD
            queries = qkv[:, base : base + LANES]
            queries = queries * tab_ref[0, rows, :] + swap_halves(queries) * tab_ref[1, rows, :]
            others = qkv[:, base + LANES : base + 2 * LANES]
            others = others * tab_ref[2, rows, :] + swap_halves(others) * tab_ref[3, rows, :]
            q_ref[2 * head, rows, :] = queries[:, :HD].astype(LOW)
            q_ref[2 * head + 1, rows, :] = queries[:, HD:].astype(LOW)
            k_ref[head, rows, :] = others[:, :HD].astype(LOW)
            v_ref[head, rows, :] = others[:, HD:].astype(LOW)

    scale = HD**-0.5
    lane = lax.broadcasted_iota(jnp.int32, (BLOCK_Q, LANES), 1)
    mix_pair, mix_far, mix_cross = (copies.receivers(chunks) for _ in range(3))

    def pass_on(block):
        piece = mix_ref.at[place.far_row, pl.ds(block * BLOCK_Q, BLOCK_Q)]
        copies.arrived(piece, mix_far + block, place.far)
        copies.send(piece, piece, mix_cross + block, place.pair)

    for block in range(chunks):
        q_start = block * BLOCK_Q
        k_start = max(0, q_start - WINDOW)
        q_rows, k_rows = slice(q_start, q_start + BLOCK_Q), slice(k_start, q_start + BLOCK_Q)
        mask = window_mask(column_ref[q_rows, 0:1], segments[0:1, k_rows], q_start, k_start)
        logs = lse_ref[q_rows, :]
        for head in range(2 * kv_heads):
            scores = dot_nt(q_ref[head, q_rows, :], k_ref[head // 2, k_rows, :]) * scale
            scores = jnp.where(mask, scores, NEG_LARGE)
            top = jnp.max(scores, axis=1, keepdims=True)
            weights = jnp.exp(scores - top)
            total = jnp.sum(weights, axis=1, keepdims=True)
            out = dot_nn(weights.astype(LOW), v_ref[head // 2, k_rows, :]) / total
            mix_ref[place.row, q_rows, head * HD : (head + 1) * HD] = out.astype(LOW)
            logs = jnp.where(lane == head, top + jnp.log(total), logs)
        lse_ref[q_rows, :] = logs
        piece = mix_ref.at[place.row, pl.ds(q_start, BLOCK_Q)]
        copies.send(piece, piece, mix_far + block, place.far)
        copies.send(piece, piece, mix_pair + block, place.pair)
        if block > 0:
            pass_on(block - 1)
    pass_on(chunks - 1)
    for k, (dp_at, row_at) in enumerate(
        ((place.dp, place.far_row), (place.other_dp, place.row), (place.other_dp, place.far_row))
    ):
        piece = cot_plane.at[dp_at, row_at]
        copies.arrived(piece, cot_in + k, place.here)
        if k == 0:
            copies.send(piece, piece, cot_in + 2, place.over)
        copies.send(piece, piece, cot_back + k, place.pair)
    zo_own.wait()
    for k in range(1, col_count):
        copies.arrived(zo_ref.at[place.col_at(-k)], zo_in + k, place.here)
    for block in range(chunks):
        rows = slice(block * BLOCK_Q, (block + 1) * BLOCK_Q)
        window = pl.ds(block * BLOCK_Q, BLOCK_Q)
        copies.arrived(mix_ref.at[place.pair_row, window], mix_pair + block, place.pair)
        copies.arrived(mix_ref.at[place.cross_row, window], mix_cross + block, place.pair)
        branch = dot_nn(mix_ref[0, rows, :], zo_ref[0])
        for part in range(1, parts):
            branch = branch + dot_nn(mix_ref[part, rows, :], zo_ref[part])
        resid = h_ref[place.row, rows, :].astype(F32) + branch
        resid_ref[rows, :] = resid
        low_ref[rows, :] = resid.astype(LOW)

    cot_kept.wait()
    copies.arrived(cot_plane.at[place.dp, place.pair_row], cot_pair, place.pair)
    for k, (dp_at, row_at) in enumerate(
        ((place.dp, place.cross_row), (place.other_dp, place.pair_row), (place.other_dp, place.cross_row))
    ):
        copies.arrived(cot_plane.at[dp_at, row_at], cot_back + k, place.pair)
    copies.finish()


def attend_backward_kernel(
    counts, grad_low_hbm, grad_ref, hidden_ref, resid_ref, wo_ref, wq_ref, normed_ref, mix_hbm, q_ref, k_ref, v_ref, lse_ref,
    seg_ref, small_ref, part_ref, tab_ref, y_hbm,
    out_ref, grad_in_ref, grads_ref, sums_ref,
    gb_ref, mixed_ref, gm_ref, dq_ref, dk_ref, dv_ref, turn_ref, column_ref, y_own_ref, y_in_ref, y_chip_ref, y_last_ref,
    away_ref, pair_in_ref, own_ref, chip_ref, last_ref, inner_ref, parts_ref,
    send_sems, recv_sems,
):
    place = Place(counts)
    copies = Copies(send_sems, recv_sems)
    dp_count, row_count, col_count = counts
    parts, length, width = gb_ref.shape
    kv_heads = k_ref.shape[0]
    features = parts * width
    chunks = length // BLOCK_Q
    scale = HD**-0.5
    far_side = [(place.other_dp, place.row, place.col_at(k)) for k in range(1, col_count)]
    greet(place.plane() + place.column() + far_side)

    def window(chunk):
        return pl.ds(chunk * BLOCK_Q, BLOCK_Q)

    blocks = range(chunks - 1, -1, -1)
    gb_far, gb_pair, gb_cross = (copies.receivers(chunks) for _ in range(3))
    for chunk in blocks:
        piece = gb_ref.at[place.row, window(chunk)]
        copies.send(grad_low_hbm.at[window(chunk)], piece, gb_far + chunk, place.far)
        copies.send(grad_low_hbm.at[window(chunk)], piece, gb_pair + chunk, place.pair)
    gb_own = copies.local(grad_low_hbm, gb_ref.at[place.row])
    mix_own = copies.local(mix_hbm.at[place.row], mixed_ref)
    y_pair = copies.receivers(2 * dp_count)
    y_held = []
    for turn, dp_at in enumerate((place.other_dp, place.dp)):
        for q, (here, there) in enumerate(
            ((place.row, place.pair_row), (place.far_row, place.cross_row))
        ):
            copies.send(y_hbm.at[dp_at, there], y_in_ref.at[turn, q], y_pair + 2 * turn + q, place.pair)
            y_held.append(copies.local(y_hbm.at[dp_at, here], y_own_ref.at[turn, q]))

    segments = seg_ref[place.col]
    for start in range(0, length, LANES):
        column_ref[start : start + LANES, :] = jnp.broadcast_to(
            segments[0:1, start : start + LANES], (LANES, LANES)
        ).T
    dk_ref[...] = jnp.zeros_like(dk_ref)
    dv_ref[...] = jnp.zeros_like(dv_ref)
    gb_own.wait()

    def pass_on(chunk):
        piece = gb_ref.at[place.far_row, window(chunk)]
        copies.arrived(piece, gb_far + chunk, place.far)
        copies.send(piece, piece, gb_cross + chunk, place.pair)

    y_last = copies.receivers(3)

    def y_sums():
        for copy in y_held:
            copy.wait()
        for turn, q, slot, peer in ((0, 1, 1, place.over_far), (1, 1, 2, place.far), (0, 0, 0, place.over)):
            copies.arrived(y_in_ref.at[turn, q], y_pair + 2 * turn + q, place.pair)
            y_chip_ref[turn, q] = (
                y_own_ref[turn, q].astype(F32) + y_in_ref[turn, q].astype(F32)
            ).astype(LOW)
            copies.send(y_chip_ref.at[turn, q], y_last_ref.at[slot], y_last + slot, peer)
        copies.arrived(y_in_ref.at[1, 0], y_pair + 2, place.pair)

    away_in = [copies.receivers(chunks) for _ in range(2)]
    last_in = copies.receivers(chunks)

    def far_share(chunk):
        rows = slice(chunk * BLOCK_Q, (chunk + 1) * BLOCK_Q)
        copies.arrived(pair_in_ref.at[1, window(chunk)], away_in[1] + chunk, place.pair)
        chip_ref[rows, :] = (own_ref[1, rows, :] + pair_in_ref[1, rows, :].astype(F32)).astype(LOW)
        copies.send(chip_ref.at[window(chunk)], last_ref.at[window(chunk)], last_in + chunk, place.far)

    pass_on(chunks - 1)
    for block in blocks:
        q_start = block * BLOCK_Q
        k_start = max(0, q_start - WINDOW)
        q_rows, k_rows = slice(q_start, q_start + BLOCK_Q), slice(k_start, q_start + BLOCK_Q)
        copies.arrived(gb_ref.at[place.pair_row, window(block)], gb_pair + block, place.pair)
        copies.arrived(gb_ref.at[place.cross_row, window(block)], gb_cross + block, place.pair)
        total = dot_nt(gb_ref[0, q_rows, :], wo_ref[0])
        for part in range(1, parts):
            total = total + dot_nt(gb_ref[part, q_rows, :], wo_ref[part])
        gm_ref[...] = total.astype(LOW)
        mask = window_mask(column_ref[q_rows, 0:1], segments[0:1, k_rows], q_start, k_start)
        logs = lse_ref[q_rows, :]
        for kv in range(kv_heads):
            keys, vals = k_ref[kv, k_rows, :], v_ref[kv, k_rows, :]
            for head in (2 * kv, 2 * kv + 1):
                queries, grad = q_ref[head, q_rows, :], gm_ref[:, head * HD : (head + 1) * HD]
                scores = dot_nt(queries, keys) * scale
                weights = jnp.where(mask, jnp.exp(scores - logs[:, head : head + 1]), 0.0)
                grad_weights = dot_nt(grad, vals)
                inner = jnp.sum(weights * grad_weights, axis=1, keepdims=True)
                grad_scores = (weights * (grad_weights - inner)).astype(LOW)
                dv_ref[kv, k_rows, :] += dot_tn(weights.astype(LOW), grad)
                dk_ref[kv, k_rows, :] += dot_tn(grad_scores, queries)
                dq_ref[:, head * HD : (head + 1) * HD] = dot_nn(grad_scores, keys) * scale
        if block > 0:
            pass_on(block - 1)
        for kv in range(kv_heads):
            base = kv * 4 * HD
            queries = dq_ref[:, kv * LANES : (kv + 1) * LANES]
            queries = queries * tab_ref[0, q_rows, :] - swap_halves(queries) * tab_ref[1, q_rows, :]
            others = jnp.concatenate([dk_ref[kv, q_rows, :] * scale, dv_ref[kv, q_rows, :]], axis=1)
            others = others * tab_ref[2, q_rows, :] - swap_halves(others) * tab_ref[3, q_rows, :]
            turn_ref[q_rows, base : base + LANES] = queries.astype(LOW)
            turn_ref[q_rows, base + LANES : base + 2 * LANES] = others.astype(LOW)
        for q, row_at in ((1, place.cross_row), (0, place.pair_row)):
            away_ref[q, q_rows, :] = dot_nt(turn_ref[q_rows, :], wq_ref[row_at]).astype(LOW)
            copies.send(
                away_ref.at[q, window(block)], pair_in_ref.at[q, window(block)], away_in[q] + block, place.pair
            )
        for q, row_at in ((1, place.far_row), (0, place.row)):
            own_ref[q, q_rows, :] = dot_nt(turn_ref[q_rows, :], wq_ref[row_at])
        if block == chunks - 1:
            y_sums()
        else:
            far_share(block + 1)

    columns = turn_ref.shape[1]
    mix_own.wait()
    for part in range(parts):
        grads_ref[part, :, :columns] = dot_tn(
            normed_ref[:, part * width : (part + 1) * width], turn_ref[...]
        ).astype(LOW)
        grads_ref[part, :, columns:] = dot_tn(mixed_ref[...], gb_ref[part]).astype(LOW)
        if part == 0:
            far_share(0)

    gain = small_ref[place.row, GAIN_ONE : GAIN_ONE + 1, :].astype(F32)
    inner_in = copies.receivers(row_count)
    gain_sum = jnp.zeros((1, width), F32)
    for chunk in blocks:
        rows = slice(chunk * BLOCK_Q, (chunk + 1) * BLOCK_Q)
        copies.arrived(pair_in_ref.at[0, window(chunk)], away_in[0] + chunk, place.pair)
        copies.arrived(last_ref.at[window(chunk)], last_in + chunk, place.far)
        grad_normed = own_ref[0, rows, :] + pair_in_ref[0, rows, :].astype(F32) + last_ref[rows, :].astype(F32)
        own_ref[0, rows, :] = grad_normed
        along = grad_normed * hidden_ref[rows, :].astype(F32)
        gain_sum = gain_sum + jnp.sum(along * lse_ref[rows, RSTD_LANE : RSTD_LANE + 1], axis=0, keepdims=True)
        inner_ref[place.row, 0:1, rows] = row_of(jnp.sum(along * gain, axis=1, keepdims=True))
    parts_ref[0] = part_ref[...]
    parts_ref[0, GAIN_ONE : GAIN_ONE + 1, :] = gain_sum
    for k in range(1, row_count):
        copies.send(
            inner_ref.at[place.row], inner_ref.at[place.row], inner_in + k, (place.dp, place.row_at(k), place.col)
        )
    others = place.column() + [place.over] + far_side
    sums_in = copies.receivers(len(others) + 1)
    for k, peer in enumerate(others):
        copies.send(parts_ref.at[0], parts_ref.at[k + 1], sums_in + k + 1, peer)

    for slot in range(3):
        copies.arrived(y_last_ref.at[slot], y_last + slot, place.here)
    for chunk in range(chunks):
        rows = slice(chunk * BLOCK_Q, (chunk + 1) * BLOCK_Q)
        mixture = y_own_ref[1, 0, rows, :].astype(F32) + y_in_ref[1, 0, rows, :].astype(F32)
        for slot in range(3):
            mixture = mixture + y_last_ref[slot, rows, :].astype(F32)
        out_ref[rows, :] = (resid_ref[rows, :] + mixture).astype(LOW)

    for k in range(1, row_count):
        copies.arrived(inner_ref.at[place.row_at(-k)], inner_in + k, place.here)
    inner = inner_ref[0, 0:1, :]
    for part in range(1, row_count):
        inner = inner + inner_ref[part, 0:1, :]
    for chunk in range(chunks):
        rows = slice(chunk * BLOCK_Q, (chunk + 1) * BLOCK_Q)
        rstd = lse_ref[rows, RSTD_LANE : RSTD_LANE + 1]
        cube = rstd * rstd * rstd * column_of(inner[:, rows]) / features
        grad_in_ref[rows, :] = (
            grad_ref[rows, :] + rstd * (own_ref[0, rows, :] * gain) - hidden_ref[rows, :].astype(F32) * cube
        )
    total = parts_ref[0]
    for k in range(len(others)):
        copies.arrived(parts_ref.at[k + 1], sums_in + k + 1, place.here)
        total = total + parts_ref[k + 1]
    sums_ref[...] = total
    copies.finish()


def expert_grads(gate_pre, up_pre, grad_hidden):
    sig = 1.0 / (1.0 + jnp.exp(-gate_pre))
    silu = gate_pre * sig
    grad_gate = grad_hidden * up_pre * (sig * (1.0 + gate_pre * (1.0 - sig)))
    return (silu * up_pre).astype(LOW), grad_gate.astype(LOW), (grad_hidden * silu).astype(LOW)


def slot_picks(rank_row, capacity):
    at = lax.broadcasted_iota(jnp.int32, (capacity, rank_row.shape[1]), 0).astype(F32)
    return at == rank_row


def column_of(row):
    return jnp.broadcast_to(row, (LANES, row.shape[1])).T[:, 0:1]


def row_of(column):
    return jnp.broadcast_to(column, (column.shape[0], LANES)).T[0:1, :]


def experts_kernel(
    counts, low_hbm, resid_ref, cot_own_ref, packed_hbm, cot_plane_hbm, small_ref, zo_hbm, wg_hbm, wu_hbm, wd_hbm,
    y_hbm, grad_ref, grad_low_ref, table_ref, part_ref, wo_hbm,
    wg_ref, wu_ref, wd_ref, res_ref, cot_ref, x_ref, packed_ref, rank_ref, gate_ref, g_ref, pick_ref, eo_ref, back_ref,
    away_ref, pair_in_ref, own_ref, chip_ref, last_ref, stage_ref, gg_ref, gg_in_ref, rstd_ref, inner_ref, nx_ref,
    send_sems, recv_sems,
):
    place = Place(counts)
    copies = Copies(send_sems, recv_sems)
    dp_count, row_count, col_count = counts
    _, parts, length, width = res_ref.shape
    experts, features, hidden_width = wg_ref.shape
    capacity = pick_ref.shape[0] // experts
    chunks = length // BLOCK_Q
    total_experts = dp_count * row_count * experts
    pair_count = length * TOP
    first_expert = (place.dp * row_count + place.row) * experts
    order = (place.other_dp, place.dp)
    greet(place.plane() + place.column())

    res_pair, res_far, res_over, res_across, res_cross, res_up, res_slant = (copies.receivers() for _ in range(7))
    own_low = res_ref.at[place.dp, place.row]
    copies.send(low_hbm, own_low, res_far, place.far)
    copies.send(low_hbm, own_low, res_over, place.over)
    copies.send(low_hbm, own_low, res_pair, place.pair)
    packed_over = copies.receivers()
    copies.send(packed_hbm, packed_ref.at[place.dp], packed_over, place.over)
    packed_own = copies.local(packed_hbm, packed_ref.at[place.dp])
    low_own = copies.local(low_hbm, own_low)
    cot_in = [copies.local(cot_plane_hbm.at[dp_at], cot_ref.at[dp_at]) for dp_at in (place.dp, place.other_dp)]
    weights_in = [copies.local(*pair) for pair in ((wg_hbm, wg_ref), (wu_hbm, wu_ref), (wd_hbm, wd_ref))]

    def pass_far():
        copies.arrived(res_ref.at[place.dp, place.far_row], res_far, place.far)
        piece = res_ref.at[place.dp, place.far_row]
        copies.send(piece, piece, res_across, place.over)
        copies.send(piece, piece, res_cross, place.pair)

    def pass_over():
        piece = res_ref.at[place.other_dp, place.row]
        copies.arrived(piece, res_over, place.over)
        copies.send(piece, piece, res_up, place.pair)

    def pass_across():
        piece = res_ref.at[place.other_dp, place.far_row]
        copies.arrived(piece, res_across, place.over)
        copies.send(piece, piece, res_slant, place.pair)

    def ranks_of(dp_at):
        ids = packed_ref[dp_at] // pair_count
        orders = (packed_ref[dp_at] - ids * pair_count).astype(F32)
        rows = []
        for e in range(experts):
            match = ids == first_expert + e
            known = jnp.max(jnp.where(match, 1.0, 0.0), axis=0, keepdims=True)
            at = jnp.sum(jnp.where(match, orders, 0.0), axis=0, keepdims=True)
            rows.append(jnp.where(known > 0.0, at, float(pair_count)))
        stacked = jnp.concatenate(rows + [jnp.zeros((LANES - experts, length), F32)], axis=0)
        columns = stacked.T
        for e in range(experts):
            count = jnp.zeros((1, length), F32)
            for start in range(0, length, BLOCK_Q):
                before = columns[start : start + BLOCK_Q, e : e + 1] < rows[e]
                count = count + jnp.sum(jnp.where(before, 1.0, 0.0), axis=0, keepdims=True)
            rank_ref[dp_at, e : e + 1, :] = jnp.where(rows[e] < float(pair_count), count, -1.0)

    def gather_grads(dp_at):
        @pl.loop(0, experts)
        def _(e):
            pick = slot_picks(rank_ref[dp_at, pl.ds(e, 1), :], capacity).astype(F32).astype(LOW)
            slots = pl.ds(pl.multiple_of(e * capacity, capacity), capacity)
            for part in range(parts):
                g_ref[dp_at, part, slots, :] = dot_nn(pick, cot_ref[dp_at, part]).astype(LOW)

    packed_own.wait()
    ranks_of(place.dp)
    pass_far()
    cot_in[0].wait()
    gather_grads(place.dp)
    pass_over()
    copies.arrived(packed_ref.at[place.other_dp], packed_over, place.over)
    ranks_of(place.other_dp)
    pass_across()
    cot_in[1].wait()
    gather_grads(place.other_dp)

    wo_in = copies.receivers(row_count)
    wo_waits = []
    for k in range(col_count):
        source = place.col_at(k)
        mine = source == place.row
        step = lax.rem(source - place.row + row_count, row_count)
        copies.send(
            zo_hbm.at[source], wo_hbm.at[place.row], wo_in + step, (place.dp, source, place.col), jnp.logical_not(mine)
        )
    own_wo = copies.local(zo_hbm.at[place.row], stage_ref.at[0, pl.ds(0, zo_hbm.shape[1])])

    low_own.wait()
    copies.arrived(res_ref.at[place.dp, place.pair_row], res_pair, place.pair)
    copies.arrived(res_ref.at[place.dp, place.cross_row], res_cross, place.pair)
    copies.arrived(res_ref.at[place.other_dp, place.pair_row], res_up, place.pair)
    copies.arrived(res_ref.at[place.other_dp, place.cross_row], res_slant, place.pair)
    for copy in weights_in:
        copy.wait()
    own_wo.wait()
    kept_wo = copies.local(stage_ref.at[0, pl.ds(0, zo_hbm.shape[1])], wo_hbm.at[place.row])
    kept_wo.wait()

    own_scaled = place.row
    gg_same, gg_other = copies.receivers(row_count), copies.receivers(row_count)
    pair_in = copies.receivers(2 * dp_count)
    last_over, last_across, last_far = (copies.receivers() for _ in range(3))
    table_in = copies.receivers(col_count)

    for turn, dp_at in enumerate(order):
        last = turn == dp_count - 1

        @pl.loop(0, chunks)
        def _(chunk):
            rows = pl.ds(pl.multiple_of(chunk * BLOCK_Q, BLOCK_Q), BLOCK_Q)
            total = jnp.zeros((BLOCK_Q, 1), F32)
            for part in range(parts):
                piece = res_ref[dp_at, part, rows, :].astype(F32)
                total = total + jnp.sum(piece * piece, axis=1, keepdims=True)
            rstd = lax.rsqrt(total / features + EPSILON)
            for part in range(parts):
                piece = res_ref[dp_at, part, rows, :].astype(F32)
                gain = small_ref[part, GAIN_TWO : GAIN_TWO + 1, :].astype(F32)
                x_ref[rows, part * width : (part + 1) * width] = (piece * rstd * gain).astype(LOW)
            table_ref[place.col, dp_at, RSTD_ROW : RSTD_ROW + 1, rows] = row_of(rstd)
            if last:
                rstd_ref[rows, :] = jnp.broadcast_to(rstd, (BLOCK_Q, LANES))
                piece = res_ref[dp_at, own_scaled, rows, :].astype(F32)
                gain = small_ref[own_scaled, GAIN_TWO : GAIN_TWO + 1, :].astype(F32)
                nx_ref[rows, :] = (piece * rstd * gain).astype(LOW)

        logits = jnp.zeros((total_experts, length), F32)
        for part in range(parts):
            logits = logits + dot_nt(
                small_ref[part, :total_experts, :], x_ref[:, part * width : (part + 1) * width]
            )
        ids = packed_ref[dp_at] // pair_count
        expert_at = lax.broadcasted_iota(jnp.int32, (total_experts, length), 0)
        chosen = expert_at == ids[0:1, :]
        for k in range(1, TOP):
            chosen = chosen | (expert_at == ids[k : k + 1, :])
        shown = jnp.where(chosen, logits, NEG_LARGE)
        weights = jnp.where(chosen, jnp.exp(shown - jnp.max(shown, axis=0, keepdims=True)), 0.0)
        gate_ref[...] = weights / jnp.sum(weights, axis=0, keepdims=True)
        table_ref[place.col, dp_at, 0:experts, :] = rank_ref[dp_at, 0:experts, :]
        for e in range(experts):
            table_ref[place.col, dp_at, experts + e : experts + e + 1, :] = gate_ref[pl.ds(first_expert + e, 1), :]

        @pl.loop(0, experts)
        def _(e):
            here = slot_picks(rank_ref[dp_at, pl.ds(e, 1), :], capacity)
            pick = here.astype(F32).astype(LOW)
            slots = pl.ds(pl.multiple_of(e * capacity, capacity), capacity)
            pick_ref[slots, :] = pick
            gate_slot = jnp.sum(
                jnp.where(here, gate_ref[pl.ds(first_expert + e, 1), :], 0.0), axis=1, keepdims=True
            )
            x = dot_nn(pick, x_ref[...]).astype(LOW)
            hidden, grad_gate, grad_up = None, None, None
            grad_hidden = jnp.zeros((capacity, hidden_width), F32)
            for part in range(parts):
                pair_grad = (g_ref[dp_at, part, slots, :].astype(F32) * gate_slot).astype(LOW)
                grad_hidden = grad_hidden + dot_nt(
                    pair_grad, wd_ref[e, :, part * width : (part + 1) * width]
                )
            hidden, grad_gate, grad_up = expert_grads(dot_nn(x, wg_ref[e]), dot_nn(x, wu_ref[e]), grad_hidden)
            along = jnp.zeros((capacity, 1), F32)
            for part in range(parts):
                cols = slice(part * width, (part + 1) * width)
                out = dot_nn(hidden, wd_ref[e, :, cols]).astype(LOW).astype(F32)
                along = along + jnp.sum(g_ref[dp_at, part, slots, :].astype(F32) * out, axis=1, keepdims=True)
                eo_ref[part, slots, :] = (out * gate_slot).astype(LOW)
                back_ref[part, slots, :] = (
                    dot_nt(grad_gate, wg_ref[e, cols, :]) + dot_nt(grad_up, wu_ref[e, cols, :])
                ).astype(LOW)
            gg_ref[dp_at, pl.ds(e, 1), :] = jnp.sum(jnp.where(here, along, 0.0), axis=0, keepdims=True)

        owner = place.dp * row_count + place.row
        if last:
            for k in range(1, row_count):
                copies.send(gg_ref.at[dp_at], gg_in_ref.at[owner], gg_same + k, (dp_at, place.row_at(k), place.col))
            gg_in_ref[owner] = gg_ref[dp_at]
        else:
            for k in range(row_count):
                copies.send(gg_ref.at[dp_at], gg_in_ref.at[owner], gg_other + k, (dp_at, place.row_at(k), place.col))

        for q, row_at in enumerate((place.pair_row, place.cross_row)):
            away_ref[turn, q] = dot_tn(pick_ref[...], back_ref[row_at]).astype(LOW)
            copies.send(away_ref.at[turn, q], pair_in_ref.at[turn, q], pair_in + 2 * turn + q, place.pair)
        for q, row_at in enumerate((place.far_row, place.row)):
            own_ref[q] = dot_tn(pick_ref[...], back_ref[row_at])
        copies.arrived(pair_in_ref.at[turn, 1], pair_in + 2 * turn + 1, place.pair)
        chip_ref[turn, 1] = (own_ref[0] + pair_in_ref[turn, 1].astype(F32)).astype(LOW)
        if last:
            copies.send(chip_ref.at[turn, 1], last_ref.at[2], last_far, place.far)
        else:
            copies.send(chip_ref.at[turn, 1], last_ref.at[1], last_across, place.over_far)
        copies.arrived(pair_in_ref.at[turn, 0], pair_in + 2 * turn, place.pair)
        if last:
            own_ref[1] = own_ref[1] + pair_in_ref[turn, 0].astype(F32)
        else:
            chip_ref[turn, 0] = (own_ref[1] + pair_in_ref[turn, 0].astype(F32)).astype(LOW)
            copies.send(chip_ref.at[turn, 0], last_ref.at[0], last_over, place.over)

        for part in range(parts):
            stage_ref[part] = dot_tn(pick_ref[...], eo_ref[part]).astype(LOW)
        kept = copies.local(stage_ref, y_hbm.at[dp_at])
        kept.wait()

    for k in range(1, col_count):
        copies.send(table_ref.at[place.col], table_ref.at[place.col], table_in + k, (place.dp, place.row, place.col_at(k)))

    for k in range(1, row_count):
        copies.arrived(gg_in_ref.at[place.dp * row_count + place.row_at(-k)], gg_same + k, place.here)
    for k in range(row_count):
        copies.arrived(gg_in_ref.at[place.other_dp * row_count + place.row_at(-k)], gg_other + k, place.here)
    along = jnp.concatenate([gg_in_ref[owner, :experts, :] for owner in range(dp_count * row_count)], axis=0)
    gates = gate_ref[...]
    grad_logits = (gates * (along - jnp.sum(gates * along, axis=0, keepdims=True))).astype(LOW)
    router = small_ref[place.row, :total_experts, :]
    gain = small_ref[place.row, GAIN_TWO : GAIN_TWO + 1, :].astype(F32)
    part_ref[...] = jnp.zeros_like(part_ref)
    part_ref[:total_experts, :] = dot_nn(grad_logits, nx_ref[...])
    own_ref[1] = own_ref[1] + dot_tn(grad_logits, router)

    copies.arrived(last_ref.at[0], last_over, place.over)
    copies.arrived(last_ref.at[1], last_across, place.over_far)
    copies.arrived(last_ref.at[2], last_far, place.far)
    inner_in = copies.receivers(row_count)
    gain_sum = jnp.zeros((1, width), F32)
    for chunk in range(chunks):
        rows = slice(chunk * BLOCK_Q, (chunk + 1) * BLOCK_Q)
        grad_normed = own_ref[1, rows, :]
        for k in range(3):
            grad_normed = grad_normed + last_ref[k, rows, :].astype(F32)
        own_ref[0, rows, :] = grad_normed
        along = grad_normed * resid_ref[rows, :]
        gain_sum = gain_sum + jnp.sum(along * rstd_ref[rows, 0:1], axis=0, keepdims=True)
        inner_ref[place.row, 0:1, rows] = row_of(jnp.sum(along * gain, axis=1, keepdims=True))
    part_ref[GAIN_TWO : GAIN_TWO + 1, :] = gain_sum
    for k in range(1, row_count):
        copies.send(
            inner_ref.at[place.row], inner_ref.at[place.row], inner_in + k, (place.dp, place.row_at(k), place.col)
        )
    for k in range(1, row_count):
        copies.arrived(inner_ref.at[place.row_at(-k)], inner_in + k, place.here)
    inner = inner_ref[0, 0:1, :]
    for part in range(1, row_count):
        inner = inner + inner_ref[part, 0:1, :]
    for chunk in range(chunks):
        rows = slice(chunk * BLOCK_Q, (chunk + 1) * BLOCK_Q)
        rstd = rstd_ref[rows, 0:1]
        cube = rstd * rstd * rstd * column_of(inner[:, rows]) / features
        grad = (
            cot_own_ref[rows, :].astype(F32) + rstd * (own_ref[0, rows, :] * gain) - resid_ref[rows, :] * cube
        )
        grad_ref[rows, :] = grad
        grad_low_ref[rows, :] = grad.astype(LOW)

    for k in range(1, row_count):
        copies.arrived(wo_hbm.at[place.row_at(-k)], wo_in + k, place.here)
    for k in range(1, col_count):
        copies.arrived(table_ref.at[place.col_at(-k)], table_in + k, place.here)
    copies.finish()


def weight_grads_kernel(
    counts, res_hbm, cot_hbm, table_ref, small_ref, wg_ref, wu_ref, wd_ref, dg_ref, du_ref, dd_ref,
    res_ref, cot_ref, sems,
):
    dp_count, row_count, col_count = counts
    blocks = dp_count * col_count
    experts, features, hidden_width = wg_ref.shape
    _, parts, length, width = res_hbm.shape
    capacity = length * TOP // (dp_count * row_count * experts)

    def fetch(step):
        slot = lax.rem(step, 2)
        return (
            pltpu.make_async_copy(res_hbm.at[step], res_ref.at[slot], sems.at[slot]),
            pltpu.make_async_copy(cot_hbm.at[step], cot_ref.at[slot], sems.at[2 + slot]),
        )

    for copy in fetch(0):
        copy.start()
    dg_ref[...] = jnp.zeros_like(dg_ref)
    du_ref[...] = jnp.zeros_like(du_ref)
    dd_ref[...] = jnp.zeros_like(dd_ref)

    @pl.loop(0, blocks)
    def _(step):
        slot = lax.rem(step, 2)
        for copy in fetch(step):
            copy.wait()

        @pl.when(step + 1 < blocks)
        def _():
            for copy in fetch(step + 1):
                copy.start()

        dp_at, col_at = step // col_count, lax.rem(step, col_count)

        @pl.loop(0, experts)
        def _(e):
            here = slot_picks(table_ref[col_at, dp_at, pl.ds(e, 1), :], capacity)
            pick = here.astype(F32).astype(LOW)
            gate_row = table_ref[col_at, dp_at, pl.ds(experts + e, 1), :]
            gate_slot = jnp.sum(jnp.where(here, gate_row, 0.0), axis=1, keepdims=True)
            rstd_row = table_ref[col_at, dp_at, RSTD_ROW : RSTD_ROW + 1, :]
            rstd_slot = jnp.sum(jnp.where(here, rstd_row, 0.0), axis=1, keepdims=True)
            x = jnp.concatenate(
                [
                    (
                        dot_nn(pick, res_ref[slot, part])
                        * rstd_slot
                        * small_ref[part, GAIN_TWO : GAIN_TWO + 1, :].astype(F32)
                    ).astype(LOW)
                    for part in range(parts)
                ],
                axis=1,
            )
            pair_grad = jnp.concatenate(
                [(dot_nn(pick, cot_ref[slot, part]) * gate_slot).astype(LOW) for part in range(parts)], axis=1
            )
            hidden, grad_gate, grad_up = expert_grads(
                dot_nn(x, wg_ref[e]), dot_nn(x, wu_ref[e]), dot_nt(pair_grad, wd_ref[e])
            )
            dd_ref[e] += dot_tn(hidden, pair_grad)
            dg_ref[e] += dot_tn(x, grad_gate)
            du_ref[e] += dot_tn(x, grad_up)


def fast_device(
    hidden_in, norm_gain, w_qkv, w_out, ffn_gain, router, w_gate, w_up, w_down, cotangent,
    segment_ids, expert_ids, pair_order,
):
    dp_count, row_count, col_count = (lax.axis_size(name) for name in ("dp", "row", "col"))
    my_dp, my_row, my_col = (lax.axis_index(name) for name in ("dp", "row", "col"))
    length, width = hidden_in.shape
    kv_local = w_qkv.shape[1]
    head_width = kv_local * (HQ // HK) * HD
    qkv_width = kv_local * (HQ // HK + 2) * HD
    exp_local, _, hidden_width = w_gate.shape
    capacity = length * TOP // EXPERTS
    blocks = dp_count * col_count
    vmem = pl.BlockSpec(memory_space=pltpu.VMEM)
    hbm = pl.BlockSpec(memory_space=pl.ANY)
    params = pltpu.CompilerParams(vmem_limit_bytes=VMEM_BYTES)

    packed = (expert_ids * (length * TOP) + pair_order).T
    cot_all = lax.all_gather(cotangent, ("dp", "col", "row"), axis=0).reshape(
        blocks, row_count, length, width
    )
    own_q = w_qkv.reshape(width, qkv_width)
    own_o = w_out.reshape(head_width, width)
    small = jnp.concatenate(
        [router.T, norm_gain[None], ffn_gain[None], jnp.zeros((SMALL_ROWS - 2 - EXPERTS, width), LOW)], axis=0
    )
    seg_rows = jnp.broadcast_to(segment_ids, (8, length)).astype(F32)
    tables = jnp.asarray(rope_lanes(length))
    counts = (dp_count, row_count, col_count)
    (
        resid_mid, resid_low, mixed_all, normed_one, query_rot, key_rot, value_low, logs,
        wq_rows, wo_cols, small_all, seg_all, cot_plane,
    ) = pl.pallas_call(
        functools.partial(attend_forward_kernel, counts),
        out_shape=(
            jax.ShapeDtypeStruct((length, width), F32),
            jax.ShapeDtypeStruct((length, width), LOW),
            jax.ShapeDtypeStruct((row_count, length, head_width), LOW),
            jax.ShapeDtypeStruct((length, D), LOW),
            jax.ShapeDtypeStruct((2 * kv_local, length, HD), LOW),
            jax.ShapeDtypeStruct((kv_local, length, HD), LOW),
            jax.ShapeDtypeStruct((kv_local, length, HD), LOW),
            jax.ShapeDtypeStruct((length, LANES), F32),
            jax.ShapeDtypeStruct((row_count, width, qkv_width), LOW),
            jax.ShapeDtypeStruct((col_count, head_width, width), LOW),
            jax.ShapeDtypeStruct((row_count, SMALL_ROWS, width), LOW),
            jax.ShapeDtypeStruct((row_count, 8, length), F32),
            jax.ShapeDtypeStruct((dp_count, row_count, length, width), LOW),
        ),
        in_specs=[hbm] * 6 + [vmem],
        out_specs=[vmem] * 12 + [hbm],
        scratch_shapes=[
            pltpu.VMEM((row_count, length, width), LOW),
            pltpu.VMEM((col_count, width, qkv_width), LOW),
            pltpu.VMEM((length, width), LOW),
            pltpu.VMEM((length, LANES), F32),
            pltpu.SemaphoreType.DMA((64,)),
            pltpu.SemaphoreType.DMA((64,)),
        ],
        compiler_params=pltpu.CompilerParams(
            vmem_limit_bytes=VMEM_BYTES, collective_id=1, has_side_effects=True
        ),
        cost_estimate=pl.CostEstimate(flops=50_000_000_000, bytes_accessed=30_000_000, transcendentals=0),
        name="attend_forward",
    )(hidden_in, own_q, own_o, small, seg_rows, cotangent, tables)
    resid_all = lax.all_gather(resid_low, ("dp", "col", "row"), axis=0).reshape(
        blocks, row_count, length, width
    )
    block_low = jax.ShapeDtypeStruct((length, width), LOW)
    block_float = jax.ShapeDtypeStruct((length, width), F32)
    slots = exp_local * capacity
    plane = (dp_count, row_count, length, width)
    y_part, grad_resid, grad_low, table, small_part, wo_rows = pl.pallas_call(
        functools.partial(experts_kernel, counts),
        out_shape=(
            jax.ShapeDtypeStruct(plane, LOW),
            block_float,
            block_low,
            jax.ShapeDtypeStruct((col_count, dp_count, 16, length), F32),
            jax.ShapeDtypeStruct((SMALL_ROWS, width), F32),
            jax.ShapeDtypeStruct((row_count, head_width, width), LOW),
        ),
        in_specs=[hbm, vmem, vmem, hbm, hbm, vmem, hbm, hbm, hbm, hbm],
        out_specs=[hbm] + [vmem] * 4 + [hbm],
        scratch_shapes=[
            pltpu.VMEM(w_gate.shape, LOW),
            pltpu.VMEM(w_up.shape, LOW),
            pltpu.VMEM(w_down.shape, LOW),
            pltpu.VMEM(plane, LOW),
            pltpu.VMEM(plane, LOW),
            pltpu.VMEM((length, D), LOW),
            pltpu.VMEM((dp_count, TOP, length), jnp.int32),
            pltpu.VMEM((dp_count, 8, length), F32),
            pltpu.VMEM((EXPERTS, length), F32),
            pltpu.VMEM((dp_count, row_count, slots, width), LOW),
            pltpu.VMEM((slots, length), LOW),
            pltpu.VMEM((row_count, slots, width), LOW),
            pltpu.VMEM((row_count, slots, width), LOW),
            pltpu.VMEM((dp_count, 2, length, width), LOW),
            pltpu.VMEM((dp_count, 2, length, width), LOW),
            pltpu.VMEM((2, length, width), F32),
            pltpu.VMEM((dp_count, 2, length, width), LOW),
            pltpu.VMEM((3, length, width), LOW),
            pltpu.VMEM((row_count, length, width), LOW),
            pltpu.VMEM((dp_count, 8, length), F32),
            pltpu.VMEM((dp_count * row_count, 8, length), F32),
            pltpu.VMEM((length, LANES), F32),
            pltpu.VMEM((row_count, 8, length), F32),
            pltpu.VMEM((length, width), LOW),
            pltpu.SemaphoreType.DMA((80,)),
            pltpu.SemaphoreType.DMA((80,)),
        ],
        compiler_params=pltpu.CompilerParams(
            vmem_limit_bytes=VMEM_BYTES, collective_id=2, has_side_effects=True
        ),
        cost_estimate=pl.CostEstimate(flops=80_000_000_000, bytes_accessed=50_000_000, transcendentals=0),
        name="experts",
    )(resid_low, resid_mid, cotangent, packed, cot_plane, small_all, wo_cols, w_gate, w_up, w_down)

    halves = (dp_count, 2, length, width)
    half = (2, length, width)
    layer_out, grad_in, grads_part, small = pl.pallas_call(
        functools.partial(attend_backward_kernel, counts),
        out_shape=(
            block_low,
            block_float,
            jax.ShapeDtypeStruct((row_count, width, qkv_width + width), LOW),
            jax.ShapeDtypeStruct((SMALL_ROWS, width), F32),
        ),
        in_specs=[hbm] + [vmem] * 6 + [hbm] + [vmem] * 8 + [hbm],
        out_specs=[vmem] * 4,
        scratch_shapes=[
            pltpu.VMEM((row_count, length, width), LOW),
            pltpu.VMEM((length, head_width), LOW),
            pltpu.VMEM((BLOCK_Q, head_width), LOW),
            pltpu.VMEM((BLOCK_Q, head_width), F32),
            pltpu.VMEM((kv_local, length, HD), F32),
            pltpu.VMEM((kv_local, length, HD), F32),
            pltpu.VMEM((length, qkv_width), LOW),
            pltpu.VMEM((length, LANES), F32),
            pltpu.VMEM(halves, LOW),
            pltpu.VMEM(halves, LOW),
            pltpu.VMEM(halves, LOW),
            pltpu.VMEM((3, length, width), LOW),
            pltpu.VMEM(half, LOW),
            pltpu.VMEM(half, LOW),
            pltpu.VMEM(half, F32),
            pltpu.VMEM((length, width), LOW),
            pltpu.VMEM((length, width), LOW),
            pltpu.VMEM((row_count, 8, length), F32),
            pltpu.VMEM((dp_count * col_count, SMALL_ROWS, width), F32),
            pltpu.SemaphoreType.DMA((80,)),
            pltpu.SemaphoreType.DMA((80,)),
        ],
        compiler_params=pltpu.CompilerParams(
            vmem_limit_bytes=VMEM_BYTES, collective_id=3, has_side_effects=True
        ),
        cost_estimate=pl.CostEstimate(flops=40_000_000_000, bytes_accessed=30_000_000, transcendentals=0),
        name="attend_backward",
    )(
        grad_low, grad_resid, hidden_in, resid_mid, wo_rows, wq_rows, normed_one, mixed_all, query_rot, key_rot,
        value_low, logs, seg_all, small_all, small_part, tables, y_part,
    )

    (grads_part, cot_all, resid_all) = lax.optimization_barrier((grads_part, cot_all, resid_all))
    grad_gate, grad_up, grad_down = pl.pallas_call(
        functools.partial(weight_grads_kernel, counts),
        out_shape=(
            jax.ShapeDtypeStruct(w_gate.shape, F32),
            jax.ShapeDtypeStruct(w_up.shape, F32),
            jax.ShapeDtypeStruct(w_down.shape, F32),
        ),
        in_specs=[hbm, hbm] + [vmem] * 5,
        out_specs=[vmem] * 3,
        scratch_shapes=[
            pltpu.VMEM((2, row_count, length, width), LOW),
            pltpu.VMEM((2, row_count, length, width), LOW),
            pltpu.SemaphoreType.DMA((4,)),
        ],
        compiler_params=params,
        cost_estimate=pl.CostEstimate(flops=86_000_000_000, bytes_accessed=70_000_000, transcendentals=0),
        name="weight_grads",
    )(resid_all, cot_all, table, small_all, w_gate, w_up, w_down)

    grads_own = lax.psum_scatter(
        grads_part.reshape(row_count * width, -1), "col", scatter_dimension=0, tiled=True
    )
    swap = [(a * col_count + b, b * col_count + a) for a in range(row_count) for b in range(col_count)]
    grads_own = lax.psum(lax.ppermute(grads_own, ("row", "col"), swap), "dp").astype(F32)
    grad_qkv = grads_own[:, :qkv_width].reshape(w_qkv.shape)
    grad_out = grads_own[:, qkv_width:].reshape(w_out.shape)
    return (
        layer_out,
        grad_in,
        small[GAIN_ONE],
        grad_qkv,
        grad_out,
        small[GAIN_TWO],
        small[:EXPERTS].T,
        grad_gate,
        grad_up,
        grad_down,
    )


def solution(mesh):
    token = P(("dp", "col"), "row")
    routed = P(("dp", "col"), None)
    expert = P(("dp", "row"), None, None)
    wide, tall = P("row", "col", None), P("col", None, "row")
    row = P("row")
    square = P("row", None)

    def step(*arrays):
        length = arrays[10].shape[1]
        tokens_here = arrays[0].shape[0] // (mesh.shape["dp"] * mesh.shape["col"])
        whole_sequence = tokens_here == length and mesh.shape["row"] == mesh.shape["col"]
        return jax.shard_map(
            fast_device if whole_sequence else on_device,
            mesh=mesh,
            in_specs=(
                token, row, wide, tall, row, square, expert, expert, expert, token,
                P(("dp", "row"), None), routed, routed,
            ),
            out_specs=(token, token, row, wide, tall, row, square, expert, expert, expert),
            check_vma=False,
        )(*arrays)

    return step
```

```python
import functools

import jax
import jax.numpy as jnp
import numpy as np
from jax import lax
from jax.experimental import pallas as pl
from jax.experimental.pallas import tpu as pltpu
from jax.sharding import PartitionSpec as P

D = 1024
HQ = 16
HK = 8
HD = 64
EXPERTS = 32
TOP = 8


EPSILON = 1e-06
ROPE_BASE = 10000.0
NEG_LARGE = -1e30
HIGHEST = lax.Precision.HIGHEST


def rotate(values, cosine, sine_table):
    half_size = values.shape[-1] // 2
    lower_half = values[..., :half_size]
    upper_half = values[..., half_size:]
    return jnp.concatenate(
        [
            lower_half * cosine - upper_half * sine_table,
            upper_half * cosine + lower_half * sine_table,
        ],
        axis=-1,
    )


def rotate_back(values, cosine, sine_table):
    half_size = values.shape[-1] // 2
    lower_half = values[..., :half_size]
    upper_half = values[..., half_size:]
    return jnp.concatenate(
        [
            lower_half * cosine + upper_half * sine_table,
            upper_half * cosine - lower_half * sine_table,
        ],
        axis=-1,
    )


def rope_tables(length, head_size):
    positions = jnp.arange(length, dtype=jnp.float32)
    frequency = ROPE_BASE ** (-2.0 * jnp.arange(head_size // 2, dtype=jnp.float32) / head_size)
    angles = positions[:, None] * frequency[None, :]
    return (jnp.cos(angles), jnp.sin(angles))


def visible(segment_row):
    positions = jnp.arange(segment_row.shape[-1], dtype=jnp.int32)
    causal = positions[:, None] >= positions[None, :]
    return causal & (segment_row[..., :, None] == segment_row[..., None, :])


def pair_ranks(expert_ids, pair_order, block_rows):
    experts_flat = expert_ids.reshape(-1, block_rows * TOP)
    order_flat = pair_order.reshape(-1, block_rows * TOP)

    def one_block(experts_row, order_row):
        pair_count = experts_row.shape[0]
        by_order = (
            jnp.zeros((pair_count,), jnp.int32)
            .at[order_row]
            .set(jnp.arange(pair_count, dtype=jnp.int32))
        )
        sorted_experts = experts_row[by_order]
        onehot = (sorted_experts[:, None] == jnp.arange(EXPERTS, dtype=jnp.int32)[None, :]).astype(
            jnp.int32
        )
        before = jnp.cumsum(onehot, axis=0) - onehot
        sorted_rank = jnp.sum(before * onehot, axis=1)
        return sorted_rank[order_row]

    return jax.vmap(one_block)(experts_flat, order_flat).reshape(expert_ids.shape)


def feature_total(values):
    return lax.psum(values, "row")


def tokens_by_col(values):
    return lax.all_gather(values, "col", axis=0, tiled=True)


def tokens_by_row(values):
    return lax.all_gather(values, "row", axis=0, tiled=True)


def col_scatter(term_fn, keep_rows):
    return lax.psum_scatter(
        term_fn(jnp.int32(0), keep_rows * lax.axis_size("col")),
        "col",
        scatter_dimension=0,
        tiled=True,
    )


def to_experts(outgoing):
    arrived = lax.all_to_all(outgoing, ("dp", "row"), split_axis=0, concat_axis=0, tiled=True)
    return arrived


def from_experts(outgoing):
    arrived = lax.all_to_all(outgoing, ("dp", "row"), split_axis=0, concat_axis=0, tiled=True)
    return arrived


def owner_layout(incoming, dp_count, row_count, exp_local):
    capacity = incoming.shape[1] // exp_local
    part_width = incoming.shape[2]
    sectioned = incoming.reshape(dp_count, row_count, exp_local, capacity, part_width)
    return sectioned.transpose(2, 0, 3, 1, 4).reshape(
        exp_local, dp_count * capacity, row_count * part_width
    )


def source_layout(owner_rows, dp_count, row_count):
    exp_local, slot_rows, full_width = owner_rows.shape
    capacity = slot_rows // dp_count
    part_width = full_width // row_count
    sectioned = owner_rows.reshape(exp_local, dp_count, capacity, row_count, part_width)
    return sectioned.transpose(1, 3, 0, 2, 4).reshape(
        dp_count * row_count, exp_local * capacity, part_width
    )


def attend_forward(pack):
    query_seq, key_seq, value_seq, segment_seq = pack
    score_scale = query_seq.shape[-1] ** (-0.5)
    scores = (
        jnp.einsum("qhgd,khd->hgqk", query_seq, key_seq, preferred_element_type=jnp.float32)
        * score_scale
    )
    scores = jnp.where(visible(segment_seq), scores, NEG_LARGE)
    row_max = jnp.max(scores, axis=-1, keepdims=True)
    weights = jnp.exp(scores - row_max)
    row_total = jnp.sum(weights, axis=-1, keepdims=True)
    weights_low = (weights / row_total).astype(jnp.bfloat16)
    mixed_seq = jnp.einsum(
        "hgqk,khd->qhgd", weights_low, value_seq, preferred_element_type=jnp.float32
    )
    return (mixed_seq.astype(jnp.bfloat16), row_max + jnp.log(row_total))


def attend_backward(pack):
    query_seq, key_seq, value_seq, segment_seq, log_total, grad_seq = pack
    score_scale = query_seq.shape[-1] ** (-0.5)
    scores = (
        jnp.einsum("qhgd,khd->hgqk", query_seq, key_seq, preferred_element_type=jnp.float32)
        * score_scale
    )
    scores = jnp.where(visible(segment_seq), scores, NEG_LARGE)
    weights = jnp.exp(scores - log_total)
    grad_weights = jnp.einsum(
        "qhgd,khd->hgqk", grad_seq, value_seq, preferred_element_type=jnp.float32
    )
    inner_sum = jnp.sum(weights * grad_weights, axis=-1, keepdims=True)
    grad_scores = (weights * (grad_weights - inner_sum)).astype(jnp.bfloat16)
    grad_values = jnp.einsum(
        "hgqk,qhgd->khd", weights.astype(jnp.bfloat16), grad_seq, preferred_element_type=jnp.float32
    )
    grad_query = (
        jnp.einsum("hgqk,khd->qhgd", grad_scores, key_seq, preferred_element_type=jnp.float32)
        * score_scale
    )
    grad_key = (
        jnp.einsum("hgqk,qhgd->khd", grad_scores, query_seq, preferred_element_type=jnp.float32)
        * score_scale
    )
    return (grad_query, grad_key, grad_values)


def on_device(
    hidden_in,
    norm_gain,
    w_qkv,
    w_out,
    ffn_gain,
    router,
    w_gate,
    w_up,
    w_down,
    cotangent,
    segment_ids,
    expert_ids,
    pair_order,
):
    dp_count = lax.axis_size("dp")
    row_count = lax.axis_size("row")
    owners = dp_count * row_count
    tok_rows, part_width = hidden_in.shape
    seq_count, length = segment_ids.shape
    att_rows = seq_count * length
    kv_local = w_qkv.shape[1]
    group_size = HQ // HK
    exp_local = w_gate.shape[0]
    capacity = tok_rows * TOP // EXPERTS
    total_slots = EXPERTS * capacity
    resid_in = hidden_in.astype(jnp.float32)
    gain_one = norm_gain.astype(jnp.float32)
    rstd_one = lax.rsqrt(feature_total(jnp.sum(resid_in * resid_in, axis=1)) / D + EPSILON)
    normed_one = (resid_in * rstd_one[:, None] * gain_one).astype(jnp.bfloat16)
    group_rows = tokens_by_col(normed_one)
    qkv_flat = w_qkv.reshape(part_width, -1)
    picked = group_rows
    qkv_local = lax.psum_scatter(
        jnp.dot(picked, qkv_flat, preferred_element_type=jnp.float32),
        "row",
        scatter_dimension=0,
        tiled=True,
    )
    qkv_local = qkv_local.reshape(seq_count, length, kv_local, -1)
    cosine, sine_table = rope_tables(length, HD)
    queries = qkv_local[..., : group_size * HD].reshape(seq_count, length, kv_local, group_size, HD)
    query_rot = rotate(
        queries, cosine[None, :, None, None, :], sine_table[None, :, None, None, :]
    ).astype(jnp.bfloat16)
    key_rot = rotate(
        qkv_local[..., group_size * HD : (group_size + 1) * HD],
        cosine[None, :, None, :],
        sine_table[None, :, None, :],
    ).astype(jnp.bfloat16)
    value_low = qkv_local[..., (group_size + 1) * HD :].astype(jnp.bfloat16)
    mixed_heads, log_total = lax.map(attend_forward, (query_rot, key_rot, value_low, segment_ids))
    mixed_rows = tokens_by_row(mixed_heads.reshape(att_rows, -1))
    out_flat = w_out.reshape(-1, part_width)

    def out_term(first_row, block_rows):
        return jnp.dot(mixed_rows, out_flat, preferred_element_type=jnp.float32)

    resid_mid = resid_in + col_scatter(out_term, tok_rows)
    gain_two = ffn_gain.astype(jnp.float32)
    router_float = router.astype(jnp.float32)
    square_two, logit_part = (
        lax.psum(jnp.sum(resid_mid * resid_mid, axis=1).astype(jnp.bfloat16), "row").astype(
            jnp.float32
        ),
        lax.psum(
            jnp.dot(resid_mid * gain_two, router_float, precision=HIGHEST).astype(jnp.bfloat16),
            "row",
        ).astype(jnp.float32),
    )
    rstd_two = lax.rsqrt(square_two / D + EPSILON)
    logits = logit_part * rstd_two[:, None]
    normed_float = resid_mid * rstd_two[:, None] * gain_two
    normed_two = normed_float.astype(jnp.bfloat16)
    choose = (expert_ids[:, :, None] == jnp.arange(EXPERTS, dtype=jnp.int32)[None, None, :]).astype(
        jnp.float32
    )
    gate_weights = jax.nn.softmax(jnp.sum(choose * logits[:, None, :], axis=2), axis=1)
    pair_rank = pair_ranks(expert_ids, pair_order, tok_rows)
    pair_slot = jnp.where(pair_rank < capacity, expert_ids * capacity + pair_rank, total_slots)
    pair_index = jnp.arange(tok_rows * TOP, dtype=jnp.int32)
    slot_pair = (
        jnp.full((total_slots + 1,), tok_rows * TOP, jnp.int32)
        .at[pair_slot.reshape(-1)]
        .set(pair_index)[:total_slots]
    )
    padded_two = jnp.concatenate([normed_two, jnp.zeros((1, part_width), jnp.bfloat16)], axis=0)
    outgoing = padded_two[slot_pair // TOP].reshape(owners, exp_local * capacity, part_width)
    expert_rows = owner_layout(to_experts(outgoing), dp_count, row_count, exp_local)
    gate_pre = jnp.einsum("erd,edf->erf", expert_rows, w_gate, preferred_element_type=jnp.float32)
    up_pre = jnp.einsum("erd,edf->erf", expert_rows, w_up, preferred_element_type=jnp.float32)
    hidden = (jax.nn.silu(gate_pre) * up_pre).astype(jnp.bfloat16)
    expert_out = jnp.einsum(
        "erf,efd->erd", hidden, w_down, preferred_element_type=jnp.float32
    ).astype(jnp.bfloat16)
    returned = from_experts(source_layout(expert_out, dp_count, row_count))
    slot_table = jnp.concatenate(
        [returned.reshape(total_slots, part_width), jnp.zeros((1, part_width), jnp.bfloat16)],
        axis=0,
    )
    pair_rows = slot_table[pair_slot].astype(jnp.float32)
    layer_sum = resid_mid + jnp.einsum("tk,tkd->td", gate_weights, pair_rows, precision=HIGHEST)
    grad_top = cotangent.astype(jnp.float32)
    grad_gates = lax.psum(jnp.einsum("td,tkd->tk", grad_top, pair_rows, precision=HIGHEST), "row")
    pair_grad = (gate_weights[:, :, None] * grad_top[:, None, :]).astype(jnp.bfloat16)
    grad_padded = jnp.concatenate(
        [pair_grad.reshape(tok_rows * TOP, part_width), jnp.zeros((1, part_width), jnp.bfloat16)],
        axis=0,
    )
    outgoing_grad = grad_padded[slot_pair].reshape(owners, exp_local * capacity, part_width)
    grad_rows = owner_layout(to_experts(outgoing_grad), dp_count, row_count, exp_local)
    grad_hidden = jnp.einsum("erd,efd->erf", grad_rows, w_down, preferred_element_type=jnp.float32)
    sigmoid_gate = jax.nn.sigmoid(gate_pre)
    grad_gate_pre = (
        grad_hidden * up_pre * sigmoid_gate * (1.0 + gate_pre * (1.0 - sigmoid_gate))
    ).astype(jnp.bfloat16)
    grad_up_pre = (grad_hidden * gate_pre * sigmoid_gate).astype(jnp.bfloat16)
    grad_down_local = jnp.einsum(
        "erf,erd->efd", hidden, grad_rows, preferred_element_type=jnp.float32
    )
    grad_gate_local = jnp.einsum(
        "erd,erf->edf", expert_rows, grad_gate_pre, preferred_element_type=jnp.float32
    )
    grad_up_local = jnp.einsum(
        "erd,erf->edf", expert_rows, grad_up_pre, preferred_element_type=jnp.float32
    )
    rows_back = jnp.einsum(
        "erf,edf->erd", grad_gate_pre, w_gate, preferred_element_type=jnp.float32
    )
    rows_back = (
        rows_back
        + jnp.einsum("erf,edf->erd", grad_up_pre, w_up, preferred_element_type=jnp.float32)
    ).astype(jnp.bfloat16)
    returned_grad = from_experts(source_layout(rows_back, dp_count, row_count))
    grad_table = jnp.concatenate(
        [returned_grad.reshape(total_slots, part_width), jnp.zeros((1, part_width), jnp.bfloat16)],
        axis=0,
    )
    inner_gate = jnp.sum(gate_weights * grad_gates, axis=1, keepdims=True)
    grad_chosen = gate_weights * (grad_gates - inner_gate)
    grad_logits = jnp.einsum("tk,tke->te", grad_chosen, choose, precision=HIGHEST)
    grad_router_part = jnp.einsum("td,te->de", normed_float, grad_logits, precision=HIGHEST)
    grad_normed = jnp.sum(grad_table[pair_slot].astype(jnp.float32), axis=1)
    grad_normed = grad_normed + jnp.einsum(
        "te,de->td", grad_logits, router_float, precision=HIGHEST
    )
    grad_gain_two_part = jnp.sum(grad_normed * resid_mid * rstd_two[:, None], axis=0)
    scaled_two = grad_normed * gain_two
    inner_two = feature_total(jnp.sum(scaled_two * resid_mid, axis=1))
    grad_resid = (
        grad_top
        + rstd_two[:, None] * scaled_two
        - resid_mid * (rstd_two * rstd_two * rstd_two * inner_two / D)[:, None]
    )
    branch_rows = tokens_by_col(grad_resid.astype(jnp.bfloat16))
    grad_out_local = jnp.einsum(
        "tc,td->cd", mixed_rows, branch_rows, preferred_element_type=jnp.float32
    ).reshape(w_out.shape)
    picked = branch_rows
    grad_mixed = lax.psum_scatter(
        jnp.einsum("td,cd->tc", picked, out_flat, preferred_element_type=jnp.float32).astype(
            jnp.bfloat16
        ),
        "row",
        scatter_dimension=0,
        tiled=True,
    ).astype(jnp.float32)
    grad_mixed = grad_mixed.astype(jnp.bfloat16).reshape(
        seq_count, length, kv_local, group_size, HD
    )
    grad_query, grad_key, grad_values = lax.map(
        attend_backward, (query_rot, key_rot, value_low, segment_ids, log_total, grad_mixed)
    )
    grad_query = rotate_back(
        grad_query, cosine[None, :, None, None, :], sine_table[None, :, None, None, :]
    )
    grad_key = rotate_back(grad_key, cosine[None, :, None, :], sine_table[None, :, None, :])
    grad_qkv_pre = jnp.concatenate(
        [grad_query.reshape(seq_count, length, kv_local, group_size * HD), grad_key, grad_values],
        axis=-1,
    )
    grad_qkv_pre = grad_qkv_pre.astype(jnp.bfloat16).reshape(att_rows, -1)
    qkv_rows = tokens_by_row(grad_qkv_pre)
    grad_qkv_local = jnp.einsum(
        "td,tc->dc", group_rows, qkv_rows, preferred_element_type=jnp.float32
    ).reshape(w_qkv.shape)

    def normed_term(first_row, block_rows):
        return jnp.einsum("tc,dc->td", qkv_rows, qkv_flat, preferred_element_type=jnp.float32)

    grad_normed_one = col_scatter(normed_term, tok_rows)
    grad_gain_one_part = jnp.sum(grad_normed_one * resid_in * rstd_one[:, None], axis=0)
    scaled_one = grad_normed_one * gain_one
    inner_one = feature_total(jnp.sum(scaled_one * resid_in, axis=1))
    grad_in = (
        grad_resid
        + rstd_one[:, None] * scaled_one
        - resid_in * (rstd_one * rstd_one * rstd_one * inner_one / D)[:, None]
    )
    col_sums = (
        lax.psum(grad_gate_local.astype(jnp.bfloat16), "col").astype(jnp.float32),
        lax.psum(grad_up_local.astype(jnp.bfloat16), "col").astype(jnp.float32),
        lax.psum(grad_down_local.astype(jnp.bfloat16), "col").astype(jnp.float32),
        lax.psum(grad_router_part.astype(jnp.bfloat16), "col").astype(jnp.float32),
        lax.psum(grad_gain_one_part.astype(jnp.bfloat16), "col").astype(jnp.float32),
        lax.psum(grad_gain_two_part.astype(jnp.bfloat16), "col").astype(jnp.float32),
    )
    dp_sums = (
        lax.psum(grad_qkv_local.astype(jnp.bfloat16), "dp").astype(jnp.float32),
        lax.psum(grad_out_local.astype(jnp.bfloat16), "dp").astype(jnp.float32),
        lax.psum(col_sums[3].astype(jnp.bfloat16), "dp").astype(jnp.float32),
        lax.psum(col_sums[4].astype(jnp.bfloat16), "dp").astype(jnp.float32),
        lax.psum(col_sums[5].astype(jnp.bfloat16), "dp").astype(jnp.float32),
    )
    return (
        layer_sum.astype(jnp.bfloat16),
        grad_in,
        dp_sums[3],
        dp_sums[0],
        dp_sums[1],
        dp_sums[4],
        dp_sums[2],
        col_sums[0],
        col_sums[1],
        col_sums[2],
    )

WINDOW = 512
BLOCK_Q = 256
LANES = 128
SMALL_ROWS = 48
GAIN_ONE = EXPERTS
GAIN_TWO = EXPERTS + 1
RSTD_LANE = LANES - 1
RSTD_ROW = 8
FIRST, SECOND, LATE = 1, 3, 2
F32 = jnp.float32
LOW = jnp.bfloat16
VMEM_BYTES = 67_000_000


def dot_nn(a, b):
    return jnp.dot(a, b, preferred_element_type=F32)


def dot_nt(a, b):
    return lax.dot_general(a, b, (((1,), (1,)), ((), ())), preferred_element_type=F32)


def dot_tn(a, b):
    return lax.dot_general(a, b, (((0,), (0,)), ((), ())), preferred_element_type=F32)


def rope_lanes(length):
    positions = np.arange(length, dtype=np.float32)
    frequency = (ROPE_BASE ** (-2.0 * np.arange(HD // 2, dtype=np.float32) / HD)).astype(np.float32)
    angles = (positions[:, None] * frequency[None, :]).astype(np.float32)
    cosine, sine = np.cos(angles), np.sin(angles)
    signed = np.concatenate([-sine, sine], axis=1)
    double = np.concatenate([cosine, cosine], axis=1)
    ones, zeros = np.ones_like(double), np.zeros_like(double)
    return np.stack(
        [
            np.concatenate([double, double], axis=1),
            np.concatenate([signed, signed], axis=1),
            np.concatenate([double, ones], axis=1),
            np.concatenate([signed, zeros], axis=1),
        ]
    ).astype(np.float32)


def swap_halves(values):
    half = HD // 2
    lane = lax.broadcasted_iota(jnp.int32, values.shape, 1)
    ahead = pltpu.roll(values, LANES - half, 1)
    behind = pltpu.roll(values, half, 1)
    return jnp.where(lane % HD < half, ahead, behind)


def window_mask(seg_col, seg_row, q_start, k_start):
    shape = (seg_col.shape[0], seg_row.shape[1])
    q_at = lax.broadcasted_iota(jnp.int32, shape, 0) + q_start
    k_at = lax.broadcasted_iota(jnp.int32, shape, 1) + k_start
    return (q_at >= k_at) & (seg_col == seg_row)


def remote(src, dst, send_sem, recv_sem, where):
    return pltpu.make_async_remote_copy(
        src_ref=src, dst_ref=dst, send_sem=send_sem, recv_sem=recv_sem,
        device_id=where, device_id_type=pl.DeviceIdType.MESH,
    )


class Copies:
    def __init__(self, send_sems, recv_sems):
        self.send_sems, self.recv_sems = send_sems, recv_sems
        self.sends = self.recvs = 0
        self.open = []

    def receivers(self, number=1):
        first = self.recvs
        self.recvs += number
        return first

    def send(self, src, dst, receiver, where, when=None):
        at = self.sends
        self.sends += 1
        copy = remote(src, dst, self.send_sems.at[at], self.recv_sems.at[receiver], where)
        if when is None:
            copy.start()
        else:
            pl.when(when)(copy.start)
        self.open.append((copy, when))

    def plan(self, src, dst, receiver, where):
        at = self.sends
        self.sends += 1
        copy = remote(src, dst, self.send_sems.at[at], self.recv_sems.at[receiver], where)
        self.open.append((copy, None))
        return copy

    def local(self, src, dst, when=None):
        at = self.sends
        self.sends += 1
        copy = pltpu.make_async_copy(src, dst, self.send_sems.at[at])
        if when is None:
            copy.start()
        else:
            pl.when(when)(copy.start)
        return copy

    def arrived(self, dst, receiver, where):
        remote(dst, dst, self.recv_sems.at[receiver], self.recv_sems.at[receiver], where).wait_recv()

    def finish(self):
        for copy, when in self.open:
            if when is None:
                copy.wait_send()
            else:
                pl.when(when)(copy.wait_send)


class Place:
    def __init__(self, counts):
        self.dp_count, self.row_count, self.col_count = counts
        self.dp, self.row, self.col = (lax.axis_index(name) for name in ("dp", "row", "col"))
        self.pair_row = self.row + 1 - 2 * lax.rem(self.row, 2)
        self.far_row = lax.rem(self.row + 2, self.row_count)
        self.cross_row = lax.rem(self.pair_row + 2, self.row_count)
        self.other_dp = self.dp_count - 1 - self.dp
        self.here = (self.dp, self.row, self.col)
        self.pair = (self.dp, self.pair_row, self.col)
        self.far = (self.dp, self.far_row, self.col)
        self.over = (self.other_dp, self.row, self.col)
        self.over_far = (self.other_dp, self.far_row, self.col)

    def row_at(self, step):
        return lax.rem(self.row + step + self.row_count, self.row_count)

    def col_at(self, step):
        return lax.rem(self.col + step + self.col_count, self.col_count)

    def block(self, dp_at, col_at):
        return dp_at * self.col_count + col_at

    def plane(self):
        peers = [(self.dp, self.row_at(k), self.col) for k in range(1, self.row_count)]
        return peers + [(self.other_dp, self.row_at(k), self.col) for k in range(self.row_count)]

    def column(self):
        return [(self.dp, self.row, self.col_at(k)) for k in range(1, self.col_count)]


class Spread:
    def __init__(self, place, copies, blocks, col_at):
        self.place, self.copies = place, copies
        dp, row, far_row = place.dp, place.row, place.far_row
        same, other = place.block(dp, col_at), place.block(place.other_dp, col_at)
        self.own, self.far = blocks.at[same, row], blocks.at[same, far_row]
        self.over, self.corner = blocks.at[other, row], blocks.at[other, far_row]
        self.pairs_same = (blocks.at[same, place.pair_row], blocks.at[same, place.cross_row])
        self.pairs_other = (blocks.at[other, place.pair_row], blocks.at[other, place.cross_row])
        self.at = copies.receivers(7)
        self.to_pair = copies.plan(self.own, self.own, self.at, place.pair)
        self.to_far = copies.plan(self.own, self.own, self.at + 1, place.far)
        self.to_over = copies.plan(self.own, self.own, self.at + 2, place.over)
        self.far_pair = copies.plan(self.far, self.far, self.at + 4, place.pair)
        self.over_pair = copies.plan(self.over, self.over, self.at + 5, place.pair)
        self.corner_pair = copies.plan(self.corner, self.corner, self.at + 6, place.pair)
        self.turn = None

    def begin(self, with_over):
        self.to_far.start()
        if with_over:
            self.to_over.start()
        self.to_pair.start()

    def send_over(self):
        self.to_over.start()

    def plan_corner(self, by_over):
        if by_over:
            self.turn = self.copies.plan(self.far, self.far, self.at + 3, self.place.over)
        else:
            self.turn = self.copies.plan(self.over, self.over, self.at + 3, self.place.far)

    def pass_far(self, corner):
        self.copies.arrived(self.far, self.at + 1, self.place.far)
        if corner:
            if self.turn is None:
                self.plan_corner(True)
            self.turn.start()
        self.far_pair.start()

    def pass_over(self, corner):
        self.copies.arrived(self.over, self.at + 2, self.place.over)
        if corner:
            if self.turn is None:
                self.plan_corner(False)
            self.turn.start()
        self.over_pair.start()

    def pass_corner(self):
        self.copies.arrived(self.corner, self.at + 3, self.place.here)
        self.corner_pair.start()

    def complete_same(self):
        for k, piece in zip((0, 4), self.pairs_same):
            self.copies.arrived(piece, self.at + k, self.place.pair)

    def complete_other(self):
        for k, piece in zip((5, 6), self.pairs_other):
            self.copies.arrived(piece, self.at + k, self.place.pair)

    def complete(self):
        self.complete_same()
        self.complete_other()


def say_hello(peers):
    barrier = pltpu.get_barrier_semaphore()
    for peer in peers:
        pl.semaphore_signal(barrier, inc=1, device_id=peer, device_id_type=pl.DeviceIdType.MESH)
    return functools.partial(pl.semaphore_wait, barrier, len(peers))


def greet(peers):
    say_hello(peers)()


def attend_forward_kernel(
    counts, hidden_hbm, own_q_hbm, own_o_hbm, small_hbm, seg_hbm, cot_hbm, tab_ref,
    resid_ref, low_ref, mix_ref, normed_ref, q_ref, k_ref, v_ref, lse_ref, wq_ref, zo_ref, small_ref, seg_ref, cot_all,
    h_ref, zq_ref, own_ref, column_ref, send_sems, recv_sems,
):
    place = Place(counts)
    row_count, col_count = place.row_count, place.col_count
    copies = Copies(send_sems, recv_sems)
    parts, length, width = h_ref.shape
    kv_heads = k_ref.shape[0]
    features = parts * width
    chunks = length // BLOCK_Q
    greet(place.plane() + place.column())

    h_pair, h_far, h_cross = (copies.receivers() for _ in range(3))
    copies.send(hidden_hbm, h_ref.at[place.row], h_far, place.far)
    copies.send(hidden_hbm, h_ref.at[place.row], h_pair, place.pair)
    h_own = copies.local(hidden_hbm, h_ref.at[place.row])
    zq_own = copies.local(own_q_hbm, zq_ref.at[place.col])
    zo_own = copies.local(own_o_hbm, zo_ref.at[place.col])
    small_own = copies.local(small_hbm, small_ref.at[place.row])
    seg_own = copies.local(seg_hbm, seg_ref.at[place.row])
    zq_in = copies.receivers(col_count)
    zo_in = copies.receivers(col_count)
    for k in range(1, col_count):
        copies.send(own_q_hbm, zq_ref.at[place.col], zq_in + k, (place.dp, place.row, place.col_at(k)))
    small_in, seg_in = copies.receivers(row_count), copies.receivers(row_count)
    for k in range(1, row_count):
        copies.send(small_hbm, small_ref.at[place.row], small_in + k, (place.dp, place.row_at(k), place.col))
        copies.send(seg_hbm, seg_ref.at[place.row], seg_in + k, (place.dp, place.row_at(k), place.col))
    cot_own = copies.local(cot_hbm, own_ref)
    cot_pair, cot_over, cot_back = copies.receivers(), copies.receivers(), copies.receivers(3)
    cot_far, cot_corner = copies.receivers(2), copies.receivers(2)
    own_cot = cot_all.at[place.block(place.dp, place.col), place.row]
    far_cot = cot_all.at[place.block(place.dp, place.col), place.far_row]
    half_rows = length // 2

    def send_cot_far(half):
        window = pl.ds(half * half_rows, half_rows)
        copies.send(cot_hbm.at[window], own_cot.at[window], cot_far + half, place.far)

    def pass_cot_far(half):
        piece = far_cot.at[pl.ds(half * half_rows, half_rows)]
        copies.arrived(piece, cot_far + half, place.far)
        copies.send(piece, piece, cot_corner + half, place.over)

    send_cot_far(0)
    copies.send(cot_hbm, own_cot, cot_over, place.over)
    copies.send(cot_hbm, own_cot, cot_pair, place.pair)

    def share_blocks(landing, result, landed, first, own):
        waits = []
        for k in range(col_count):
            source = place.col_at(-k)
            if k == 0:
                own.wait()
            else:
                copies.arrived(landing.at[source], landed + k, place.here)
            mine = source == place.row
            step = lax.rem(source - place.row + row_count, row_count)
            copies.send(
                landing.at[source], result.at[place.row], first + step, (place.dp, source, place.col), source != place.row
            )
            waits.append((copies.local(landing.at[source], result.at[place.row], mine), mine))
        return waits

    def blocks_shared(result, first, waits):
        for copy, mine in waits:
            pl.when(mine)(copy.wait)
        for k in range(1, row_count):
            copies.arrived(result.at[place.row_at(-k)], first + k, place.here)

    copies.arrived(h_ref.at[place.far_row], h_far, place.far)
    copies.send(h_ref.at[place.far_row], h_ref.at[place.far_row], h_cross, place.pair)
    wq_in = copies.receivers(row_count)
    wq_waits = share_blocks(zq_ref, wq_ref, zq_in, wq_in, zq_own)

    for k in range(1, col_count):
        copies.send(own_o_hbm, zo_ref.at[place.col], zo_in + k, (place.dp, place.row, place.col_at(k)))
    send_cot_far(1)
    pass_cot_far(0)
    cot_z = copies.receivers(col_count)
    for k in (FIRST,):
        copies.send(cot_hbm, own_cot, cot_z + k, (place.dp, place.row, place.col_at(k)))
    h_own.wait()
    copies.arrived(h_ref.at[place.pair_row], h_pair, place.pair)
    copies.arrived(h_ref.at[place.cross_row], h_cross, place.pair)
    small_own.wait()
    for k in range(1, row_count):
        copies.arrived(small_ref.at[place.row_at(-k)], small_in + k, place.here)

    @pl.loop(0, chunks)
    def _(chunk):
        rows = pl.ds(pl.multiple_of(chunk * BLOCK_Q, BLOCK_Q), BLOCK_Q)
        total = jnp.zeros((BLOCK_Q, 1), F32)
        for part in range(parts):
            piece = h_ref[part, rows, :].astype(F32)
            total = total + jnp.sum(piece * piece, axis=1, keepdims=True)
        rstd = lax.rsqrt(total / features + EPSILON)
        lse_ref[rows, :] = jnp.broadcast_to(rstd, (BLOCK_Q, LANES))
        for part in range(parts):
            piece = h_ref[part, rows, :].astype(F32)
            gain = small_ref[part, GAIN_ONE : GAIN_ONE + 1, :].astype(F32)
            normed_ref[rows, part * width : (part + 1) * width] = (piece * rstd * gain).astype(LOW)

    seg_own.wait()
    for k in range(1, row_count):
        copies.arrived(seg_ref.at[place.row_at(-k)], seg_in + k, place.here)
    segments = seg_ref[place.col]
    for start in range(0, length, LANES):
        column_ref[start : start + LANES, :] = jnp.broadcast_to(
            segments[0:1, start : start + LANES], (LANES, LANES)
        ).T

    cot_own.wait()
    cot_kept = copies.local(own_ref, own_cot)

    blocks_shared(wq_ref, wq_in, wq_waits)

    @pl.loop(0, chunks)
    def _(chunk):
        rows = pl.ds(pl.multiple_of(chunk * BLOCK_Q, BLOCK_Q), BLOCK_Q)
        qkv = dot_nn(normed_ref[rows, :], wq_ref[...].reshape(features, -1))
        for head in range(kv_heads):
            base = head * 4 * HD
            queries = qkv[:, base : base + LANES]
            queries = queries * tab_ref[0, rows, :] + swap_halves(queries) * tab_ref[1, rows, :]
            others = qkv[:, base + LANES : base + 2 * LANES]
            others = others * tab_ref[2, rows, :] + swap_halves(others) * tab_ref[3, rows, :]
            q_ref[2 * head, rows, :] = queries[:, :HD].astype(LOW)
            q_ref[2 * head + 1, rows, :] = queries[:, HD:].astype(LOW)
            k_ref[head, rows, :] = others[:, :HD].astype(LOW)
            v_ref[head, rows, :] = others[:, HD:].astype(LOW)

    scale = HD**-0.5
    lane = lax.broadcasted_iota(jnp.int32, (BLOCK_Q, LANES), 1)
    mix_pair, mix_far, mix_cross = (copies.receivers(chunks) for _ in range(3))

    def pass_on(block):
        piece = mix_ref.at[place.far_row, pl.ds(block * BLOCK_Q, BLOCK_Q)]
        copies.arrived(piece, mix_far + block, place.far)
        copies.send(piece, piece, mix_cross + block, place.pair)

    for block in range(chunks):
        q_start = block * BLOCK_Q
        k_start = max(0, q_start - WINDOW)
        q_rows, k_rows = slice(q_start, q_start + BLOCK_Q), slice(k_start, q_start + BLOCK_Q)
        mask = window_mask(column_ref[q_rows, 0:1], segments[0:1, k_rows], q_start, k_start)
        logs = lse_ref[q_rows, :]
        for head in range(2 * kv_heads):
            scores = dot_nt(q_ref[head, q_rows, :], k_ref[head // 2, k_rows, :]) * scale
            scores = jnp.where(mask, scores, NEG_LARGE)
            top = jnp.max(scores, axis=1, keepdims=True)
            weights = jnp.exp(scores - top)
            total = jnp.sum(weights, axis=1, keepdims=True)
            out = dot_nn(weights.astype(LOW), v_ref[head // 2, k_rows, :]) / total
            mix_ref[place.row, q_rows, head * HD : (head + 1) * HD] = out.astype(LOW)
            logs = jnp.where(lane == head, top + jnp.log(total), logs)
        lse_ref[q_rows, :] = logs
        piece = mix_ref.at[place.row, pl.ds(q_start, BLOCK_Q)]
        copies.send(piece, piece, mix_far + block, place.far)
        copies.send(piece, piece, mix_pair + block, place.pair)
        if block > 0:
            pass_on(block - 1)
        if block == 0:
            pass_cot_far(1)
            copies.send(far_cot, far_cot, cot_back, place.pair)
            over_cot = cot_all.at[place.block(place.other_dp, place.col), place.row]
            copies.arrived(over_cot, cot_over, place.over)
            copies.send(over_cot, over_cot, cot_back + 1, place.pair)
    pass_on(chunks - 1)
    corner_cot = cot_all.at[place.block(place.other_dp, place.col), place.far_row]
    for half in range(2):
        copies.arrived(
            corner_cot.at[pl.ds(half * half_rows, half_rows)], cot_corner + half, place.over
        )
    copies.send(corner_cot, corner_cot, cot_back + 2, place.pair)
    zo_own.wait()
    for k in range(1, col_count):
        copies.arrived(zo_ref.at[place.col_at(-k)], zo_in + k, place.here)
    for block in range(chunks):
        rows = slice(block * BLOCK_Q, (block + 1) * BLOCK_Q)
        window = pl.ds(block * BLOCK_Q, BLOCK_Q)
        copies.arrived(mix_ref.at[place.pair_row, window], mix_pair + block, place.pair)
        copies.arrived(mix_ref.at[place.cross_row, window], mix_cross + block, place.pair)
        branch = dot_nn(mix_ref[0, rows, :], zo_ref[0])
        for part in range(1, parts):
            branch = branch + dot_nn(mix_ref[part, rows, :], zo_ref[part])
        resid = h_ref[place.row, rows, :].astype(F32) + branch
        resid_ref[rows, :] = resid
        low_ref[rows, :] = resid.astype(LOW)

    cot_kept.wait()
    copies.arrived(cot_all.at[place.block(place.dp, place.col), place.pair_row], cot_pair, place.pair)
    for k, (dp_at, row_at) in enumerate(
        ((place.dp, place.cross_row), (place.other_dp, place.pair_row), (place.other_dp, place.cross_row))
    ):
        copies.arrived(cot_all.at[place.block(dp_at, place.col), row_at], cot_back + k, place.pair)
    for k in (FIRST,):
        copies.arrived(
            cot_all.at[place.block(place.dp, place.col_at(-k)), place.row], cot_z + k, place.here
        )
    copies.finish()


def attend_backward_kernel(
    counts, grad_low_hbm, grad_ref, hidden_ref, resid_ref, wo_ref, wq_ref, normed_ref, mix_hbm, q_ref, k_ref, v_ref, lse_ref,
    seg_ref, small_ref, part_ref, tab_ref, y_hbm, res_given, cot_given, low_hbm,
    out_ref, grad_in_ref, grads_ref, sums_ref, res_all, cot_all,
    gb_ref, mixed_ref, gm_ref, dq_ref, dk_ref, dv_ref, turn_ref, column_ref, y_own_ref, y_in_ref, y_chip_ref, y_last_ref,
    away_ref, pair_in_ref, own_ref, chip_ref, last_ref, inner_ref,
    send_sems, recv_sems,
):
    place = Place(counts)
    copies = Copies(send_sems, recv_sems)
    dp_count, row_count, col_count = counts
    parts, length, width = gb_ref.shape
    kv_heads = k_ref.shape[0]
    features = parts * width
    chunks = length // BLOCK_Q
    scale = HD**-0.5
    all_here = say_hello(place.plane() + place.column())
    segments = seg_ref[place.col]
    for start in range(0, length, LANES):
        column_ref[start : start + LANES, :] = jnp.broadcast_to(
            segments[0:1, start : start + LANES], (LANES, LANES)
        ).T
    dk_ref[...] = jnp.zeros_like(dk_ref)
    dv_ref[...] = jnp.zeros_like(dv_ref)
    all_here()

    def window(chunk):
        return pl.ds(chunk * BLOCK_Q, BLOCK_Q)

    blocks = range(chunks - 1, -1, -1)
    gb_far, gb_pair, gb_cross = (copies.receivers(chunks) for _ in range(3))
    for chunk in blocks:
        piece = gb_ref.at[place.row, window(chunk)]
        copies.send(grad_low_hbm.at[window(chunk)], piece, gb_far + chunk, place.far)
        copies.send(grad_low_hbm.at[window(chunk)], piece, gb_pair + chunk, place.pair)
    gb_own = copies.local(grad_low_hbm, gb_ref.at[place.row])
    mix_own = copies.local(mix_hbm.at[place.row], mixed_ref)
    y_pair = copies.receivers(2 * dp_count)
    y_held = []
    for turn, dp_at in enumerate((place.other_dp, place.dp)):
        for q, (here, there) in enumerate(
            ((place.row, place.pair_row), (place.far_row, place.cross_row))
        ):
            copies.send(y_hbm.at[dp_at, there], y_in_ref.at[turn, q], y_pair + 2 * turn + q, place.pair)
            y_held.append(copies.local(y_hbm.at[dp_at, here], y_own_ref.at[turn, q]))

    first = Spread(place, copies, res_all, place.col_at(-FIRST))
    first.plan_corner(True)
    own_block = place.block(place.dp, place.col)
    late_in = copies.receivers(2)
    late = (place.dp, place.row, place.col_at(LATE))
    own_cot = cot_all.at[own_block, place.row]
    copies.send(low_hbm, res_all.at[own_block, place.row], late_in, late)
    copies.send(own_cot, own_cot, late_in + 1, late)
    gb_own.wait()

    def pass_on(chunk):
        piece = gb_ref.at[place.far_row, window(chunk)]
        copies.arrived(piece, gb_far + chunk, place.far)
        copies.send(piece, piece, gb_cross + chunk, place.pair)

    y_last = copies.receivers(3)

    def y_over():
        for copy in y_held:
            copy.wait()
        for q in range(2):
            copies.arrived(y_in_ref.at[0, q], y_pair + q, place.pair)
            y_chip_ref[0, q] = (y_own_ref[0, q].astype(F32) + y_in_ref[0, q].astype(F32)).astype(LOW)
            copies.send(y_chip_ref.at[0, q], y_last_ref.at[q], y_last + q, place.over)

    def y_far():
        for q in range(2):
            copies.arrived(y_in_ref.at[1, q], y_pair + 2 + q, place.pair)
            copies.arrived(y_last_ref.at[q], y_last + q, place.over)
        y_chip_ref[1, 1] = (
            y_own_ref[1, 1].astype(F32) + y_in_ref[1, 1].astype(F32) + y_last_ref[1].astype(F32)
        ).astype(LOW)
        copies.send(y_chip_ref.at[1, 1], y_last_ref.at[2], y_last + 2, place.far)

    away_in = [copies.receivers(chunks) for _ in range(2)]
    last_in = copies.receivers(chunks)

    def far_share(chunk):
        rows = slice(chunk * BLOCK_Q, (chunk + 1) * BLOCK_Q)
        copies.arrived(pair_in_ref.at[1, window(chunk)], away_in[1] + chunk, place.pair)
        chip_ref[rows, :] = (own_ref[1, rows, :] + pair_in_ref[1, rows, :].astype(F32)).astype(LOW)
        copies.send(chip_ref.at[window(chunk)], last_ref.at[window(chunk)], last_in + chunk, place.far)

    y_over()
    first.begin(True)
    pass_on(chunks - 1)
    for block in blocks:
        q_start = block * BLOCK_Q
        k_start = max(0, q_start - WINDOW)
        q_rows, k_rows = slice(q_start, q_start + BLOCK_Q), slice(k_start, q_start + BLOCK_Q)
        copies.arrived(gb_ref.at[place.pair_row, window(block)], gb_pair + block, place.pair)
        copies.arrived(gb_ref.at[place.cross_row, window(block)], gb_cross + block, place.pair)
        total = dot_nt(gb_ref[0, q_rows, :], wo_ref[0])
        for part in range(1, parts):
            total = total + dot_nt(gb_ref[part, q_rows, :], wo_ref[part])
        gm_ref[...] = total.astype(LOW)
        mask = window_mask(column_ref[q_rows, 0:1], segments[0:1, k_rows], q_start, k_start)
        logs = lse_ref[q_rows, :]
        for kv in range(kv_heads):
            keys, vals = k_ref[kv, k_rows, :], v_ref[kv, k_rows, :]
            for head in (2 * kv, 2 * kv + 1):
                queries, grad = q_ref[head, q_rows, :], gm_ref[:, head * HD : (head + 1) * HD]
                scores = dot_nt(queries, keys) * scale
                weights = jnp.where(mask, jnp.exp(scores - logs[:, head : head + 1]), 0.0)
                grad_weights = dot_nt(grad, vals)
                inner = jnp.sum(weights * grad_weights, axis=1, keepdims=True)
                grad_scores = (weights * (grad_weights - inner)).astype(LOW)
                dv_ref[kv, k_rows, :] += dot_tn(weights.astype(LOW), grad)
                dk_ref[kv, k_rows, :] += dot_tn(grad_scores, queries)
                dq_ref[:, head * HD : (head + 1) * HD] = dot_nn(grad_scores, keys) * scale
        if block > 0:
            pass_on(block - 1)
        for kv in range(kv_heads):
            base = kv * 4 * HD
            queries = dq_ref[:, kv * LANES : (kv + 1) * LANES]
            queries = queries * tab_ref[0, q_rows, :] - swap_halves(queries) * tab_ref[1, q_rows, :]
            others = jnp.concatenate([dk_ref[kv, q_rows, :] * scale, dv_ref[kv, q_rows, :]], axis=1)
            others = others * tab_ref[2, q_rows, :] - swap_halves(others) * tab_ref[3, q_rows, :]
            turn_ref[q_rows, base : base + LANES] = queries.astype(LOW)
            turn_ref[q_rows, base + LANES : base + 2 * LANES] = others.astype(LOW)
        for q, row_at in ((1, place.cross_row), (0, place.pair_row)):
            away_ref[q, q_rows, :] = dot_nt(turn_ref[q_rows, :], wq_ref[row_at]).astype(LOW)
            copies.send(
                away_ref.at[q, window(block)], pair_in_ref.at[q, window(block)], away_in[q] + block, place.pair
            )
        for q, row_at in ((1, place.far_row), (0, place.row)):
            own_ref[q, q_rows, :] = dot_nt(turn_ref[q_rows, :], wq_ref[row_at])
        if block < chunks - 1:
            far_share(block + 1)
        if block == chunks - 2:
            y_far()
        if block == 0:
            first.pass_far(True)
            first.pass_over(False)

    columns = turn_ref.shape[1]
    mix_own.wait()
    for part in range(parts):
        grads_ref[part, :, :columns] = dot_tn(
            normed_ref[:, part * width : (part + 1) * width], turn_ref[...]
        ).astype(LOW)
        grads_ref[part, :, columns:] = dot_tn(mixed_ref[...], gb_ref[part]).astype(LOW)
        if part == 0:
            far_share(0)

    gain = small_ref[place.row, GAIN_ONE : GAIN_ONE + 1, :].astype(F32)
    inner_in = copies.receivers(row_count)
    gain_sum = jnp.zeros((1, width), F32)
    for chunk in blocks:
        rows = slice(chunk * BLOCK_Q, (chunk + 1) * BLOCK_Q)
        copies.arrived(pair_in_ref.at[0, window(chunk)], away_in[0] + chunk, place.pair)
        copies.arrived(last_ref.at[window(chunk)], last_in + chunk, place.far)
        grad_normed = own_ref[0, rows, :] + pair_in_ref[0, rows, :].astype(F32) + last_ref[rows, :].astype(F32)
        own_ref[0, rows, :] = grad_normed
        along = grad_normed * hidden_ref[rows, :].astype(F32)
        gain_sum = gain_sum + jnp.sum(along * lse_ref[rows, RSTD_LANE : RSTD_LANE + 1], axis=0, keepdims=True)
        inner_ref[place.row, 0:1, rows] = row_of(jnp.sum(along * gain, axis=1, keepdims=True))
    sums_ref[...] = part_ref[...]
    sums_ref[GAIN_ONE : GAIN_ONE + 1, :] = gain_sum
    for k in range(1, row_count):
        copies.send(
            inner_ref.at[place.row], inner_ref.at[place.row], inner_in + k, (place.dp, place.row_at(k), place.col)
        )
    copies.arrived(y_last_ref.at[2], y_last + 2, place.far)
    for chunk in range(chunks):
        rows = slice(chunk * BLOCK_Q, (chunk + 1) * BLOCK_Q)
        mixture = y_own_ref[1, 0, rows, :].astype(F32) + y_in_ref[1, 0, rows, :].astype(F32)
        for slot in (0, 2):
            mixture = mixture + y_last_ref[slot, rows, :].astype(F32)
        out_ref[rows, :] = (resid_ref[rows, :] + mixture).astype(LOW)

    for k in range(1, row_count):
        copies.arrived(inner_ref.at[place.row_at(-k)], inner_in + k, place.here)
    inner = inner_ref[0, 0:1, :]
    for part in range(1, row_count):
        inner = inner + inner_ref[part, 0:1, :]
    for chunk in range(chunks):
        rows = slice(chunk * BLOCK_Q, (chunk + 1) * BLOCK_Q)
        rstd = lse_ref[rows, RSTD_LANE : RSTD_LANE + 1]
        cube = rstd * rstd * rstd * column_of(inner[:, rows]) / features
        grad_in_ref[rows, :] = (
            grad_ref[rows, :] + rstd * (own_ref[0, rows, :] * gain) - hidden_ref[rows, :].astype(F32) * cube
        )
    first.pass_corner()
    first.complete()
    z_shard = (place.block(place.dp, place.col_at(-LATE)), place.row)
    copies.arrived(res_all.at[z_shard], late_in, place.here)
    copies.arrived(cot_all.at[z_shard], late_in + 1, place.here)
    copies.finish()


def expert_grads(gate_pre, up_pre, grad_hidden):
    sig = 1.0 / (1.0 + jnp.exp(-gate_pre))
    silu = gate_pre * sig
    grad_gate = grad_hidden * up_pre * (sig * (1.0 + gate_pre * (1.0 - sig)))
    return (silu * up_pre).astype(LOW), grad_gate.astype(LOW), (grad_hidden * silu).astype(LOW)


def slot_picks(rank_row, capacity):
    at = lax.broadcasted_iota(jnp.int32, (capacity, rank_row.shape[1]), 0).astype(F32)
    return at == rank_row


def column_of(row):
    return jnp.broadcast_to(row, (LANES, row.shape[1])).T[:, 0:1]


def row_of(column):
    return jnp.broadcast_to(column, (column.shape[0], LANES)).T[0:1, :]


def experts_kernel(
    counts, low_hbm, resid_ref, cot_own_ref, packed_hbm, cot_given, small_ref, zo_hbm, wg_hbm, wu_hbm, wd_hbm,
    y_hbm, grad_ref, grad_low_ref, table_ref, part_ref, wo_hbm, cot_all, res_all, slots_x, slots_g, slots_mid,
    wg_ref, wu_ref, wd_ref, res_ref, cot_ref, x_ref, packed_ref, rank_ref, gate_ref, g_ref, pick_ref, eo_ref, back_ref,
    away_ref, pair_in_ref, own_ref, chip_ref, last_ref, stage_ref, gg_ref, gg_in_ref, rstd_ref, inner_ref, nx_ref,
    keep_x_ref, keep_g_ref, keep_mid_ref, keep_sems,
    send_sems, recv_sems,
):
    place = Place(counts)
    copies = Copies(send_sems, recv_sems)
    dp_count, row_count, col_count = counts
    _, parts, length, width = res_ref.shape
    experts, features, hidden_width = wg_ref.shape
    capacity = pick_ref.shape[0] // experts
    chunks = length // BLOCK_Q
    total_experts = dp_count * row_count * experts
    pair_count = length * TOP
    first_expert = (place.dp * row_count + place.row) * experts
    order = (place.other_dp, place.dp)
    all_here = say_hello(place.plane() + place.column())
    packed_own = copies.local(packed_hbm, packed_ref.at[place.dp])
    cot_in = [
        copies.local(cot_all.at[place.block(dp_at, place.col)], cot_ref.at[dp_at])
        for dp_at in (place.dp, place.other_dp)
    ]

    weights_in = [copies.local(*pair) for pair in ((wg_hbm, wg_ref), (wu_hbm, wu_ref), (wd_hbm, wd_ref))]

    def ranks_of(dp_at):
        ids = packed_ref[dp_at] // pair_count
        orders = (packed_ref[dp_at] - ids * pair_count).astype(F32)
        rows = []
        for e in range(experts):
            match = ids == first_expert + e
            known = jnp.max(jnp.where(match, 1.0, 0.0), axis=0, keepdims=True)
            at = jnp.sum(jnp.where(match, orders, 0.0), axis=0, keepdims=True)
            rows.append(jnp.where(known > 0.0, at, float(pair_count)))
        stacked = jnp.concatenate(rows + [jnp.zeros((LANES - experts, length), F32)], axis=0)
        columns = stacked.T
        for e in range(experts):
            count = jnp.zeros((1, length), F32)
            for start in range(0, length, BLOCK_Q):
                before = columns[start : start + BLOCK_Q, e : e + 1] < rows[e]
                count = count + jnp.sum(jnp.where(before, 1.0, 0.0), axis=0, keepdims=True)
            rank_ref[dp_at, e : e + 1, :] = jnp.where(rows[e] < float(pair_count), count, -1.0)

    def gather_grads(dp_at):
        @pl.loop(0, experts)
        def _(e):
            pick = slot_picks(rank_ref[dp_at, pl.ds(e, 1), :], capacity).astype(F32).astype(LOW)
            slots = pl.ds(pl.multiple_of(e * capacity, capacity), capacity)
            for part in range(parts):
                g_ref[dp_at, part, slots, :] = dot_nn(pick, cot_ref[dp_at, part]).astype(LOW)

    packed_own.wait()
    ranks_of(place.dp)
    cot_in[0].wait()
    gather_grads(place.dp)
    all_here()

    own_low = res_ref.at[place.dp, place.row]
    packed_over = copies.receivers()
    copies.send(packed_hbm, packed_ref.at[place.dp], packed_over, place.over)
    low_own = copies.local(low_hbm, own_low)
    halves = 2
    half_rows = length // halves
    res_at = copies.receivers(7 * halves)

    def halved(ref, half):
        return ref.at[pl.ds(half * half_rows, half_rows)]

    far_low = res_ref.at[place.dp, place.far_row]
    over_low = res_ref.at[place.other_dp, place.row]
    corner_low = res_ref.at[place.other_dp, place.far_row]
    for half in range(halves):
        source, target = halved(low_hbm, half), halved(own_low, half)
        copies.send(source, target, res_at + half, place.far)
        copies.send(source, target, res_at + halves + half, place.over)
    copies.send(low_hbm, own_low, res_at + 2 * halves, place.pair)
    own_block = place.block(place.dp, place.col)
    res_z, cot_z = copies.receivers(col_count), copies.receivers(col_count)
    for k, on_cot in ((FIRST, False), (SECOND, True), (SECOND, False)):
        peer = (place.dp, place.row, place.col_at(k))
        if on_cot:
            own_cot = cot_all.at[own_block, place.row]
            copies.send(own_cot, own_cot, cot_z + k, peer)
        else:
            copies.send(low_hbm, res_all.at[own_block, place.row], res_z + k, peer)

    def pass_side(half):
        copies.arrived(halved(far_low, half), res_at + half, place.far)
        copies.arrived(halved(over_low, half), res_at + halves + half, place.over)
        corner, peer = (far_low, place.over) if half == 0 else (over_low, place.far)
        copies.send(halved(corner, half), halved(corner, half), res_at + 3 * halves + half, peer)
        for k, ref in ((4, far_low), (5, over_low)):
            copies.send(halved(ref, half), halved(ref, half), res_at + k * halves + half, place.pair)

    def pass_corner(half):
        copies.arrived(halved(corner_low, half), res_at + 3 * halves + half, place.here)
        copies.send(
            halved(corner_low, half), halved(corner_low, half), res_at + 6 * halves + half, place.pair
        )

    copies.arrived(packed_ref.at[place.other_dp], packed_over, place.over)
    ranks_of(place.other_dp)
    pass_side(0)
    cot_in[1].wait()
    gather_grads(place.other_dp)
    pass_side(1)
    pass_corner(0)
    pass_corner(1)

    wo_in = copies.receivers(row_count)
    own_wo = copies.local(zo_hbm.at[place.row], stage_ref.at[0, pl.ds(0, zo_hbm.shape[1])])

    low_own.wait()
    copies.arrived(res_ref.at[place.dp, place.pair_row], res_at + 2 * halves, place.pair)
    for half in range(halves):
        for k, dp_at, row_at in (
            (4, place.dp, place.cross_row), (5, place.other_dp, place.pair_row), (6, place.other_dp, place.cross_row)
        ):
            copies.arrived(halved(res_ref.at[dp_at, row_at], half), res_at + k * halves + half, place.pair)
    for copy in weights_in:
        copy.wait()
    own_wo.wait()
    kept_wo = copies.local(stage_ref.at[0, pl.ds(0, zo_hbm.shape[1])], wo_hbm.at[place.row])
    kept_wo.wait()
    res_kept = [
        copies.local(res_ref.at[dp_at], res_all.at[place.block(dp_at, place.col)])
        for dp_at in (place.dp, place.other_dp)
    ]
    first = Spread(place, copies, cot_all, place.col_at(-FIRST))
    first.plan_corner(True)
    first.begin(True)

    own_scaled = place.row
    gg_same, gg_other = copies.receivers(row_count), copies.receivers(row_count)
    pair_in = copies.receivers(2 * dp_count)
    last_over, last_across, last_far = (copies.receivers() for _ in range(3))
    table_in = copies.receivers(col_count)

    kept_pairs = ((keep_x_ref, slots_x), (keep_g_ref, slots_g), (keep_mid_ref, slots_mid))
    for turn, dp_at in enumerate(order):
        last = turn == dp_count - 1

        @pl.loop(0, chunks)
        def _(chunk):
            rows = pl.ds(pl.multiple_of(chunk * BLOCK_Q, BLOCK_Q), BLOCK_Q)
            total = jnp.zeros((BLOCK_Q, 1), F32)
            for part in range(parts):
                piece = res_ref[dp_at, part, rows, :].astype(F32)
                total = total + jnp.sum(piece * piece, axis=1, keepdims=True)
            rstd = lax.rsqrt(total / features + EPSILON)
            for part in range(parts):
                piece = res_ref[dp_at, part, rows, :].astype(F32)
                gain = small_ref[part, GAIN_TWO : GAIN_TWO + 1, :].astype(F32)
                x_ref[rows, part * width : (part + 1) * width] = (piece * rstd * gain).astype(LOW)
            table_ref[place.col, dp_at, RSTD_ROW : RSTD_ROW + 1, rows] = row_of(rstd)
            if last:
                rstd_ref[rows, :] = jnp.broadcast_to(rstd, (BLOCK_Q, LANES))
                piece = res_ref[dp_at, own_scaled, rows, :].astype(F32)
                gain = small_ref[own_scaled, GAIN_TWO : GAIN_TWO + 1, :].astype(F32)
                nx_ref[rows, :] = (piece * rstd * gain).astype(LOW)

        logits = jnp.zeros((total_experts, length), F32)
        for part in range(parts):
            logits = logits + dot_nt(
                small_ref[part, :total_experts, :], x_ref[:, part * width : (part + 1) * width]
            )
        ids = packed_ref[dp_at] // pair_count
        expert_at = lax.broadcasted_iota(jnp.int32, (total_experts, length), 0)
        chosen = expert_at == ids[0:1, :]
        for k in range(1, TOP):
            chosen = chosen | (expert_at == ids[k : k + 1, :])
        shown = jnp.where(chosen, logits, NEG_LARGE)
        weights = jnp.where(chosen, jnp.exp(shown - jnp.max(shown, axis=0, keepdims=True)), 0.0)
        gate_ref[...] = weights / jnp.sum(weights, axis=0, keepdims=True)
        table_ref[place.col, dp_at, 0:experts, :] = rank_ref[dp_at, 0:experts, :]
        for e in range(experts):
            table_ref[place.col, dp_at, experts + e : experts + e + 1, :] = gate_ref[pl.ds(first_expert + e, 1), :]

        @pl.loop(0, experts)
        def _(e):
            if last:
                pl.when(e == experts - 2)(first.pass_corner)

            keep = lax.rem(e, 2)
            kept = [
                pltpu.make_async_copy(held.at[keep], target.at[turn, e], keep_sems.at[k, keep])
                for k, (held, target) in enumerate(kept_pairs)
            ]

            @pl.when(e + turn * experts >= 2)
            def _():
                for copy in kept:
                    copy.wait()

            here = slot_picks(rank_ref[dp_at, pl.ds(e, 1), :], capacity)
            pick = here.astype(F32).astype(LOW)
            slots = pl.ds(pl.multiple_of(e * capacity, capacity), capacity)
            pick_ref[slots, :] = pick
            gate_slot = jnp.sum(
                jnp.where(here, gate_ref[pl.ds(first_expert + e, 1), :], 0.0), axis=1, keepdims=True
            )
            x = dot_nn(pick, x_ref[...]).astype(LOW)
            keep_x_ref[keep] = x
            grad_hidden = jnp.zeros((capacity, hidden_width), F32)
            for part in range(parts):
                pair_grad = (g_ref[dp_at, part, slots, :].astype(F32) * gate_slot).astype(LOW)
                keep_g_ref[keep, :, part * width : (part + 1) * width] = pair_grad
                grad_hidden = grad_hidden + dot_nt(
                    pair_grad, wd_ref[e, :, part * width : (part + 1) * width]
                )
            hidden, grad_gate, grad_up = expert_grads(dot_nn(x, wg_ref[e]), dot_nn(x, wu_ref[e]), grad_hidden)
            keep_mid_ref[keep, 0] = hidden
            keep_mid_ref[keep, 1] = grad_gate
            keep_mid_ref[keep, 2] = grad_up
            for copy in kept:
                copy.start()
            along = jnp.zeros((capacity, 1), F32)
            for part in range(parts):
                cols = slice(part * width, (part + 1) * width)
                out = dot_nn(hidden, wd_ref[e, :, cols]).astype(LOW).astype(F32)
                along = along + jnp.sum(g_ref[dp_at, part, slots, :].astype(F32) * out, axis=1, keepdims=True)
                eo_ref[part, slots, :] = (out * gate_slot).astype(LOW)
                back_ref[part, slots, :] = (
                    dot_nt(grad_gate, wg_ref[e, cols, :]) + dot_nt(grad_up, wu_ref[e, cols, :])
                ).astype(LOW)
            gg_ref[dp_at, pl.ds(e, 1), :] = jnp.sum(jnp.where(here, along, 0.0), axis=0, keepdims=True)

        if not last:
            first.pass_far(True)
            first.pass_over(False)
        owner = place.dp * row_count + place.row
        if last:
            for k in range(1, row_count):
                copies.send(gg_ref.at[dp_at], gg_in_ref.at[owner], gg_same + k, (dp_at, place.row_at(k), place.col))
            gg_in_ref[owner] = gg_ref[dp_at]
        else:
            for k in range(row_count):
                copies.send(gg_ref.at[dp_at], gg_in_ref.at[owner], gg_other + k, (dp_at, place.row_at(k), place.col))

        for q, row_at in enumerate((place.pair_row, place.cross_row)):
            away_ref[turn, q] = dot_tn(pick_ref[...], back_ref[row_at]).astype(LOW)
            copies.send(away_ref.at[turn, q], pair_in_ref.at[turn, q], pair_in + 2 * turn + q, place.pair)
        for q, row_at in enumerate((place.far_row, place.row)):
            own_ref[q] = dot_tn(pick_ref[...], back_ref[row_at])
        copies.arrived(pair_in_ref.at[turn, 1], pair_in + 2 * turn + 1, place.pair)
        far_sum = own_ref[0] + pair_in_ref[turn, 1].astype(F32)
        if last:
            copies.arrived(last_ref.at[1], last_across, place.over)
            chip_ref[turn, 1] = (far_sum + last_ref[1].astype(F32)).astype(LOW)
            copies.send(chip_ref.at[turn, 1], last_ref.at[2], last_far, place.far)
        else:
            chip_ref[turn, 1] = far_sum.astype(LOW)
            copies.send(chip_ref.at[turn, 1], last_ref.at[1], last_across, place.over)
        copies.arrived(pair_in_ref.at[turn, 0], pair_in + 2 * turn, place.pair)
        if last:
            own_ref[1] = own_ref[1] + pair_in_ref[turn, 0].astype(F32)
        else:
            chip_ref[turn, 0] = (own_ref[1] + pair_in_ref[turn, 0].astype(F32)).astype(LOW)
            copies.send(chip_ref.at[turn, 0], last_ref.at[0], last_over, place.over)
            for k in range(col_count):
                source = place.col_at(k)
                mine = source == place.row
                step = lax.rem(source - place.row + row_count, row_count)
                copies.send(
                    zo_hbm.at[source], wo_hbm.at[place.row], wo_in + step, (place.dp, source, place.col), jnp.logical_not(mine)
                )

        for part in range(parts):
            stage_ref[part] = dot_tn(pick_ref[...], eo_ref[part]).astype(LOW)
        kept = copies.local(stage_ref, y_hbm.at[dp_at])
        kept.wait()

    for k in range(1, col_count):
        copies.send(table_ref.at[place.col], table_ref.at[place.col], table_in + k, (place.dp, place.row, place.col_at(k)))

    for k in range(1, row_count):
        copies.arrived(gg_in_ref.at[place.dp * row_count + place.row_at(-k)], gg_same + k, place.here)
    for k in range(row_count):
        copies.arrived(gg_in_ref.at[place.other_dp * row_count + place.row_at(-k)], gg_other + k, place.here)
    along = jnp.concatenate([gg_in_ref[owner, :experts, :] for owner in range(dp_count * row_count)], axis=0)
    gates = gate_ref[...]
    grad_logits = (gates * (along - jnp.sum(gates * along, axis=0, keepdims=True))).astype(LOW)
    router = small_ref[place.row, :total_experts, :]
    gain = small_ref[place.row, GAIN_TWO : GAIN_TWO + 1, :].astype(F32)
    part_ref[...] = jnp.zeros_like(part_ref)
    part_ref[:total_experts, :] = dot_nn(grad_logits, nx_ref[...])
    own_ref[1] = own_ref[1] + dot_tn(grad_logits, router)

    copies.arrived(last_ref.at[0], last_over, place.over)
    copies.arrived(last_ref.at[2], last_far, place.far)
    inner_in = copies.receivers(row_count)
    gain_sum = jnp.zeros((1, width), F32)
    for chunk in range(chunks):
        rows = slice(chunk * BLOCK_Q, (chunk + 1) * BLOCK_Q)
        grad_normed = own_ref[1, rows, :]
        for k in (0, 2):
            grad_normed = grad_normed + last_ref[k, rows, :].astype(F32)
        own_ref[0, rows, :] = grad_normed
        along = grad_normed * resid_ref[rows, :]
        gain_sum = gain_sum + jnp.sum(along * rstd_ref[rows, 0:1], axis=0, keepdims=True)
        inner_ref[place.row, 0:1, rows] = row_of(jnp.sum(along * gain, axis=1, keepdims=True))
    part_ref[GAIN_TWO : GAIN_TWO + 1, :] = gain_sum
    for k in range(1, row_count):
        copies.send(
            inner_ref.at[place.row], inner_ref.at[place.row], inner_in + k, (place.dp, place.row_at(k), place.col)
        )
    for k in range(1, row_count):
        copies.arrived(inner_ref.at[place.row_at(-k)], inner_in + k, place.here)
    inner = inner_ref[0, 0:1, :]
    for part in range(1, row_count):
        inner = inner + inner_ref[part, 0:1, :]
    for chunk in range(chunks):
        rows = slice(chunk * BLOCK_Q, (chunk + 1) * BLOCK_Q)
        rstd = rstd_ref[rows, 0:1]
        cube = rstd * rstd * rstd * column_of(inner[:, rows]) / features
        grad = (
            cot_own_ref[rows, :].astype(F32) + rstd * (own_ref[0, rows, :] * gain) - resid_ref[rows, :] * cube
        )
        grad_ref[rows, :] = grad
        grad_low_ref[rows, :] = grad.astype(LOW)

    for copy in res_kept:
        copy.wait()
    for keep in range(2):
        for k, (held, target) in enumerate(kept_pairs):
            pltpu.make_async_copy(held.at[keep], target.at[0, 0], keep_sems.at[k, keep]).wait()
    first.complete()
    for k in (FIRST, SECOND):
        z_shard = (place.block(place.dp, place.col_at(-k)), place.row)
        copies.arrived(res_all.at[z_shard], res_z + k, place.here)
        if k != FIRST:
            copies.arrived(cot_all.at[z_shard], cot_z + k, place.here)
    for k in range(1, row_count):
        copies.arrived(wo_hbm.at[place.row_at(-k)], wo_in + k, place.here)
    for k in range(1, col_count):
        copies.arrived(table_ref.at[place.col_at(-k)], table_in + k, place.here)
    copies.finish()


def slot_grads(picked, rank_row, gate_row, rstd_row, res, cot, small_ref, wg, wu, wd):
    here = slot_picks(rank_row, picked)
    pick = here.astype(F32).astype(LOW)
    gate_slot = jnp.sum(jnp.where(here, gate_row, 0.0), axis=1, keepdims=True)
    rstd_slot = jnp.sum(jnp.where(here, rstd_row, 0.0), axis=1, keepdims=True)
    parts = res.shape[0]
    x = jnp.concatenate(
        [
            (
                dot_nn(pick, res[part]) * rstd_slot * small_ref[part, GAIN_TWO : GAIN_TWO + 1, :].astype(F32)
            ).astype(LOW)
            for part in range(parts)
        ],
        axis=1,
    )
    pair_grad = jnp.concatenate(
        [(dot_nn(pick, cot[part]) * gate_slot).astype(LOW) for part in range(parts)], axis=1
    )
    hidden, grad_gate, grad_up = expert_grads(dot_nn(x, wg), dot_nn(x, wu), dot_nt(pair_grad, wd))
    return x, pair_grad, hidden, grad_gate, grad_up


def weight_grads_kernel(
    counts, res_given, cot_given, grads_hbm, slots_x, slots_g, slots_mid, part_ref, table_ref, small_ref,
    wg_hbm, wu_hbm, wd_hbm,
    res_all, cot_all, dg_hbm, du_hbm, dd_hbm, own_ref, sums_ref,
    wg_ref, wu_ref, wd_ref, parts_ref, dg_ref, du_ref, dd_ref, res_ref, cot_ref, x_ref, g_ref, mid_ref, grads_in_ref, sum_ref,
    sems, keep_sems, out_sems, send_sems, recv_sems,
):
    place = Place(counts)
    copies = Copies(send_sems, recv_sems)
    dp_count, row_count, col_count = counts
    experts = wg_ref.shape[0]
    _, parts, length, width = res_all.shape
    capacity = length * TOP // (dp_count * row_count * experts)
    far_side = [(place.other_dp, place.row, place.col_at(k)) for k in range(1, col_count)]
    all_here = say_hello(
        place.plane()
        + place.column()
        + [
            (place.dp, place.row_at(j), place.col_at(k))
            for j in range(1, row_count)
            for k in range(1, col_count)
        ]
        + far_side
    )
    steps = 5
    before_late = 4 * experts

    def fetch(step):
        back = jnp.where(step < 2, FIRST, jnp.where(step < 4, SECOND, LATE))
        dp_at = lax.rem(place.dp + lax.rem(step, 2), dp_count)
        col_at = place.col_at(-back)
        b, slot = place.block(dp_at, col_at), lax.rem(step, 2)
        return dp_at, col_at, slot, (
            pltpu.make_async_copy(res_all.at[b], res_ref.at[slot], sems.at[slot]),
            pltpu.make_async_copy(cot_all.at[b], cot_ref.at[slot], sems.at[2 + slot]),
        )

    def kept_slots(turn):
        at, e, slot = turn // experts, lax.rem(turn, experts), lax.rem(turn, 2)
        pairs = ((slots_x, x_ref), (slots_g, g_ref), (slots_mid, mid_ref))
        return [
            pltpu.make_async_copy(source.at[at, e], target.at[slot], keep_sems.at[k, slot])
            for k, (source, target) in enumerate(pairs)
        ]

    for copy in fetch(0)[3]:
        copy.start()
    weights_in = [copies.local(*pair) for pair in ((wg_hbm, wg_ref), (wu_hbm, wu_ref), (wd_hbm, wd_ref))]
    for copy in kept_slots(0):
        copy.start()
    parts_ref[0] = part_ref[...]
    others = place.column() + [place.over] + far_side
    sums_in = copies.receivers(len(others) + 1)
    sum_sends = [
        copies.plan(parts_ref.at[0], parts_ref.at[k + 1], sums_in + k + 1, peer) for k, peer in enumerate(others)
    ]

    grads_in = copies.receivers(col_count)
    grads_kept = copies.local(grads_hbm.at[place.col], grads_in_ref.at[place.col])
    mine = place.row == place.col
    over_in, swap_in = copies.receivers(), copies.receivers()
    to_over = copies.plan(sum_ref.at[0], sum_ref.at[1], over_in, place.over)
    to_swap = remote(
        sum_ref.at[2], sum_ref.at[3], copies.send_sems.at[copies.sends], copies.recv_sems.at[swap_in],
        (place.dp, place.col, place.row),
    )
    copies.sends += 1
    copies.open.append((to_swap, jnp.logical_not(mine)))
    two_res, two_cot, three_res, three_cot = (
        Spread(place, copies, array, place.col_at(-k)) for k in (SECOND, LATE) for array in (res_all, cot_all)
    )
    for spread, by_over in ((two_res, True), (two_cot, False), (three_res, True), (three_cot, False)):
        spread.plan_corner(by_over)

    grad_sends = [
        copies.plan(
            grads_hbm.at[place.col_at(k)], grads_in_ref.at[place.col], grads_in + k,
            (place.dp, place.row, place.col_at(k)),
        )
        for k in range(1, col_count)
    ]

    def begin():
        all_here()
        two_res.begin(True)
        two_cot.begin(True)
        for copy in grad_sends + sum_sends:
            copy.start()

    def sum_columns():
        grads_kept.wait()
        for k in range(1, col_count):
            copies.arrived(grads_in_ref.at[place.col_at(-k)], grads_in + k, place.here)
        total = grads_in_ref[0].astype(F32)
        for col_at in range(1, col_count):
            total = total + grads_in_ref[col_at].astype(F32)
        sum_ref[0] = total.astype(LOW)
        to_over.start()

    def sum_over():
        copies.arrived(sum_ref.at[1], over_in, place.over)
        total = sum_ref[0].astype(F32) + sum_ref[1].astype(F32)
        sum_ref[2] = total.astype(LOW)
        own_ref[...] = total
        pl.when(jnp.logical_not(mine))(to_swap.start)

    def sum_parts():
        total = parts_ref[0]
        for k in range(len(others)):
            copies.arrived(parts_ref.at[k + 1], sums_in + k + 1, place.here)
            total = total + parts_ref[k + 1]
        sums_ref[...] = total

    def take_swapped():
        @pl.when(jnp.logical_not(mine))
        def _():
            copies.arrived(sum_ref.at[3], swap_in, place.here)
            own_ref[...] = sum_ref[3].astype(F32)

    def begin_late():
        three_res.to_far.start()
        three_res.to_over.start()
        three_res.to_pair.start()
        three_cot.to_pair.start()

    events = {
        1: [begin],
        5: [lambda: two_res.pass_far(True), lambda: two_res.pass_over(False)],
        7: [two_res.complete_same],
        8: [
            lambda: two_cot.pass_far(False), lambda: two_cot.pass_over(True), begin_late, two_cot.complete_same
        ],
        12: [
            two_res.pass_corner, two_cot.pass_corner, three_cot.to_far.start, three_cot.to_over.start,
            two_res.complete_other, two_cot.complete_other,
        ],
        13: [sum_columns],
        14: [sum_parts],
        15: [lambda: three_res.pass_far(True), lambda: three_res.pass_over(False), sum_over],
        16: [
            lambda: three_cot.pass_far(False), lambda: three_cot.pass_over(True),
            three_res.complete_same, three_cot.complete_same,
        ],
        18: [three_res.pass_corner, take_swapped],
    }
    for copy in weights_in:
        copy.wait()

    def other_blocks(turn):
        step, e = turn // experts, lax.rem(turn, experts)
        for at, actions in events.items():

            @pl.when(turn == at)
            def _(actions=actions):
                for action in actions:
                    action()

        dp_at, col_at, slot, arriving = fetch(step)

        @pl.when(e == 0)
        def _():
            @pl.when(step >= 2)
            def _():
                for copy in arriving:
                    copy.start()

            for copy in arriving:
                copy.wait()

        @pl.when(turn == experts - 1)
        def _():
            for copy in fetch(1)[3]:
                copy.start()

        x, pair_grad, hidden, grad_gate, grad_up = slot_grads(
            capacity,
            table_ref[col_at, dp_at, pl.ds(e, 1), :],
            table_ref[col_at, dp_at, pl.ds(experts + e, 1), :],
            table_ref[col_at, dp_at, RSTD_ROW : RSTD_ROW + 1, :],
            res_ref.at[slot], cot_ref.at[slot], small_ref, wg_ref[e], wu_ref[e], wd_ref[e],
        )
        down, gate, up = dot_tn(hidden, pair_grad), dot_tn(x, grad_gate), dot_tn(x, grad_up)

        @pl.when(step == 0)
        def _():
            dd_ref[e], dg_ref[e], du_ref[e] = down, gate, up

        @pl.when(step > 0)
        def _():
            dd_ref[e] += down
            dg_ref[e] += gate
            du_ref[e] += up

        @pl.when(step == steps - 1)
        def _():
            for k, (source, target) in enumerate(((dg_ref, dg_hbm), (du_ref, du_hbm), (dd_ref, dd_hbm))):
                pltpu.make_async_copy(source.at[e], target.at[e], out_sems.at[k, e]).start()

    pl.loop(0, before_late)(other_blocks)

    @pl.loop(0, dp_count * experts)
    def _(turn):
        e, slot = lax.rem(turn, experts), lax.rem(turn, 2)
        for copy in kept_slots(turn):
            copy.wait()

        @pl.when(turn + 1 < dp_count * experts)
        def _():
            for copy in kept_slots(turn + 1):
                copy.start()

        down, gate, up = (
            dot_tn(mid_ref[slot, 0], g_ref[slot]),
            dot_tn(x_ref[slot], mid_ref[slot, 1]),
            dot_tn(x_ref[slot], mid_ref[slot, 2]),
        )

        dd_ref[e] += down
        dg_ref[e] += gate
        du_ref[e] += up

    pl.loop(before_late, steps * experts)(other_blocks)
    three_cot.pass_corner()
    three_res.complete_other()
    three_cot.complete_other()
    for e in range(experts):
        for k, (source, target) in enumerate(((dg_ref, dg_hbm), (du_ref, du_hbm), (dd_ref, dd_hbm))):
            pltpu.make_async_copy(source.at[e], target.at[e], out_sems.at[k, e]).wait()
    copies.finish()


def last_grads_kernel(
    counts, res_all, cot_all, table_ref, small_ref, wg_ref, wu_ref, wd_ref, dg_in, du_in, dd_in,
    out_in, grad_in_in, attn_in,
    dg_ref, du_ref, dd_ref, out_ref, grad_in_ref, qkv_ref, wo_ref, res_ref, cot_ref, sems,
):
    dp_count, row_count, col_count = counts
    e = pl.program_id(0)
    experts = pl.num_programs(0)
    _, parts, length, width = res_all.shape
    capacity = length * TOP // (dp_count * row_count * experts)
    col_at = lax.rem(lax.axis_index("col") + col_count - LATE, col_count)
    dp_at = dp_count - 1 - lax.axis_index("dp")

    @pl.when(e == 0)
    def _():
        b = dp_at * col_count + col_at
        arriving = [
            pltpu.make_async_copy(res_all.at[b], res_ref, sems.at[0]),
            pltpu.make_async_copy(cot_all.at[b], cot_ref, sems.at[1]),
        ]
        for copy in arriving:
            copy.start()
        for copy in arriving:
            copy.wait()

    out_ref[...] = out_in[...]
    grad_in_ref[...] = grad_in_in[...]
    columns = qkv_ref.shape[1]
    qkv_ref[...] = attn_in[:, :columns]
    wo_ref[...] = attn_in[:, columns:]
    x, pair_grad, hidden, grad_gate, grad_up = slot_grads(
        capacity,
        table_ref[col_at, dp_at, pl.ds(e, 1), :],
        table_ref[col_at, dp_at, pl.ds(experts + e, 1), :],
        table_ref[col_at, dp_at, RSTD_ROW : RSTD_ROW + 1, :],
        res_ref, cot_ref, small_ref, wg_ref[0], wu_ref[0], wd_ref[0],
    )
    dd_ref[0] = dd_in[0] + dot_tn(hidden, pair_grad)
    dg_ref[0] = dg_in[0] + dot_tn(x, grad_gate)
    du_ref[0] = du_in[0] + dot_tn(x, grad_up)


def fast_device(
    hidden_in, norm_gain, w_qkv, w_out, ffn_gain, router, w_gate, w_up, w_down, cotangent,
    segment_ids, expert_ids, pair_order,
):
    dp_count, row_count, col_count = (lax.axis_size(name) for name in ("dp", "row", "col"))
    my_dp, my_row, my_col = (lax.axis_index(name) for name in ("dp", "row", "col"))
    length, width = hidden_in.shape
    kv_local = w_qkv.shape[1]
    head_width = kv_local * (HQ // HK) * HD
    qkv_width = kv_local * (HQ // HK + 2) * HD
    exp_local, _, hidden_width = w_gate.shape
    capacity = length * TOP // EXPERTS
    blocks = dp_count * col_count
    vmem = pl.BlockSpec(memory_space=pltpu.VMEM)
    hbm = pl.BlockSpec(memory_space=pl.ANY)
    params = pltpu.CompilerParams(vmem_limit_bytes=VMEM_BYTES)

    packed = (expert_ids * (length * TOP) + pair_order).T
    own_q = w_qkv.reshape(width, qkv_width)
    own_o = w_out.reshape(head_width, width)
    small = jnp.concatenate(
        [router.T, norm_gain[None], ffn_gain[None], jnp.zeros((SMALL_ROWS - 2 - EXPERTS, width), LOW)], axis=0
    )
    seg_rows = jnp.broadcast_to(segment_ids, (8, length)).astype(F32)
    tables = jnp.asarray(rope_lanes(length))
    counts = (dp_count, row_count, col_count)
    (
        resid_mid, resid_low, mixed_all, normed_one, query_rot, key_rot, value_low, logs,
        wq_rows, wo_cols, small_all, seg_all, cot_all,
    ) = pl.pallas_call(
        functools.partial(attend_forward_kernel, counts),
        out_shape=(
            jax.ShapeDtypeStruct((length, width), F32),
            jax.ShapeDtypeStruct((length, width), LOW),
            jax.ShapeDtypeStruct((row_count, length, head_width), LOW),
            jax.ShapeDtypeStruct((length, D), LOW),
            jax.ShapeDtypeStruct((2 * kv_local, length, HD), LOW),
            jax.ShapeDtypeStruct((kv_local, length, HD), LOW),
            jax.ShapeDtypeStruct((kv_local, length, HD), LOW),
            jax.ShapeDtypeStruct((length, LANES), F32),
            jax.ShapeDtypeStruct((row_count, width, qkv_width), LOW),
            jax.ShapeDtypeStruct((col_count, head_width, width), LOW),
            jax.ShapeDtypeStruct((row_count, SMALL_ROWS, width), LOW),
            jax.ShapeDtypeStruct((row_count, 8, length), F32),
            jax.ShapeDtypeStruct((blocks, row_count, length, width), LOW),
        ),
        in_specs=[hbm] * 6 + [vmem],
        out_specs=[vmem] * 12 + [hbm],
        scratch_shapes=[
            pltpu.VMEM((row_count, length, width), LOW),
            pltpu.VMEM((col_count, width, qkv_width), LOW),
            pltpu.VMEM((length, width), LOW),
            pltpu.VMEM((length, LANES), F32),
            pltpu.SemaphoreType.DMA((64,)),
            pltpu.SemaphoreType.DMA((64,)),
        ],
        compiler_params=pltpu.CompilerParams(
            vmem_limit_bytes=VMEM_BYTES, collective_id=1, has_side_effects=True
        ),
        cost_estimate=pl.CostEstimate(flops=50_000_000_000, bytes_accessed=30_000_000, transcendentals=0),
        name="attend_forward",
    )(hidden_in, own_q, own_o, small, seg_rows, cotangent, tables)
    block_low = jax.ShapeDtypeStruct((length, width), LOW)
    block_float = jax.ShapeDtypeStruct((length, width), F32)
    slots = exp_local * capacity
    plane = (dp_count, row_count, length, width)
    every = jax.ShapeDtypeStruct((blocks, row_count, length, width), LOW)
    y_part, grad_resid, grad_low, table, small_part, wo_rows, cot_all, res_all, *kept_slots = pl.pallas_call(
        functools.partial(experts_kernel, counts),
        out_shape=(
            jax.ShapeDtypeStruct(plane, LOW),
            block_float,
            block_low,
            jax.ShapeDtypeStruct((col_count, dp_count, 16, length), F32),
            jax.ShapeDtypeStruct((SMALL_ROWS, width), F32),
            jax.ShapeDtypeStruct((row_count, head_width, width), LOW),
            every,
            every,
            jax.ShapeDtypeStruct((dp_count, exp_local, capacity, D), LOW),
            jax.ShapeDtypeStruct((dp_count, exp_local, capacity, D), LOW),
            jax.ShapeDtypeStruct((dp_count, exp_local, 3, capacity, hidden_width), LOW),
        ),
        input_output_aliases={4: 6},
        in_specs=[hbm, vmem, vmem, hbm, hbm, vmem, hbm, hbm, hbm, hbm],
        out_specs=[hbm] + [vmem] * 4 + [hbm] * 6,
        scratch_shapes=[
            pltpu.VMEM(w_gate.shape, LOW),
            pltpu.VMEM(w_up.shape, LOW),
            pltpu.VMEM(w_down.shape, LOW),
            pltpu.VMEM(plane, LOW),
            pltpu.VMEM(plane, LOW),
            pltpu.VMEM((length, D), LOW),
            pltpu.VMEM((dp_count, TOP, length), jnp.int32),
            pltpu.VMEM((dp_count, 8, length), F32),
            pltpu.VMEM((EXPERTS, length), F32),
            pltpu.VMEM((dp_count, row_count, slots, width), LOW),
            pltpu.VMEM((slots, length), LOW),
            pltpu.VMEM((row_count, slots, width), LOW),
            pltpu.VMEM((row_count, slots, width), LOW),
            pltpu.VMEM((dp_count, 2, length, width), LOW),
            pltpu.VMEM((dp_count, 2, length, width), LOW),
            pltpu.VMEM((2, length, width), F32),
            pltpu.VMEM((dp_count, 2, length, width), LOW),
            pltpu.VMEM((3, length, width), LOW),
            pltpu.VMEM((row_count, length, width), LOW),
            pltpu.VMEM((dp_count, 8, length), F32),
            pltpu.VMEM((dp_count * row_count, 8, length), F32),
            pltpu.VMEM((length, LANES), F32),
            pltpu.VMEM((row_count, 8, length), F32),
            pltpu.VMEM((length, width), LOW),
            pltpu.VMEM((2, capacity, D), LOW),
            pltpu.VMEM((2, capacity, D), LOW),
            pltpu.VMEM((2, 3, capacity, hidden_width), LOW),
            pltpu.SemaphoreType.DMA((3, 2)),
            pltpu.SemaphoreType.DMA((80,)),
            pltpu.SemaphoreType.DMA((80,)),
        ],
        compiler_params=pltpu.CompilerParams(
            vmem_limit_bytes=VMEM_BYTES, collective_id=2, has_side_effects=True
        ),
        cost_estimate=pl.CostEstimate(flops=80_000_000_000, bytes_accessed=50_000_000, transcendentals=0),
        name="experts",
    )(resid_low, resid_mid, cotangent, packed, cot_all, small_all, wo_cols, w_gate, w_up, w_down)

    halves = (dp_count, 2, length, width)
    half = (2, length, width)
    layer_out, grad_in, grads_part, small_part, res_all, cot_all = pl.pallas_call(
        functools.partial(attend_backward_kernel, counts),
        out_shape=(
            block_low,
            block_float,
            jax.ShapeDtypeStruct((row_count, width, qkv_width + width), LOW),
            jax.ShapeDtypeStruct((SMALL_ROWS, width), F32),
            every,
            every,
        ),
        input_output_aliases={17: 4, 18: 5},
        in_specs=[hbm] + [vmem] * 6 + [hbm] + [vmem] * 8 + [hbm] * 4,
        out_specs=[vmem] * 4 + [hbm] * 2,
        scratch_shapes=[
            pltpu.VMEM((row_count, length, width), LOW),
            pltpu.VMEM((length, head_width), LOW),
            pltpu.VMEM((BLOCK_Q, head_width), LOW),
            pltpu.VMEM((BLOCK_Q, head_width), F32),
            pltpu.VMEM((kv_local, length, HD), F32),
            pltpu.VMEM((kv_local, length, HD), F32),
            pltpu.VMEM((length, qkv_width), LOW),
            pltpu.VMEM((length, LANES), F32),
            pltpu.VMEM(halves, LOW),
            pltpu.VMEM(halves, LOW),
            pltpu.VMEM(halves, LOW),
            pltpu.VMEM((3, length, width), LOW),
            pltpu.VMEM(half, LOW),
            pltpu.VMEM(half, LOW),
            pltpu.VMEM(half, F32),
            pltpu.VMEM((length, width), LOW),
            pltpu.VMEM((length, width), LOW),
            pltpu.VMEM((row_count, 8, length), F32),
            pltpu.SemaphoreType.DMA((80,)),
            pltpu.SemaphoreType.DMA((80,)),
        ],
        compiler_params=pltpu.CompilerParams(
            vmem_limit_bytes=VMEM_BYTES, collective_id=3, has_side_effects=True
        ),
        cost_estimate=pl.CostEstimate(flops=40_000_000_000, bytes_accessed=30_000_000, transcendentals=0),
        name="attend_backward",
    )(
        grad_low, grad_resid, hidden_in, resid_mid, wo_rows, wq_rows, normed_one, mixed_all, query_rot, key_rot,
        value_low, logs, seg_all, small_all, small_part, tables, y_part, res_all,
        cot_all, resid_low,
    )

    gate_shape, down_shape = (jax.ShapeDtypeStruct(w.shape, F32) for w in (w_gate, w_down))
    one_gate = pl.BlockSpec((1,) + w_gate.shape[1:], lambda e: (e, 0, 0))
    one_down = pl.BlockSpec((1,) + w_down.shape[1:], lambda e: (e, 0, 0))
    token_pair = (2, row_count, length, width)
    res_all, cot_all, grad_gate, grad_up, grad_down, grads_own, small = pl.pallas_call(
        functools.partial(weight_grads_kernel, counts),
        out_shape=(
            every, every, gate_shape, gate_shape, down_shape,
            jax.ShapeDtypeStruct((width, qkv_width + width), F32),
            jax.ShapeDtypeStruct((SMALL_ROWS, width), F32),
        ),
        input_output_aliases={0: 0, 1: 1},
        in_specs=[hbm] * 6 + [vmem] * 3 + [hbm] * 3,
        out_specs=[hbm] * 5 + [vmem] * 2,
        scratch_shapes=[
            pltpu.VMEM(w_gate.shape, LOW),
            pltpu.VMEM(w_up.shape, LOW),
            pltpu.VMEM(w_down.shape, LOW),
            pltpu.VMEM((dp_count * col_count, SMALL_ROWS, width), F32),
            pltpu.VMEM(w_gate.shape, F32),
            pltpu.VMEM(w_up.shape, F32),
            pltpu.VMEM(w_down.shape, F32),
            pltpu.VMEM(token_pair, LOW),
            pltpu.VMEM(token_pair, LOW),
            pltpu.VMEM((2, capacity, D), LOW),
            pltpu.VMEM((2, capacity, D), LOW),
            pltpu.VMEM((2, 3, capacity, hidden_width), LOW),
            pltpu.VMEM((col_count, width, qkv_width + width), LOW),
            pltpu.VMEM((4, width, qkv_width + width), LOW),
            pltpu.SemaphoreType.DMA((4,)),
            pltpu.SemaphoreType.DMA((3, 2)),
            pltpu.SemaphoreType.DMA((3, exp_local)),
            pltpu.SemaphoreType.DMA((64,)),
            pltpu.SemaphoreType.DMA((64,)),
        ],
        compiler_params=pltpu.CompilerParams(
            vmem_limit_bytes=VMEM_BYTES, collective_id=4, has_side_effects=True
        ),
        name="weight_grads",
    )(res_all, cot_all, grads_part, *kept_slots, small_part, table, small_all, w_gate, w_up, w_down)
    def strips(rows, columns):
        return pl.BlockSpec((rows // exp_local, columns), lambda e: (e, 0))

    tokens, attn = strips(length, width), strips(width, qkv_width + width)
    grad_gate, grad_up, grad_down, layer_out, grad_in, grad_qkv, grad_out = pl.pallas_call(
        functools.partial(last_grads_kernel, counts),
        grid=(exp_local,),
        out_shape=(
            gate_shape, gate_shape, down_shape, block_low, block_float,
            jax.ShapeDtypeStruct((width, qkv_width), F32),
            jax.ShapeDtypeStruct((head_width, width), F32),
        ),
        in_specs=[hbm, hbm, vmem, vmem] + [one_gate, one_gate, one_down] * 2 + [tokens, tokens, attn],
        out_specs=[one_gate, one_gate, one_down, tokens, tokens, strips(width, qkv_width), strips(head_width, width)],
        scratch_shapes=[
            pltpu.VMEM((row_count, length, width), LOW),
            pltpu.VMEM((row_count, length, width), LOW),
            pltpu.SemaphoreType.DMA((2,)),
        ],
        compiler_params=params,
        name="last_grads",
    )(
        res_all, cot_all, table, small_all, w_gate, w_up, w_down, grad_gate, grad_up, grad_down,
        layer_out, grad_in, grads_own,
    )
    return (
        layer_out,
        grad_in,
        small[GAIN_ONE],
        grad_qkv.reshape(w_qkv.shape),
        grad_out.reshape(w_out.shape),
        small[GAIN_TWO],
        small[:EXPERTS].T,
        grad_gate,
        grad_up,
        grad_down,
    )


def solution(mesh):
    token = P(("dp", "col"), "row")
    routed = P(("dp", "col"), None)
    expert = P(("dp", "row"), None, None)
    wide, tall = P("row", "col", None), P("col", None, "row")
    row = P("row")
    square = P("row", None)

    def step(*arrays):
        length = arrays[10].shape[1]
        tokens_here = arrays[0].shape[0] // (mesh.shape["dp"] * mesh.shape["col"])
        whole_sequence = tokens_here == length and mesh.shape["row"] == mesh.shape["col"]
        return jax.shard_map(
            fast_device if whole_sequence else on_device,
            mesh=mesh,
            in_specs=(
                token, row, wide, tall, row, square, expert, expert, expert, token,
                P(("dp", "row"), None), routed, routed,
            ),
            out_specs=(token, token, row, wide, tall, row, square, expert, expert, expert),
            check_vma=False,
        )(*arrays)

    return step
```

```python
import functools

import jax
import jax.numpy as jnp
import numpy as np
from jax import lax
from jax.experimental import pallas as pl
from jax.experimental.pallas import tpu as pltpu
from jax.sharding import PartitionSpec as P

D = 1024
HQ = 16
HK = 8
HD = 64
EXPERTS = 32
TOP = 8


EPSILON = 1e-06
ROPE_BASE = 10000.0
NEG_LARGE = -1e30
HIGHEST = lax.Precision.HIGHEST


def rotate(values, cosine, sine_table):
    half_size = values.shape[-1] // 2
    lower_half = values[..., :half_size]
    upper_half = values[..., half_size:]
    return jnp.concatenate(
        [
            lower_half * cosine - upper_half * sine_table,
            upper_half * cosine + lower_half * sine_table,
        ],
        axis=-1,
    )


def rotate_back(values, cosine, sine_table):
    half_size = values.shape[-1] // 2
    lower_half = values[..., :half_size]
    upper_half = values[..., half_size:]
    return jnp.concatenate(
        [
            lower_half * cosine + upper_half * sine_table,
            upper_half * cosine - lower_half * sine_table,
        ],
        axis=-1,
    )


def rope_tables(length, head_size):
    positions = jnp.arange(length, dtype=jnp.float32)
    frequency = ROPE_BASE ** (-2.0 * jnp.arange(head_size // 2, dtype=jnp.float32) / head_size)
    angles = positions[:, None] * frequency[None, :]
    return (jnp.cos(angles), jnp.sin(angles))


def visible(segment_row):
    positions = jnp.arange(segment_row.shape[-1], dtype=jnp.int32)
    causal = positions[:, None] >= positions[None, :]
    return causal & (segment_row[..., :, None] == segment_row[..., None, :])


def pair_ranks(expert_ids, pair_order, block_rows):
    experts_flat = expert_ids.reshape(-1, block_rows * TOP)
    order_flat = pair_order.reshape(-1, block_rows * TOP)

    def one_block(experts_row, order_row):
        pair_count = experts_row.shape[0]
        by_order = (
            jnp.zeros((pair_count,), jnp.int32)
            .at[order_row]
            .set(jnp.arange(pair_count, dtype=jnp.int32))
        )
        sorted_experts = experts_row[by_order]
        onehot = (sorted_experts[:, None] == jnp.arange(EXPERTS, dtype=jnp.int32)[None, :]).astype(
            jnp.int32
        )
        before = jnp.cumsum(onehot, axis=0) - onehot
        sorted_rank = jnp.sum(before * onehot, axis=1)
        return sorted_rank[order_row]

    return jax.vmap(one_block)(experts_flat, order_flat).reshape(expert_ids.shape)


def feature_total(values):
    return lax.psum(values, "row")


def tokens_by_col(values):
    return lax.all_gather(values, "col", axis=0, tiled=True)


def tokens_by_row(values):
    return lax.all_gather(values, "row", axis=0, tiled=True)


def col_scatter(term_fn, keep_rows):
    return lax.psum_scatter(
        term_fn(jnp.int32(0), keep_rows * lax.axis_size("col")),
        "col",
        scatter_dimension=0,
        tiled=True,
    )


def to_experts(outgoing):
    arrived = lax.all_to_all(outgoing, ("dp", "row"), split_axis=0, concat_axis=0, tiled=True)
    return arrived


def from_experts(outgoing):
    arrived = lax.all_to_all(outgoing, ("dp", "row"), split_axis=0, concat_axis=0, tiled=True)
    return arrived


def owner_layout(incoming, dp_count, row_count, exp_local):
    capacity = incoming.shape[1] // exp_local
    part_width = incoming.shape[2]
    sectioned = incoming.reshape(dp_count, row_count, exp_local, capacity, part_width)
    return sectioned.transpose(2, 0, 3, 1, 4).reshape(
        exp_local, dp_count * capacity, row_count * part_width
    )


def source_layout(owner_rows, dp_count, row_count):
    exp_local, slot_rows, full_width = owner_rows.shape
    capacity = slot_rows // dp_count
    part_width = full_width // row_count
    sectioned = owner_rows.reshape(exp_local, dp_count, capacity, row_count, part_width)
    return sectioned.transpose(1, 3, 0, 2, 4).reshape(
        dp_count * row_count, exp_local * capacity, part_width
    )


def attend_forward(pack):
    query_seq, key_seq, value_seq, segment_seq = pack
    score_scale = query_seq.shape[-1] ** (-0.5)
    scores = (
        jnp.einsum("qhgd,khd->hgqk", query_seq, key_seq, preferred_element_type=jnp.float32)
        * score_scale
    )
    scores = jnp.where(visible(segment_seq), scores, NEG_LARGE)
    row_max = jnp.max(scores, axis=-1, keepdims=True)
    weights = jnp.exp(scores - row_max)
    row_total = jnp.sum(weights, axis=-1, keepdims=True)
    weights_low = (weights / row_total).astype(jnp.bfloat16)
    mixed_seq = jnp.einsum(
        "hgqk,khd->qhgd", weights_low, value_seq, preferred_element_type=jnp.float32
    )
    return (mixed_seq.astype(jnp.bfloat16), row_max + jnp.log(row_total))


def attend_backward(pack):
    query_seq, key_seq, value_seq, segment_seq, log_total, grad_seq = pack
    score_scale = query_seq.shape[-1] ** (-0.5)
    scores = (
        jnp.einsum("qhgd,khd->hgqk", query_seq, key_seq, preferred_element_type=jnp.float32)
        * score_scale
    )
    scores = jnp.where(visible(segment_seq), scores, NEG_LARGE)
    weights = jnp.exp(scores - log_total)
    grad_weights = jnp.einsum(
        "qhgd,khd->hgqk", grad_seq, value_seq, preferred_element_type=jnp.float32
    )
    inner_sum = jnp.sum(weights * grad_weights, axis=-1, keepdims=True)
    grad_scores = (weights * (grad_weights - inner_sum)).astype(jnp.bfloat16)
    grad_values = jnp.einsum(
        "hgqk,qhgd->khd", weights.astype(jnp.bfloat16), grad_seq, preferred_element_type=jnp.float32
    )
    grad_query = (
        jnp.einsum("hgqk,khd->qhgd", grad_scores, key_seq, preferred_element_type=jnp.float32)
        * score_scale
    )
    grad_key = (
        jnp.einsum("hgqk,qhgd->khd", grad_scores, query_seq, preferred_element_type=jnp.float32)
        * score_scale
    )
    return (grad_query, grad_key, grad_values)


def on_device(
    hidden_in,
    norm_gain,
    w_qkv,
    w_out,
    ffn_gain,
    router,
    w_gate,
    w_up,
    w_down,
    cotangent,
    segment_ids,
    expert_ids,
    pair_order,
):
    dp_count = lax.axis_size("dp")
    row_count = lax.axis_size("row")
    owners = dp_count * row_count
    tok_rows, part_width = hidden_in.shape
    seq_count, length = segment_ids.shape
    att_rows = seq_count * length
    kv_local = w_qkv.shape[1]
    group_size = HQ // HK
    exp_local = w_gate.shape[0]
    capacity = tok_rows * TOP // EXPERTS
    total_slots = EXPERTS * capacity
    resid_in = hidden_in.astype(jnp.float32)
    gain_one = norm_gain.astype(jnp.float32)
    rstd_one = lax.rsqrt(feature_total(jnp.sum(resid_in * resid_in, axis=1)) / D + EPSILON)
    normed_one = (resid_in * rstd_one[:, None] * gain_one).astype(jnp.bfloat16)
    group_rows = tokens_by_col(normed_one)
    qkv_flat = w_qkv.reshape(part_width, -1)
    picked = group_rows
    qkv_local = lax.psum_scatter(
        jnp.dot(picked, qkv_flat, preferred_element_type=jnp.float32),
        "row",
        scatter_dimension=0,
        tiled=True,
    )
    qkv_local = qkv_local.reshape(seq_count, length, kv_local, -1)
    cosine, sine_table = rope_tables(length, HD)
    queries = qkv_local[..., : group_size * HD].reshape(seq_count, length, kv_local, group_size, HD)
    query_rot = rotate(
        queries, cosine[None, :, None, None, :], sine_table[None, :, None, None, :]
    ).astype(jnp.bfloat16)
    key_rot = rotate(
        qkv_local[..., group_size * HD : (group_size + 1) * HD],
        cosine[None, :, None, :],
        sine_table[None, :, None, :],
    ).astype(jnp.bfloat16)
    value_low = qkv_local[..., (group_size + 1) * HD :].astype(jnp.bfloat16)
    mixed_heads, log_total = lax.map(attend_forward, (query_rot, key_rot, value_low, segment_ids))
    mixed_rows = tokens_by_row(mixed_heads.reshape(att_rows, -1))
    out_flat = w_out.reshape(-1, part_width)

    def out_term(first_row, block_rows):
        return jnp.dot(mixed_rows, out_flat, preferred_element_type=jnp.float32)

    resid_mid = resid_in + col_scatter(out_term, tok_rows)
    gain_two = ffn_gain.astype(jnp.float32)
    router_float = router.astype(jnp.float32)
    square_two, logit_part = (
        lax.psum(jnp.sum(resid_mid * resid_mid, axis=1).astype(jnp.bfloat16), "row").astype(
            jnp.float32
        ),
        lax.psum(
            jnp.dot(resid_mid * gain_two, router_float, precision=HIGHEST).astype(jnp.bfloat16),
            "row",
        ).astype(jnp.float32),
    )
    rstd_two = lax.rsqrt(square_two / D + EPSILON)
    logits = logit_part * rstd_two[:, None]
    normed_float = resid_mid * rstd_two[:, None] * gain_two
    normed_two = normed_float.astype(jnp.bfloat16)
    choose = (expert_ids[:, :, None] == jnp.arange(EXPERTS, dtype=jnp.int32)[None, None, :]).astype(
        jnp.float32
    )
    gate_weights = jax.nn.softmax(jnp.sum(choose * logits[:, None, :], axis=2), axis=1)
    pair_rank = pair_ranks(expert_ids, pair_order, tok_rows)
    pair_slot = jnp.where(pair_rank < capacity, expert_ids * capacity + pair_rank, total_slots)
    pair_index = jnp.arange(tok_rows * TOP, dtype=jnp.int32)
    slot_pair = (
        jnp.full((total_slots + 1,), tok_rows * TOP, jnp.int32)
        .at[pair_slot.reshape(-1)]
        .set(pair_index)[:total_slots]
    )
    padded_two = jnp.concatenate([normed_two, jnp.zeros((1, part_width), jnp.bfloat16)], axis=0)
    outgoing = padded_two[slot_pair // TOP].reshape(owners, exp_local * capacity, part_width)
    expert_rows = owner_layout(to_experts(outgoing), dp_count, row_count, exp_local)
    gate_pre = jnp.einsum("erd,edf->erf", expert_rows, w_gate, preferred_element_type=jnp.float32)
    up_pre = jnp.einsum("erd,edf->erf", expert_rows, w_up, preferred_element_type=jnp.float32)
    hidden = (jax.nn.silu(gate_pre) * up_pre).astype(jnp.bfloat16)
    expert_out = jnp.einsum(
        "erf,efd->erd", hidden, w_down, preferred_element_type=jnp.float32
    ).astype(jnp.bfloat16)
    returned = from_experts(source_layout(expert_out, dp_count, row_count))
    slot_table = jnp.concatenate(
        [returned.reshape(total_slots, part_width), jnp.zeros((1, part_width), jnp.bfloat16)],
        axis=0,
    )
    pair_rows = slot_table[pair_slot].astype(jnp.float32)
    layer_sum = resid_mid + jnp.einsum("tk,tkd->td", gate_weights, pair_rows, precision=HIGHEST)
    grad_top = cotangent.astype(jnp.float32)
    grad_gates = lax.psum(jnp.einsum("td,tkd->tk", grad_top, pair_rows, precision=HIGHEST), "row")
    pair_grad = (gate_weights[:, :, None] * grad_top[:, None, :]).astype(jnp.bfloat16)
    grad_padded = jnp.concatenate(
        [pair_grad.reshape(tok_rows * TOP, part_width), jnp.zeros((1, part_width), jnp.bfloat16)],
        axis=0,
    )
    outgoing_grad = grad_padded[slot_pair].reshape(owners, exp_local * capacity, part_width)
    grad_rows = owner_layout(to_experts(outgoing_grad), dp_count, row_count, exp_local)
    grad_hidden = jnp.einsum("erd,efd->erf", grad_rows, w_down, preferred_element_type=jnp.float32)
    sigmoid_gate = jax.nn.sigmoid(gate_pre)
    grad_gate_pre = (
        grad_hidden * up_pre * sigmoid_gate * (1.0 + gate_pre * (1.0 - sigmoid_gate))
    ).astype(jnp.bfloat16)
    grad_up_pre = (grad_hidden * gate_pre * sigmoid_gate).astype(jnp.bfloat16)
    grad_down_local = jnp.einsum(
        "erf,erd->efd", hidden, grad_rows, preferred_element_type=jnp.float32
    )
    grad_gate_local = jnp.einsum(
        "erd,erf->edf", expert_rows, grad_gate_pre, preferred_element_type=jnp.float32
    )
    grad_up_local = jnp.einsum(
        "erd,erf->edf", expert_rows, grad_up_pre, preferred_element_type=jnp.float32
    )
    rows_back = jnp.einsum(
        "erf,edf->erd", grad_gate_pre, w_gate, preferred_element_type=jnp.float32
    )
    rows_back = (
        rows_back
        + jnp.einsum("erf,edf->erd", grad_up_pre, w_up, preferred_element_type=jnp.float32)
    ).astype(jnp.bfloat16)
    returned_grad = from_experts(source_layout(rows_back, dp_count, row_count))
    grad_table = jnp.concatenate(
        [returned_grad.reshape(total_slots, part_width), jnp.zeros((1, part_width), jnp.bfloat16)],
        axis=0,
    )
    inner_gate = jnp.sum(gate_weights * grad_gates, axis=1, keepdims=True)
    grad_chosen = gate_weights * (grad_gates - inner_gate)
    grad_logits = jnp.einsum("tk,tke->te", grad_chosen, choose, precision=HIGHEST)
    grad_router_part = jnp.einsum("td,te->de", normed_float, grad_logits, precision=HIGHEST)
    grad_normed = jnp.sum(grad_table[pair_slot].astype(jnp.float32), axis=1)
    grad_normed = grad_normed + jnp.einsum(
        "te,de->td", grad_logits, router_float, precision=HIGHEST
    )
    grad_gain_two_part = jnp.sum(grad_normed * resid_mid * rstd_two[:, None], axis=0)
    scaled_two = grad_normed * gain_two
    inner_two = feature_total(jnp.sum(scaled_two * resid_mid, axis=1))
    grad_resid = (
        grad_top
        + rstd_two[:, None] * scaled_two
        - resid_mid * (rstd_two * rstd_two * rstd_two * inner_two / D)[:, None]
    )
    branch_rows = tokens_by_col(grad_resid.astype(jnp.bfloat16))
    grad_out_local = jnp.einsum(
        "tc,td->cd", mixed_rows, branch_rows, preferred_element_type=jnp.float32
    ).reshape(w_out.shape)
    picked = branch_rows
    grad_mixed = lax.psum_scatter(
        jnp.einsum("td,cd->tc", picked, out_flat, preferred_element_type=jnp.float32).astype(
            jnp.bfloat16
        ),
        "row",
        scatter_dimension=0,
        tiled=True,
    ).astype(jnp.float32)
    grad_mixed = grad_mixed.astype(jnp.bfloat16).reshape(
        seq_count, length, kv_local, group_size, HD
    )
    grad_query, grad_key, grad_values = lax.map(
        attend_backward, (query_rot, key_rot, value_low, segment_ids, log_total, grad_mixed)
    )
    grad_query = rotate_back(
        grad_query, cosine[None, :, None, None, :], sine_table[None, :, None, None, :]
    )
    grad_key = rotate_back(grad_key, cosine[None, :, None, :], sine_table[None, :, None, :])
    grad_qkv_pre = jnp.concatenate(
        [grad_query.reshape(seq_count, length, kv_local, group_size * HD), grad_key, grad_values],
        axis=-1,
    )
    grad_qkv_pre = grad_qkv_pre.astype(jnp.bfloat16).reshape(att_rows, -1)
    qkv_rows = tokens_by_row(grad_qkv_pre)
    grad_qkv_local = jnp.einsum(
        "td,tc->dc", group_rows, qkv_rows, preferred_element_type=jnp.float32
    ).reshape(w_qkv.shape)

    def normed_term(first_row, block_rows):
        return jnp.einsum("tc,dc->td", qkv_rows, qkv_flat, preferred_element_type=jnp.float32)

    grad_normed_one = col_scatter(normed_term, tok_rows)
    grad_gain_one_part = jnp.sum(grad_normed_one * resid_in * rstd_one[:, None], axis=0)
    scaled_one = grad_normed_one * gain_one
    inner_one = feature_total(jnp.sum(scaled_one * resid_in, axis=1))
    grad_in = (
        grad_resid
        + rstd_one[:, None] * scaled_one
        - resid_in * (rstd_one * rstd_one * rstd_one * inner_one / D)[:, None]
    )
    col_sums = (
        lax.psum(grad_gate_local.astype(jnp.bfloat16), "col").astype(jnp.float32),
        lax.psum(grad_up_local.astype(jnp.bfloat16), "col").astype(jnp.float32),
        lax.psum(grad_down_local.astype(jnp.bfloat16), "col").astype(jnp.float32),
        lax.psum(grad_router_part.astype(jnp.bfloat16), "col").astype(jnp.float32),
        lax.psum(grad_gain_one_part.astype(jnp.bfloat16), "col").astype(jnp.float32),
        lax.psum(grad_gain_two_part.astype(jnp.bfloat16), "col").astype(jnp.float32),
    )
    dp_sums = (
        lax.psum(grad_qkv_local.astype(jnp.bfloat16), "dp").astype(jnp.float32),
        lax.psum(grad_out_local.astype(jnp.bfloat16), "dp").astype(jnp.float32),
        lax.psum(col_sums[3].astype(jnp.bfloat16), "dp").astype(jnp.float32),
        lax.psum(col_sums[4].astype(jnp.bfloat16), "dp").astype(jnp.float32),
        lax.psum(col_sums[5].astype(jnp.bfloat16), "dp").astype(jnp.float32),
    )
    return (
        layer_sum.astype(jnp.bfloat16),
        grad_in,
        dp_sums[3],
        dp_sums[0],
        dp_sums[1],
        dp_sums[4],
        dp_sums[2],
        col_sums[0],
        col_sums[1],
        col_sums[2],
    )

WINDOW = 512
BLOCK_Q = 256
LANES = 128
SMALL_ROWS = 48
GAIN_ONE = EXPERTS
GAIN_TWO = EXPERTS + 1
RSTD_LANE = LANES - 1
RSTD_ROW = 8
FIRST, SECOND, LATE = 1, 3, 2
F32 = jnp.float32
LOW = jnp.bfloat16
VMEM_BYTES = 67_000_000


def dot_nn(a, b):
    return jnp.dot(a, b, preferred_element_type=F32)


def dot_nt(a, b):
    return lax.dot_general(a, b, (((1,), (1,)), ((), ())), preferred_element_type=F32)


def dot_tn(a, b):
    return lax.dot_general(a, b, (((0,), (0,)), ((), ())), preferred_element_type=F32)


def rope_lanes(length):
    positions = np.arange(length, dtype=np.float32)
    frequency = (ROPE_BASE ** (-2.0 * np.arange(HD // 2, dtype=np.float32) / HD)).astype(np.float32)
    angles = (positions[:, None] * frequency[None, :]).astype(np.float32)
    cosine, sine = np.cos(angles), np.sin(angles)
    signed = np.concatenate([-sine, sine], axis=1)
    double = np.concatenate([cosine, cosine], axis=1)
    ones, zeros = np.ones_like(double), np.zeros_like(double)
    return np.stack(
        [
            np.concatenate([double, double], axis=1),
            np.concatenate([signed, signed], axis=1),
            np.concatenate([double, ones], axis=1),
            np.concatenate([signed, zeros], axis=1),
        ]
    ).astype(np.float32)


def swap_halves(values):
    half = HD // 2
    lane = lax.broadcasted_iota(jnp.int32, values.shape, 1)
    ahead = pltpu.roll(values, LANES - half, 1)
    behind = pltpu.roll(values, half, 1)
    return jnp.where(lane % HD < half, ahead, behind)


def window_mask(seg_col, seg_row, q_start, k_start):
    shape = (seg_col.shape[0], seg_row.shape[1])
    q_at = lax.broadcasted_iota(jnp.int32, shape, 0) + q_start
    k_at = lax.broadcasted_iota(jnp.int32, shape, 1) + k_start
    return (q_at >= k_at) & (seg_col == seg_row)


def remote(src, dst, send_sem, recv_sem, where):
    return pltpu.make_async_remote_copy(
        src_ref=src, dst_ref=dst, send_sem=send_sem, recv_sem=recv_sem,
        device_id=where, device_id_type=pl.DeviceIdType.MESH,
    )


class Copies:
    def __init__(self, send_sems, recv_sems):
        self.send_sems, self.recv_sems = send_sems, recv_sems
        self.sends = self.recvs = 0
        self.open = []

    def receivers(self, number=1):
        first = self.recvs
        self.recvs += number
        return first

    def send(self, src, dst, receiver, where, when=None):
        at = self.sends
        self.sends += 1
        copy = remote(src, dst, self.send_sems.at[at], self.recv_sems.at[receiver], where)
        if when is None:
            copy.start()
        else:
            pl.when(when)(copy.start)
        self.open.append((copy, when))

    def plan(self, src, dst, receiver, where):
        at = self.sends
        self.sends += 1
        copy = remote(src, dst, self.send_sems.at[at], self.recv_sems.at[receiver], where)
        self.open.append((copy, None))
        return copy

    def local(self, src, dst, when=None):
        at = self.sends
        self.sends += 1
        copy = pltpu.make_async_copy(src, dst, self.send_sems.at[at])
        if when is None:
            copy.start()
        else:
            pl.when(when)(copy.start)
        return copy

    def arrived(self, dst, receiver, where):
        remote(dst, dst, self.recv_sems.at[receiver], self.recv_sems.at[receiver], where).wait_recv()

    def finish(self):
        for copy, when in self.open:
            if when is None:
                copy.wait_send()
            else:
                pl.when(when)(copy.wait_send)


class Place:
    def __init__(self, counts):
        self.dp_count, self.row_count, self.col_count = counts
        self.dp, self.row, self.col = (lax.axis_index(name) for name in ("dp", "row", "col"))
        self.pair_row = self.row + 1 - 2 * lax.rem(self.row, 2)
        self.far_row = lax.rem(self.row + 2, self.row_count)
        self.cross_row = lax.rem(self.pair_row + 2, self.row_count)
        self.other_dp = self.dp_count - 1 - self.dp
        self.here = (self.dp, self.row, self.col)
        self.pair = (self.dp, self.pair_row, self.col)
        self.far = (self.dp, self.far_row, self.col)
        self.over = (self.other_dp, self.row, self.col)
        self.over_far = (self.other_dp, self.far_row, self.col)

    def row_at(self, step):
        return lax.rem(self.row + step + self.row_count, self.row_count)

    def col_at(self, step):
        return lax.rem(self.col + step + self.col_count, self.col_count)

    def block(self, dp_at, col_at):
        return dp_at * self.col_count + col_at

    def plane(self):
        peers = [(self.dp, self.row_at(k), self.col) for k in range(1, self.row_count)]
        return peers + [(self.other_dp, self.row_at(k), self.col) for k in range(self.row_count)]

    def column(self):
        return [(self.dp, self.row, self.col_at(k)) for k in range(1, self.col_count)]


class Spread:
    def __init__(self, place, copies, blocks, col_at):
        self.place, self.copies = place, copies
        dp, row, far_row = place.dp, place.row, place.far_row
        same, other = place.block(dp, col_at), place.block(place.other_dp, col_at)
        self.own, self.far = blocks.at[same, row], blocks.at[same, far_row]
        self.over, self.corner = blocks.at[other, row], blocks.at[other, far_row]
        self.pairs_same = (blocks.at[same, place.pair_row], blocks.at[same, place.cross_row])
        self.pairs_other = (blocks.at[other, place.pair_row], blocks.at[other, place.cross_row])
        self.at = copies.receivers(7)
        self.to_pair = copies.plan(self.own, self.own, self.at, place.pair)
        self.to_far = copies.plan(self.own, self.own, self.at + 1, place.far)
        self.to_over = copies.plan(self.own, self.own, self.at + 2, place.over)
        self.far_pair = copies.plan(self.far, self.far, self.at + 4, place.pair)
        self.over_pair = copies.plan(self.over, self.over, self.at + 5, place.pair)
        self.corner_pair = copies.plan(self.corner, self.corner, self.at + 6, place.pair)
        self.turn = None

    def begin(self, with_over):
        self.to_far.start()
        if with_over:
            self.to_over.start()
        self.to_pair.start()

    def send_over(self):
        self.to_over.start()

    def plan_corner(self, by_over):
        if by_over:
            self.turn = self.copies.plan(self.far, self.far, self.at + 3, self.place.over)
        else:
            self.turn = self.copies.plan(self.over, self.over, self.at + 3, self.place.far)

    def pass_far(self, corner):
        self.copies.arrived(self.far, self.at + 1, self.place.far)
        if corner:
            if self.turn is None:
                self.plan_corner(True)
            self.turn.start()
        self.far_pair.start()

    def pass_over(self, corner):
        self.copies.arrived(self.over, self.at + 2, self.place.over)
        if corner:
            if self.turn is None:
                self.plan_corner(False)
            self.turn.start()
        self.over_pair.start()

    def pass_corner(self):
        self.copies.arrived(self.corner, self.at + 3, self.place.here)
        self.corner_pair.start()

    def complete_same(self):
        for k, piece in zip((0, 4), self.pairs_same):
            self.copies.arrived(piece, self.at + k, self.place.pair)

    def complete_other(self):
        for k, piece in zip((5, 6), self.pairs_other):
            self.copies.arrived(piece, self.at + k, self.place.pair)

    def complete(self):
        self.complete_same()
        self.complete_other()


def say_hello(peers):
    barrier = pltpu.get_barrier_semaphore()
    for peer in peers:
        pl.semaphore_signal(barrier, inc=1, device_id=peer, device_id_type=pl.DeviceIdType.MESH)
    return functools.partial(pl.semaphore_wait, barrier, len(peers))


def greet(peers):
    say_hello(peers)()


def attend_forward_kernel(
    counts, hidden_hbm, own_q_hbm, own_o_hbm, small_hbm, seg_hbm, cot_hbm, tab_ref,
    resid_ref, low_ref, mix_ref, normed_ref, q_ref, k_ref, v_ref, lse_ref, wq_ref, zo_ref, small_ref, seg_ref, cot_all,
    h_ref, zq_ref, own_ref, column_ref, send_sems, recv_sems,
):
    place = Place(counts)
    row_count, col_count = place.row_count, place.col_count
    copies = Copies(send_sems, recv_sems)
    parts, length, width = h_ref.shape
    kv_heads = k_ref.shape[0]
    features = parts * width
    chunks = length // BLOCK_Q
    greet(place.plane() + place.column())

    h_pair, h_far, h_cross = (copies.receivers() for _ in range(3))
    copies.send(hidden_hbm, h_ref.at[place.row], h_far, place.far)
    copies.send(hidden_hbm, h_ref.at[place.row], h_pair, place.pair)
    h_own = copies.local(hidden_hbm, h_ref.at[place.row])
    zq_own = copies.local(own_q_hbm, zq_ref.at[place.col])
    zo_own = copies.local(own_o_hbm, zo_ref.at[place.col])
    small_own = copies.local(small_hbm, small_ref.at[place.row])
    seg_own = copies.local(seg_hbm, seg_ref.at[place.row])
    zq_in = copies.receivers(col_count)
    zo_in = copies.receivers(col_count)
    for k in range(1, col_count):
        copies.send(own_q_hbm, zq_ref.at[place.col], zq_in + k, (place.dp, place.row, place.col_at(k)))
    small_in, seg_in = copies.receivers(row_count), copies.receivers(row_count)
    for k in range(1, row_count):
        copies.send(small_hbm, small_ref.at[place.row], small_in + k, (place.dp, place.row_at(k), place.col))
        copies.send(seg_hbm, seg_ref.at[place.row], seg_in + k, (place.dp, place.row_at(k), place.col))
    cot_own = copies.local(cot_hbm, own_ref)
    cot_pair, cot_over, cot_back = copies.receivers(), copies.receivers(), copies.receivers(3)
    cot_far, cot_corner = copies.receivers(2), copies.receivers(2)
    own_cot = cot_all.at[place.block(place.dp, place.col), place.row]
    far_cot = cot_all.at[place.block(place.dp, place.col), place.far_row]
    half_rows = length // 2

    def send_cot_far(half):
        window = pl.ds(half * half_rows, half_rows)
        copies.send(cot_hbm.at[window], own_cot.at[window], cot_far + half, place.far)

    def pass_cot_far(half):
        piece = far_cot.at[pl.ds(half * half_rows, half_rows)]
        copies.arrived(piece, cot_far + half, place.far)
        copies.send(piece, piece, cot_corner + half, place.over)

    send_cot_far(0)
    copies.send(cot_hbm, own_cot, cot_over, place.over)
    copies.send(cot_hbm, own_cot, cot_pair, place.pair)

    def share_blocks(landing, result, landed, first, own):
        waits = []
        for k in range(col_count):
            source = place.col_at(-k)
            if k == 0:
                own.wait()
            else:
                copies.arrived(landing.at[source], landed + k, place.here)
            mine = source == place.row
            step = lax.rem(source - place.row + row_count, row_count)
            copies.send(
                landing.at[source], result.at[place.row], first + step, (place.dp, source, place.col), source != place.row
            )
            waits.append((copies.local(landing.at[source], result.at[place.row], mine), mine))
        return waits

    def blocks_shared(result, first, waits):
        for copy, mine in waits:
            pl.when(mine)(copy.wait)
        for k in range(1, row_count):
            copies.arrived(result.at[place.row_at(-k)], first + k, place.here)

    copies.arrived(h_ref.at[place.far_row], h_far, place.far)
    copies.send(h_ref.at[place.far_row], h_ref.at[place.far_row], h_cross, place.pair)
    wq_in = copies.receivers(row_count)
    wq_waits = share_blocks(zq_ref, wq_ref, zq_in, wq_in, zq_own)

    for k in range(1, col_count):
        copies.send(own_o_hbm, zo_ref.at[place.col], zo_in + k, (place.dp, place.row, place.col_at(k)))
    send_cot_far(1)
    pass_cot_far(0)
    cot_z = copies.receivers(col_count)
    for k in (FIRST,):
        copies.send(cot_hbm, own_cot, cot_z + k, (place.dp, place.row, place.col_at(k)))
    h_own.wait()
    copies.arrived(h_ref.at[place.pair_row], h_pair, place.pair)
    copies.arrived(h_ref.at[place.cross_row], h_cross, place.pair)
    small_own.wait()
    for k in range(1, row_count):
        copies.arrived(small_ref.at[place.row_at(-k)], small_in + k, place.here)

    @pl.loop(0, chunks)
    def _(chunk):
        rows = pl.ds(pl.multiple_of(chunk * BLOCK_Q, BLOCK_Q), BLOCK_Q)
        total = jnp.zeros((BLOCK_Q, 1), F32)
        for part in range(parts):
            piece = h_ref[part, rows, :].astype(F32)
            total = total + jnp.sum(piece * piece, axis=1, keepdims=True)
        rstd = lax.rsqrt(total / features + EPSILON)
        lse_ref[rows, :] = jnp.broadcast_to(rstd, (BLOCK_Q, LANES))
        for part in range(parts):
            piece = h_ref[part, rows, :].astype(F32)
            gain = small_ref[part, GAIN_ONE : GAIN_ONE + 1, :].astype(F32)
            normed_ref[rows, part * width : (part + 1) * width] = (piece * rstd * gain).astype(LOW)

    seg_own.wait()
    for k in range(1, row_count):
        copies.arrived(seg_ref.at[place.row_at(-k)], seg_in + k, place.here)
    segments = seg_ref[place.col]
    for start in range(0, length, LANES):
        column_ref[start : start + LANES, :] = jnp.broadcast_to(
            segments[0:1, start : start + LANES], (LANES, LANES)
        ).T

    cot_own.wait()
    cot_kept = copies.local(own_ref, own_cot)

    blocks_shared(wq_ref, wq_in, wq_waits)

    @pl.loop(0, chunks)
    def _(chunk):
        rows = pl.ds(pl.multiple_of(chunk * BLOCK_Q, BLOCK_Q), BLOCK_Q)
        qkv = dot_nn(normed_ref[rows, :], wq_ref[...].reshape(features, -1))
        for head in range(kv_heads):
            base = head * 4 * HD
            queries = qkv[:, base : base + LANES]
            queries = queries * tab_ref[0, rows, :] + swap_halves(queries) * tab_ref[1, rows, :]
            others = qkv[:, base + LANES : base + 2 * LANES]
            others = others * tab_ref[2, rows, :] + swap_halves(others) * tab_ref[3, rows, :]
            q_ref[2 * head, rows, :] = queries[:, :HD].astype(LOW)
            q_ref[2 * head + 1, rows, :] = queries[:, HD:].astype(LOW)
            k_ref[head, rows, :] = others[:, :HD].astype(LOW)
            v_ref[head, rows, :] = others[:, HD:].astype(LOW)

    scale = HD**-0.5
    lane = lax.broadcasted_iota(jnp.int32, (BLOCK_Q, LANES), 1)
    mix_pair, mix_far, mix_cross = (copies.receivers(chunks) for _ in range(3))

    def pass_on(block):
        piece = mix_ref.at[place.far_row, pl.ds(block * BLOCK_Q, BLOCK_Q)]
        copies.arrived(piece, mix_far + block, place.far)
        copies.send(piece, piece, mix_cross + block, place.pair)

    for block in range(chunks):
        q_start = block * BLOCK_Q
        k_start = max(0, q_start - WINDOW)
        q_rows, k_rows = slice(q_start, q_start + BLOCK_Q), slice(k_start, q_start + BLOCK_Q)
        mask = window_mask(column_ref[q_rows, 0:1], segments[0:1, k_rows], q_start, k_start)

        @pl.loop(0, kv_heads)
        def _(kv):
            keys, vals = k_ref[kv, k_rows, :], v_ref[kv, k_rows, :]
            logs, outs = lse_ref[q_rows, :], []
            for half in range(2):
                head = 2 * kv + half
                scores = dot_nt(q_ref[head, q_rows, :], keys) * scale
                scores = jnp.where(mask, scores, NEG_LARGE)
                top = jnp.max(scores, axis=1, keepdims=True)
                weights = jnp.exp(scores - top)
                total = jnp.sum(weights, axis=1, keepdims=True)
                outs.append((dot_nn(weights.astype(LOW), vals) / total).astype(LOW))
                logs = jnp.where(lane == head, top + jnp.log(total), logs)
            lse_ref[q_rows, :] = logs
            mix_ref[place.row, q_rows, pl.ds(pl.multiple_of(kv * LANES, LANES), LANES)] = jnp.concatenate(
                outs, axis=1
            )

        piece = mix_ref.at[place.row, pl.ds(q_start, BLOCK_Q)]
        copies.send(piece, piece, mix_far + block, place.far)
        copies.send(piece, piece, mix_pair + block, place.pair)
        if block > 0:
            pass_on(block - 1)
        if block == 0:
            pass_cot_far(1)
            copies.send(far_cot, far_cot, cot_back, place.pair)
            over_cot = cot_all.at[place.block(place.other_dp, place.col), place.row]
            copies.arrived(over_cot, cot_over, place.over)
            copies.send(over_cot, over_cot, cot_back + 1, place.pair)
    pass_on(chunks - 1)
    corner_cot = cot_all.at[place.block(place.other_dp, place.col), place.far_row]
    for half in range(2):
        copies.arrived(
            corner_cot.at[pl.ds(half * half_rows, half_rows)], cot_corner + half, place.over
        )
    copies.send(corner_cot, corner_cot, cot_back + 2, place.pair)
    zo_own.wait()
    for k in range(1, col_count):
        copies.arrived(zo_ref.at[place.col_at(-k)], zo_in + k, place.here)
    for block in range(chunks):
        rows = slice(block * BLOCK_Q, (block + 1) * BLOCK_Q)
        window = pl.ds(block * BLOCK_Q, BLOCK_Q)
        copies.arrived(mix_ref.at[place.pair_row, window], mix_pair + block, place.pair)
        copies.arrived(mix_ref.at[place.cross_row, window], mix_cross + block, place.pair)
        branch = dot_nn(mix_ref[0, rows, :], zo_ref[0])
        for part in range(1, parts):
            branch = branch + dot_nn(mix_ref[part, rows, :], zo_ref[part])
        resid = h_ref[place.row, rows, :].astype(F32) + branch
        resid_ref[rows, :] = resid
        low_ref[rows, :] = resid.astype(LOW)

    cot_kept.wait()
    copies.arrived(cot_all.at[place.block(place.dp, place.col), place.pair_row], cot_pair, place.pair)
    for k, (dp_at, row_at) in enumerate(
        ((place.dp, place.cross_row), (place.other_dp, place.pair_row), (place.other_dp, place.cross_row))
    ):
        copies.arrived(cot_all.at[place.block(dp_at, place.col), row_at], cot_back + k, place.pair)
    for k in (FIRST,):
        copies.arrived(
            cot_all.at[place.block(place.dp, place.col_at(-k)), place.row], cot_z + k, place.here
        )
    copies.finish()


def attend_backward_kernel(
    counts, grad_low_hbm, grad_ref, hidden_ref, resid_ref, wo_ref, wq_ref, normed_ref, mix_hbm, q_ref, k_ref, v_ref, lse_ref,
    seg_ref, small_ref, part_ref, tab_ref, y_hbm, res_given, cot_given, low_hbm,
    out_ref, grad_in_ref, grads_ref, sums_ref, res_all, cot_all,
    gb_ref, mixed_ref, gm_ref, dq_ref, dk_ref, dv_ref, turn_ref, column_ref, y_own_ref, y_in_ref, y_chip_ref, y_last_ref,
    away_ref, pair_in_ref, own_ref, chip_ref, last_ref, inner_ref,
    send_sems, recv_sems,
):
    place = Place(counts)
    copies = Copies(send_sems, recv_sems)
    dp_count, row_count, col_count = counts
    parts, length, width = gb_ref.shape
    kv_heads = k_ref.shape[0]
    features = parts * width
    chunks = length // BLOCK_Q
    scale = HD**-0.5
    all_here = say_hello(place.plane() + place.column())
    segments = seg_ref[place.col]
    for start in range(0, length, LANES):
        column_ref[start : start + LANES, :] = jnp.broadcast_to(
            segments[0:1, start : start + LANES], (LANES, LANES)
        ).T
    dk_ref[...] = jnp.zeros_like(dk_ref)
    dv_ref[...] = jnp.zeros_like(dv_ref)
    all_here()

    def window(chunk):
        return pl.ds(chunk * BLOCK_Q, BLOCK_Q)

    blocks = range(chunks - 1, -1, -1)
    gb_far, gb_pair, gb_cross = (copies.receivers(chunks) for _ in range(3))
    for chunk in blocks:
        piece = gb_ref.at[place.row, window(chunk)]
        copies.send(grad_low_hbm.at[window(chunk)], piece, gb_far + chunk, place.far)
        copies.send(grad_low_hbm.at[window(chunk)], piece, gb_pair + chunk, place.pair)
    gb_own = copies.local(grad_low_hbm, gb_ref.at[place.row])
    mix_own = copies.local(mix_hbm.at[place.row], mixed_ref)
    y_pair = copies.receivers(2 * dp_count)
    y_held = []
    for turn, dp_at in enumerate((place.other_dp, place.dp)):
        for q, (here, there) in enumerate(
            ((place.row, place.pair_row), (place.far_row, place.cross_row))
        ):
            copies.send(y_hbm.at[dp_at, there], y_in_ref.at[turn, q], y_pair + 2 * turn + q, place.pair)
            y_held.append(copies.local(y_hbm.at[dp_at, here], y_own_ref.at[turn, q]))

    first = Spread(place, copies, res_all, place.col_at(-FIRST))
    first.plan_corner(True)
    own_block = place.block(place.dp, place.col)
    late_in = copies.receivers(2)
    late = (place.dp, place.row, place.col_at(LATE))
    own_cot = cot_all.at[own_block, place.row]
    copies.send(low_hbm, res_all.at[own_block, place.row], late_in, late)
    copies.send(own_cot, own_cot, late_in + 1, late)
    gb_own.wait()

    def pass_on(chunk):
        piece = gb_ref.at[place.far_row, window(chunk)]
        copies.arrived(piece, gb_far + chunk, place.far)
        copies.send(piece, piece, gb_cross + chunk, place.pair)

    y_last = copies.receivers(3)

    def y_over():
        for copy in y_held:
            copy.wait()
        for q in range(2):
            copies.arrived(y_in_ref.at[0, q], y_pair + q, place.pair)
            y_chip_ref[0, q] = (y_own_ref[0, q].astype(F32) + y_in_ref[0, q].astype(F32)).astype(LOW)
            copies.send(y_chip_ref.at[0, q], y_last_ref.at[q], y_last + q, place.over)

    def y_far():
        for q in range(2):
            copies.arrived(y_in_ref.at[1, q], y_pair + 2 + q, place.pair)
            copies.arrived(y_last_ref.at[q], y_last + q, place.over)
        y_chip_ref[1, 1] = (
            y_own_ref[1, 1].astype(F32) + y_in_ref[1, 1].astype(F32) + y_last_ref[1].astype(F32)
        ).astype(LOW)
        copies.send(y_chip_ref.at[1, 1], y_last_ref.at[2], y_last + 2, place.far)

    away_in = [copies.receivers(chunks) for _ in range(2)]
    last_in = copies.receivers(chunks)

    def far_share(chunk):
        rows = slice(chunk * BLOCK_Q, (chunk + 1) * BLOCK_Q)
        copies.arrived(pair_in_ref.at[1, window(chunk)], away_in[1] + chunk, place.pair)
        chip_ref[rows, :] = (own_ref[1, rows, :] + pair_in_ref[1, rows, :].astype(F32)).astype(LOW)
        copies.send(chip_ref.at[window(chunk)], last_ref.at[window(chunk)], last_in + chunk, place.far)

    lane = lax.broadcasted_iota(jnp.int32, (BLOCK_Q, LANES), 1)
    y_over()
    first.begin(True)
    pass_on(chunks - 1)
    for block in blocks:
        q_start = block * BLOCK_Q
        k_start = max(0, q_start - WINDOW)
        q_rows, k_rows = slice(q_start, q_start + BLOCK_Q), slice(k_start, q_start + BLOCK_Q)
        copies.arrived(gb_ref.at[place.pair_row, window(block)], gb_pair + block, place.pair)
        copies.arrived(gb_ref.at[place.cross_row, window(block)], gb_cross + block, place.pair)
        total = dot_nt(gb_ref[0, q_rows, :], wo_ref[0])
        for part in range(1, parts):
            total = total + dot_nt(gb_ref[part, q_rows, :], wo_ref[part])
        gm_ref[...] = total.astype(LOW)
        mask = window_mask(column_ref[q_rows, 0:1], segments[0:1, k_rows], q_start, k_start)

        @pl.loop(0, kv_heads)
        def _(kv):
            keys, vals = k_ref[kv, k_rows, :], v_ref[kv, k_rows, :]
            lanes = pl.ds(pl.multiple_of(kv * LANES, LANES), LANES)
            both, logs, queried = gm_ref[:, lanes], lse_ref[q_rows, :], []
            for half in range(2):
                head = 2 * kv + half
                queries, grad = q_ref[head, q_rows, :], both[:, half * HD : (half + 1) * HD]
                scores = dot_nt(queries, keys) * scale
                log = jnp.sum(jnp.where(lane == head, logs, 0.0), axis=1, keepdims=True)
                weights = jnp.where(mask, jnp.exp(scores - log), 0.0)
                grad_weights = dot_nt(grad, vals)
                inner = jnp.sum(weights * grad_weights, axis=1, keepdims=True)
                grad_scores = (weights * (grad_weights - inner)).astype(LOW)
                dv_ref[kv, k_rows, :] += dot_tn(weights.astype(LOW), grad)
                dk_ref[kv, k_rows, :] += dot_tn(grad_scores, queries)
                queried.append(dot_nn(grad_scores, keys) * scale)
            dq_ref[:, lanes] = jnp.concatenate(queried, axis=1)

        if block > 0:
            pass_on(block - 1)
        for kv in range(kv_heads):
            base = kv * 4 * HD
            queries = dq_ref[:, kv * LANES : (kv + 1) * LANES]
            queries = queries * tab_ref[0, q_rows, :] - swap_halves(queries) * tab_ref[1, q_rows, :]
            others = jnp.concatenate([dk_ref[kv, q_rows, :] * scale, dv_ref[kv, q_rows, :]], axis=1)
            others = others * tab_ref[2, q_rows, :] - swap_halves(others) * tab_ref[3, q_rows, :]
            turn_ref[q_rows, base : base + LANES] = queries.astype(LOW)
            turn_ref[q_rows, base + LANES : base + 2 * LANES] = others.astype(LOW)
        for q, row_at in ((1, place.cross_row), (0, place.pair_row)):
            away_ref[q, q_rows, :] = dot_nt(turn_ref[q_rows, :], wq_ref[row_at]).astype(LOW)
            copies.send(
                away_ref.at[q, window(block)], pair_in_ref.at[q, window(block)], away_in[q] + block, place.pair
            )
        for q, row_at in ((1, place.far_row), (0, place.row)):
            own_ref[q, q_rows, :] = dot_nt(turn_ref[q_rows, :], wq_ref[row_at])
        if block < chunks - 1:
            far_share(block + 1)
        if block == chunks - 2:
            y_far()
        if block == 0:
            first.pass_far(True)
            first.pass_over(False)

    columns = turn_ref.shape[1]
    mix_own.wait()
    far_share(0)

    @pl.loop(0, parts)
    def _(part):
        features_here = pl.ds(pl.multiple_of(part * width, width), width)
        grads_ref[part, :, :columns] = dot_tn(normed_ref[:, features_here], turn_ref[...]).astype(LOW)
        grads_ref[part, :, columns:] = dot_tn(mixed_ref[...], gb_ref[part]).astype(LOW)

    gain = small_ref[place.row, GAIN_ONE : GAIN_ONE + 1, :].astype(F32)
    inner_in = copies.receivers(row_count)
    gain_sum = jnp.zeros((1, width), F32)
    for chunk in blocks:
        rows = slice(chunk * BLOCK_Q, (chunk + 1) * BLOCK_Q)
        copies.arrived(pair_in_ref.at[0, window(chunk)], away_in[0] + chunk, place.pair)
        copies.arrived(last_ref.at[window(chunk)], last_in + chunk, place.far)
        grad_normed = own_ref[0, rows, :] + pair_in_ref[0, rows, :].astype(F32) + last_ref[rows, :].astype(F32)
        own_ref[0, rows, :] = grad_normed
        along = grad_normed * hidden_ref[rows, :].astype(F32)
        gain_sum = gain_sum + jnp.sum(along * lse_ref[rows, RSTD_LANE : RSTD_LANE + 1], axis=0, keepdims=True)
        inner_ref[place.row, 0:1, rows] = row_of(jnp.sum(along * gain, axis=1, keepdims=True))
    sums_ref[...] = part_ref[...]
    sums_ref[GAIN_ONE : GAIN_ONE + 1, :] = gain_sum
    for k in range(1, row_count):
        copies.send(
            inner_ref.at[place.row], inner_ref.at[place.row], inner_in + k, (place.dp, place.row_at(k), place.col)
        )
    copies.arrived(y_last_ref.at[2], y_last + 2, place.far)
    for chunk in range(chunks):
        rows = slice(chunk * BLOCK_Q, (chunk + 1) * BLOCK_Q)
        mixture = y_own_ref[1, 0, rows, :].astype(F32) + y_in_ref[1, 0, rows, :].astype(F32)
        for slot in (0, 2):
            mixture = mixture + y_last_ref[slot, rows, :].astype(F32)
        out_ref[rows, :] = (resid_ref[rows, :] + mixture).astype(LOW)

    for k in range(1, row_count):
        copies.arrived(inner_ref.at[place.row_at(-k)], inner_in + k, place.here)
    inner = inner_ref[0, 0:1, :]
    for part in range(1, row_count):
        inner = inner + inner_ref[part, 0:1, :]
    for chunk in range(chunks):
        rows = slice(chunk * BLOCK_Q, (chunk + 1) * BLOCK_Q)
        rstd = lse_ref[rows, RSTD_LANE : RSTD_LANE + 1]
        cube = rstd * rstd * rstd * column_of(inner[:, rows]) / features
        grad_in_ref[rows, :] = (
            grad_ref[rows, :] + rstd * (own_ref[0, rows, :] * gain) - hidden_ref[rows, :].astype(F32) * cube
        )
    first.pass_corner()
    first.complete()
    z_shard = (place.block(place.dp, place.col_at(-LATE)), place.row)
    copies.arrived(res_all.at[z_shard], late_in, place.here)
    copies.arrived(cot_all.at[z_shard], late_in + 1, place.here)
    copies.finish()


def expert_grads(gate_pre, up_pre, grad_hidden):
    sig = 1.0 / (1.0 + jnp.exp(-gate_pre))
    silu = gate_pre * sig
    grad_gate = grad_hidden * up_pre * (sig * (1.0 + gate_pre * (1.0 - sig)))
    return (silu * up_pre).astype(LOW), grad_gate.astype(LOW), (grad_hidden * silu).astype(LOW)


def slot_picks(rank_row, capacity):
    at = lax.broadcasted_iota(jnp.int32, (capacity, rank_row.shape[1]), 0).astype(F32)
    return at == rank_row


def column_of(row):
    return jnp.broadcast_to(row, (LANES, row.shape[1])).T[:, 0:1]


def row_of(column):
    return jnp.broadcast_to(column, (column.shape[0], LANES)).T[0:1, :]


def experts_kernel(
    counts, low_hbm, resid_ref, cot_own_ref, packed_hbm, cot_given, small_ref, zo_hbm, wg_hbm, wu_hbm, wd_hbm,
    y_hbm, grad_ref, grad_low_ref, table_ref, part_ref, wo_hbm, cot_all, res_all, slots_x, slots_g, slots_mid,
    wg_ref, wu_ref, wd_ref, res_ref, cot_ref, x_ref, packed_ref, rank_ref, gate_ref, g_ref, pick_ref, eo_ref, back_ref,
    away_ref, pair_in_ref, own_ref, chip_ref, last_ref, stage_ref, gg_ref, gg_in_ref, rstd_ref, inner_ref, nx_ref,
    keep_x_ref, keep_g_ref, keep_mid_ref, keep_sems,
    send_sems, recv_sems,
):
    place = Place(counts)
    copies = Copies(send_sems, recv_sems)
    dp_count, row_count, col_count = counts
    _, parts, length, width = res_ref.shape
    experts, features, hidden_width = wg_ref.shape
    capacity = pick_ref.shape[0] // experts
    chunks = length // BLOCK_Q
    total_experts = dp_count * row_count * experts
    pair_count = length * TOP
    first_expert = (place.dp * row_count + place.row) * experts
    order = (place.other_dp, place.dp)
    all_here = say_hello(place.plane() + place.column())
    packed_own = copies.local(packed_hbm, packed_ref.at[place.dp])
    cot_in = [
        copies.local(cot_all.at[place.block(dp_at, place.col)], cot_ref.at[dp_at])
        for dp_at in (place.dp, place.other_dp)
    ]

    weights_in = [copies.local(*pair) for pair in ((wg_hbm, wg_ref), (wu_hbm, wu_ref), (wd_hbm, wd_ref))]

    def ranks_of(dp_at):
        ids = packed_ref[dp_at] // pair_count
        orders = (packed_ref[dp_at] - ids * pair_count).astype(F32)
        rows = []
        for e in range(experts):
            match = ids == first_expert + e
            known = jnp.max(jnp.where(match, 1.0, 0.0), axis=0, keepdims=True)
            at = jnp.sum(jnp.where(match, orders, 0.0), axis=0, keepdims=True)
            rows.append(jnp.where(known > 0.0, at, float(pair_count)))
        stacked = jnp.concatenate(rows + [jnp.zeros((LANES - experts, length), F32)], axis=0)
        columns = stacked.T
        for e in range(experts):
            count = jnp.zeros((1, length), F32)
            for start in range(0, length, BLOCK_Q):
                before = columns[start : start + BLOCK_Q, e : e + 1] < rows[e]
                count = count + jnp.sum(jnp.where(before, 1.0, 0.0), axis=0, keepdims=True)
            rank_ref[dp_at, e : e + 1, :] = jnp.where(rows[e] < float(pair_count), count, -1.0)

    def gather_grads(dp_at):
        @pl.loop(0, experts)
        def _(e):
            pick = slot_picks(rank_ref[dp_at, pl.ds(e, 1), :], capacity).astype(F32).astype(LOW)
            slots = pl.ds(pl.multiple_of(e * capacity, capacity), capacity)
            for part in range(parts):
                g_ref[dp_at, part, slots, :] = dot_nn(pick, cot_ref[dp_at, part]).astype(LOW)

    packed_own.wait()
    ranks_of(place.dp)
    cot_in[0].wait()
    gather_grads(place.dp)
    all_here()

    own_low = res_ref.at[place.dp, place.row]
    packed_over = copies.receivers()
    copies.send(packed_hbm, packed_ref.at[place.dp], packed_over, place.over)
    low_own = copies.local(low_hbm, own_low)
    halves = 2
    half_rows = length // halves
    res_at = copies.receivers(7 * halves)

    def halved(ref, half):
        return ref.at[pl.ds(half * half_rows, half_rows)]

    far_low = res_ref.at[place.dp, place.far_row]
    over_low = res_ref.at[place.other_dp, place.row]
    corner_low = res_ref.at[place.other_dp, place.far_row]
    for half in range(halves):
        source, target = halved(low_hbm, half), halved(own_low, half)
        copies.send(source, target, res_at + half, place.far)
        copies.send(source, target, res_at + halves + half, place.over)
    copies.send(low_hbm, own_low, res_at + 2 * halves, place.pair)
    own_block = place.block(place.dp, place.col)
    res_z, cot_z = copies.receivers(col_count), copies.receivers(col_count)
    for k, on_cot in ((SECOND, True), (FIRST, False), (SECOND, False)):
        peer = (place.dp, place.row, place.col_at(k))
        if on_cot:
            own_cot = cot_all.at[own_block, place.row]
            copies.send(own_cot, own_cot, cot_z + k, peer)
        else:
            copies.send(low_hbm, res_all.at[own_block, place.row], res_z + k, peer)

    def pass_side(half):
        copies.arrived(halved(far_low, half), res_at + half, place.far)
        copies.arrived(halved(over_low, half), res_at + halves + half, place.over)
        corner, peer = (far_low, place.over) if half == 0 else (over_low, place.far)
        copies.send(halved(corner, half), halved(corner, half), res_at + 3 * halves + half, peer)
        for k, ref in ((4, far_low), (5, over_low)):
            copies.send(halved(ref, half), halved(ref, half), res_at + k * halves + half, place.pair)

    def pass_corner(half):
        copies.arrived(halved(corner_low, half), res_at + 3 * halves + half, place.here)
        copies.send(
            halved(corner_low, half), halved(corner_low, half), res_at + 6 * halves + half, place.pair
        )

    copies.arrived(packed_ref.at[place.other_dp], packed_over, place.over)
    ranks_of(place.other_dp)
    pass_side(0)
    cot_in[1].wait()
    gather_grads(place.other_dp)
    pass_side(1)
    pass_corner(0)
    pass_corner(1)

    wo_in = copies.receivers(row_count)
    own_wo = copies.local(zo_hbm.at[place.row], stage_ref.at[0, pl.ds(0, zo_hbm.shape[1])])

    low_own.wait()
    copies.arrived(res_ref.at[place.dp, place.pair_row], res_at + 2 * halves, place.pair)
    for half in range(halves):
        for k, dp_at, row_at in (
            (4, place.dp, place.cross_row), (5, place.other_dp, place.pair_row), (6, place.other_dp, place.cross_row)
        ):
            copies.arrived(halved(res_ref.at[dp_at, row_at], half), res_at + k * halves + half, place.pair)
    for copy in weights_in:
        copy.wait()
    own_wo.wait()
    kept_wo = copies.local(stage_ref.at[0, pl.ds(0, zo_hbm.shape[1])], wo_hbm.at[place.row])
    kept_wo.wait()
    res_kept = [
        copies.local(res_ref.at[dp_at], res_all.at[place.block(dp_at, place.col)])
        for dp_at in (place.dp, place.other_dp)
    ]
    first, second = (Spread(place, copies, cot_all, place.col_at(-k)) for k in (FIRST, SECOND))
    first.plan_corner(False)
    second.plan_corner(True)
    first.begin(True)
    copies.arrived(
        cot_all.at[place.block(place.dp, place.col_at(-SECOND)), place.row], cot_z + SECOND, place.here
    )
    second.begin(True)

    own_scaled = place.row
    gg_same, gg_other = copies.receivers(row_count), copies.receivers(row_count)
    pair_in = copies.receivers(2 * dp_count)
    last_over, last_across, last_far = (copies.receivers() for _ in range(3))
    table_in = copies.receivers(col_count)

    kept_pairs = ((keep_x_ref, slots_x), (keep_g_ref, slots_g), (keep_mid_ref, slots_mid))
    for turn, dp_at in enumerate(order):
        last = turn == dp_count - 1

        @pl.loop(0, chunks)
        def _(chunk):
            rows = pl.ds(pl.multiple_of(chunk * BLOCK_Q, BLOCK_Q), BLOCK_Q)
            total = jnp.zeros((BLOCK_Q, 1), F32)
            for part in range(parts):
                piece = res_ref[dp_at, part, rows, :].astype(F32)
                total = total + jnp.sum(piece * piece, axis=1, keepdims=True)
            rstd = lax.rsqrt(total / features + EPSILON)
            for part in range(parts):
                piece = res_ref[dp_at, part, rows, :].astype(F32)
                gain = small_ref[part, GAIN_TWO : GAIN_TWO + 1, :].astype(F32)
                x_ref[rows, part * width : (part + 1) * width] = (piece * rstd * gain).astype(LOW)
            table_ref[place.col, dp_at, RSTD_ROW : RSTD_ROW + 1, rows] = row_of(rstd)
            if last:
                rstd_ref[rows, :] = jnp.broadcast_to(rstd, (BLOCK_Q, LANES))
                piece = res_ref[dp_at, own_scaled, rows, :].astype(F32)
                gain = small_ref[own_scaled, GAIN_TWO : GAIN_TWO + 1, :].astype(F32)
                nx_ref[rows, :] = (piece * rstd * gain).astype(LOW)

        logits = jnp.zeros((total_experts, length), F32)
        for part in range(parts):
            logits = logits + dot_nt(
                small_ref[part, :total_experts, :], x_ref[:, part * width : (part + 1) * width]
            )
        ids = packed_ref[dp_at] // pair_count
        expert_at = lax.broadcasted_iota(jnp.int32, (total_experts, length), 0)
        chosen = expert_at == ids[0:1, :]
        for k in range(1, TOP):
            chosen = chosen | (expert_at == ids[k : k + 1, :])
        shown = jnp.where(chosen, logits, NEG_LARGE)
        weights = jnp.where(chosen, jnp.exp(shown - jnp.max(shown, axis=0, keepdims=True)), 0.0)
        gate_ref[...] = weights / jnp.sum(weights, axis=0, keepdims=True)
        table_ref[place.col, dp_at, 0:experts, :] = rank_ref[dp_at, 0:experts, :]
        for e in range(experts):
            table_ref[place.col, dp_at, experts + e : experts + e + 1, :] = gate_ref[pl.ds(first_expert + e, 1), :]

        @pl.loop(0, experts)
        def _(e):
            if last:

                @pl.when(e == 1)
                def _():
                    second.pass_far(True)
                    second.pass_over(False)

                pl.when(e == experts - 1)(first.pass_corner)


            keep = lax.rem(e, 2)
            kept = [
                pltpu.make_async_copy(held.at[keep], target.at[turn, e], keep_sems.at[k, keep])
                for k, (held, target) in enumerate(kept_pairs)
            ]

            @pl.when(e + turn * experts >= 2)
            def _():
                for copy in kept:
                    copy.wait()

            here = slot_picks(rank_ref[dp_at, pl.ds(e, 1), :], capacity)
            pick = here.astype(F32).astype(LOW)
            slots = pl.ds(pl.multiple_of(e * capacity, capacity), capacity)
            pick_ref[slots, :] = pick
            gate_slot = jnp.sum(
                jnp.where(here, gate_ref[pl.ds(first_expert + e, 1), :], 0.0), axis=1, keepdims=True
            )
            x = dot_nn(pick, x_ref[...]).astype(LOW)
            keep_x_ref[keep] = x
            grad_hidden = jnp.zeros((capacity, hidden_width), F32)
            for part in range(parts):
                pair_grad = (g_ref[dp_at, part, slots, :].astype(F32) * gate_slot).astype(LOW)
                keep_g_ref[keep, :, part * width : (part + 1) * width] = pair_grad
                grad_hidden = grad_hidden + dot_nt(
                    pair_grad, wd_ref[e, :, part * width : (part + 1) * width]
                )
            hidden, grad_gate, grad_up = expert_grads(dot_nn(x, wg_ref[e]), dot_nn(x, wu_ref[e]), grad_hidden)
            keep_mid_ref[keep, 0] = hidden
            keep_mid_ref[keep, 1] = grad_gate
            keep_mid_ref[keep, 2] = grad_up
            for copy in kept:
                copy.start()
            along = jnp.zeros((capacity, 1), F32)
            for part in range(parts):
                cols = slice(part * width, (part + 1) * width)
                out = dot_nn(hidden, wd_ref[e, :, cols]).astype(LOW).astype(F32)
                along = along + jnp.sum(g_ref[dp_at, part, slots, :].astype(F32) * out, axis=1, keepdims=True)
                eo_ref[part, slots, :] = (out * gate_slot).astype(LOW)
                back_ref[part, slots, :] = (
                    dot_nt(grad_gate, wg_ref[e, cols, :]) + dot_nt(grad_up, wu_ref[e, cols, :])
                ).astype(LOW)
            gg_ref[dp_at, pl.ds(e, 1), :] = jnp.sum(jnp.where(here, along, 0.0), axis=0, keepdims=True)

        if not last:
            first.pass_far(False)
            first.pass_over(True)
        owner = place.dp * row_count + place.row
        if last:
            for k in range(1, row_count):
                copies.send(gg_ref.at[dp_at], gg_in_ref.at[owner], gg_same + k, (dp_at, place.row_at(k), place.col))
            gg_in_ref[owner] = gg_ref[dp_at]
        else:
            for k in range(row_count):
                copies.send(gg_ref.at[dp_at], gg_in_ref.at[owner], gg_other + k, (dp_at, place.row_at(k), place.col))

        for q, row_at in enumerate((place.pair_row, place.cross_row)):
            away_ref[turn, q] = dot_tn(pick_ref[...], back_ref[row_at]).astype(LOW)
            copies.send(away_ref.at[turn, q], pair_in_ref.at[turn, q], pair_in + 2 * turn + q, place.pair)
        for q, row_at in enumerate((place.far_row, place.row)):
            own_ref[q] = dot_tn(pick_ref[...], back_ref[row_at])
        copies.arrived(pair_in_ref.at[turn, 1], pair_in + 2 * turn + 1, place.pair)
        far_sum = own_ref[0] + pair_in_ref[turn, 1].astype(F32)
        if last:
            copies.arrived(last_ref.at[1], last_across, place.over)
            chip_ref[turn, 1] = (far_sum + last_ref[1].astype(F32)).astype(LOW)
            copies.send(chip_ref.at[turn, 1], last_ref.at[2], last_far, place.far)
        else:
            chip_ref[turn, 1] = far_sum.astype(LOW)
            copies.send(chip_ref.at[turn, 1], last_ref.at[1], last_across, place.over)
        copies.arrived(pair_in_ref.at[turn, 0], pair_in + 2 * turn, place.pair)
        if last:
            own_ref[1] = own_ref[1] + pair_in_ref[turn, 0].astype(F32)
        else:
            chip_ref[turn, 0] = (own_ref[1] + pair_in_ref[turn, 0].astype(F32)).astype(LOW)
            copies.send(chip_ref.at[turn, 0], last_ref.at[0], last_over, place.over)
            for k in range(col_count):
                source = place.col_at(k)
                mine = source == place.row
                step = lax.rem(source - place.row + row_count, row_count)
                copies.send(
                    zo_hbm.at[source], wo_hbm.at[place.row], wo_in + step, (place.dp, source, place.col), jnp.logical_not(mine)
                )

        for part in range(parts):
            stage_ref[part] = dot_tn(pick_ref[...], eo_ref[part]).astype(LOW)
        kept = copies.local(stage_ref, y_hbm.at[dp_at])
        kept.wait()

    for k in range(1, col_count):
        copies.send(table_ref.at[place.col], table_ref.at[place.col], table_in + k, (place.dp, place.row, place.col_at(k)))

    for k in range(1, row_count):
        copies.arrived(gg_in_ref.at[place.dp * row_count + place.row_at(-k)], gg_same + k, place.here)
    for k in range(row_count):
        copies.arrived(gg_in_ref.at[place.other_dp * row_count + place.row_at(-k)], gg_other + k, place.here)
    along = jnp.concatenate([gg_in_ref[owner, :experts, :] for owner in range(dp_count * row_count)], axis=0)
    gates = gate_ref[...]
    grad_logits = (gates * (along - jnp.sum(gates * along, axis=0, keepdims=True))).astype(LOW)
    router = small_ref[place.row, :total_experts, :]
    gain = small_ref[place.row, GAIN_TWO : GAIN_TWO + 1, :].astype(F32)
    part_ref[...] = jnp.zeros_like(part_ref)
    part_ref[:total_experts, :] = dot_nn(grad_logits, nx_ref[...])
    own_ref[1] = own_ref[1] + dot_tn(grad_logits, router)

    copies.arrived(last_ref.at[0], last_over, place.over)
    copies.arrived(last_ref.at[2], last_far, place.far)
    inner_in = copies.receivers(row_count)
    gain_sum = jnp.zeros((1, width), F32)
    for chunk in range(chunks):
        rows = slice(chunk * BLOCK_Q, (chunk + 1) * BLOCK_Q)
        grad_normed = own_ref[1, rows, :]
        for k in (0, 2):
            grad_normed = grad_normed + last_ref[k, rows, :].astype(F32)
        own_ref[0, rows, :] = grad_normed
        along = grad_normed * resid_ref[rows, :]
        gain_sum = gain_sum + jnp.sum(along * rstd_ref[rows, 0:1], axis=0, keepdims=True)
        inner_ref[place.row, 0:1, rows] = row_of(jnp.sum(along * gain, axis=1, keepdims=True))
    part_ref[GAIN_TWO : GAIN_TWO + 1, :] = gain_sum
    for k in range(1, row_count):
        copies.send(
            inner_ref.at[place.row], inner_ref.at[place.row], inner_in + k, (place.dp, place.row_at(k), place.col)
        )
    for k in range(1, row_count):
        copies.arrived(inner_ref.at[place.row_at(-k)], inner_in + k, place.here)
    inner = inner_ref[0, 0:1, :]
    for part in range(1, row_count):
        inner = inner + inner_ref[part, 0:1, :]
    for chunk in range(chunks):
        rows = slice(chunk * BLOCK_Q, (chunk + 1) * BLOCK_Q)
        rstd = rstd_ref[rows, 0:1]
        cube = rstd * rstd * rstd * column_of(inner[:, rows]) / features
        grad = (
            cot_own_ref[rows, :].astype(F32) + rstd * (own_ref[0, rows, :] * gain) - resid_ref[rows, :] * cube
        )
        grad_ref[rows, :] = grad
        grad_low_ref[rows, :] = grad.astype(LOW)

    for copy in res_kept:
        copy.wait()
    for keep in range(2):
        for k, (held, target) in enumerate(kept_pairs):
            pltpu.make_async_copy(held.at[keep], target.at[0, 0], keep_sems.at[k, keep]).wait()
    second.pass_corner()
    first.complete()
    second.complete()
    for k in (FIRST, SECOND):
        z_shard = (place.block(place.dp, place.col_at(-k)), place.row)
        copies.arrived(res_all.at[z_shard], res_z + k, place.here)
    for k in range(1, row_count):
        copies.arrived(wo_hbm.at[place.row_at(-k)], wo_in + k, place.here)
    for k in range(1, col_count):
        copies.arrived(table_ref.at[place.col_at(-k)], table_in + k, place.here)
    copies.finish()


def slot_grads(picked, rank_row, gate_row, rstd_row, res, cot, small_ref, wg, wu, wd):
    here = slot_picks(rank_row, picked)
    pick = here.astype(F32).astype(LOW)
    gate_slot = jnp.sum(jnp.where(here, gate_row, 0.0), axis=1, keepdims=True)
    rstd_slot = jnp.sum(jnp.where(here, rstd_row, 0.0), axis=1, keepdims=True)
    parts = res.shape[0]
    x = jnp.concatenate(
        [
            (
                dot_nn(pick, res[part]) * rstd_slot * small_ref[part, GAIN_TWO : GAIN_TWO + 1, :].astype(F32)
            ).astype(LOW)
            for part in range(parts)
        ],
        axis=1,
    )
    pair_grad = jnp.concatenate(
        [(dot_nn(pick, cot[part]) * gate_slot).astype(LOW) for part in range(parts)], axis=1
    )
    hidden, grad_gate, grad_up = expert_grads(dot_nn(x, wg), dot_nn(x, wu), dot_nt(pair_grad, wd))
    return x, pair_grad, hidden, grad_gate, grad_up


def weight_grads_kernel(
    counts, res_given, cot_given, grads_hbm, slots_x, slots_g, slots_mid, part_ref, table_ref, small_ref,
    wg_hbm, wu_hbm, wd_hbm,
    res_all, cot_all, dg_hbm, du_hbm, dd_hbm, own_ref, sums_ref,
    wg_ref, wu_ref, wd_ref, parts_ref, dg_ref, du_ref, dd_ref, res_ref, cot_ref, x_ref, g_ref, mid_ref, grads_in_ref, sum_ref,
    sems, keep_sems, out_sems, send_sems, recv_sems,
):
    place = Place(counts)
    copies = Copies(send_sems, recv_sems)
    dp_count, row_count, col_count = counts
    experts = wg_ref.shape[0]
    _, parts, length, width = res_all.shape
    capacity = length * TOP // (dp_count * row_count * experts)
    far_side = [(place.other_dp, place.row, place.col_at(k)) for k in range(1, col_count)]
    all_here = say_hello(
        place.plane()
        + place.column()
        + [
            (place.dp, place.row_at(j), place.col_at(k))
            for j in range(1, row_count)
            for k in range(1, col_count)
        ]
        + far_side
    )
    steps = 5
    before_late = 4 * experts

    def fetch(step):
        back = jnp.where(step < 2, FIRST, jnp.where(step < 4, SECOND, LATE))
        dp_at = lax.rem(place.dp + lax.rem(step, 2), dp_count)
        col_at = place.col_at(-back)
        b, slot = place.block(dp_at, col_at), lax.rem(step, 2)
        return dp_at, col_at, slot, (
            pltpu.make_async_copy(res_all.at[b], res_ref.at[slot], sems.at[slot]),
            pltpu.make_async_copy(cot_all.at[b], cot_ref.at[slot], sems.at[2 + slot]),
        )

    def kept_slots(turn):
        at, e, slot = turn // experts, lax.rem(turn, experts), lax.rem(turn, 2)
        pairs = ((slots_x, x_ref), (slots_g, g_ref), (slots_mid, mid_ref))
        return [
            pltpu.make_async_copy(source.at[at, e], target.at[slot], keep_sems.at[k, slot])
            for k, (source, target) in enumerate(pairs)
        ]

    for copy in fetch(0)[3]:
        copy.start()
    weights_in = [copies.local(*pair) for pair in ((wg_hbm, wg_ref), (wu_hbm, wu_ref), (wd_hbm, wd_ref))]
    for copy in kept_slots(0):
        copy.start()
    parts_ref[0] = part_ref[...]
    others = place.column() + [place.over] + far_side
    sums_in = copies.receivers(len(others) + 1)
    sum_sends = [
        copies.plan(parts_ref.at[0], parts_ref.at[k + 1], sums_in + k + 1, peer) for k, peer in enumerate(others)
    ]

    grads_in = copies.receivers(col_count)
    grads_kept = copies.local(grads_hbm.at[place.col], grads_in_ref.at[place.col])
    mine = place.row == place.col
    over_in, swap_in = copies.receivers(), copies.receivers()
    to_over = copies.plan(sum_ref.at[0], sum_ref.at[1], over_in, place.over)
    to_swap = remote(
        sum_ref.at[2], sum_ref.at[3], copies.send_sems.at[copies.sends], copies.recv_sems.at[swap_in],
        (place.dp, place.col, place.row),
    )
    copies.sends += 1
    copies.open.append((to_swap, jnp.logical_not(mine)))
    two_res, three_res, three_cot = (
        Spread(place, copies, array, place.col_at(-k))
        for k, array in ((SECOND, res_all), (LATE, res_all), (LATE, cot_all))
    )
    for spread, by_over in ((two_res, True), (three_res, True), (three_cot, False)):
        spread.plan_corner(by_over)
    grad_sends = [
        copies.plan(
            grads_hbm.at[place.col_at(k)], grads_in_ref.at[place.col], grads_in + k,
            (place.dp, place.row, place.col_at(k)),
        )
        for k in range(1, col_count)
    ]

    def begin():
        all_here()
        two_res.begin(True)
        three_res.begin(True)
        three_cot.begin(False)
        for copy in grad_sends + sum_sends:
            copy.start()

    def sum_columns():
        grads_kept.wait()
        for k in range(1, col_count):
            copies.arrived(grads_in_ref.at[place.col_at(-k)], grads_in + k, place.here)
        total = grads_in_ref[0].astype(F32)
        for col_at in range(1, col_count):
            total = total + grads_in_ref[col_at].astype(F32)
        sum_ref[0] = total.astype(LOW)
        to_over.start()

    def sum_over():
        copies.arrived(sum_ref.at[1], over_in, place.over)
        total = sum_ref[0].astype(F32) + sum_ref[1].astype(F32)
        sum_ref[2] = total.astype(LOW)
        own_ref[...] = total
        pl.when(jnp.logical_not(mine))(to_swap.start)

    def sum_parts():
        total = parts_ref[0]
        for k in range(len(others)):
            copies.arrived(parts_ref.at[k + 1], sums_in + k + 1, place.here)
            total = total + parts_ref[k + 1]
        sums_ref[...] = total

    def take_swapped():
        @pl.when(jnp.logical_not(mine))
        def _():
            copies.arrived(sum_ref.at[3], swap_in, place.here)
            own_ref[...] = sum_ref[3].astype(F32)

    events = {
        1: [begin],
        5: [lambda: two_res.pass_far(True), lambda: two_res.pass_over(False), three_cot.send_over],
        7: [two_res.complete_same],
        10: [lambda: three_res.pass_far(True), lambda: three_res.pass_over(False)],
        12: [two_res.pass_corner, lambda: three_cot.pass_far(False), two_res.complete_other, sum_columns],
        15: [lambda: three_cot.pass_over(True), three_res.complete_same, three_cot.complete_same],
        16: [three_res.pass_corner, sum_over],
        18: [three_cot.pass_corner],
        19: [sum_parts],
    }
    dg_ref[...] = jnp.zeros_like(dg_ref)
    du_ref[...] = jnp.zeros_like(du_ref)
    dd_ref[...] = jnp.zeros_like(dd_ref)
    for copy in weights_in:
        copy.wait()

    def other_blocks(turn):
        step, e = turn // experts, lax.rem(turn, experts)
        for at, actions in events.items():

            @pl.when(turn == at)
            def _(actions=actions):
                for action in actions:
                    action()

        dp_at, col_at, slot, arriving = fetch(step)

        @pl.when(e == 0)
        def _():
            @pl.when(step == 3)
            def _():
                for copy in arriving:
                    copy.start()

            for copy in arriving:
                copy.wait()

        @pl.when((e == experts - 1) & (step != 2) & (step + 1 < steps))
        def _():
            for copy in fetch(step + 1)[3]:
                copy.start()

        x, pair_grad, hidden, grad_gate, grad_up = slot_grads(
            capacity,
            table_ref[col_at, dp_at, pl.ds(e, 1), :],
            table_ref[col_at, dp_at, pl.ds(experts + e, 1), :],
            table_ref[col_at, dp_at, RSTD_ROW : RSTD_ROW + 1, :],
            res_ref.at[slot], cot_ref.at[slot], small_ref, wg_ref[e], wu_ref[e], wd_ref[e],
        )
        dd_ref[e] += dot_tn(hidden, pair_grad)
        dg_ref[e] += dot_tn(x, grad_gate)
        du_ref[e] += dot_tn(x, grad_up)

        @pl.when(step == steps - 1)
        def _():
            for k, (source, target) in enumerate(((dg_ref, dg_hbm), (du_ref, du_hbm), (dd_ref, dd_hbm))):
                pltpu.make_async_copy(source.at[e], target.at[e], out_sems.at[k, e]).start()

    pl.loop(0, before_late)(other_blocks)

    @pl.loop(0, dp_count * experts)
    def _(turn):
        e, slot = lax.rem(turn, experts), lax.rem(turn, 2)
        for copy in kept_slots(turn):
            copy.wait()

        @pl.when(turn + 1 < dp_count * experts)
        def _():
            for copy in kept_slots(turn + 1):
                copy.start()

        dd_ref[e] += dot_tn(mid_ref[slot, 0], g_ref[slot])
        dg_ref[e] += dot_tn(x_ref[slot], mid_ref[slot, 1])
        du_ref[e] += dot_tn(x_ref[slot], mid_ref[slot, 2])

    pl.loop(before_late, steps * experts)(other_blocks)
    take_swapped()
    three_res.complete_other()
    three_cot.complete_other()
    for e in range(experts):
        for k, (source, target) in enumerate(((dg_ref, dg_hbm), (du_ref, du_hbm), (dd_ref, dd_hbm))):
            pltpu.make_async_copy(source.at[e], target.at[e], out_sems.at[k, e]).wait()
    copies.finish()


def last_grads_kernel(
    counts, res_all, cot_all, table_ref, small_ref, wg_ref, wu_ref, wd_ref, dg_in, du_in, dd_in,
    out_in, grad_in_in, attn_in, sums_in,
    dg_ref, du_ref, dd_ref, out_ref, grad_in_ref, qkv_ref, wo_ref, router_ref, one_ref, two_ref,
    res_ref, cot_ref, sems,
):
    dp_count, row_count, col_count = counts
    e = pl.program_id(0)
    experts = pl.num_programs(0)
    _, parts, length, width = res_all.shape
    capacity = length * TOP // (dp_count * row_count * experts)
    col_at = lax.rem(lax.axis_index("col") + col_count - LATE, col_count)

    dp_at = dp_count - 1 - lax.axis_index("dp")
    b = dp_at * col_count + col_at
    arriving = (
        pltpu.make_async_copy(res_all.at[b], res_ref, sems.at[0]),
        pltpu.make_async_copy(cot_all.at[b], cot_ref, sems.at[1]),
    )

    @pl.when(e == 0)
    def _():
        for copy in arriving:
            copy.start()

    out_ref[...] = out_in[...]
    grad_in_ref[...] = grad_in_in[...]
    group, columns = qkv_ref.shape[1:]
    for head in range(group):
        qkv_ref[:, head, :] = attn_in[:, head * columns : (head + 1) * columns]
    wo_ref[...] = attn_in[:, group * columns :]

    @pl.when(e == experts - 1)
    def _():
        router_ref[...] = sums_in[:GAIN_ONE, :].T
        one_ref[...] = sums_in[GAIN_ONE : GAIN_ONE + 1, :]
        two_ref[...] = sums_in[GAIN_TWO : GAIN_TWO + 1, :]

    @pl.when(e == 0)
    def _():
        for copy in arriving:
            copy.wait()

    x, pair_grad, hidden, grad_gate, grad_up = slot_grads(
        capacity,
        table_ref[col_at, dp_at, pl.ds(e, 1), :],
        table_ref[col_at, dp_at, pl.ds(experts + e, 1), :],
        table_ref[col_at, dp_at, RSTD_ROW : RSTD_ROW + 1, :],
        res_ref, cot_ref, small_ref, wg_ref[0], wu_ref[0], wd_ref[0],
    )
    dd_ref[0] = dd_in[0] + dot_tn(hidden, pair_grad)
    dg_ref[0] = dg_in[0] + dot_tn(x, grad_gate)
    du_ref[0] = du_in[0] + dot_tn(x, grad_up)


def fast_device(
    hidden_in, norm_gain, w_qkv, w_out, ffn_gain, router, w_gate, w_up, w_down, cotangent,
    segment_ids, expert_ids, pair_order,
):
    dp_count, row_count, col_count = (lax.axis_size(name) for name in ("dp", "row", "col"))
    my_dp, my_row, my_col = (lax.axis_index(name) for name in ("dp", "row", "col"))
    length, width = hidden_in.shape
    kv_local = w_qkv.shape[1]
    head_width = kv_local * (HQ // HK) * HD
    qkv_width = kv_local * (HQ // HK + 2) * HD
    exp_local, _, hidden_width = w_gate.shape
    capacity = length * TOP // EXPERTS
    blocks = dp_count * col_count
    vmem = pl.BlockSpec(memory_space=pltpu.VMEM)
    hbm = pl.BlockSpec(memory_space=pl.ANY)
    params = pltpu.CompilerParams(vmem_limit_bytes=VMEM_BYTES)

    packed = (expert_ids * (length * TOP) + pair_order).T
    own_q = w_qkv.reshape(width, qkv_width)
    own_o = w_out.reshape(head_width, width)
    small = jnp.concatenate(
        [router.T, norm_gain[None], ffn_gain[None], jnp.zeros((SMALL_ROWS - 2 - EXPERTS, width), LOW)], axis=0
    )
    seg_rows = jnp.broadcast_to(segment_ids, (8, length)).astype(F32)
    tables = jnp.asarray(rope_lanes(length))
    counts = (dp_count, row_count, col_count)
    (
        resid_mid, resid_low, mixed_all, normed_one, query_rot, key_rot, value_low, logs,
        wq_rows, wo_cols, small_all, seg_all, cot_all,
    ) = pl.pallas_call(
        functools.partial(attend_forward_kernel, counts),
        out_shape=(
            jax.ShapeDtypeStruct((length, width), F32),
            jax.ShapeDtypeStruct((length, width), LOW),
            jax.ShapeDtypeStruct((row_count, length, head_width), LOW),
            jax.ShapeDtypeStruct((length, D), LOW),
            jax.ShapeDtypeStruct((2 * kv_local, length, HD), LOW),
            jax.ShapeDtypeStruct((kv_local, length, HD), LOW),
            jax.ShapeDtypeStruct((kv_local, length, HD), LOW),
            jax.ShapeDtypeStruct((length, LANES), F32),
            jax.ShapeDtypeStruct((row_count, width, qkv_width), LOW),
            jax.ShapeDtypeStruct((col_count, head_width, width), LOW),
            jax.ShapeDtypeStruct((row_count, SMALL_ROWS, width), LOW),
            jax.ShapeDtypeStruct((row_count, 8, length), F32),
            jax.ShapeDtypeStruct((blocks, row_count, length, width), LOW),
        ),
        in_specs=[hbm] * 6 + [vmem],
        out_specs=[vmem] * 12 + [hbm],
        scratch_shapes=[
            pltpu.VMEM((row_count, length, width), LOW),
            pltpu.VMEM((col_count, width, qkv_width), LOW),
            pltpu.VMEM((length, width), LOW),
            pltpu.VMEM((length, LANES), F32),
            pltpu.SemaphoreType.DMA((64,)),
            pltpu.SemaphoreType.DMA((64,)),
        ],
        compiler_params=pltpu.CompilerParams(
            vmem_limit_bytes=VMEM_BYTES, collective_id=1, has_side_effects=True
        ),
        cost_estimate=pl.CostEstimate(flops=50_000_000_000, bytes_accessed=30_000_000, transcendentals=0),
        name="attend_forward",
    )(hidden_in, own_q, own_o, small, seg_rows, cotangent, tables)
    block_low = jax.ShapeDtypeStruct((length, width), LOW)
    block_float = jax.ShapeDtypeStruct((length, width), F32)
    slots = exp_local * capacity
    plane = (dp_count, row_count, length, width)
    every = jax.ShapeDtypeStruct((blocks, row_count, length, width), LOW)
    y_part, grad_resid, grad_low, table, small_part, wo_rows, cot_all, res_all, *kept_slots = pl.pallas_call(
        functools.partial(experts_kernel, counts),
        out_shape=(
            jax.ShapeDtypeStruct(plane, LOW),
            block_float,
            block_low,
            jax.ShapeDtypeStruct((col_count, dp_count, 16, length), F32),
            jax.ShapeDtypeStruct((SMALL_ROWS, width), F32),
            jax.ShapeDtypeStruct((row_count, head_width, width), LOW),
            every,
            every,
            jax.ShapeDtypeStruct((dp_count, exp_local, capacity, D), LOW),
            jax.ShapeDtypeStruct((dp_count, exp_local, capacity, D), LOW),
            jax.ShapeDtypeStruct((dp_count, exp_local, 3, capacity, hidden_width), LOW),
        ),
        input_output_aliases={4: 6},
        in_specs=[hbm, vmem, vmem, hbm, hbm, vmem, hbm, hbm, hbm, hbm],
        out_specs=[hbm] + [vmem] * 4 + [hbm] * 6,
        scratch_shapes=[
            pltpu.VMEM(w_gate.shape, LOW),
            pltpu.VMEM(w_up.shape, LOW),
            pltpu.VMEM(w_down.shape, LOW),
            pltpu.VMEM(plane, LOW),
            pltpu.VMEM(plane, LOW),
            pltpu.VMEM((length, D), LOW),
            pltpu.VMEM((dp_count, TOP, length), jnp.int32),
            pltpu.VMEM((dp_count, 8, length), F32),
            pltpu.VMEM((EXPERTS, length), F32),
            pltpu.VMEM((dp_count, row_count, slots, width), LOW),
            pltpu.VMEM((slots, length), LOW),
            pltpu.VMEM((row_count, slots, width), LOW),
            pltpu.VMEM((row_count, slots, width), LOW),
            pltpu.VMEM((dp_count, 2, length, width), LOW),
            pltpu.VMEM((dp_count, 2, length, width), LOW),
            pltpu.VMEM((2, length, width), F32),
            pltpu.VMEM((dp_count, 2, length, width), LOW),
            pltpu.VMEM((3, length, width), LOW),
            pltpu.VMEM((row_count, length, width), LOW),
            pltpu.VMEM((dp_count, 8, length), F32),
            pltpu.VMEM((dp_count * row_count, 8, length), F32),
            pltpu.VMEM((length, LANES), F32),
            pltpu.VMEM((row_count, 8, length), F32),
            pltpu.VMEM((length, width), LOW),
            pltpu.VMEM((2, capacity, D), LOW),
            pltpu.VMEM((2, capacity, D), LOW),
            pltpu.VMEM((2, 3, capacity, hidden_width), LOW),
            pltpu.SemaphoreType.DMA((3, 2)),
            pltpu.SemaphoreType.DMA((80,)),
            pltpu.SemaphoreType.DMA((80,)),
        ],
        compiler_params=pltpu.CompilerParams(
            vmem_limit_bytes=VMEM_BYTES, collective_id=2, has_side_effects=True
        ),
        cost_estimate=pl.CostEstimate(flops=80_000_000_000, bytes_accessed=50_000_000, transcendentals=0),
        name="experts",
    )(resid_low, resid_mid, cotangent, packed, cot_all, small_all, wo_cols, w_gate, w_up, w_down)

    halves = (dp_count, 2, length, width)
    half = (2, length, width)
    layer_out, grad_in, grads_part, small_part, res_all, cot_all = pl.pallas_call(
        functools.partial(attend_backward_kernel, counts),
        out_shape=(
            block_low,
            block_float,
            jax.ShapeDtypeStruct((row_count, width, qkv_width + width), LOW),
            jax.ShapeDtypeStruct((SMALL_ROWS, width), F32),
            every,
            every,
        ),
        input_output_aliases={17: 4, 18: 5},
        in_specs=[hbm] + [vmem] * 6 + [hbm] + [vmem] * 8 + [hbm] * 4,
        out_specs=[vmem] * 4 + [hbm] * 2,
        scratch_shapes=[
            pltpu.VMEM((row_count, length, width), LOW),
            pltpu.VMEM((length, head_width), LOW),
            pltpu.VMEM((BLOCK_Q, head_width), LOW),
            pltpu.VMEM((BLOCK_Q, head_width), F32),
            pltpu.VMEM((kv_local, length, HD), F32),
            pltpu.VMEM((kv_local, length, HD), F32),
            pltpu.VMEM((length, qkv_width), LOW),
            pltpu.VMEM((length, LANES), F32),
            pltpu.VMEM(halves, LOW),
            pltpu.VMEM(halves, LOW),
            pltpu.VMEM(halves, LOW),
            pltpu.VMEM((3, length, width), LOW),
            pltpu.VMEM(half, LOW),
            pltpu.VMEM(half, LOW),
            pltpu.VMEM(half, F32),
            pltpu.VMEM((length, width), LOW),
            pltpu.VMEM((length, width), LOW),
            pltpu.VMEM((row_count, 8, length), F32),
            pltpu.SemaphoreType.DMA((80,)),
            pltpu.SemaphoreType.DMA((80,)),
        ],
        compiler_params=pltpu.CompilerParams(
            vmem_limit_bytes=VMEM_BYTES, collective_id=3, has_side_effects=True
        ),
        cost_estimate=pl.CostEstimate(flops=40_000_000_000, bytes_accessed=30_000_000, transcendentals=0),
        name="attend_backward",
    )(
        grad_low, grad_resid, hidden_in, resid_mid, wo_rows, wq_rows, normed_one, mixed_all, query_rot, key_rot,
        value_low, logs, seg_all, small_all, small_part, tables, y_part, res_all,
        cot_all, resid_low,
    )

    gate_shape, down_shape = (jax.ShapeDtypeStruct(w.shape, F32) for w in (w_gate, w_down))
    one_gate = pl.BlockSpec((1,) + w_gate.shape[1:], lambda e: (e, 0, 0))
    one_down = pl.BlockSpec((1,) + w_down.shape[1:], lambda e: (e, 0, 0))
    token_pair = (2, row_count, length, width)
    res_all, cot_all, grad_gate, grad_up, grad_down, grads_own, small = pl.pallas_call(
        functools.partial(weight_grads_kernel, counts),
        out_shape=(
            every, every, gate_shape, gate_shape, down_shape,
            jax.ShapeDtypeStruct((width, qkv_width + width), F32),
            jax.ShapeDtypeStruct((SMALL_ROWS, width), F32),
        ),
        input_output_aliases={0: 0, 1: 1},
        in_specs=[hbm] * 6 + [vmem] * 3 + [hbm] * 3,
        out_specs=[hbm] * 5 + [vmem] * 2,
        scratch_shapes=[
            pltpu.VMEM(w_gate.shape, LOW),
            pltpu.VMEM(w_up.shape, LOW),
            pltpu.VMEM(w_down.shape, LOW),
            pltpu.VMEM((dp_count * col_count, SMALL_ROWS, width), F32),
            pltpu.VMEM(w_gate.shape, F32),
            pltpu.VMEM(w_up.shape, F32),
            pltpu.VMEM(w_down.shape, F32),
            pltpu.VMEM(token_pair, LOW),
            pltpu.VMEM(token_pair, LOW),
            pltpu.VMEM((2, capacity, D), LOW),
            pltpu.VMEM((2, capacity, D), LOW),
            pltpu.VMEM((2, 3, capacity, hidden_width), LOW),
            pltpu.VMEM((col_count, width, qkv_width + width), LOW),
            pltpu.VMEM((4, width, qkv_width + width), LOW),
            pltpu.SemaphoreType.DMA((4,)),
            pltpu.SemaphoreType.DMA((3, 2)),
            pltpu.SemaphoreType.DMA((3, exp_local)),
            pltpu.SemaphoreType.DMA((64,)),
            pltpu.SemaphoreType.DMA((64,)),
        ],
        compiler_params=pltpu.CompilerParams(
            vmem_limit_bytes=VMEM_BYTES, collective_id=4, has_side_effects=True
        ),
        name="weight_grads",
    )(res_all, cot_all, grads_part, *kept_slots, small_part, table, small_all, w_gate, w_up, w_down)
    def strips(rows, columns):
        return pl.BlockSpec((rows // exp_local, columns), lambda e: (e, 0))

    tokens, attn = strips(length, width), strips(width, qkv_width + width)
    whole = [pl.BlockSpec((width, EXPERTS), lambda e: (0, 0))] + [pl.BlockSpec((1, width), lambda e: (0, 0))] * 2
    gain_row = jax.ShapeDtypeStruct((1, width), F32)
    grad_gate, grad_up, grad_down, layer_out, grad_in, grad_qkv, grad_out, grad_router, *grad_gains = pl.pallas_call(
        functools.partial(last_grads_kernel, counts),
        grid=(exp_local,),
        out_shape=(
            gate_shape, gate_shape, down_shape, block_low, block_float,
            jax.ShapeDtypeStruct(w_qkv.shape, F32),
            jax.ShapeDtypeStruct((head_width, width), F32),
            jax.ShapeDtypeStruct((width, EXPERTS), F32),
            gain_row,
            gain_row,
        ),
        in_specs=[hbm, hbm, vmem, vmem] + [one_gate, one_gate, one_down] * 2 + [tokens, tokens, attn, vmem],
        out_specs=[
            one_gate, one_gate, one_down, tokens, tokens,
            pl.BlockSpec((width // exp_local,) + w_qkv.shape[1:], lambda e: (e, 0, 0)), strips(head_width, width),
        ]
        + whole,
        scratch_shapes=[
            pltpu.VMEM((row_count, length, width), LOW),
            pltpu.VMEM((row_count, length, width), LOW),
            pltpu.SemaphoreType.DMA((2,)),
        ],
        compiler_params=params,
        name="last_grads",
    )(
        res_all, cot_all, table, small_all, w_gate, w_up, w_down, grad_gate, grad_up, grad_down,
        layer_out, grad_in, grads_own, small,
    )
    return (
        layer_out,
        grad_in,
        grad_gains[0].reshape(width),
        grad_qkv,
        grad_out.reshape(w_out.shape),
        grad_gains[1].reshape(width),
        grad_router,
        grad_gate,
        grad_up,
        grad_down,
    )


def solution(mesh):
    token = P(("dp", "col"), "row")
    routed = P(("dp", "col"), None)
    expert = P(("dp", "row"), None, None)
    wide, tall = P("row", "col", None), P("col", None, "row")
    row = P("row")
    square = P("row", None)

    def step(*arrays):
        length = arrays[10].shape[1]
        tokens_here = arrays[0].shape[0] // (mesh.shape["dp"] * mesh.shape["col"])
        whole_sequence = tokens_here == length and mesh.shape["row"] == mesh.shape["col"]
        return jax.shard_map(
            fast_device if whole_sequence else on_device,
            mesh=mesh,
            in_specs=(
                token, row, wide, tall, row, square, expert, expert, expert, token,
                P(("dp", "row"), None), routed, routed,
            ),
            out_specs=(token, token, row, wide, tall, row, square, expert, expert, expert),
            check_vma=False,
        )(*arrays)

    return step
```

```python
import functools

import jax
import jax.numpy as jnp
import numpy as np
from jax import lax
from jax.experimental import pallas as pl
from jax.experimental.pallas import tpu as pltpu
from jax.sharding import PartitionSpec as P

D = 1024
HQ = 16
HK = 8
HD = 64
EXPERTS = 32
TOP = 8


EPSILON = 1e-06
ROPE_BASE = 10000.0
NEG_LARGE = -1e30
HIGHEST = lax.Precision.HIGHEST


def rotate(values, cosine, sine_table):
    half_size = values.shape[-1] // 2
    lower_half = values[..., :half_size]
    upper_half = values[..., half_size:]
    return jnp.concatenate(
        [
            lower_half * cosine - upper_half * sine_table,
            upper_half * cosine + lower_half * sine_table,
        ],
        axis=-1,
    )


def rotate_back(values, cosine, sine_table):
    half_size = values.shape[-1] // 2
    lower_half = values[..., :half_size]
    upper_half = values[..., half_size:]
    return jnp.concatenate(
        [
            lower_half * cosine + upper_half * sine_table,
            upper_half * cosine - lower_half * sine_table,
        ],
        axis=-1,
    )


def rope_tables(length, head_size):
    positions = jnp.arange(length, dtype=jnp.float32)
    frequency = ROPE_BASE ** (-2.0 * jnp.arange(head_size // 2, dtype=jnp.float32) / head_size)
    angles = positions[:, None] * frequency[None, :]
    return (jnp.cos(angles), jnp.sin(angles))


def visible(segment_row):
    positions = jnp.arange(segment_row.shape[-1], dtype=jnp.int32)
    causal = positions[:, None] >= positions[None, :]
    return causal & (segment_row[..., :, None] == segment_row[..., None, :])


def pair_ranks(expert_ids, pair_order, block_rows):
    experts_flat = expert_ids.reshape(-1, block_rows * TOP)
    order_flat = pair_order.reshape(-1, block_rows * TOP)

    def one_block(experts_row, order_row):
        pair_count = experts_row.shape[0]
        by_order = (
            jnp.zeros((pair_count,), jnp.int32)
            .at[order_row]
            .set(jnp.arange(pair_count, dtype=jnp.int32))
        )
        sorted_experts = experts_row[by_order]
        onehot = (sorted_experts[:, None] == jnp.arange(EXPERTS, dtype=jnp.int32)[None, :]).astype(
            jnp.int32
        )
        before = jnp.cumsum(onehot, axis=0) - onehot
        sorted_rank = jnp.sum(before * onehot, axis=1)
        return sorted_rank[order_row]

    return jax.vmap(one_block)(experts_flat, order_flat).reshape(expert_ids.shape)


def feature_total(values):
    return lax.psum(values, "row")


def tokens_by_col(values):
    return lax.all_gather(values, "col", axis=0, tiled=True)


def tokens_by_row(values):
    return lax.all_gather(values, "row", axis=0, tiled=True)


def col_scatter(term_fn, keep_rows):
    return lax.psum_scatter(
        term_fn(jnp.int32(0), keep_rows * lax.axis_size("col")),
        "col",
        scatter_dimension=0,
        tiled=True,
    )


def to_experts(outgoing):
    arrived = lax.all_to_all(outgoing, ("dp", "row"), split_axis=0, concat_axis=0, tiled=True)
    return arrived


def from_experts(outgoing):
    arrived = lax.all_to_all(outgoing, ("dp", "row"), split_axis=0, concat_axis=0, tiled=True)
    return arrived


def owner_layout(incoming, dp_count, row_count, exp_local):
    capacity = incoming.shape[1] // exp_local
    part_width = incoming.shape[2]
    sectioned = incoming.reshape(dp_count, row_count, exp_local, capacity, part_width)
    return sectioned.transpose(2, 0, 3, 1, 4).reshape(
        exp_local, dp_count * capacity, row_count * part_width
    )


def source_layout(owner_rows, dp_count, row_count):
    exp_local, slot_rows, full_width = owner_rows.shape
    capacity = slot_rows // dp_count
    part_width = full_width // row_count
    sectioned = owner_rows.reshape(exp_local, dp_count, capacity, row_count, part_width)
    return sectioned.transpose(1, 3, 0, 2, 4).reshape(
        dp_count * row_count, exp_local * capacity, part_width
    )


def attend_forward(pack):
    query_seq, key_seq, value_seq, segment_seq = pack
    score_scale = query_seq.shape[-1] ** (-0.5)
    scores = (
        jnp.einsum("qhgd,khd->hgqk", query_seq, key_seq, preferred_element_type=jnp.float32)
        * score_scale
    )
    scores = jnp.where(visible(segment_seq), scores, NEG_LARGE)
    row_max = jnp.max(scores, axis=-1, keepdims=True)
    weights = jnp.exp(scores - row_max)
    row_total = jnp.sum(weights, axis=-1, keepdims=True)
    weights_low = (weights / row_total).astype(jnp.bfloat16)
    mixed_seq = jnp.einsum(
        "hgqk,khd->qhgd", weights_low, value_seq, preferred_element_type=jnp.float32
    )
    return (mixed_seq.astype(jnp.bfloat16), row_max + jnp.log(row_total))


def attend_backward(pack):
    query_seq, key_seq, value_seq, segment_seq, log_total, grad_seq = pack
    score_scale = query_seq.shape[-1] ** (-0.5)
    scores = (
        jnp.einsum("qhgd,khd->hgqk", query_seq, key_seq, preferred_element_type=jnp.float32)
        * score_scale
    )
    scores = jnp.where(visible(segment_seq), scores, NEG_LARGE)
    weights = jnp.exp(scores - log_total)
    grad_weights = jnp.einsum(
        "qhgd,khd->hgqk", grad_seq, value_seq, preferred_element_type=jnp.float32
    )
    inner_sum = jnp.sum(weights * grad_weights, axis=-1, keepdims=True)
    grad_scores = (weights * (grad_weights - inner_sum)).astype(jnp.bfloat16)
    grad_values = jnp.einsum(
        "hgqk,qhgd->khd", weights.astype(jnp.bfloat16), grad_seq, preferred_element_type=jnp.float32
    )
    grad_query = (
        jnp.einsum("hgqk,khd->qhgd", grad_scores, key_seq, preferred_element_type=jnp.float32)
        * score_scale
    )
    grad_key = (
        jnp.einsum("hgqk,qhgd->khd", grad_scores, query_seq, preferred_element_type=jnp.float32)
        * score_scale
    )
    return (grad_query, grad_key, grad_values)


def on_device(
    hidden_in,
    norm_gain,
    w_qkv,
    w_out,
    ffn_gain,
    router,
    w_gate,
    w_up,
    w_down,
    cotangent,
    segment_ids,
    expert_ids,
    pair_order,
):
    dp_count = lax.axis_size("dp")
    row_count = lax.axis_size("row")
    owners = dp_count * row_count
    tok_rows, part_width = hidden_in.shape
    seq_count, length = segment_ids.shape
    att_rows = seq_count * length
    kv_local = w_qkv.shape[1]
    group_size = HQ // HK
    exp_local = w_gate.shape[0]
    capacity = tok_rows * TOP // EXPERTS
    total_slots = EXPERTS * capacity
    resid_in = hidden_in.astype(jnp.float32)
    gain_one = norm_gain.astype(jnp.float32)
    rstd_one = lax.rsqrt(feature_total(jnp.sum(resid_in * resid_in, axis=1)) / D + EPSILON)
    normed_one = (resid_in * rstd_one[:, None] * gain_one).astype(jnp.bfloat16)
    group_rows = tokens_by_col(normed_one)
    qkv_flat = w_qkv.reshape(part_width, -1)
    picked = group_rows
    qkv_local = lax.psum_scatter(
        jnp.dot(picked, qkv_flat, preferred_element_type=jnp.float32),
        "row",
        scatter_dimension=0,
        tiled=True,
    )
    qkv_local = qkv_local.reshape(seq_count, length, kv_local, -1)
    cosine, sine_table = rope_tables(length, HD)
    queries = qkv_local[..., : group_size * HD].reshape(seq_count, length, kv_local, group_size, HD)
    query_rot = rotate(
        queries, cosine[None, :, None, None, :], sine_table[None, :, None, None, :]
    ).astype(jnp.bfloat16)
    key_rot = rotate(
        qkv_local[..., group_size * HD : (group_size + 1) * HD],
        cosine[None, :, None, :],
        sine_table[None, :, None, :],
    ).astype(jnp.bfloat16)
    value_low = qkv_local[..., (group_size + 1) * HD :].astype(jnp.bfloat16)
    mixed_heads, log_total = lax.map(attend_forward, (query_rot, key_rot, value_low, segment_ids))
    mixed_rows = tokens_by_row(mixed_heads.reshape(att_rows, -1))
    out_flat = w_out.reshape(-1, part_width)

    def out_term(first_row, block_rows):
        return jnp.dot(mixed_rows, out_flat, preferred_element_type=jnp.float32)

    resid_mid = resid_in + col_scatter(out_term, tok_rows)
    gain_two = ffn_gain.astype(jnp.float32)
    router_float = router.astype(jnp.float32)
    square_two, logit_part = (
        lax.psum(jnp.sum(resid_mid * resid_mid, axis=1).astype(jnp.bfloat16), "row").astype(
            jnp.float32
        ),
        lax.psum(
            jnp.dot(resid_mid * gain_two, router_float, precision=HIGHEST).astype(jnp.bfloat16),
            "row",
        ).astype(jnp.float32),
    )
    rstd_two = lax.rsqrt(square_two / D + EPSILON)
    logits = logit_part * rstd_two[:, None]
    normed_float = resid_mid * rstd_two[:, None] * gain_two
    normed_two = normed_float.astype(jnp.bfloat16)
    choose = (expert_ids[:, :, None] == jnp.arange(EXPERTS, dtype=jnp.int32)[None, None, :]).astype(
        jnp.float32
    )
    gate_weights = jax.nn.softmax(jnp.sum(choose * logits[:, None, :], axis=2), axis=1)
    pair_rank = pair_ranks(expert_ids, pair_order, tok_rows)
    pair_slot = jnp.where(pair_rank < capacity, expert_ids * capacity + pair_rank, total_slots)
    pair_index = jnp.arange(tok_rows * TOP, dtype=jnp.int32)
    slot_pair = (
        jnp.full((total_slots + 1,), tok_rows * TOP, jnp.int32)
        .at[pair_slot.reshape(-1)]
        .set(pair_index)[:total_slots]
    )
    padded_two = jnp.concatenate([normed_two, jnp.zeros((1, part_width), jnp.bfloat16)], axis=0)
    outgoing = padded_two[slot_pair // TOP].reshape(owners, exp_local * capacity, part_width)
    expert_rows = owner_layout(to_experts(outgoing), dp_count, row_count, exp_local)
    gate_pre = jnp.einsum("erd,edf->erf", expert_rows, w_gate, preferred_element_type=jnp.float32)
    up_pre = jnp.einsum("erd,edf->erf", expert_rows, w_up, preferred_element_type=jnp.float32)
    hidden = (jax.nn.silu(gate_pre) * up_pre).astype(jnp.bfloat16)
    expert_out = jnp.einsum(
        "erf,efd->erd", hidden, w_down, preferred_element_type=jnp.float32
    ).astype(jnp.bfloat16)
    returned = from_experts(source_layout(expert_out, dp_count, row_count))
    slot_table = jnp.concatenate(
        [returned.reshape(total_slots, part_width), jnp.zeros((1, part_width), jnp.bfloat16)],
        axis=0,
    )
    pair_rows = slot_table[pair_slot].astype(jnp.float32)
    layer_sum = resid_mid + jnp.einsum("tk,tkd->td", gate_weights, pair_rows, precision=HIGHEST)
    grad_top = cotangent.astype(jnp.float32)
    grad_gates = lax.psum(jnp.einsum("td,tkd->tk", grad_top, pair_rows, precision=HIGHEST), "row")
    pair_grad = (gate_weights[:, :, None] * grad_top[:, None, :]).astype(jnp.bfloat16)
    grad_padded = jnp.concatenate(
        [pair_grad.reshape(tok_rows * TOP, part_width), jnp.zeros((1, part_width), jnp.bfloat16)],
        axis=0,
    )
    outgoing_grad = grad_padded[slot_pair].reshape(owners, exp_local * capacity, part_width)
    grad_rows = owner_layout(to_experts(outgoing_grad), dp_count, row_count, exp_local)
    grad_hidden = jnp.einsum("erd,efd->erf", grad_rows, w_down, preferred_element_type=jnp.float32)
    sigmoid_gate = jax.nn.sigmoid(gate_pre)
    grad_gate_pre = (
        grad_hidden * up_pre * sigmoid_gate * (1.0 + gate_pre * (1.0 - sigmoid_gate))
    ).astype(jnp.bfloat16)
    grad_up_pre = (grad_hidden * gate_pre * sigmoid_gate).astype(jnp.bfloat16)
    grad_down_local = jnp.einsum(
        "erf,erd->efd", hidden, grad_rows, preferred_element_type=jnp.float32
    )
    grad_gate_local = jnp.einsum(
        "erd,erf->edf", expert_rows, grad_gate_pre, preferred_element_type=jnp.float32
    )
    grad_up_local = jnp.einsum(
        "erd,erf->edf", expert_rows, grad_up_pre, preferred_element_type=jnp.float32
    )
    rows_back = jnp.einsum(
        "erf,edf->erd", grad_gate_pre, w_gate, preferred_element_type=jnp.float32
    )
    rows_back = (
        rows_back
        + jnp.einsum("erf,edf->erd", grad_up_pre, w_up, preferred_element_type=jnp.float32)
    ).astype(jnp.bfloat16)
    returned_grad = from_experts(source_layout(rows_back, dp_count, row_count))
    grad_table = jnp.concatenate(
        [returned_grad.reshape(total_slots, part_width), jnp.zeros((1, part_width), jnp.bfloat16)],
        axis=0,
    )
    inner_gate = jnp.sum(gate_weights * grad_gates, axis=1, keepdims=True)
    grad_chosen = gate_weights * (grad_gates - inner_gate)
    grad_logits = jnp.einsum("tk,tke->te", grad_chosen, choose, precision=HIGHEST)
    grad_router_part = jnp.einsum("td,te->de", normed_float, grad_logits, precision=HIGHEST)
    grad_normed = jnp.sum(grad_table[pair_slot].astype(jnp.float32), axis=1)
    grad_normed = grad_normed + jnp.einsum(
        "te,de->td", grad_logits, router_float, precision=HIGHEST
    )
    grad_gain_two_part = jnp.sum(grad_normed * resid_mid * rstd_two[:, None], axis=0)
    scaled_two = grad_normed * gain_two
    inner_two = feature_total(jnp.sum(scaled_two * resid_mid, axis=1))
    grad_resid = (
        grad_top
        + rstd_two[:, None] * scaled_two
        - resid_mid * (rstd_two * rstd_two * rstd_two * inner_two / D)[:, None]
    )
    branch_rows = tokens_by_col(grad_resid.astype(jnp.bfloat16))
    grad_out_local = jnp.einsum(
        "tc,td->cd", mixed_rows, branch_rows, preferred_element_type=jnp.float32
    ).reshape(w_out.shape)
    picked = branch_rows
    grad_mixed = lax.psum_scatter(
        jnp.einsum("td,cd->tc", picked, out_flat, preferred_element_type=jnp.float32).astype(
            jnp.bfloat16
        ),
        "row",
        scatter_dimension=0,
        tiled=True,
    ).astype(jnp.float32)
    grad_mixed = grad_mixed.astype(jnp.bfloat16).reshape(
        seq_count, length, kv_local, group_size, HD
    )
    grad_query, grad_key, grad_values = lax.map(
        attend_backward, (query_rot, key_rot, value_low, segment_ids, log_total, grad_mixed)
    )
    grad_query = rotate_back(
        grad_query, cosine[None, :, None, None, :], sine_table[None, :, None, None, :]
    )
    grad_key = rotate_back(grad_key, cosine[None, :, None, :], sine_table[None, :, None, :])
    grad_qkv_pre = jnp.concatenate(
        [grad_query.reshape(seq_count, length, kv_local, group_size * HD), grad_key, grad_values],
        axis=-1,
    )
    grad_qkv_pre = grad_qkv_pre.astype(jnp.bfloat16).reshape(att_rows, -1)
    qkv_rows = tokens_by_row(grad_qkv_pre)
    grad_qkv_local = jnp.einsum(
        "td,tc->dc", group_rows, qkv_rows, preferred_element_type=jnp.float32
    ).reshape(w_qkv.shape)

    def normed_term(first_row, block_rows):
        return jnp.einsum("tc,dc->td", qkv_rows, qkv_flat, preferred_element_type=jnp.float32)

    grad_normed_one = col_scatter(normed_term, tok_rows)
    grad_gain_one_part = jnp.sum(grad_normed_one * resid_in * rstd_one[:, None], axis=0)
    scaled_one = grad_normed_one * gain_one
    inner_one = feature_total(jnp.sum(scaled_one * resid_in, axis=1))
    grad_in = (
        grad_resid
        + rstd_one[:, None] * scaled_one
        - resid_in * (rstd_one * rstd_one * rstd_one * inner_one / D)[:, None]
    )
    col_sums = (
        lax.psum(grad_gate_local.astype(jnp.bfloat16), "col").astype(jnp.float32),
        lax.psum(grad_up_local.astype(jnp.bfloat16), "col").astype(jnp.float32),
        lax.psum(grad_down_local.astype(jnp.bfloat16), "col").astype(jnp.float32),
        lax.psum(grad_router_part.astype(jnp.bfloat16), "col").astype(jnp.float32),
        lax.psum(grad_gain_one_part.astype(jnp.bfloat16), "col").astype(jnp.float32),
        lax.psum(grad_gain_two_part.astype(jnp.bfloat16), "col").astype(jnp.float32),
    )
    dp_sums = (
        lax.psum(grad_qkv_local.astype(jnp.bfloat16), "dp").astype(jnp.float32),
        lax.psum(grad_out_local.astype(jnp.bfloat16), "dp").astype(jnp.float32),
        lax.psum(col_sums[3].astype(jnp.bfloat16), "dp").astype(jnp.float32),
        lax.psum(col_sums[4].astype(jnp.bfloat16), "dp").astype(jnp.float32),
        lax.psum(col_sums[5].astype(jnp.bfloat16), "dp").astype(jnp.float32),
    )
    return (
        layer_sum.astype(jnp.bfloat16),
        grad_in,
        dp_sums[3],
        dp_sums[0],
        dp_sums[1],
        dp_sums[4],
        dp_sums[2],
        col_sums[0],
        col_sums[1],
        col_sums[2],
    )

WINDOW = 512
BLOCK_Q = 256
LANES = 128
SMALL_ROWS = 48
GAIN_ONE = EXPERTS
GAIN_TWO = EXPERTS + 1
RSTD_LANE = LANES - 1
RSTD_ROW = 8
FIRST, SECOND, LATE = 1, 3, 2
F32 = jnp.float32
LOW = jnp.bfloat16
VMEM_BYTES = 67_000_000


def dot_nn(a, b):
    return jnp.dot(a, b, preferred_element_type=F32)


def dot_nt(a, b):
    return lax.dot_general(a, b, (((1,), (1,)), ((), ())), preferred_element_type=F32)


def dot_tn(a, b):
    return lax.dot_general(a, b, (((0,), (0,)), ((), ())), preferred_element_type=F32)


def rope_lanes(length):
    positions = np.arange(length, dtype=np.float32)
    frequency = (ROPE_BASE ** (-2.0 * np.arange(HD // 2, dtype=np.float32) / HD)).astype(np.float32)
    angles = (positions[:, None] * frequency[None, :]).astype(np.float32)
    cosine, sine = np.cos(angles), np.sin(angles)
    signed = np.concatenate([-sine, sine], axis=1)
    double = np.concatenate([cosine, cosine], axis=1)
    ones, zeros = np.ones_like(double), np.zeros_like(double)
    return np.stack(
        [
            np.concatenate([double, double], axis=1),
            np.concatenate([signed, signed], axis=1),
            np.concatenate([double, ones], axis=1),
            np.concatenate([signed, zeros], axis=1),
        ]
    ).astype(np.float32)


def swap_halves(values):
    half = HD // 2
    lane = lax.broadcasted_iota(jnp.int32, values.shape, 1)
    ahead = pltpu.roll(values, LANES - half, 1)
    behind = pltpu.roll(values, half, 1)
    return jnp.where(lane % HD < half, ahead, behind)


def window_mask(seg_col, seg_row, q_start, k_start):
    shape = (seg_col.shape[0], seg_row.shape[1])
    q_at = lax.broadcasted_iota(jnp.int32, shape, 0) + q_start
    k_at = lax.broadcasted_iota(jnp.int32, shape, 1) + k_start
    return (q_at >= k_at) & (seg_col == seg_row)


def remote(src, dst, send_sem, recv_sem, where):
    return pltpu.make_async_remote_copy(
        src_ref=src, dst_ref=dst, send_sem=send_sem, recv_sem=recv_sem,
        device_id=where, device_id_type=pl.DeviceIdType.MESH,
    )


class Copies:
    def __init__(self, send_sems, recv_sems):
        self.send_sems, self.recv_sems = send_sems, recv_sems
        self.sends = self.recvs = 0
        self.open = []

    def receivers(self, number=1):
        first = self.recvs
        self.recvs += number
        return first

    def send(self, src, dst, receiver, where, when=None):
        at = self.sends
        self.sends += 1
        copy = remote(src, dst, self.send_sems.at[at], self.recv_sems.at[receiver], where)
        if when is None:
            copy.start()
        else:
            pl.when(when)(copy.start)
        self.open.append((copy, when))

    def plan(self, src, dst, receiver, where):
        at = self.sends
        self.sends += 1
        copy = remote(src, dst, self.send_sems.at[at], self.recv_sems.at[receiver], where)
        self.open.append((copy, None))
        return copy

    def local(self, src, dst, when=None):
        at = self.sends
        self.sends += 1
        copy = pltpu.make_async_copy(src, dst, self.send_sems.at[at])
        if when is None:
            copy.start()
        else:
            pl.when(when)(copy.start)
        return copy

    def arrived(self, dst, receiver, where):
        remote(dst, dst, self.recv_sems.at[receiver], self.recv_sems.at[receiver], where).wait_recv()

    def finish(self):
        for copy, when in self.open:
            if when is None:
                copy.wait_send()
            else:
                pl.when(when)(copy.wait_send)


class Place:
    def __init__(self, counts):
        self.dp_count, self.row_count, self.col_count = counts
        self.dp, self.row, self.col = (lax.axis_index(name) for name in ("dp", "row", "col"))
        self.pair_row = self.row + 1 - 2 * lax.rem(self.row, 2)
        self.far_row = lax.rem(self.row + 2, self.row_count)
        self.cross_row = lax.rem(self.pair_row + 2, self.row_count)
        self.other_dp = self.dp_count - 1 - self.dp
        self.here = (self.dp, self.row, self.col)
        self.pair = (self.dp, self.pair_row, self.col)
        self.far = (self.dp, self.far_row, self.col)
        self.over = (self.other_dp, self.row, self.col)
        self.over_far = (self.other_dp, self.far_row, self.col)

    def row_at(self, step):
        return lax.rem(self.row + step + self.row_count, self.row_count)

    def col_at(self, step):
        return lax.rem(self.col + step + self.col_count, self.col_count)

    def block(self, dp_at, col_at):
        return dp_at * self.col_count + col_at

    def plane(self):
        peers = [(self.dp, self.row_at(k), self.col) for k in range(1, self.row_count)]
        return peers + [(self.other_dp, self.row_at(k), self.col) for k in range(self.row_count)]

    def column(self):
        return [(self.dp, self.row, self.col_at(k)) for k in range(1, self.col_count)]


class Spread:
    def __init__(self, place, copies, blocks, col_at):
        self.place, self.copies = place, copies
        dp, row, far_row = place.dp, place.row, place.far_row
        same, other = place.block(dp, col_at), place.block(place.other_dp, col_at)
        self.own, self.far = blocks.at[same, row], blocks.at[same, far_row]
        self.over, self.corner = blocks.at[other, row], blocks.at[other, far_row]
        self.pairs_same = (blocks.at[same, place.pair_row], blocks.at[same, place.cross_row])
        self.pairs_other = (blocks.at[other, place.pair_row], blocks.at[other, place.cross_row])
        self.at = copies.receivers(7)
        self.to_pair = copies.plan(self.own, self.own, self.at, place.pair)
        self.to_far = copies.plan(self.own, self.own, self.at + 1, place.far)
        self.to_over = copies.plan(self.own, self.own, self.at + 2, place.over)
        self.far_pair = copies.plan(self.far, self.far, self.at + 4, place.pair)
        self.over_pair = copies.plan(self.over, self.over, self.at + 5, place.pair)
        self.corner_pair = copies.plan(self.corner, self.corner, self.at + 6, place.pair)
        self.turn = None

    def begin(self, with_over):
        self.to_far.start()
        if with_over:
            self.to_over.start()
        self.to_pair.start()

    def send_over(self):
        self.to_over.start()

    def plan_corner(self, by_over):
        if by_over:
            self.turn = self.copies.plan(self.far, self.far, self.at + 3, self.place.over)
        else:
            self.turn = self.copies.plan(self.over, self.over, self.at + 3, self.place.far)

    def pass_far(self, corner):
        self.copies.arrived(self.far, self.at + 1, self.place.far)
        if corner:
            if self.turn is None:
                self.plan_corner(True)
            self.turn.start()
        self.far_pair.start()

    def pass_over(self, corner):
        self.copies.arrived(self.over, self.at + 2, self.place.over)
        if corner:
            if self.turn is None:
                self.plan_corner(False)
            self.turn.start()
        self.over_pair.start()

    def pass_corner(self):
        self.copies.arrived(self.corner, self.at + 3, self.place.here)
        self.corner_pair.start()

    def complete_same(self):
        for k, piece in zip((0, 4), self.pairs_same):
            self.copies.arrived(piece, self.at + k, self.place.pair)

    def complete_other(self):
        for k, piece in zip((5, 6), self.pairs_other):
            self.copies.arrived(piece, self.at + k, self.place.pair)

    def complete(self):
        self.complete_same()
        self.complete_other()


def say_hello(peers):
    barrier = pltpu.get_barrier_semaphore()
    for peer in peers:
        pl.semaphore_signal(barrier, inc=1, device_id=peer, device_id_type=pl.DeviceIdType.MESH)
    return functools.partial(pl.semaphore_wait, barrier, len(peers))


def greet(peers):
    say_hello(peers)()


def attend_forward_kernel(
    counts, hidden_hbm, own_q_hbm, own_o_hbm, small_hbm, seg_hbm, cot_hbm, tab_ref,
    resid_ref, low_ref, mix_ref, normed_ref, q_ref, k_ref, v_ref, lse_ref, wq_ref, zo_ref, small_ref, seg_ref, cot_all,
    h_ref, zq_ref, own_ref, column_ref, send_sems, recv_sems,
):
    place = Place(counts)
    row_count, col_count = place.row_count, place.col_count
    copies = Copies(send_sems, recv_sems)
    parts, length, width = h_ref.shape
    kv_heads = k_ref.shape[0]
    features = parts * width
    chunks = length // BLOCK_Q
    greet(place.plane() + place.column())

    h_pair, h_far, h_cross = (copies.receivers() for _ in range(3))
    copies.send(hidden_hbm, h_ref.at[place.row], h_far, place.far)
    copies.send(hidden_hbm, h_ref.at[place.row], h_pair, place.pair)
    h_own = copies.local(hidden_hbm, h_ref.at[place.row])
    zq_own = copies.local(own_q_hbm, zq_ref.at[place.col])
    zo_own = copies.local(own_o_hbm, zo_ref.at[place.col])
    small_own = copies.local(small_hbm, small_ref.at[place.row])
    seg_own = copies.local(seg_hbm, seg_ref.at[place.row])
    half_width = width // 2
    half, other_half = (
        pl.ds(pl.multiple_of(dp_at * half_width, half_width), half_width) for dp_at in (place.dp, place.other_dp)
    )
    mine = place.row == place.col
    zq_in = copies.receivers(col_count)
    zo_in = copies.receivers(col_count)
    for k in range(1, col_count):
        copies.send(
            own_q_hbm.at[half], zq_ref.at[place.col, half], zq_in + k, (place.dp, place.row, place.col_at(k))
        )
    small_in, seg_in = copies.receivers(row_count), copies.receivers(row_count)
    for k in range(1, row_count):
        copies.send(small_hbm, small_ref.at[place.row], small_in + k, (place.dp, place.row_at(k), place.col))
        copies.send(seg_hbm, seg_ref.at[place.row], seg_in + k, (place.dp, place.row_at(k), place.col))
    cot_own = copies.local(cot_hbm, own_ref)
    cot_pair, cot_over, cot_back = copies.receivers(), copies.receivers(), copies.receivers(3)
    cot_far, cot_corner = copies.receivers(2), copies.receivers(2)
    own_cot = cot_all.at[place.block(place.dp, place.col), place.row]
    far_cot = cot_all.at[place.block(place.dp, place.col), place.far_row]
    half_rows = length // 2

    def send_cot_far(half):
        window = pl.ds(half * half_rows, half_rows)
        copies.send(cot_hbm.at[window], own_cot.at[window], cot_far + half, place.far)

    def pass_cot_far(half):
        piece = far_cot.at[pl.ds(half * half_rows, half_rows)]
        copies.arrived(piece, cot_far + half, place.far)
        copies.send(piece, piece, cot_corner + half, place.over)

    copies.send(cot_hbm, own_cot, cot_over, place.over)
    copies.send(cot_hbm, own_cot, cot_pair, place.pair)

    copies.arrived(h_ref.at[place.far_row], h_far, place.far)
    copies.send(h_ref.at[place.far_row], h_ref.at[place.far_row], h_cross, place.pair)
    wq_in, wq_over = copies.receivers(row_count), copies.receivers(row_count)
    zq_own.wait()
    copies.send(
        zq_ref.at[place.col], wq_ref.at[place.row], wq_in + lax.rem(place.col - place.row + row_count, row_count),
        (place.dp, place.col, place.col), jnp.logical_not(mine),
    )
    wq_kept = [(copies.local(zq_ref.at[place.col], wq_ref.at[place.row], mine), mine)]
    for k in range(1, col_count):
        source = place.col_at(-k)
        piece, target = zq_ref.at[source, half], wq_ref.at[place.row, half]
        copies.arrived(piece, zq_in + k, place.here)
        step = lax.rem(source - place.row + row_count, row_count)
        copies.send(piece, target, wq_in + step, (place.dp, source, place.col), source != place.row)
        copies.send(piece, target, wq_over + step, (place.other_dp, source, place.col))
        wq_kept.append((copies.local(piece, target, source == place.row), source == place.row))

    for k in range(1, col_count):
        copies.send(own_o_hbm, zo_ref.at[place.col], zo_in + k, (place.dp, place.row, place.col_at(k)))
    send_cot_far(0)
    send_cot_far(1)
    cot_z = copies.receivers(col_count)
    for k in (FIRST,):
        copies.send(cot_hbm, own_cot, cot_z + k, (place.dp, place.row, place.col_at(k)))
    h_own.wait()
    copies.arrived(h_ref.at[place.pair_row], h_pair, place.pair)
    copies.arrived(h_ref.at[place.cross_row], h_cross, place.pair)
    small_own.wait()
    for k in range(1, row_count):
        copies.arrived(small_ref.at[place.row_at(-k)], small_in + k, place.here)

    @pl.loop(0, chunks)
    def _(chunk):
        rows = pl.ds(pl.multiple_of(chunk * BLOCK_Q, BLOCK_Q), BLOCK_Q)
        total = jnp.zeros((BLOCK_Q, 1), F32)
        for part in range(parts):
            piece = h_ref[part, rows, :].astype(F32)
            total = total + jnp.sum(piece * piece, axis=1, keepdims=True)
        rstd = lax.rsqrt(total / features + EPSILON)
        lse_ref[rows, :] = jnp.broadcast_to(rstd, (BLOCK_Q, LANES))
        for part in range(parts):
            piece = h_ref[part, rows, :].astype(F32)
            gain = small_ref[part, GAIN_ONE : GAIN_ONE + 1, :].astype(F32)
            normed_ref[rows, part * width : (part + 1) * width] = (piece * rstd * gain).astype(LOW)

    seg_own.wait()
    for k in range(1, row_count):
        copies.arrived(seg_ref.at[place.row_at(-k)], seg_in + k, place.here)
    segments = seg_ref[place.col]
    for start in range(0, length, LANES):
        column_ref[start : start + LANES, :] = jnp.broadcast_to(
            segments[0:1, start : start + LANES], (LANES, LANES)
        ).T

    cot_own.wait()
    cot_kept = copies.local(own_ref, own_cot)

    for copy, here in wq_kept:
        pl.when(here)(copy.wait)

    @pl.when(mine)
    def _():
        for k in range(1, row_count):
            copies.arrived(wq_ref.at[place.row_at(-k)], wq_in + k, place.here)

    @pl.when(jnp.logical_not(mine))
    def _():
        for k in range(row_count):
            if k > 0:
                copies.arrived(wq_ref.at[place.row_at(-k), half], wq_in + k, place.here)
            copies.arrived(wq_ref.at[place.row_at(-k), other_half], wq_over + k, place.here)


    @pl.loop(0, chunks)
    def _(chunk):
        rows = pl.ds(pl.multiple_of(chunk * BLOCK_Q, BLOCK_Q), BLOCK_Q)
        qkv = dot_nn(normed_ref[rows, :], wq_ref[...].reshape(features, -1))
        for head in range(kv_heads):
            base = head * 4 * HD
            queries = qkv[:, base : base + LANES]
            queries = queries * tab_ref[0, rows, :] + swap_halves(queries) * tab_ref[1, rows, :]
            others = qkv[:, base + LANES : base + 2 * LANES]
            others = others * tab_ref[2, rows, :] + swap_halves(others) * tab_ref[3, rows, :]
            q_ref[2 * head, rows, :] = queries[:, :HD].astype(LOW)
            q_ref[2 * head + 1, rows, :] = queries[:, HD:].astype(LOW)
            k_ref[head, rows, :] = others[:, :HD].astype(LOW)
            v_ref[head, rows, :] = others[:, HD:].astype(LOW)

    scale = HD**-0.5
    lane = lax.broadcasted_iota(jnp.int32, (BLOCK_Q, LANES), 1)
    mix_pair, mix_far, mix_cross = (copies.receivers(chunks) for _ in range(3))

    def pass_on(block):
        piece = mix_ref.at[place.far_row, pl.ds(block * BLOCK_Q, BLOCK_Q)]
        copies.arrived(piece, mix_far + block, place.far)
        copies.send(piece, piece, mix_cross + block, place.pair)

    for block in range(chunks):
        q_start = block * BLOCK_Q
        k_start = max(0, q_start - WINDOW)
        q_rows, k_rows = slice(q_start, q_start + BLOCK_Q), slice(k_start, q_start + BLOCK_Q)
        mask = window_mask(column_ref[q_rows, 0:1], segments[0:1, k_rows], q_start, k_start)

        @pl.loop(0, kv_heads)
        def _(kv):
            keys, vals = k_ref[kv, k_rows, :], v_ref[kv, k_rows, :]
            logs, outs = lse_ref[q_rows, :], []
            for half in range(2):
                head = 2 * kv + half
                scores = dot_nt(q_ref[head, q_rows, :], keys) * scale
                scores = jnp.where(mask, scores, NEG_LARGE)
                top = jnp.max(scores, axis=1, keepdims=True)
                weights = jnp.exp(scores - top)
                total = jnp.sum(weights, axis=1, keepdims=True)
                outs.append((dot_nn(weights.astype(LOW), vals) / total).astype(LOW))
                logs = jnp.where(lane == head, top + jnp.log(total), logs)
            lse_ref[q_rows, :] = logs
            mix_ref[place.row, q_rows, pl.ds(pl.multiple_of(kv * LANES, LANES), LANES)] = jnp.concatenate(
                outs, axis=1
            )

        piece = mix_ref.at[place.row, pl.ds(q_start, BLOCK_Q)]
        copies.send(piece, piece, mix_far + block, place.far)
        copies.send(piece, piece, mix_pair + block, place.pair)
        if block > 0:
            pass_on(block - 1)
        if block == 1:
            pass_cot_far(0)
        if block == 2:
            pass_cot_far(1)
            copies.send(far_cot, far_cot, cot_back, place.pair)
            over_cot = cot_all.at[place.block(place.other_dp, place.col), place.row]
            copies.arrived(over_cot, cot_over, place.over)
            copies.send(over_cot, over_cot, cot_back + 1, place.pair)
    pass_on(chunks - 1)
    corner_cot = cot_all.at[place.block(place.other_dp, place.col), place.far_row]
    for half in range(2):
        copies.arrived(
            corner_cot.at[pl.ds(half * half_rows, half_rows)], cot_corner + half, place.over
        )
    copies.send(corner_cot, corner_cot, cot_back + 2, place.pair)
    zo_own.wait()
    for k in range(1, col_count):
        copies.arrived(zo_ref.at[place.col_at(-k)], zo_in + k, place.here)
    for block in range(chunks):
        rows = slice(block * BLOCK_Q, (block + 1) * BLOCK_Q)
        window = pl.ds(block * BLOCK_Q, BLOCK_Q)
        copies.arrived(mix_ref.at[place.pair_row, window], mix_pair + block, place.pair)
        copies.arrived(mix_ref.at[place.cross_row, window], mix_cross + block, place.pair)
        branch = dot_nn(mix_ref[0, rows, :], zo_ref[0])
        for part in range(1, parts):
            branch = branch + dot_nn(mix_ref[part, rows, :], zo_ref[part])
        resid = h_ref[place.row, rows, :].astype(F32) + branch
        resid_ref[rows, :] = resid
        low_ref[rows, :] = resid.astype(LOW)

    cot_kept.wait()
    copies.arrived(cot_all.at[place.block(place.dp, place.col), place.pair_row], cot_pair, place.pair)
    for k, (dp_at, row_at) in enumerate(
        ((place.dp, place.cross_row), (place.other_dp, place.pair_row), (place.other_dp, place.cross_row))
    ):
        copies.arrived(cot_all.at[place.block(dp_at, place.col), row_at], cot_back + k, place.pair)
    for k in (FIRST,):
        copies.arrived(
            cot_all.at[place.block(place.dp, place.col_at(-k)), place.row], cot_z + k, place.here
        )
    copies.finish()


def attend_backward_kernel(
    counts, grad_low_hbm, grad_ref, hidden_ref, resid_ref, wo_ref, wq_ref, normed_ref, mix_hbm, q_ref, k_ref, v_ref, lse_ref,
    seg_ref, small_ref, part_ref, tab_ref, y_hbm, res_given, cot_given, low_hbm,
    out_ref, grad_in_ref, grads_ref, sums_ref, res_all, cot_all,
    gb_ref, mixed_ref, gm_ref, dq_ref, dk_ref, dv_ref, turn_ref, column_ref, y_own_ref, y_in_ref, y_chip_ref, y_last_ref,
    away_ref, pair_in_ref, own_ref, chip_ref, last_ref, inner_ref,
    send_sems, recv_sems,
):
    place = Place(counts)
    copies = Copies(send_sems, recv_sems)
    dp_count, row_count, col_count = counts
    parts, length, width = gb_ref.shape
    kv_heads = k_ref.shape[0]
    features = parts * width
    chunks = length // BLOCK_Q
    scale = HD**-0.5
    all_here = say_hello(place.plane() + place.column())
    segments = seg_ref[place.col]
    for start in range(0, length, LANES):
        column_ref[start : start + LANES, :] = jnp.broadcast_to(
            segments[0:1, start : start + LANES], (LANES, LANES)
        ).T
    dk_ref[...] = jnp.zeros_like(dk_ref)
    dv_ref[...] = jnp.zeros_like(dv_ref)
    all_here()

    def window(chunk):
        return pl.ds(chunk * BLOCK_Q, BLOCK_Q)

    blocks = range(chunks - 1, -1, -1)
    gb_far, gb_pair, gb_cross = (copies.receivers(chunks) for _ in range(3))
    for chunk in blocks:
        piece = gb_ref.at[place.row, window(chunk)]
        copies.send(grad_low_hbm.at[window(chunk)], piece, gb_far + chunk, place.far)
        copies.send(grad_low_hbm.at[window(chunk)], piece, gb_pair + chunk, place.pair)
    gb_own = copies.local(grad_low_hbm, gb_ref.at[place.row])
    mix_own = copies.local(mix_hbm.at[place.row], mixed_ref)
    y_pair = copies.receivers(2 * dp_count)
    y_held = []
    for turn, dp_at in enumerate((place.other_dp, place.dp)):
        for q, (here, there) in enumerate(
            ((place.row, place.pair_row), (place.far_row, place.cross_row))
        ):
            copies.send(y_hbm.at[dp_at, there], y_in_ref.at[turn, q], y_pair + 2 * turn + q, place.pair)
            y_held.append(copies.local(y_hbm.at[dp_at, here], y_own_ref.at[turn, q]))

    first = Spread(place, copies, res_all, place.col_at(-FIRST))
    first.plan_corner(True)
    own_block = place.block(place.dp, place.col)
    late_in = copies.receivers(2)
    late = (place.dp, place.row, place.col_at(LATE))
    own_cot = cot_all.at[own_block, place.row]
    copies.send(low_hbm, res_all.at[own_block, place.row], late_in, late)
    copies.send(own_cot, own_cot, late_in + 1, late)
    gb_own.wait()

    def pass_on(chunk):
        piece = gb_ref.at[place.far_row, window(chunk)]
        copies.arrived(piece, gb_far + chunk, place.far)
        copies.send(piece, piece, gb_cross + chunk, place.pair)

    y_last = copies.receivers(3)

    def y_over():
        for copy in y_held:
            copy.wait()
        for q in range(2):
            copies.arrived(y_in_ref.at[0, q], y_pair + q, place.pair)
            y_chip_ref[0, q] = (y_own_ref[0, q].astype(F32) + y_in_ref[0, q].astype(F32)).astype(LOW)
            copies.send(y_chip_ref.at[0, q], y_last_ref.at[q], y_last + q, place.over)

    def y_far():
        for q in range(2):
            copies.arrived(y_in_ref.at[1, q], y_pair + 2 + q, place.pair)
            copies.arrived(y_last_ref.at[q], y_last + q, place.over)
        y_chip_ref[1, 1] = (
            y_own_ref[1, 1].astype(F32) + y_in_ref[1, 1].astype(F32) + y_last_ref[1].astype(F32)
        ).astype(LOW)
        copies.send(y_chip_ref.at[1, 1], y_last_ref.at[2], y_last + 2, place.far)

    away_in = [copies.receivers(chunks) for _ in range(2)]
    last_in = copies.receivers(chunks)

    def far_share(chunk):
        rows = slice(chunk * BLOCK_Q, (chunk + 1) * BLOCK_Q)
        copies.arrived(pair_in_ref.at[1, window(chunk)], away_in[1] + chunk, place.pair)
        chip_ref[rows, :] = (own_ref[1, rows, :] + pair_in_ref[1, rows, :].astype(F32)).astype(LOW)
        copies.send(chip_ref.at[window(chunk)], last_ref.at[window(chunk)], last_in + chunk, place.far)

    lane = lax.broadcasted_iota(jnp.int32, (BLOCK_Q, LANES), 1)
    y_over()
    first.begin(True)
    pass_on(chunks - 1)
    for block in blocks:
        q_start = block * BLOCK_Q
        k_start = max(0, q_start - WINDOW)
        q_rows, k_rows = slice(q_start, q_start + BLOCK_Q), slice(k_start, q_start + BLOCK_Q)
        copies.arrived(gb_ref.at[place.pair_row, window(block)], gb_pair + block, place.pair)
        copies.arrived(gb_ref.at[place.cross_row, window(block)], gb_cross + block, place.pair)
        total = dot_nt(gb_ref[0, q_rows, :], wo_ref[0])
        for part in range(1, parts):
            total = total + dot_nt(gb_ref[part, q_rows, :], wo_ref[part])
        gm_ref[...] = total.astype(LOW)
        mask = window_mask(column_ref[q_rows, 0:1], segments[0:1, k_rows], q_start, k_start)

        @pl.loop(0, kv_heads)
        def _(kv):
            keys, vals = k_ref[kv, k_rows, :], v_ref[kv, k_rows, :]
            lanes = pl.ds(pl.multiple_of(kv * LANES, LANES), LANES)
            both, logs, queried = gm_ref[:, lanes], lse_ref[q_rows, :], []
            for half in range(2):
                head = 2 * kv + half
                queries, grad = q_ref[head, q_rows, :], both[:, half * HD : (half + 1) * HD]
                scores = dot_nt(queries, keys) * scale
                log = jnp.sum(jnp.where(lane == head, logs, 0.0), axis=1, keepdims=True)
                weights = jnp.where(mask, jnp.exp(scores - log), 0.0)
                grad_weights = dot_nt(grad, vals)
                inner = jnp.sum(weights * grad_weights, axis=1, keepdims=True)
                grad_scores = (weights * (grad_weights - inner)).astype(LOW)
                dv_ref[kv, k_rows, :] += dot_tn(weights.astype(LOW), grad)
                dk_ref[kv, k_rows, :] += dot_tn(grad_scores, queries)
                queried.append(dot_nn(grad_scores, keys) * scale)
            dq_ref[:, lanes] = jnp.concatenate(queried, axis=1)

        if block > 0:
            pass_on(block - 1)
        for kv in range(kv_heads):
            base = kv * 4 * HD
            queries = dq_ref[:, kv * LANES : (kv + 1) * LANES]
            queries = queries * tab_ref[0, q_rows, :] - swap_halves(queries) * tab_ref[1, q_rows, :]
            others = jnp.concatenate([dk_ref[kv, q_rows, :] * scale, dv_ref[kv, q_rows, :]], axis=1)
            others = others * tab_ref[2, q_rows, :] - swap_halves(others) * tab_ref[3, q_rows, :]
            turn_ref[q_rows, base : base + LANES] = queries.astype(LOW)
            turn_ref[q_rows, base + LANES : base + 2 * LANES] = others.astype(LOW)
        for q, row_at in ((1, place.cross_row), (0, place.pair_row)):
            away_ref[q, q_rows, :] = dot_nt(turn_ref[q_rows, :], wq_ref[row_at]).astype(LOW)
            copies.send(
                away_ref.at[q, window(block)], pair_in_ref.at[q, window(block)], away_in[q] + block, place.pair
            )
        for q, row_at in ((1, place.far_row), (0, place.row)):
            own_ref[q, q_rows, :] = dot_nt(turn_ref[q_rows, :], wq_ref[row_at])
        if block < chunks - 1:
            far_share(block + 1)
        if block == chunks - 2:
            y_far()
        if block == 0:
            first.pass_far(True)
            first.pass_over(False)

    columns = turn_ref.shape[1]
    mix_own.wait()
    far_share(0)

    @pl.loop(0, parts)
    def _(part):
        features_here = pl.ds(pl.multiple_of(part * width, width), width)
        grads_ref[part, :, :columns] = dot_tn(normed_ref[:, features_here], turn_ref[...]).astype(LOW)
        grads_ref[part, :, columns:] = dot_tn(mixed_ref[...], gb_ref[part]).astype(LOW)

    gain = small_ref[place.row, GAIN_ONE : GAIN_ONE + 1, :].astype(F32)
    inner_in = copies.receivers(row_count)
    gain_sum = jnp.zeros((1, width), F32)
    for chunk in blocks:
        rows = slice(chunk * BLOCK_Q, (chunk + 1) * BLOCK_Q)
        copies.arrived(pair_in_ref.at[0, window(chunk)], away_in[0] + chunk, place.pair)
        copies.arrived(last_ref.at[window(chunk)], last_in + chunk, place.far)
        grad_normed = own_ref[0, rows, :] + pair_in_ref[0, rows, :].astype(F32) + last_ref[rows, :].astype(F32)
        own_ref[0, rows, :] = grad_normed
        along = grad_normed * hidden_ref[rows, :].astype(F32)
        gain_sum = gain_sum + jnp.sum(along * lse_ref[rows, RSTD_LANE : RSTD_LANE + 1], axis=0, keepdims=True)
        inner_ref[place.row, 0:1, rows] = row_of(jnp.sum(along * gain, axis=1, keepdims=True))
    sums_ref[...] = part_ref[...]
    sums_ref[GAIN_ONE : GAIN_ONE + 1, :] = gain_sum
    for k in range(1, row_count):
        copies.send(
            inner_ref.at[place.row], inner_ref.at[place.row], inner_in + k, (place.dp, place.row_at(k), place.col)
        )
    copies.arrived(y_last_ref.at[2], y_last + 2, place.far)
    for chunk in range(chunks):
        rows = slice(chunk * BLOCK_Q, (chunk + 1) * BLOCK_Q)
        mixture = y_own_ref[1, 0, rows, :].astype(F32) + y_in_ref[1, 0, rows, :].astype(F32)
        for slot in (0, 2):
            mixture = mixture + y_last_ref[slot, rows, :].astype(F32)
        out_ref[rows, :] = (resid_ref[rows, :] + mixture).astype(LOW)

    for k in range(1, row_count):
        copies.arrived(inner_ref.at[place.row_at(-k)], inner_in + k, place.here)
    inner = inner_ref[0, 0:1, :]
    for part in range(1, row_count):
        inner = inner + inner_ref[part, 0:1, :]
    for chunk in range(chunks):
        rows = slice(chunk * BLOCK_Q, (chunk + 1) * BLOCK_Q)
        rstd = lse_ref[rows, RSTD_LANE : RSTD_LANE + 1]
        cube = rstd * rstd * rstd * column_of(inner[:, rows]) / features
        grad_in_ref[rows, :] = (
            grad_ref[rows, :] + rstd * (own_ref[0, rows, :] * gain) - hidden_ref[rows, :].astype(F32) * cube
        )
    first.pass_corner()
    first.complete()
    z_shard = (place.block(place.dp, place.col_at(-LATE)), place.row)
    copies.arrived(res_all.at[z_shard], late_in, place.here)
    copies.arrived(cot_all.at[z_shard], late_in + 1, place.here)
    copies.finish()


def expert_grads(gate_pre, up_pre, grad_hidden):
    sig = 1.0 / (1.0 + jnp.exp(-gate_pre))
    silu = gate_pre * sig
    grad_gate = grad_hidden * up_pre * (sig * (1.0 + gate_pre * (1.0 - sig)))
    return (silu * up_pre).astype(LOW), grad_gate.astype(LOW), (grad_hidden * silu).astype(LOW)


def slot_picks(rank_row, capacity):
    at = lax.broadcasted_iota(jnp.int32, (capacity, rank_row.shape[1]), 0).astype(F32)
    return at == rank_row


def column_of(row):
    return jnp.broadcast_to(row, (LANES, row.shape[1])).T[:, 0:1]


def row_of(column):
    return jnp.broadcast_to(column, (column.shape[0], LANES)).T[0:1, :]


def experts_kernel(
    counts, low_hbm, resid_ref, cot_own_ref, packed_hbm, cot_given, small_ref, zo_hbm, wg_hbm, wu_hbm, wd_hbm,
    y_hbm, grad_ref, grad_low_ref, table_ref, part_ref, wo_hbm, cot_all, res_all, slots_x, slots_g, slots_mid,
    wg_ref, wu_ref, wd_ref, res_ref, cot_ref, x_ref, packed_ref, rank_ref, gate_ref, g_ref, pick_ref, eo_ref, back_ref,
    away_ref, pair_in_ref, own_ref, chip_ref, last_ref, stage_ref, gg_ref, gg_in_ref, rstd_ref, inner_ref, nx_ref,
    keep_x_ref, keep_g_ref, keep_mid_ref, keep_sems,
    send_sems, recv_sems,
):
    place = Place(counts)
    copies = Copies(send_sems, recv_sems)
    dp_count, row_count, col_count = counts
    _, parts, length, width = res_ref.shape
    experts, features, hidden_width = wg_ref.shape
    capacity = pick_ref.shape[0] // experts
    chunks = length // BLOCK_Q
    total_experts = dp_count * row_count * experts
    pair_count = length * TOP
    first_expert = (place.dp * row_count + place.row) * experts
    order = (place.other_dp, place.dp)
    all_here = say_hello(place.plane() + place.column())
    packed_own = copies.local(packed_hbm, packed_ref.at[place.dp])
    cot_in = [
        copies.local(cot_all.at[place.block(dp_at, place.col)], cot_ref.at[dp_at])
        for dp_at in (place.dp, place.other_dp)
    ]

    weights_in = [copies.local(*pair) for pair in ((wg_hbm, wg_ref), (wu_hbm, wu_ref), (wd_hbm, wd_ref))]

    def ranks_of(dp_at):
        ids = packed_ref[dp_at] // pair_count
        orders = (packed_ref[dp_at] - ids * pair_count).astype(F32)
        rows = []
        for e in range(experts):
            match = ids == first_expert + e
            known = jnp.max(jnp.where(match, 1.0, 0.0), axis=0, keepdims=True)
            at = jnp.sum(jnp.where(match, orders, 0.0), axis=0, keepdims=True)
            rows.append(jnp.where(known > 0.0, at, float(pair_count)))
        stacked = jnp.concatenate(rows + [jnp.zeros((LANES - experts, length), F32)], axis=0)
        columns = stacked.T
        for e in range(experts):
            count = jnp.zeros((1, length), F32)
            for start in range(0, length, BLOCK_Q):
                before = columns[start : start + BLOCK_Q, e : e + 1] < rows[e]
                count = count + jnp.sum(jnp.where(before, 1.0, 0.0), axis=0, keepdims=True)
            rank_ref[dp_at, e : e + 1, :] = jnp.where(rows[e] < float(pair_count), count, -1.0)

    def gather_grads(dp_at):
        @pl.loop(0, experts)
        def _(e):
            pick = slot_picks(rank_ref[dp_at, pl.ds(e, 1), :], capacity).astype(F32).astype(LOW)
            slots = pl.ds(pl.multiple_of(e * capacity, capacity), capacity)
            for part in range(parts):
                g_ref[dp_at, part, slots, :] = dot_nn(pick, cot_ref[dp_at, part]).astype(LOW)

    packed_own.wait()
    ranks_of(place.dp)
    cot_in[0].wait()
    gather_grads(place.dp)
    all_here()

    own_low = res_ref.at[place.dp, place.row]
    packed_over = copies.receivers()
    copies.send(packed_hbm, packed_ref.at[place.dp], packed_over, place.over)
    low_own = copies.local(low_hbm, own_low)
    halves = 2
    half_rows = length // halves
    res_at = copies.receivers(7 * halves)

    def halved(ref, half):
        return ref.at[pl.ds(half * half_rows, half_rows)]

    far_low = res_ref.at[place.dp, place.far_row]
    over_low = res_ref.at[place.other_dp, place.row]
    corner_low = res_ref.at[place.other_dp, place.far_row]
    for half in range(halves):
        source, target = halved(low_hbm, half), halved(own_low, half)
        copies.send(source, target, res_at + half, place.far)
        copies.send(source, target, res_at + halves + half, place.over)
    copies.send(low_hbm, own_low, res_at + 2 * halves, place.pair)
    own_block = place.block(place.dp, place.col)
    res_z, cot_z = copies.receivers(col_count), copies.receivers(col_count)
    for k, on_cot in ((SECOND, True), (FIRST, False), (SECOND, False)):
        peer = (place.dp, place.row, place.col_at(k))
        if on_cot:
            own_cot = cot_all.at[own_block, place.row]
            copies.send(own_cot, own_cot, cot_z + k, peer)
        else:
            copies.send(low_hbm, res_all.at[own_block, place.row], res_z + k, peer)

    def pass_side(half):
        copies.arrived(halved(far_low, half), res_at + half, place.far)
        copies.arrived(halved(over_low, half), res_at + halves + half, place.over)
        corner, peer = (far_low, place.over) if half == 0 else (over_low, place.far)
        copies.send(halved(corner, half), halved(corner, half), res_at + 3 * halves + half, peer)
        for k, ref in ((4, far_low), (5, over_low)):
            copies.send(halved(ref, half), halved(ref, half), res_at + k * halves + half, place.pair)

    def pass_corner(half):
        copies.arrived(halved(corner_low, half), res_at + 3 * halves + half, place.here)
        copies.send(
            halved(corner_low, half), halved(corner_low, half), res_at + 6 * halves + half, place.pair
        )

    copies.arrived(packed_ref.at[place.other_dp], packed_over, place.over)
    ranks_of(place.other_dp)
    pass_side(0)
    cot_in[1].wait()
    gather_grads(place.other_dp)
    pass_side(1)
    pass_corner(0)
    pass_corner(1)

    wo_in = copies.receivers(row_count)
    own_wo = copies.local(zo_hbm.at[place.row], stage_ref.at[0, pl.ds(0, zo_hbm.shape[1])])

    low_own.wait()
    copies.arrived(res_ref.at[place.dp, place.pair_row], res_at + 2 * halves, place.pair)
    for half in range(halves):
        for k, dp_at, row_at in (
            (4, place.dp, place.cross_row), (5, place.other_dp, place.pair_row), (6, place.other_dp, place.cross_row)
        ):
            copies.arrived(halved(res_ref.at[dp_at, row_at], half), res_at + k * halves + half, place.pair)
    for copy in weights_in:
        copy.wait()
    own_wo.wait()
    kept_wo = copies.local(stage_ref.at[0, pl.ds(0, zo_hbm.shape[1])], wo_hbm.at[place.row])
    kept_wo.wait()
    res_kept = [
        copies.local(res_ref.at[dp_at], res_all.at[place.block(dp_at, place.col)])
        for dp_at in (place.dp, place.other_dp)
    ]
    first, second = (Spread(place, copies, cot_all, place.col_at(-k)) for k in (FIRST, SECOND))
    first.plan_corner(False)
    second.plan_corner(True)
    first.begin(True)
    copies.arrived(
        cot_all.at[place.block(place.dp, place.col_at(-SECOND)), place.row], cot_z + SECOND, place.here
    )
    second.begin(True)

    own_scaled = place.row
    gg_same, gg_other = copies.receivers(row_count), copies.receivers(row_count)
    pair_in = copies.receivers(2 * dp_count)
    last_over, last_across, last_far = (copies.receivers() for _ in range(3))
    table_in = copies.receivers(col_count)

    kept_pairs = ((keep_x_ref, slots_x), (keep_g_ref, slots_g), (keep_mid_ref, slots_mid))
    for turn, dp_at in enumerate(order):
        last = turn == dp_count - 1

        @pl.loop(0, chunks)
        def _(chunk):
            rows = pl.ds(pl.multiple_of(chunk * BLOCK_Q, BLOCK_Q), BLOCK_Q)
            total = jnp.zeros((BLOCK_Q, 1), F32)
            for part in range(parts):
                piece = res_ref[dp_at, part, rows, :].astype(F32)
                total = total + jnp.sum(piece * piece, axis=1, keepdims=True)
            rstd = lax.rsqrt(total / features + EPSILON)
            for part in range(parts):
                piece = res_ref[dp_at, part, rows, :].astype(F32)
                gain = small_ref[part, GAIN_TWO : GAIN_TWO + 1, :].astype(F32)
                x_ref[rows, part * width : (part + 1) * width] = (piece * rstd * gain).astype(LOW)
            table_ref[place.col, dp_at, RSTD_ROW : RSTD_ROW + 1, rows] = row_of(rstd)
            if last:
                rstd_ref[rows, :] = jnp.broadcast_to(rstd, (BLOCK_Q, LANES))
                piece = res_ref[dp_at, own_scaled, rows, :].astype(F32)
                gain = small_ref[own_scaled, GAIN_TWO : GAIN_TWO + 1, :].astype(F32)
                nx_ref[rows, :] = (piece * rstd * gain).astype(LOW)

        logits = jnp.zeros((total_experts, length), F32)
        for part in range(parts):
            logits = logits + dot_nt(
                small_ref[part, :total_experts, :], x_ref[:, part * width : (part + 1) * width]
            )
        ids = packed_ref[dp_at] // pair_count
        expert_at = lax.broadcasted_iota(jnp.int32, (total_experts, length), 0)
        chosen = expert_at == ids[0:1, :]
        for k in range(1, TOP):
            chosen = chosen | (expert_at == ids[k : k + 1, :])
        shown = jnp.where(chosen, logits, NEG_LARGE)
        weights = jnp.where(chosen, jnp.exp(shown - jnp.max(shown, axis=0, keepdims=True)), 0.0)
        gate_ref[...] = weights / jnp.sum(weights, axis=0, keepdims=True)
        table_ref[place.col, dp_at, 0:experts, :] = rank_ref[dp_at, 0:experts, :]
        for e in range(experts):
            table_ref[place.col, dp_at, experts + e : experts + e + 1, :] = gate_ref[pl.ds(first_expert + e, 1), :]

        @pl.loop(0, experts)
        def _(e):
            if last:

                @pl.when(e == 1)
                def _():
                    second.pass_far(True)
                    second.pass_over(False)

                pl.when(e == experts - 1)(first.pass_corner)


            keep = lax.rem(e, 2)
            kept = [
                pltpu.make_async_copy(held.at[keep], target.at[turn, e], keep_sems.at[k, keep])
                for k, (held, target) in enumerate(kept_pairs)
            ]

            @pl.when(e + turn * experts >= 2)
            def _():
                for copy in kept:
                    copy.wait()

            here = slot_picks(rank_ref[dp_at, pl.ds(e, 1), :], capacity)
            pick = here.astype(F32).astype(LOW)
            slots = pl.ds(pl.multiple_of(e * capacity, capacity), capacity)
            pick_ref[slots, :] = pick
            gate_slot = jnp.sum(
                jnp.where(here, gate_ref[pl.ds(first_expert + e, 1), :], 0.0), axis=1, keepdims=True
            )
            x = dot_nn(pick, x_ref[...]).astype(LOW)
            keep_x_ref[keep] = x
            grad_hidden = jnp.zeros((capacity, hidden_width), F32)
            for part in range(parts):
                pair_grad = (g_ref[dp_at, part, slots, :].astype(F32) * gate_slot).astype(LOW)
                keep_g_ref[keep, :, part * width : (part + 1) * width] = pair_grad
                grad_hidden = grad_hidden + dot_nt(
                    pair_grad, wd_ref[e, :, part * width : (part + 1) * width]
                )
            hidden, grad_gate, grad_up = expert_grads(dot_nn(x, wg_ref[e]), dot_nn(x, wu_ref[e]), grad_hidden)
            keep_mid_ref[keep, 0] = hidden
            keep_mid_ref[keep, 1] = grad_gate
            keep_mid_ref[keep, 2] = grad_up
            for copy in kept:
                copy.start()
            along = jnp.zeros((capacity, 1), F32)
            for part in range(parts):
                cols = slice(part * width, (part + 1) * width)
                out = dot_nn(hidden, wd_ref[e, :, cols]).astype(LOW).astype(F32)
                along = along + jnp.sum(g_ref[dp_at, part, slots, :].astype(F32) * out, axis=1, keepdims=True)
                eo_ref[part, slots, :] = (out * gate_slot).astype(LOW)
                back_ref[part, slots, :] = (
                    dot_nt(grad_gate, wg_ref[e, cols, :]) + dot_nt(grad_up, wu_ref[e, cols, :])
                ).astype(LOW)
            gg_ref[dp_at, pl.ds(e, 1), :] = jnp.sum(jnp.where(here, along, 0.0), axis=0, keepdims=True)

        if not last:
            first.pass_far(False)
            first.pass_over(True)
        owner = place.dp * row_count + place.row
        if last:
            for k in range(1, row_count):
                copies.send(gg_ref.at[dp_at], gg_in_ref.at[owner], gg_same + k, (dp_at, place.row_at(k), place.col))
            gg_in_ref[owner] = gg_ref[dp_at]
        else:
            for k in range(row_count):
                copies.send(gg_ref.at[dp_at], gg_in_ref.at[owner], gg_other + k, (dp_at, place.row_at(k), place.col))

        for q, row_at in enumerate((place.pair_row, place.cross_row)):
            away_ref[turn, q] = dot_tn(pick_ref[...], back_ref[row_at]).astype(LOW)
            copies.send(away_ref.at[turn, q], pair_in_ref.at[turn, q], pair_in + 2 * turn + q, place.pair)
        for q, row_at in enumerate((place.far_row, place.row)):
            own_ref[q] = dot_tn(pick_ref[...], back_ref[row_at])
        copies.arrived(pair_in_ref.at[turn, 1], pair_in + 2 * turn + 1, place.pair)
        far_sum = own_ref[0] + pair_in_ref[turn, 1].astype(F32)
        if last:
            copies.arrived(last_ref.at[1], last_across, place.over)
            chip_ref[turn, 1] = (far_sum + last_ref[1].astype(F32)).astype(LOW)
            copies.send(chip_ref.at[turn, 1], last_ref.at[2], last_far, place.far)
        else:
            chip_ref[turn, 1] = far_sum.astype(LOW)
            copies.send(chip_ref.at[turn, 1], last_ref.at[1], last_across, place.over)
        copies.arrived(pair_in_ref.at[turn, 0], pair_in + 2 * turn, place.pair)
        if last:
            own_ref[1] = own_ref[1] + pair_in_ref[turn, 0].astype(F32)
        else:
            chip_ref[turn, 0] = (own_ref[1] + pair_in_ref[turn, 0].astype(F32)).astype(LOW)
            copies.send(chip_ref.at[turn, 0], last_ref.at[0], last_over, place.over)
            for k in range(col_count):
                source = place.col_at(k)
                mine = source == place.row
                step = lax.rem(source - place.row + row_count, row_count)
                copies.send(
                    zo_hbm.at[source], wo_hbm.at[place.row], wo_in + step, (place.dp, source, place.col), jnp.logical_not(mine)
                )

        for part in range(parts):
            stage_ref[part] = dot_tn(pick_ref[...], eo_ref[part]).astype(LOW)
        kept = copies.local(stage_ref, y_hbm.at[dp_at])
        kept.wait()

    for k in range(1, col_count):
        copies.send(table_ref.at[place.col], table_ref.at[place.col], table_in + k, (place.dp, place.row, place.col_at(k)))

    for k in range(1, row_count):
        copies.arrived(gg_in_ref.at[place.dp * row_count + place.row_at(-k)], gg_same + k, place.here)
    for k in range(row_count):
        copies.arrived(gg_in_ref.at[place.other_dp * row_count + place.row_at(-k)], gg_other + k, place.here)
    along = jnp.concatenate([gg_in_ref[owner, :experts, :] for owner in range(dp_count * row_count)], axis=0)
    gates = gate_ref[...]
    grad_logits = (gates * (along - jnp.sum(gates * along, axis=0, keepdims=True))).astype(LOW)
    router = small_ref[place.row, :total_experts, :]
    gain = small_ref[place.row, GAIN_TWO : GAIN_TWO + 1, :].astype(F32)
    part_ref[...] = jnp.zeros_like(part_ref)
    part_ref[:total_experts, :] = dot_nn(grad_logits, nx_ref[...])
    own_ref[1] = own_ref[1] + dot_tn(grad_logits, router)

    copies.arrived(last_ref.at[0], last_over, place.over)
    copies.arrived(last_ref.at[2], last_far, place.far)
    inner_in = copies.receivers(row_count)
    gain_sum = jnp.zeros((1, width), F32)
    for chunk in range(chunks):
        rows = slice(chunk * BLOCK_Q, (chunk + 1) * BLOCK_Q)
        grad_normed = own_ref[1, rows, :]
        for k in (0, 2):
            grad_normed = grad_normed + last_ref[k, rows, :].astype(F32)
        own_ref[0, rows, :] = grad_normed
        along = grad_normed * resid_ref[rows, :]
        gain_sum = gain_sum + jnp.sum(along * rstd_ref[rows, 0:1], axis=0, keepdims=True)
        inner_ref[place.row, 0:1, rows] = row_of(jnp.sum(along * gain, axis=1, keepdims=True))
    part_ref[GAIN_TWO : GAIN_TWO + 1, :] = gain_sum
    for k in range(1, row_count):
        copies.send(
            inner_ref.at[place.row], inner_ref.at[place.row], inner_in + k, (place.dp, place.row_at(k), place.col)
        )
    for k in range(1, row_count):
        copies.arrived(inner_ref.at[place.row_at(-k)], inner_in + k, place.here)
    inner = inner_ref[0, 0:1, :]
    for part in range(1, row_count):
        inner = inner + inner_ref[part, 0:1, :]
    for chunk in range(chunks):
        rows = slice(chunk * BLOCK_Q, (chunk + 1) * BLOCK_Q)
        rstd = rstd_ref[rows, 0:1]
        cube = rstd * rstd * rstd * column_of(inner[:, rows]) / features
        grad = (
            cot_own_ref[rows, :].astype(F32) + rstd * (own_ref[0, rows, :] * gain) - resid_ref[rows, :] * cube
        )
        grad_ref[rows, :] = grad
        grad_low_ref[rows, :] = grad.astype(LOW)

    for copy in res_kept:
        copy.wait()
    for keep in range(2):
        for k, (held, target) in enumerate(kept_pairs):
            pltpu.make_async_copy(held.at[keep], target.at[0, 0], keep_sems.at[k, keep]).wait()
    second.pass_corner()
    first.complete()
    second.complete()
    for k in (FIRST, SECOND):
        z_shard = (place.block(place.dp, place.col_at(-k)), place.row)
        copies.arrived(res_all.at[z_shard], res_z + k, place.here)
    for k in range(1, row_count):
        copies.arrived(wo_hbm.at[place.row_at(-k)], wo_in + k, place.here)
    for k in range(1, col_count):
        copies.arrived(table_ref.at[place.col_at(-k)], table_in + k, place.here)
    copies.finish()


def slot_grads(picked, rank_row, gate_row, rstd_row, res, cot, small_ref, wg, wu, wd):
    here = slot_picks(rank_row, picked)
    pick = here.astype(F32).astype(LOW)
    gate_slot = jnp.sum(jnp.where(here, gate_row, 0.0), axis=1, keepdims=True)
    rstd_slot = jnp.sum(jnp.where(here, rstd_row, 0.0), axis=1, keepdims=True)
    parts = res.shape[0]
    x = jnp.concatenate(
        [
            (
                dot_nn(pick, res[part]) * rstd_slot * small_ref[part, GAIN_TWO : GAIN_TWO + 1, :].astype(F32)
            ).astype(LOW)
            for part in range(parts)
        ],
        axis=1,
    )
    pair_grad = jnp.concatenate(
        [(dot_nn(pick, cot[part]) * gate_slot).astype(LOW) for part in range(parts)], axis=1
    )
    hidden, grad_gate, grad_up = expert_grads(dot_nn(x, wg), dot_nn(x, wu), dot_nt(pair_grad, wd))
    return x, pair_grad, hidden, grad_gate, grad_up


def weight_grads_kernel(
    counts, res_given, cot_given, grads_hbm, slots_x, slots_g, slots_mid, part_ref, table_ref, small_ref,
    wg_hbm, wu_hbm, wd_hbm,
    res_all, cot_all, dg_hbm, du_hbm, dd_hbm, own_ref, sums_ref,
    wg_ref, wu_ref, wd_ref, parts_ref, dg_ref, du_ref, dd_ref, res_ref, cot_ref, x_ref, g_ref, mid_ref, grads_in_ref, sum_ref,
    sems, keep_sems, out_sems, send_sems, recv_sems,
):
    place = Place(counts)
    copies = Copies(send_sems, recv_sems)
    dp_count, row_count, col_count = counts
    experts = wg_ref.shape[0]
    _, parts, length, width = res_all.shape
    capacity = length * TOP // (dp_count * row_count * experts)
    far_side = [(place.other_dp, place.row, place.col_at(k)) for k in range(1, col_count)]
    all_here = say_hello(
        place.plane()
        + place.column()
        + [
            (place.dp, place.row_at(j), place.col_at(k))
            for j in range(1, row_count)
            for k in range(1, col_count)
        ]
        + far_side
    )
    steps = 5
    before_late = 4 * experts

    def fetch(step):
        back = jnp.where(step < 2, FIRST, jnp.where(step < 4, SECOND, LATE))
        dp_at = lax.rem(place.dp + lax.rem(step, 2), dp_count)
        col_at = place.col_at(-back)
        b, slot = place.block(dp_at, col_at), lax.rem(step, 2)
        return dp_at, col_at, slot, (
            pltpu.make_async_copy(res_all.at[b], res_ref.at[slot], sems.at[slot]),
            pltpu.make_async_copy(cot_all.at[b], cot_ref.at[slot], sems.at[2 + slot]),
        )

    def kept_slots(turn):
        at, e, slot = turn // experts, lax.rem(turn, experts), lax.rem(turn, 2)
        pairs = ((slots_x, x_ref), (slots_g, g_ref), (slots_mid, mid_ref))
        return [
            pltpu.make_async_copy(source.at[at, e], target.at[slot], keep_sems.at[k, slot])
            for k, (source, target) in enumerate(pairs)
        ]

    for copy in fetch(0)[3]:
        copy.start()
    weights_in = [copies.local(*pair) for pair in ((wg_hbm, wg_ref), (wu_hbm, wu_ref), (wd_hbm, wd_ref))]
    for copy in kept_slots(0):
        copy.start()
    parts_ref[0] = part_ref[...]
    others = place.column() + [place.over] + far_side
    sums_in = copies.receivers(len(others) + 1)
    sum_sends = [
        copies.plan(parts_ref.at[0], parts_ref.at[k + 1], sums_in + k + 1, peer) for k, peer in enumerate(others)
    ]

    grads_in = copies.receivers(col_count)
    grads_kept = copies.local(grads_hbm.at[place.col], grads_in_ref.at[place.col])
    mine = place.row == place.col
    over_in, swap_in = copies.receivers(), copies.receivers()
    to_over = copies.plan(sum_ref.at[0], sum_ref.at[1], over_in, place.over)
    to_swap = remote(
        sum_ref.at[2], sum_ref.at[3], copies.send_sems.at[copies.sends], copies.recv_sems.at[swap_in],
        (place.dp, place.col, place.row),
    )
    copies.sends += 1
    copies.open.append((to_swap, jnp.logical_not(mine)))
    two_res, three_res, three_cot = (
        Spread(place, copies, array, place.col_at(-k))
        for k, array in ((SECOND, res_all), (LATE, res_all), (LATE, cot_all))
    )
    for spread, by_over in ((two_res, True), (three_res, True), (three_cot, False)):
        spread.plan_corner(by_over)
    grad_sends = [
        copies.plan(
            grads_hbm.at[place.col_at(k)], grads_in_ref.at[place.col], grads_in + k,
            (place.dp, place.row, place.col_at(k)),
        )
        for k in range(1, col_count)
    ]

    def begin():
        all_here()
        two_res.begin(True)
        three_res.begin(True)
        three_cot.begin(False)
        for copy in grad_sends + sum_sends:
            copy.start()

    def sum_columns():
        grads_kept.wait()
        for k in range(1, col_count):
            copies.arrived(grads_in_ref.at[place.col_at(-k)], grads_in + k, place.here)
        total = grads_in_ref[0].astype(F32)
        for col_at in range(1, col_count):
            total = total + grads_in_ref[col_at].astype(F32)
        sum_ref[0] = total.astype(LOW)
        to_over.start()

    def sum_over():
        copies.arrived(sum_ref.at[1], over_in, place.over)
        total = sum_ref[0].astype(F32) + sum_ref[1].astype(F32)
        sum_ref[2] = total.astype(LOW)
        own_ref[...] = total
        pl.when(jnp.logical_not(mine))(to_swap.start)

    def sum_parts():
        total = parts_ref[0]
        for k in range(len(others)):
            copies.arrived(parts_ref.at[k + 1], sums_in + k + 1, place.here)
            total = total + parts_ref[k + 1]
        sums_ref[...] = total

    def take_swapped():
        @pl.when(jnp.logical_not(mine))
        def _():
            copies.arrived(sum_ref.at[3], swap_in, place.here)
            own_ref[...] = sum_ref[3].astype(F32)

    events = {
        1: [begin],
        5: [lambda: two_res.pass_far(True), lambda: two_res.pass_over(False), three_cot.send_over],
        7: [two_res.complete_same],
        10: [lambda: three_res.pass_far(True), lambda: three_res.pass_over(False)],
        12: [two_res.pass_corner, lambda: three_cot.pass_far(False), two_res.complete_other, sum_columns],
        15: [lambda: three_cot.pass_over(True), three_res.complete_same, three_cot.complete_same],
        16: [three_res.pass_corner, sum_over],
        18: [three_cot.pass_corner],
        19: [sum_parts],
    }
    dg_ref[...] = jnp.zeros_like(dg_ref)
    du_ref[...] = jnp.zeros_like(du_ref)
    dd_ref[...] = jnp.zeros_like(dd_ref)
    for copy in weights_in:
        copy.wait()

    def other_blocks(turn):
        step, e = turn // experts, lax.rem(turn, experts)
        for at, actions in events.items():

            @pl.when(turn == at)
            def _(actions=actions):
                for action in actions:
                    action()

        dp_at, col_at, slot, arriving = fetch(step)

        @pl.when(e == 0)
        def _():
            @pl.when(step == 3)
            def _():
                for copy in arriving:
                    copy.start()

            for copy in arriving:
                copy.wait()

        @pl.when((e == experts - 1) & (step != 2) & (step + 1 < steps))
        def _():
            for copy in fetch(step + 1)[3]:
                copy.start()

        x, pair_grad, hidden, grad_gate, grad_up = slot_grads(
            capacity,
            table_ref[col_at, dp_at, pl.ds(e, 1), :],
            table_ref[col_at, dp_at, pl.ds(experts + e, 1), :],
            table_ref[col_at, dp_at, RSTD_ROW : RSTD_ROW + 1, :],
            res_ref.at[slot], cot_ref.at[slot], small_ref, wg_ref[e], wu_ref[e], wd_ref[e],
        )
        dd_ref[e] += dot_tn(hidden, pair_grad)
        dg_ref[e] += dot_tn(x, grad_gate)
        du_ref[e] += dot_tn(x, grad_up)

        @pl.when(step == steps - 1)
        def _():
            for k, (source, target) in enumerate(((dg_ref, dg_hbm), (du_ref, du_hbm), (dd_ref, dd_hbm))):
                pltpu.make_async_copy(source.at[e], target.at[e], out_sems.at[k, e]).start()

    pl.loop(0, before_late)(other_blocks)

    @pl.loop(0, dp_count * experts)
    def _(turn):
        e, slot = lax.rem(turn, experts), lax.rem(turn, 2)
        for copy in kept_slots(turn):
            copy.wait()

        @pl.when(turn + 1 < dp_count * experts)
        def _():
            for copy in kept_slots(turn + 1):
                copy.start()

        dd_ref[e] += dot_tn(mid_ref[slot, 0], g_ref[slot])
        dg_ref[e] += dot_tn(x_ref[slot], mid_ref[slot, 1])
        du_ref[e] += dot_tn(x_ref[slot], mid_ref[slot, 2])

    pl.loop(before_late, steps * experts)(other_blocks)
    take_swapped()
    three_res.complete_other()
    three_cot.complete_other()
    for e in range(experts):
        for k, (source, target) in enumerate(((dg_ref, dg_hbm), (du_ref, du_hbm), (dd_ref, dd_hbm))):
            pltpu.make_async_copy(source.at[e], target.at[e], out_sems.at[k, e]).wait()
    copies.finish()


def last_grads_kernel(
    counts, res_all, cot_all, table_ref, small_ref, wg_ref, wu_ref, wd_ref, dg_in, du_in, dd_in,
    out_in, grad_in_in, attn_in, sums_in,
    dg_ref, du_ref, dd_ref, out_ref, grad_in_ref, qkv_ref, wo_ref, router_ref, one_ref, two_ref,
    res_ref, cot_ref, sems,
):
    dp_count, row_count, col_count = counts
    e = pl.program_id(0)
    experts = pl.num_programs(0)
    _, parts, length, width = res_all.shape
    capacity = length * TOP // (dp_count * row_count * experts)
    col_at = lax.rem(lax.axis_index("col") + col_count - LATE, col_count)

    dp_at = dp_count - 1 - lax.axis_index("dp")
    b = dp_at * col_count + col_at
    arriving = (
        pltpu.make_async_copy(res_all.at[b], res_ref, sems.at[0]),
        pltpu.make_async_copy(cot_all.at[b], cot_ref, sems.at[1]),
    )

    @pl.when(e == 0)
    def _():
        for copy in arriving:
            copy.start()

    out_ref[...] = out_in[...]
    grad_in_ref[...] = grad_in_in[...]
    group, columns = qkv_ref.shape[1:]
    for head in range(group):
        qkv_ref[:, head, :] = attn_in[:, head * columns : (head + 1) * columns]
    wo_ref[...] = attn_in[:, group * columns :]

    @pl.when(e == experts - 1)
    def _():
        router_ref[...] = sums_in[:GAIN_ONE, :]
        one_ref[...] = sums_in[GAIN_ONE : GAIN_ONE + 1, :]
        two_ref[...] = sums_in[GAIN_TWO : GAIN_TWO + 1, :]

    @pl.when(e == 0)
    def _():
        for copy in arriving:
            copy.wait()

    x, pair_grad, hidden, grad_gate, grad_up = slot_grads(
        capacity,
        table_ref[col_at, dp_at, pl.ds(e, 1), :],
        table_ref[col_at, dp_at, pl.ds(experts + e, 1), :],
        table_ref[col_at, dp_at, RSTD_ROW : RSTD_ROW + 1, :],
        res_ref, cot_ref, small_ref, wg_ref[0], wu_ref[0], wd_ref[0],
    )
    dd_ref[0] = dd_in[0] + dot_tn(hidden, pair_grad)
    dg_ref[0] = dg_in[0] + dot_tn(x, grad_gate)
    du_ref[0] = du_in[0] + dot_tn(x, grad_up)


def fast_device(
    hidden_in, norm_gain, w_qkv, w_out, ffn_gain, router, w_gate, w_up, w_down, cotangent,
    segment_ids, expert_ids, pair_order,
):
    dp_count, row_count, col_count = (lax.axis_size(name) for name in ("dp", "row", "col"))
    my_dp, my_row, my_col = (lax.axis_index(name) for name in ("dp", "row", "col"))
    length, width = hidden_in.shape
    kv_local = w_qkv.shape[1]
    head_width = kv_local * (HQ // HK) * HD
    qkv_width = kv_local * (HQ // HK + 2) * HD
    exp_local, _, hidden_width = w_gate.shape
    capacity = length * TOP // EXPERTS
    blocks = dp_count * col_count
    vmem = pl.BlockSpec(memory_space=pltpu.VMEM)
    hbm = pl.BlockSpec(memory_space=pl.ANY)
    params = pltpu.CompilerParams(vmem_limit_bytes=VMEM_BYTES)

    packed = (expert_ids * (length * TOP) + pair_order).T
    own_q = w_qkv.reshape(width, qkv_width)
    own_o = w_out.reshape(head_width, width)
    small = jnp.concatenate(
        [router.T, norm_gain[None], ffn_gain[None], jnp.zeros((SMALL_ROWS - 2 - EXPERTS, width), LOW)], axis=0
    )
    seg_rows = jnp.broadcast_to(segment_ids, (8, length)).astype(F32)
    tables = jnp.asarray(rope_lanes(length))
    counts = (dp_count, row_count, col_count)
    (
        resid_mid, resid_low, mixed_all, normed_one, query_rot, key_rot, value_low, logs,
        wq_rows, wo_cols, small_all, seg_all, cot_all,
    ) = pl.pallas_call(
        functools.partial(attend_forward_kernel, counts),
        out_shape=(
            jax.ShapeDtypeStruct((length, width), F32),
            jax.ShapeDtypeStruct((length, width), LOW),
            jax.ShapeDtypeStruct((row_count, length, head_width), LOW),
            jax.ShapeDtypeStruct((length, D), LOW),
            jax.ShapeDtypeStruct((2 * kv_local, length, HD), LOW),
            jax.ShapeDtypeStruct((kv_local, length, HD), LOW),
            jax.ShapeDtypeStruct((kv_local, length, HD), LOW),
            jax.ShapeDtypeStruct((length, LANES), F32),
            jax.ShapeDtypeStruct((row_count, width, qkv_width), LOW),
            jax.ShapeDtypeStruct((col_count, head_width, width), LOW),
            jax.ShapeDtypeStruct((row_count, SMALL_ROWS, width), LOW),
            jax.ShapeDtypeStruct((row_count, 8, length), F32),
            jax.ShapeDtypeStruct((blocks, row_count, length, width), LOW),
        ),
        in_specs=[hbm] * 6 + [vmem],
        out_specs=[vmem] * 12 + [hbm],
        scratch_shapes=[
            pltpu.VMEM((row_count, length, width), LOW),
            pltpu.VMEM((col_count, width, qkv_width), LOW),
            pltpu.VMEM((length, width), LOW),
            pltpu.VMEM((length, LANES), F32),
            pltpu.SemaphoreType.DMA((64,)),
            pltpu.SemaphoreType.DMA((64,)),
        ],
        compiler_params=pltpu.CompilerParams(
            vmem_limit_bytes=VMEM_BYTES, collective_id=1, has_side_effects=True
        ),
        cost_estimate=pl.CostEstimate(flops=50_000_000_000, bytes_accessed=30_000_000, transcendentals=0),
        name="attend_forward",
    )(hidden_in, own_q, own_o, small, seg_rows, cotangent, tables)
    block_low = jax.ShapeDtypeStruct((length, width), LOW)
    block_float = jax.ShapeDtypeStruct((length, width), F32)
    slots = exp_local * capacity
    plane = (dp_count, row_count, length, width)
    every = jax.ShapeDtypeStruct((blocks, row_count, length, width), LOW)
    y_part, grad_resid, grad_low, table, small_part, wo_rows, cot_all, res_all, *kept_slots = pl.pallas_call(
        functools.partial(experts_kernel, counts),
        out_shape=(
            jax.ShapeDtypeStruct(plane, LOW),
            block_float,
            block_low,
            jax.ShapeDtypeStruct((col_count, dp_count, 16, length), F32),
            jax.ShapeDtypeStruct((SMALL_ROWS, width), F32),
            jax.ShapeDtypeStruct((row_count, head_width, width), LOW),
            every,
            every,
            jax.ShapeDtypeStruct((dp_count, exp_local, capacity, D), LOW),
            jax.ShapeDtypeStruct((dp_count, exp_local, capacity, D), LOW),
            jax.ShapeDtypeStruct((dp_count, exp_local, 3, capacity, hidden_width), LOW),
        ),
        input_output_aliases={4: 6},
        in_specs=[hbm, vmem, vmem, hbm, hbm, vmem, hbm, hbm, hbm, hbm],
        out_specs=[hbm] + [vmem] * 4 + [hbm] * 6,
        scratch_shapes=[
            pltpu.VMEM(w_gate.shape, LOW),
            pltpu.VMEM(w_up.shape, LOW),
            pltpu.VMEM(w_down.shape, LOW),
            pltpu.VMEM(plane, LOW),
            pltpu.VMEM(plane, LOW),
            pltpu.VMEM((length, D), LOW),
            pltpu.VMEM((dp_count, TOP, length), jnp.int32),
            pltpu.VMEM((dp_count, 8, length), F32),
            pltpu.VMEM((EXPERTS, length), F32),
            pltpu.VMEM((dp_count, row_count, slots, width), LOW),
            pltpu.VMEM((slots, length), LOW),
            pltpu.VMEM((row_count, slots, width), LOW),
            pltpu.VMEM((row_count, slots, width), LOW),
            pltpu.VMEM((dp_count, 2, length, width), LOW),
            pltpu.VMEM((dp_count, 2, length, width), LOW),
            pltpu.VMEM((2, length, width), F32),
            pltpu.VMEM((dp_count, 2, length, width), LOW),
            pltpu.VMEM((3, length, width), LOW),
            pltpu.VMEM((row_count, length, width), LOW),
            pltpu.VMEM((dp_count, 8, length), F32),
            pltpu.VMEM((dp_count * row_count, 8, length), F32),
            pltpu.VMEM((length, LANES), F32),
            pltpu.VMEM((row_count, 8, length), F32),
            pltpu.VMEM((length, width), LOW),
            pltpu.VMEM((2, capacity, D), LOW),
            pltpu.VMEM((2, capacity, D), LOW),
            pltpu.VMEM((2, 3, capacity, hidden_width), LOW),
            pltpu.SemaphoreType.DMA((3, 2)),
            pltpu.SemaphoreType.DMA((80,)),
            pltpu.SemaphoreType.DMA((80,)),
        ],
        compiler_params=pltpu.CompilerParams(
            vmem_limit_bytes=VMEM_BYTES, collective_id=2, has_side_effects=True
        ),
        cost_estimate=pl.CostEstimate(flops=80_000_000_000, bytes_accessed=50_000_000, transcendentals=0),
        name="experts",
    )(resid_low, resid_mid, cotangent, packed, cot_all, small_all, wo_cols, w_gate, w_up, w_down)

    halves = (dp_count, 2, length, width)
    half = (2, length, width)
    layer_out, grad_in, grads_part, small_part, res_all, cot_all = pl.pallas_call(
        functools.partial(attend_backward_kernel, counts),
        out_shape=(
            block_low,
            block_float,
            jax.ShapeDtypeStruct((row_count, width, qkv_width + width), LOW),
            jax.ShapeDtypeStruct((SMALL_ROWS, width), F32),
            every,
            every,
        ),
        input_output_aliases={17: 4, 18: 5},
        in_specs=[hbm] + [vmem] * 6 + [hbm] + [vmem] * 8 + [hbm] * 4,
        out_specs=[vmem] * 4 + [hbm] * 2,
        scratch_shapes=[
            pltpu.VMEM((row_count, length, width), LOW),
            pltpu.VMEM((length, head_width), LOW),
            pltpu.VMEM((BLOCK_Q, head_width), LOW),
            pltpu.VMEM((BLOCK_Q, head_width), F32),
            pltpu.VMEM((kv_local, length, HD), F32),
            pltpu.VMEM((kv_local, length, HD), F32),
            pltpu.VMEM((length, qkv_width), LOW),
            pltpu.VMEM((length, LANES), F32),
            pltpu.VMEM(halves, LOW),
            pltpu.VMEM(halves, LOW),
            pltpu.VMEM(halves, LOW),
            pltpu.VMEM((3, length, width), LOW),
            pltpu.VMEM(half, LOW),
            pltpu.VMEM(half, LOW),
            pltpu.VMEM(half, F32),
            pltpu.VMEM((length, width), LOW),
            pltpu.VMEM((length, width), LOW),
            pltpu.VMEM((row_count, 8, length), F32),
            pltpu.SemaphoreType.DMA((80,)),
            pltpu.SemaphoreType.DMA((80,)),
        ],
        compiler_params=pltpu.CompilerParams(
            vmem_limit_bytes=VMEM_BYTES, collective_id=3, has_side_effects=True
        ),
        cost_estimate=pl.CostEstimate(flops=40_000_000_000, bytes_accessed=30_000_000, transcendentals=0),
        name="attend_backward",
    )(
        grad_low, grad_resid, hidden_in, resid_mid, wo_rows, wq_rows, normed_one, mixed_all, query_rot, key_rot,
        value_low, logs, seg_all, small_all, small_part, tables, y_part, res_all,
        cot_all, resid_low,
    )

    gate_shape, down_shape = (jax.ShapeDtypeStruct(w.shape, F32) for w in (w_gate, w_down))
    one_gate = pl.BlockSpec((1,) + w_gate.shape[1:], lambda e: (e, 0, 0))
    one_down = pl.BlockSpec((1,) + w_down.shape[1:], lambda e: (e, 0, 0))
    token_pair = (2, row_count, length, width)
    res_all, cot_all, grad_gate, grad_up, grad_down, grads_own, small = pl.pallas_call(
        functools.partial(weight_grads_kernel, counts),
        out_shape=(
            every, every, gate_shape, gate_shape, down_shape,
            jax.ShapeDtypeStruct((width, qkv_width + width), F32),
            jax.ShapeDtypeStruct((SMALL_ROWS, width), F32),
        ),
        input_output_aliases={0: 0, 1: 1},
        in_specs=[hbm] * 6 + [vmem] * 3 + [hbm] * 3,
        out_specs=[hbm] * 5 + [vmem] * 2,
        scratch_shapes=[
            pltpu.VMEM(w_gate.shape, LOW),
            pltpu.VMEM(w_up.shape, LOW),
            pltpu.VMEM(w_down.shape, LOW),
            pltpu.VMEM((dp_count * col_count, SMALL_ROWS, width), F32),
            pltpu.VMEM(w_gate.shape, F32),
            pltpu.VMEM(w_up.shape, F32),
            pltpu.VMEM(w_down.shape, F32),
            pltpu.VMEM(token_pair, LOW),
            pltpu.VMEM(token_pair, LOW),
            pltpu.VMEM((2, capacity, D), LOW),
            pltpu.VMEM((2, capacity, D), LOW),
            pltpu.VMEM((2, 3, capacity, hidden_width), LOW),
            pltpu.VMEM((col_count, width, qkv_width + width), LOW),
            pltpu.VMEM((4, width, qkv_width + width), LOW),
            pltpu.SemaphoreType.DMA((4,)),
            pltpu.SemaphoreType.DMA((3, 2)),
            pltpu.SemaphoreType.DMA((3, exp_local)),
            pltpu.SemaphoreType.DMA((64,)),
            pltpu.SemaphoreType.DMA((64,)),
        ],
        compiler_params=pltpu.CompilerParams(
            vmem_limit_bytes=VMEM_BYTES, collective_id=4, has_side_effects=True
        ),
        name="weight_grads",
    )(res_all, cot_all, grads_part, *kept_slots, small_part, table, small_all, w_gate, w_up, w_down)
    def strips(rows, columns):
        return pl.BlockSpec((rows // exp_local, columns), lambda e: (e, 0))

    tokens, attn = strips(length, width), strips(width, qkv_width + width)
    whole = [pl.BlockSpec((EXPERTS, width), lambda e: (0, 0))] + [pl.BlockSpec((1, width), lambda e: (0, 0))] * 2
    gain_row = jax.ShapeDtypeStruct((1, width), F32)
    grad_gate, grad_up, grad_down, layer_out, grad_in, grad_qkv, grad_out, grad_router, *grad_gains = pl.pallas_call(
        functools.partial(last_grads_kernel, counts),
        grid=(exp_local,),
        out_shape=(
            gate_shape, gate_shape, down_shape, block_low, block_float,
            jax.ShapeDtypeStruct(w_qkv.shape, F32),
            jax.ShapeDtypeStruct((head_width, width), F32),
            jax.ShapeDtypeStruct((EXPERTS, width), F32),
            gain_row,
            gain_row,
        ),
        in_specs=[hbm, hbm, vmem, vmem] + [one_gate, one_gate, one_down] * 2 + [tokens, tokens, attn, vmem],
        out_specs=[
            one_gate, one_gate, one_down, tokens, tokens,
            pl.BlockSpec((width // exp_local,) + w_qkv.shape[1:], lambda e: (e, 0, 0)), strips(head_width, width),
        ]
        + whole,
        scratch_shapes=[
            pltpu.VMEM((row_count, length, width), LOW),
            pltpu.VMEM((row_count, length, width), LOW),
            pltpu.SemaphoreType.DMA((2,)),
        ],
        compiler_params=params,
        name="last_grads",
    )(
        res_all, cot_all, table, small_all, w_gate, w_up, w_down, grad_gate, grad_up, grad_down,
        layer_out, grad_in, grads_own, small,
    )
    return (
        layer_out,
        grad_in,
        grad_gains[0].reshape(width),
        grad_qkv,
        grad_out.reshape(w_out.shape),
        grad_gains[1].reshape(width),
        grad_router.T,
        grad_gate,
        grad_up,
        grad_down,
    )


def solution(mesh):
    token = P(("dp", "col"), "row")
    routed = P(("dp", "col"), None)
    expert = P(("dp", "row"), None, None)
    wide, tall = P("row", "col", None), P("col", None, "row")
    row = P("row")
    square = P("row", None)

    def step(*arrays):
        length = arrays[10].shape[1]
        tokens_here = arrays[0].shape[0] // (mesh.shape["dp"] * mesh.shape["col"])
        whole_sequence = tokens_here == length and mesh.shape["row"] == mesh.shape["col"]
        return jax.shard_map(
            fast_device if whole_sequence else on_device,
            mesh=mesh,
            in_specs=(
                token, row, wide, tall, row, square, expert, expert, expert, token,
                P(("dp", "row"), None), routed, routed,
            ),
            out_specs=(token, token, row, wide, tall, row, square, expert, expert, expert),
            check_vma=False,
        )(*arrays)

    return step
```

```python
import functools

import jax
import jax.numpy as jnp
import numpy as np
from jax import lax
from jax.experimental import pallas as pl
from jax.experimental.pallas import tpu as pltpu
from jax.sharding import PartitionSpec as P

D = 1024
HQ = 16
HK = 8
HD = 64
EXPERTS = 32
TOP = 8


EPSILON = 1e-06
ROPE_BASE = 10000.0
NEG_LARGE = -1e30
HIGHEST = lax.Precision.HIGHEST


def rotate(values, cosine, sine_table):
    half_size = values.shape[-1] // 2
    lower_half = values[..., :half_size]
    upper_half = values[..., half_size:]
    return jnp.concatenate(
        [
            lower_half * cosine - upper_half * sine_table,
            upper_half * cosine + lower_half * sine_table,
        ],
        axis=-1,
    )


def rotate_back(values, cosine, sine_table):
    half_size = values.shape[-1] // 2
    lower_half = values[..., :half_size]
    upper_half = values[..., half_size:]
    return jnp.concatenate(
        [
            lower_half * cosine + upper_half * sine_table,
            upper_half * cosine - lower_half * sine_table,
        ],
        axis=-1,
    )


def rope_tables(length, head_size):
    positions = jnp.arange(length, dtype=jnp.float32)
    frequency = ROPE_BASE ** (-2.0 * jnp.arange(head_size // 2, dtype=jnp.float32) / head_size)
    angles = positions[:, None] * frequency[None, :]
    return (jnp.cos(angles), jnp.sin(angles))


def visible(segment_row):
    positions = jnp.arange(segment_row.shape[-1], dtype=jnp.int32)
    causal = positions[:, None] >= positions[None, :]
    return causal & (segment_row[..., :, None] == segment_row[..., None, :])


def pair_ranks(expert_ids, pair_order, block_rows):
    experts_flat = expert_ids.reshape(-1, block_rows * TOP)
    order_flat = pair_order.reshape(-1, block_rows * TOP)

    def one_block(experts_row, order_row):
        pair_count = experts_row.shape[0]
        by_order = (
            jnp.zeros((pair_count,), jnp.int32)
            .at[order_row]
            .set(jnp.arange(pair_count, dtype=jnp.int32))
        )
        sorted_experts = experts_row[by_order]
        onehot = (sorted_experts[:, None] == jnp.arange(EXPERTS, dtype=jnp.int32)[None, :]).astype(
            jnp.int32
        )
        before = jnp.cumsum(onehot, axis=0) - onehot
        sorted_rank = jnp.sum(before * onehot, axis=1)
        return sorted_rank[order_row]

    return jax.vmap(one_block)(experts_flat, order_flat).reshape(expert_ids.shape)


def feature_total(values):
    return lax.psum(values, "row")


def tokens_by_col(values):
    return lax.all_gather(values, "col", axis=0, tiled=True)


def tokens_by_row(values):
    return lax.all_gather(values, "row", axis=0, tiled=True)


def col_scatter(term_fn, keep_rows):
    return lax.psum_scatter(
        term_fn(jnp.int32(0), keep_rows * lax.axis_size("col")),
        "col",
        scatter_dimension=0,
        tiled=True,
    )


def to_experts(outgoing):
    arrived = lax.all_to_all(outgoing, ("dp", "row"), split_axis=0, concat_axis=0, tiled=True)
    return arrived


def from_experts(outgoing):
    arrived = lax.all_to_all(outgoing, ("dp", "row"), split_axis=0, concat_axis=0, tiled=True)
    return arrived


def owner_layout(incoming, dp_count, row_count, exp_local):
    capacity = incoming.shape[1] // exp_local
    part_width = incoming.shape[2]
    sectioned = incoming.reshape(dp_count, row_count, exp_local, capacity, part_width)
    return sectioned.transpose(2, 0, 3, 1, 4).reshape(
        exp_local, dp_count * capacity, row_count * part_width
    )


def source_layout(owner_rows, dp_count, row_count):
    exp_local, slot_rows, full_width = owner_rows.shape
    capacity = slot_rows // dp_count
    part_width = full_width // row_count
    sectioned = owner_rows.reshape(exp_local, dp_count, capacity, row_count, part_width)
    return sectioned.transpose(1, 3, 0, 2, 4).reshape(
        dp_count * row_count, exp_local * capacity, part_width
    )


def attend_forward(pack):
    query_seq, key_seq, value_seq, segment_seq = pack
    score_scale = query_seq.shape[-1] ** (-0.5)
    scores = (
        jnp.einsum("qhgd,khd->hgqk", query_seq, key_seq, preferred_element_type=jnp.float32)
        * score_scale
    )
    scores = jnp.where(visible(segment_seq), scores, NEG_LARGE)
    row_max = jnp.max(scores, axis=-1, keepdims=True)
    weights = jnp.exp(scores - row_max)
    row_total = jnp.sum(weights, axis=-1, keepdims=True)
    weights_low = (weights / row_total).astype(jnp.bfloat16)
    mixed_seq = jnp.einsum(
        "hgqk,khd->qhgd", weights_low, value_seq, preferred_element_type=jnp.float32
    )
    return (mixed_seq.astype(jnp.bfloat16), row_max + jnp.log(row_total))


def attend_backward(pack):
    query_seq, key_seq, value_seq, segment_seq, log_total, grad_seq = pack
    score_scale = query_seq.shape[-1] ** (-0.5)
    scores = (
        jnp.einsum("qhgd,khd->hgqk", query_seq, key_seq, preferred_element_type=jnp.float32)
        * score_scale
    )
    scores = jnp.where(visible(segment_seq), scores, NEG_LARGE)
    weights = jnp.exp(scores - log_total)
    grad_weights = jnp.einsum(
        "qhgd,khd->hgqk", grad_seq, value_seq, preferred_element_type=jnp.float32
    )
    inner_sum = jnp.sum(weights * grad_weights, axis=-1, keepdims=True)
    grad_scores = (weights * (grad_weights - inner_sum)).astype(jnp.bfloat16)
    grad_values = jnp.einsum(
        "hgqk,qhgd->khd", weights.astype(jnp.bfloat16), grad_seq, preferred_element_type=jnp.float32
    )
    grad_query = (
        jnp.einsum("hgqk,khd->qhgd", grad_scores, key_seq, preferred_element_type=jnp.float32)
        * score_scale
    )
    grad_key = (
        jnp.einsum("hgqk,qhgd->khd", grad_scores, query_seq, preferred_element_type=jnp.float32)
        * score_scale
    )
    return (grad_query, grad_key, grad_values)


def on_device(
    hidden_in,
    norm_gain,
    w_qkv,
    w_out,
    ffn_gain,
    router,
    w_gate,
    w_up,
    w_down,
    cotangent,
    segment_ids,
    expert_ids,
    pair_order,
):
    dp_count = lax.axis_size("dp")
    row_count = lax.axis_size("row")
    owners = dp_count * row_count
    tok_rows, part_width = hidden_in.shape
    seq_count, length = segment_ids.shape
    att_rows = seq_count * length
    kv_local = w_qkv.shape[1]
    group_size = HQ // HK
    exp_local = w_gate.shape[0]
    capacity = tok_rows * TOP // EXPERTS
    total_slots = EXPERTS * capacity
    resid_in = hidden_in.astype(jnp.float32)
    gain_one = norm_gain.astype(jnp.float32)
    rstd_one = lax.rsqrt(feature_total(jnp.sum(resid_in * resid_in, axis=1)) / D + EPSILON)
    normed_one = (resid_in * rstd_one[:, None] * gain_one).astype(jnp.bfloat16)
    group_rows = tokens_by_col(normed_one)
    qkv_flat = w_qkv.reshape(part_width, -1)
    picked = group_rows
    qkv_local = lax.psum_scatter(
        jnp.dot(picked, qkv_flat, preferred_element_type=jnp.float32),
        "row",
        scatter_dimension=0,
        tiled=True,
    )
    qkv_local = qkv_local.reshape(seq_count, length, kv_local, -1)
    cosine, sine_table = rope_tables(length, HD)
    queries = qkv_local[..., : group_size * HD].reshape(seq_count, length, kv_local, group_size, HD)
    query_rot = rotate(
        queries, cosine[None, :, None, None, :], sine_table[None, :, None, None, :]
    ).astype(jnp.bfloat16)
    key_rot = rotate(
        qkv_local[..., group_size * HD : (group_size + 1) * HD],
        cosine[None, :, None, :],
        sine_table[None, :, None, :],
    ).astype(jnp.bfloat16)
    value_low = qkv_local[..., (group_size + 1) * HD :].astype(jnp.bfloat16)
    mixed_heads, log_total = lax.map(attend_forward, (query_rot, key_rot, value_low, segment_ids))
    mixed_rows = tokens_by_row(mixed_heads.reshape(att_rows, -1))
    out_flat = w_out.reshape(-1, part_width)

    def out_term(first_row, block_rows):
        return jnp.dot(mixed_rows, out_flat, preferred_element_type=jnp.float32)

    resid_mid = resid_in + col_scatter(out_term, tok_rows)
    gain_two = ffn_gain.astype(jnp.float32)
    router_float = router.astype(jnp.float32)
    square_two, logit_part = (
        lax.psum(jnp.sum(resid_mid * resid_mid, axis=1).astype(jnp.bfloat16), "row").astype(
            jnp.float32
        ),
        lax.psum(
            jnp.dot(resid_mid * gain_two, router_float, precision=HIGHEST).astype(jnp.bfloat16),
            "row",
        ).astype(jnp.float32),
    )
    rstd_two = lax.rsqrt(square_two / D + EPSILON)
    logits = logit_part * rstd_two[:, None]
    normed_float = resid_mid * rstd_two[:, None] * gain_two
    normed_two = normed_float.astype(jnp.bfloat16)
    choose = (expert_ids[:, :, None] == jnp.arange(EXPERTS, dtype=jnp.int32)[None, None, :]).astype(
        jnp.float32
    )
    gate_weights = jax.nn.softmax(jnp.sum(choose * logits[:, None, :], axis=2), axis=1)
    pair_rank = pair_ranks(expert_ids, pair_order, tok_rows)
    pair_slot = jnp.where(pair_rank < capacity, expert_ids * capacity + pair_rank, total_slots)
    pair_index = jnp.arange(tok_rows * TOP, dtype=jnp.int32)
    slot_pair = (
        jnp.full((total_slots + 1,), tok_rows * TOP, jnp.int32)
        .at[pair_slot.reshape(-1)]
        .set(pair_index)[:total_slots]
    )
    padded_two = jnp.concatenate([normed_two, jnp.zeros((1, part_width), jnp.bfloat16)], axis=0)
    outgoing = padded_two[slot_pair // TOP].reshape(owners, exp_local * capacity, part_width)
    expert_rows = owner_layout(to_experts(outgoing), dp_count, row_count, exp_local)
    gate_pre = jnp.einsum("erd,edf->erf", expert_rows, w_gate, preferred_element_type=jnp.float32)
    up_pre = jnp.einsum("erd,edf->erf", expert_rows, w_up, preferred_element_type=jnp.float32)
    hidden = (jax.nn.silu(gate_pre) * up_pre).astype(jnp.bfloat16)
    expert_out = jnp.einsum(
        "erf,efd->erd", hidden, w_down, preferred_element_type=jnp.float32
    ).astype(jnp.bfloat16)
    returned = from_experts(source_layout(expert_out, dp_count, row_count))
    slot_table = jnp.concatenate(
        [returned.reshape(total_slots, part_width), jnp.zeros((1, part_width), jnp.bfloat16)],
        axis=0,
    )
    pair_rows = slot_table[pair_slot].astype(jnp.float32)
    layer_sum = resid_mid + jnp.einsum("tk,tkd->td", gate_weights, pair_rows, precision=HIGHEST)
    grad_top = cotangent.astype(jnp.float32)
    grad_gates = lax.psum(jnp.einsum("td,tkd->tk", grad_top, pair_rows, precision=HIGHEST), "row")
    pair_grad = (gate_weights[:, :, None] * grad_top[:, None, :]).astype(jnp.bfloat16)
    grad_padded = jnp.concatenate(
        [pair_grad.reshape(tok_rows * TOP, part_width), jnp.zeros((1, part_width), jnp.bfloat16)],
        axis=0,
    )
    outgoing_grad = grad_padded[slot_pair].reshape(owners, exp_local * capacity, part_width)
    grad_rows = owner_layout(to_experts(outgoing_grad), dp_count, row_count, exp_local)
    grad_hidden = jnp.einsum("erd,efd->erf", grad_rows, w_down, preferred_element_type=jnp.float32)
    sigmoid_gate = jax.nn.sigmoid(gate_pre)
    grad_gate_pre = (
        grad_hidden * up_pre * sigmoid_gate * (1.0 + gate_pre * (1.0 - sigmoid_gate))
    ).astype(jnp.bfloat16)
    grad_up_pre = (grad_hidden * gate_pre * sigmoid_gate).astype(jnp.bfloat16)
    grad_down_local = jnp.einsum(
        "erf,erd->efd", hidden, grad_rows, preferred_element_type=jnp.float32
    )
    grad_gate_local = jnp.einsum(
        "erd,erf->edf", expert_rows, grad_gate_pre, preferred_element_type=jnp.float32
    )
    grad_up_local = jnp.einsum(
        "erd,erf->edf", expert_rows, grad_up_pre, preferred_element_type=jnp.float32
    )
    rows_back = jnp.einsum(
        "erf,edf->erd", grad_gate_pre, w_gate, preferred_element_type=jnp.float32
    )
    rows_back = (
        rows_back
        + jnp.einsum("erf,edf->erd", grad_up_pre, w_up, preferred_element_type=jnp.float32)
    ).astype(jnp.bfloat16)
    returned_grad = from_experts(source_layout(rows_back, dp_count, row_count))
    grad_table = jnp.concatenate(
        [returned_grad.reshape(total_slots, part_width), jnp.zeros((1, part_width), jnp.bfloat16)],
        axis=0,
    )
    inner_gate = jnp.sum(gate_weights * grad_gates, axis=1, keepdims=True)
    grad_chosen = gate_weights * (grad_gates - inner_gate)
    grad_logits = jnp.einsum("tk,tke->te", grad_chosen, choose, precision=HIGHEST)
    grad_router_part = jnp.einsum("td,te->de", normed_float, grad_logits, precision=HIGHEST)
    grad_normed = jnp.sum(grad_table[pair_slot].astype(jnp.float32), axis=1)
    grad_normed = grad_normed + jnp.einsum(
        "te,de->td", grad_logits, router_float, precision=HIGHEST
    )
    grad_gain_two_part = jnp.sum(grad_normed * resid_mid * rstd_two[:, None], axis=0)
    scaled_two = grad_normed * gain_two
    inner_two = feature_total(jnp.sum(scaled_two * resid_mid, axis=1))
    grad_resid = (
        grad_top
        + rstd_two[:, None] * scaled_two
        - resid_mid * (rstd_two * rstd_two * rstd_two * inner_two / D)[:, None]
    )
    branch_rows = tokens_by_col(grad_resid.astype(jnp.bfloat16))
    grad_out_local = jnp.einsum(
        "tc,td->cd", mixed_rows, branch_rows, preferred_element_type=jnp.float32
    ).reshape(w_out.shape)
    picked = branch_rows
    grad_mixed = lax.psum_scatter(
        jnp.einsum("td,cd->tc", picked, out_flat, preferred_element_type=jnp.float32).astype(
            jnp.bfloat16
        ),
        "row",
        scatter_dimension=0,
        tiled=True,
    ).astype(jnp.float32)
    grad_mixed = grad_mixed.astype(jnp.bfloat16).reshape(
        seq_count, length, kv_local, group_size, HD
    )
    grad_query, grad_key, grad_values = lax.map(
        attend_backward, (query_rot, key_rot, value_low, segment_ids, log_total, grad_mixed)
    )
    grad_query = rotate_back(
        grad_query, cosine[None, :, None, None, :], sine_table[None, :, None, None, :]
    )
    grad_key = rotate_back(grad_key, cosine[None, :, None, :], sine_table[None, :, None, :])
    grad_qkv_pre = jnp.concatenate(
        [grad_query.reshape(seq_count, length, kv_local, group_size * HD), grad_key, grad_values],
        axis=-1,
    )
    grad_qkv_pre = grad_qkv_pre.astype(jnp.bfloat16).reshape(att_rows, -1)
    qkv_rows = tokens_by_row(grad_qkv_pre)
    grad_qkv_local = jnp.einsum(
        "td,tc->dc", group_rows, qkv_rows, preferred_element_type=jnp.float32
    ).reshape(w_qkv.shape)

    def normed_term(first_row, block_rows):
        return jnp.einsum("tc,dc->td", qkv_rows, qkv_flat, preferred_element_type=jnp.float32)

    grad_normed_one = col_scatter(normed_term, tok_rows)
    grad_gain_one_part = jnp.sum(grad_normed_one * resid_in * rstd_one[:, None], axis=0)
    scaled_one = grad_normed_one * gain_one
    inner_one = feature_total(jnp.sum(scaled_one * resid_in, axis=1))
    grad_in = (
        grad_resid
        + rstd_one[:, None] * scaled_one
        - resid_in * (rstd_one * rstd_one * rstd_one * inner_one / D)[:, None]
    )
    col_sums = (
        lax.psum(grad_gate_local.astype(jnp.bfloat16), "col").astype(jnp.float32),
        lax.psum(grad_up_local.astype(jnp.bfloat16), "col").astype(jnp.float32),
        lax.psum(grad_down_local.astype(jnp.bfloat16), "col").astype(jnp.float32),
        lax.psum(grad_router_part.astype(jnp.bfloat16), "col").astype(jnp.float32),
        lax.psum(grad_gain_one_part.astype(jnp.bfloat16), "col").astype(jnp.float32),
        lax.psum(grad_gain_two_part.astype(jnp.bfloat16), "col").astype(jnp.float32),
    )
    dp_sums = (
        lax.psum(grad_qkv_local.astype(jnp.bfloat16), "dp").astype(jnp.float32),
        lax.psum(grad_out_local.astype(jnp.bfloat16), "dp").astype(jnp.float32),
        lax.psum(col_sums[3].astype(jnp.bfloat16), "dp").astype(jnp.float32),
        lax.psum(col_sums[4].astype(jnp.bfloat16), "dp").astype(jnp.float32),
        lax.psum(col_sums[5].astype(jnp.bfloat16), "dp").astype(jnp.float32),
    )
    return (
        layer_sum.astype(jnp.bfloat16),
        grad_in,
        dp_sums[3],
        dp_sums[0],
        dp_sums[1],
        dp_sums[4],
        dp_sums[2],
        col_sums[0],
        col_sums[1],
        col_sums[2],
    )

WINDOW = 512
BLOCK_Q = 256
LANES = 128
SMALL_ROWS = 48
GAIN_ONE = EXPERTS
GAIN_TWO = EXPERTS + 1
RSTD_LANE = LANES - 1
RSTD_ROW = 8
FIRST, SECOND, LATE = 1, 3, 2
F32 = jnp.float32
LOW = jnp.bfloat16
VMEM_BYTES = 67_000_000


def dot_nn(a, b):
    return jnp.dot(a, b, preferred_element_type=F32)


def dot_nt(a, b):
    return lax.dot_general(a, b, (((1,), (1,)), ((), ())), preferred_element_type=F32)


def dot_tn(a, b):
    return lax.dot_general(a, b, (((0,), (0,)), ((), ())), preferred_element_type=F32)


def rope_lanes(length):
    positions = np.arange(length, dtype=np.float32)
    frequency = (ROPE_BASE ** (-2.0 * np.arange(HD // 2, dtype=np.float32) / HD)).astype(np.float32)
    angles = (positions[:, None] * frequency[None, :]).astype(np.float32)
    cosine, sine = np.cos(angles), np.sin(angles)
    signed = np.concatenate([-sine, sine], axis=1)
    double = np.concatenate([cosine, cosine], axis=1)
    ones, zeros = np.ones_like(double), np.zeros_like(double)
    return np.stack(
        [
            np.concatenate([double, double], axis=1),
            np.concatenate([signed, signed], axis=1),
            np.concatenate([double, ones], axis=1),
            np.concatenate([signed, zeros], axis=1),
        ]
    ).astype(np.float32)


def swap_halves(values):
    half = HD // 2
    lane = lax.broadcasted_iota(jnp.int32, values.shape, 1)
    ahead = pltpu.roll(values, LANES - half, 1)
    behind = pltpu.roll(values, half, 1)
    return jnp.where(lane % HD < half, ahead, behind)


def window_mask(seg_col, seg_row, q_start, k_start):
    shape = (seg_col.shape[0], seg_row.shape[1])
    q_at = lax.broadcasted_iota(jnp.int32, shape, 0) + q_start
    k_at = lax.broadcasted_iota(jnp.int32, shape, 1) + k_start
    return (q_at >= k_at) & (seg_col == seg_row)


def remote(src, dst, send_sem, recv_sem, where):
    return pltpu.make_async_remote_copy(
        src_ref=src, dst_ref=dst, send_sem=send_sem, recv_sem=recv_sem,
        device_id=where, device_id_type=pl.DeviceIdType.MESH,
    )


class Copies:
    def __init__(self, send_sems, recv_sems):
        self.send_sems, self.recv_sems = send_sems, recv_sems
        self.sends = self.recvs = 0
        self.open = []

    def receivers(self, number=1):
        first = self.recvs
        self.recvs += number
        return first

    def send(self, src, dst, receiver, where, when=None):
        at = self.sends
        self.sends += 1
        copy = remote(src, dst, self.send_sems.at[at], self.recv_sems.at[receiver], where)
        if when is None:
            copy.start()
        else:
            pl.when(when)(copy.start)
        self.open.append((copy, when))

    def plan(self, src, dst, receiver, where):
        at = self.sends
        self.sends += 1
        copy = remote(src, dst, self.send_sems.at[at], self.recv_sems.at[receiver], where)
        self.open.append((copy, None))
        return copy

    def local(self, src, dst, when=None):
        at = self.sends
        self.sends += 1
        copy = pltpu.make_async_copy(src, dst, self.send_sems.at[at])
        if when is None:
            copy.start()
        else:
            pl.when(when)(copy.start)
        return copy

    def arrived(self, dst, receiver, where):
        remote(dst, dst, self.recv_sems.at[receiver], self.recv_sems.at[receiver], where).wait_recv()

    def finish(self):
        for copy, when in self.open:
            if when is None:
                copy.wait_send()
            else:
                pl.when(when)(copy.wait_send)


class Place:
    def __init__(self, counts):
        self.dp_count, self.row_count, self.col_count = counts
        self.dp, self.row, self.col = (lax.axis_index(name) for name in ("dp", "row", "col"))
        self.pair_row = self.row + 1 - 2 * lax.rem(self.row, 2)
        self.far_row = lax.rem(self.row + 2, self.row_count)
        self.cross_row = lax.rem(self.pair_row + 2, self.row_count)
        self.other_dp = self.dp_count - 1 - self.dp
        self.here = (self.dp, self.row, self.col)
        self.pair = (self.dp, self.pair_row, self.col)
        self.far = (self.dp, self.far_row, self.col)
        self.over = (self.other_dp, self.row, self.col)
        self.over_far = (self.other_dp, self.far_row, self.col)

    def row_at(self, step):
        return lax.rem(self.row + step + self.row_count, self.row_count)

    def col_at(self, step):
        return lax.rem(self.col + step + self.col_count, self.col_count)

    def block(self, dp_at, col_at):
        return dp_at * self.col_count + col_at

    def plane(self):
        peers = [(self.dp, self.row_at(k), self.col) for k in range(1, self.row_count)]
        return peers + [(self.other_dp, self.row_at(k), self.col) for k in range(self.row_count)]

    def column(self):
        return [(self.dp, self.row, self.col_at(k)) for k in range(1, self.col_count)]


class Spread:
    def __init__(self, place, copies, blocks, col_at):
        self.place, self.copies = place, copies
        dp, row, far_row = place.dp, place.row, place.far_row
        same, other = place.block(dp, col_at), place.block(place.other_dp, col_at)
        self.own, self.far = blocks.at[same, row], blocks.at[same, far_row]
        self.over, self.corner = blocks.at[other, row], blocks.at[other, far_row]
        self.pairs_same = (blocks.at[same, place.pair_row], blocks.at[same, place.cross_row])
        self.pairs_other = (blocks.at[other, place.pair_row], blocks.at[other, place.cross_row])
        self.at = copies.receivers(7)
        self.to_pair = copies.plan(self.own, self.own, self.at, place.pair)
        self.to_far = copies.plan(self.own, self.own, self.at + 1, place.far)
        self.to_over = copies.plan(self.own, self.own, self.at + 2, place.over)
        self.far_pair = copies.plan(self.far, self.far, self.at + 4, place.pair)
        self.over_pair = copies.plan(self.over, self.over, self.at + 5, place.pair)
        self.corner_pair = copies.plan(self.corner, self.corner, self.at + 6, place.pair)
        self.turn = None

    def begin(self, with_over):
        self.to_far.start()
        if with_over:
            self.to_over.start()
        self.to_pair.start()

    def send_over(self):
        self.to_over.start()

    def plan_corner(self, by_over):
        if by_over:
            self.turn = self.copies.plan(self.far, self.far, self.at + 3, self.place.over)
        else:
            self.turn = self.copies.plan(self.over, self.over, self.at + 3, self.place.far)

    def pass_far(self, corner):
        self.copies.arrived(self.far, self.at + 1, self.place.far)
        if corner:
            if self.turn is None:
                self.plan_corner(True)
            self.turn.start()
        self.far_pair.start()

    def pass_over(self, corner):
        self.copies.arrived(self.over, self.at + 2, self.place.over)
        if corner:
            if self.turn is None:
                self.plan_corner(False)
            self.turn.start()
        self.over_pair.start()

    def pass_corner(self):
        self.copies.arrived(self.corner, self.at + 3, self.place.here)
        self.corner_pair.start()

    def complete_same(self):
        for k, piece in zip((0, 4), self.pairs_same):
            self.copies.arrived(piece, self.at + k, self.place.pair)

    def complete_other(self):
        for k, piece in zip((5, 6), self.pairs_other):
            self.copies.arrived(piece, self.at + k, self.place.pair)

    def complete(self):
        self.complete_same()
        self.complete_other()


def say_hello(peers):
    barrier = pltpu.get_barrier_semaphore()
    for peer in peers:
        pl.semaphore_signal(barrier, inc=1, device_id=peer, device_id_type=pl.DeviceIdType.MESH)
    return functools.partial(pl.semaphore_wait, barrier, len(peers))


def greet(peers):
    say_hello(peers)()


def attend_forward_kernel(
    counts, hidden_hbm, own_q_hbm, own_o_hbm, small_hbm, seg_hbm, cot_hbm, tab_hbm,
    resid_ref, low_ref, mix_hbm, normed_hbm, q_ref, k_ref, v_ref, lse_ref, wq_hbm, zo_ref, small_ref, seg_ref, cot_all,
    mix_ref, normed_ref, wq_ref, tab_ref, h_ref, zq_ref, own_ref, column_ref, send_sems, recv_sems,
):
    place = Place(counts)
    row_count, col_count = place.row_count, place.col_count
    copies = Copies(send_sems, recv_sems)
    parts, length, width = h_ref.shape
    kv_heads = k_ref.shape[0]
    features = parts * width
    chunks = length // BLOCK_Q
    greet(place.plane() + place.column())

    h_pair, h_far, h_cross = (copies.receivers() for _ in range(3))
    copies.send(hidden_hbm, h_ref.at[place.row], h_far, place.far)
    copies.send(hidden_hbm, h_ref.at[place.row], h_pair, place.pair)
    h_own = copies.local(hidden_hbm, h_ref.at[place.row])
    tab_in = copies.local(tab_hbm, tab_ref)
    zq_own = copies.local(own_q_hbm, zq_ref.at[place.col])
    zo_own = copies.local(own_o_hbm, zo_ref.at[place.col])
    small_own = copies.local(small_hbm, small_ref.at[place.row])
    seg_own = copies.local(seg_hbm, seg_ref.at[place.row])
    half_width = width // 2
    half, other_half = (
        pl.ds(pl.multiple_of(dp_at * half_width, half_width), half_width) for dp_at in (place.dp, place.other_dp)
    )
    mine = place.row == place.col
    zq_in = copies.receivers(col_count)
    zo_in = copies.receivers(col_count)
    for k in range(1, col_count):
        copies.send(
            own_q_hbm.at[half], zq_ref.at[place.col, half], zq_in + k, (place.dp, place.row, place.col_at(k))
        )
    small_in, seg_in = copies.receivers(row_count), copies.receivers(row_count)
    for k in range(1, row_count):
        copies.send(small_hbm, small_ref.at[place.row], small_in + k, (place.dp, place.row_at(k), place.col))
        copies.send(seg_hbm, seg_ref.at[place.row], seg_in + k, (place.dp, place.row_at(k), place.col))
    cot_own = copies.local(cot_hbm, own_ref)
    cot_pair, cot_over, cot_back = copies.receivers(), copies.receivers(), copies.receivers(3)
    cot_far, cot_corner = copies.receivers(2), copies.receivers(2)
    own_cot = cot_all.at[place.block(place.dp, place.col), place.row]
    far_cot = cot_all.at[place.block(place.dp, place.col), place.far_row]
    half_rows = length // 2

    def send_cot_far(half):
        window = pl.ds(half * half_rows, half_rows)
        copies.send(cot_hbm.at[window], own_cot.at[window], cot_far + half, place.far)

    def pass_cot_far(half):
        piece = far_cot.at[pl.ds(half * half_rows, half_rows)]
        copies.arrived(piece, cot_far + half, place.far)
        copies.send(piece, piece, cot_corner + half, place.over)

    copies.send(cot_hbm, own_cot, cot_over, place.over)
    copies.send(cot_hbm, own_cot, cot_pair, place.pair)

    copies.arrived(h_ref.at[place.far_row], h_far, place.far)
    copies.send(h_ref.at[place.far_row], h_ref.at[place.far_row], h_cross, place.pair)
    wq_in, wq_over = copies.receivers(row_count), copies.receivers(row_count)
    zq_own.wait()
    copies.send(
        zq_ref.at[place.col], wq_ref.at[place.row], wq_in + lax.rem(place.col - place.row + row_count, row_count),
        (place.dp, place.col, place.col), jnp.logical_not(mine),
    )
    wq_kept = [(copies.local(zq_ref.at[place.col], wq_ref.at[place.row], mine), mine)]
    for k in range(1, col_count):
        source = place.col_at(-k)
        piece, target = zq_ref.at[source, half], wq_ref.at[place.row, half]
        copies.arrived(piece, zq_in + k, place.here)
        step = lax.rem(source - place.row + row_count, row_count)
        copies.send(piece, target, wq_in + step, (place.dp, source, place.col), source != place.row)
        copies.send(piece, target, wq_over + step, (place.other_dp, source, place.col))
        wq_kept.append((copies.local(piece, target, source == place.row), source == place.row))

    for k in range(1, col_count):
        copies.send(own_o_hbm, zo_ref.at[place.col], zo_in + k, (place.dp, place.row, place.col_at(k)))
    send_cot_far(0)
    send_cot_far(1)
    cot_z = copies.receivers(col_count)
    for k in (FIRST,):
        copies.send(cot_hbm, own_cot, cot_z + k, (place.dp, place.row, place.col_at(k)))
    h_own.wait()
    copies.arrived(h_ref.at[place.pair_row], h_pair, place.pair)
    copies.arrived(h_ref.at[place.cross_row], h_cross, place.pair)
    small_own.wait()
    for k in range(1, row_count):
        copies.arrived(small_ref.at[place.row_at(-k)], small_in + k, place.here)

    @pl.loop(0, chunks)
    def _(chunk):
        rows = pl.ds(pl.multiple_of(chunk * BLOCK_Q, BLOCK_Q), BLOCK_Q)
        total = jnp.zeros((BLOCK_Q, 1), F32)
        for part in range(parts):
            piece = h_ref[part, rows, :].astype(F32)
            total = total + jnp.sum(piece * piece, axis=1, keepdims=True)
        rstd = lax.rsqrt(total / features + EPSILON)
        lse_ref[rows, :] = jnp.broadcast_to(rstd, (BLOCK_Q, LANES))
        for part in range(parts):
            piece = h_ref[part, rows, :].astype(F32)
            gain = small_ref[part, GAIN_ONE : GAIN_ONE + 1, :].astype(F32)
            normed_ref[rows, part * width : (part + 1) * width] = (piece * rstd * gain).astype(LOW)

    written = [copies.local(normed_ref, normed_hbm)]
    seg_own.wait()
    for k in range(1, row_count):
        copies.arrived(seg_ref.at[place.row_at(-k)], seg_in + k, place.here)
    segments = seg_ref[place.col]
    for start in range(0, length, LANES):
        column_ref[start : start + LANES, :] = jnp.broadcast_to(
            segments[0:1, start : start + LANES], (LANES, LANES)
        ).T

    cot_own.wait()
    cot_kept = copies.local(own_ref, own_cot)

    for copy, here in wq_kept:
        pl.when(here)(copy.wait)

    @pl.when(mine)
    def _():
        for k in range(1, row_count):
            copies.arrived(wq_ref.at[place.row_at(-k)], wq_in + k, place.here)

    @pl.when(jnp.logical_not(mine))
    def _():
        for k in range(row_count):
            if k > 0:
                copies.arrived(wq_ref.at[place.row_at(-k), half], wq_in + k, place.here)
            copies.arrived(wq_ref.at[place.row_at(-k), other_half], wq_over + k, place.here)

    written.append(copies.local(wq_ref, wq_hbm))
    tab_in.wait()

    @pl.loop(0, chunks)
    def _(chunk):
        rows = pl.ds(pl.multiple_of(chunk * BLOCK_Q, BLOCK_Q), BLOCK_Q)
        qkv = dot_nn(normed_ref[rows, :], wq_ref[...].reshape(features, -1))
        for head in range(kv_heads):
            base = head * 4 * HD
            queries = qkv[:, base : base + LANES]
            queries = queries * tab_ref[0, rows, :] + swap_halves(queries) * tab_ref[1, rows, :]
            others = qkv[:, base + LANES : base + 2 * LANES]
            others = others * tab_ref[2, rows, :] + swap_halves(others) * tab_ref[3, rows, :]
            q_ref[2 * head, rows, :] = queries[:, :HD].astype(LOW)
            q_ref[2 * head + 1, rows, :] = queries[:, HD:].astype(LOW)
            k_ref[head, rows, :] = others[:, :HD].astype(LOW)
            v_ref[head, rows, :] = others[:, HD:].astype(LOW)

    scale = HD**-0.5
    lane = lax.broadcasted_iota(jnp.int32, (BLOCK_Q, LANES), 1)
    mix_pair, mix_far, mix_cross = (copies.receivers(chunks) for _ in range(3))

    def pass_on(block):
        piece = mix_ref.at[place.far_row, pl.ds(block * BLOCK_Q, BLOCK_Q)]
        copies.arrived(piece, mix_far + block, place.far)
        copies.send(piece, piece, mix_cross + block, place.pair)

    for block in range(chunks):
        q_start = block * BLOCK_Q
        k_start = max(0, q_start - WINDOW)
        q_rows, k_rows = slice(q_start, q_start + BLOCK_Q), slice(k_start, q_start + BLOCK_Q)
        mask = window_mask(column_ref[q_rows, 0:1], segments[0:1, k_rows], q_start, k_start)

        @pl.loop(0, kv_heads)
        def _(kv):
            keys, vals = k_ref[kv, k_rows, :], v_ref[kv, k_rows, :]
            logs, outs = lse_ref[q_rows, :], []
            for half in range(2):
                head = 2 * kv + half
                scores = dot_nt(q_ref[head, q_rows, :], keys) * scale
                scores = jnp.where(mask, scores, NEG_LARGE)
                top = jnp.max(scores, axis=1, keepdims=True)
                weights = jnp.exp(scores - top)
                total = jnp.sum(weights, axis=1, keepdims=True)
                outs.append((dot_nn(weights.astype(LOW), vals) / total).astype(LOW))
                logs = jnp.where(lane == head, top + jnp.log(total), logs)
            lse_ref[q_rows, :] = logs
            mix_ref[place.row, q_rows, pl.ds(pl.multiple_of(kv * LANES, LANES), LANES)] = jnp.concatenate(
                outs, axis=1
            )

        piece = mix_ref.at[place.row, pl.ds(q_start, BLOCK_Q)]
        copies.send(piece, piece, mix_far + block, place.far)
        copies.send(piece, piece, mix_pair + block, place.pair)
        if block > 0:
            pass_on(block - 1)
        if block == 1:
            pass_cot_far(0)
        if block == 2:
            pass_cot_far(1)
            copies.send(far_cot, far_cot, cot_back, place.pair)
            over_cot = cot_all.at[place.block(place.other_dp, place.col), place.row]
            copies.arrived(over_cot, cot_over, place.over)
            copies.send(over_cot, over_cot, cot_back + 1, place.pair)
    written.append(copies.local(mix_ref.at[place.row], mix_hbm))
    pass_on(chunks - 1)
    corner_cot = cot_all.at[place.block(place.other_dp, place.col), place.far_row]
    for half in range(2):
        copies.arrived(
            corner_cot.at[pl.ds(half * half_rows, half_rows)], cot_corner + half, place.over
        )
    copies.send(corner_cot, corner_cot, cot_back + 2, place.pair)
    zo_own.wait()
    for k in range(1, col_count):
        copies.arrived(zo_ref.at[place.col_at(-k)], zo_in + k, place.here)
    for block in range(chunks):
        rows = slice(block * BLOCK_Q, (block + 1) * BLOCK_Q)
        window = pl.ds(block * BLOCK_Q, BLOCK_Q)
        copies.arrived(mix_ref.at[place.pair_row, window], mix_pair + block, place.pair)
        copies.arrived(mix_ref.at[place.cross_row, window], mix_cross + block, place.pair)
        branch = dot_nn(mix_ref[0, rows, :], zo_ref[0])
        for part in range(1, parts):
            branch = branch + dot_nn(mix_ref[part, rows, :], zo_ref[part])
        resid = h_ref[place.row, rows, :].astype(F32) + branch
        resid_ref[rows, :] = resid
        low_ref[rows, :] = resid.astype(LOW)

    for copy in written:
        copy.wait()
    cot_kept.wait()
    copies.arrived(cot_all.at[place.block(place.dp, place.col), place.pair_row], cot_pair, place.pair)
    for k, (dp_at, row_at) in enumerate(
        ((place.dp, place.cross_row), (place.other_dp, place.pair_row), (place.other_dp, place.cross_row))
    ):
        copies.arrived(cot_all.at[place.block(dp_at, place.col), row_at], cot_back + k, place.pair)
    for k in (FIRST,):
        copies.arrived(
            cot_all.at[place.block(place.dp, place.col_at(-k)), place.row], cot_z + k, place.here
        )
    copies.finish()


def attend_backward_kernel(
    counts, grad_low_hbm, grad_hbm, hidden_hbm, resid_hbm, wo_ref, wq_ref, normed_hbm, mix_hbm, q_ref, k_ref, v_ref, lse_ref,
    seg_ref, small_ref, part_ref, tab_hbm, y_hbm, res_given, cot_given, low_hbm,
    out_ref, grad_in_ref, grads_ref, sums_ref, res_all, cot_all,
    grad_ref, hidden_ref, resid_ref, normed_ref, tab_ref, gb_ref, mixed_ref, gm_ref, dq_ref, dk_ref, dv_ref, turn_ref, column_ref, y_own_ref, y_in_ref, y_chip_ref, y_last_ref,
    away_ref, pair_in_ref, own_ref, chip_ref, last_ref, inner_ref,
    send_sems, recv_sems,
):
    place = Place(counts)
    copies = Copies(send_sems, recv_sems)
    dp_count, row_count, col_count = counts
    parts, length, width = gb_ref.shape
    kv_heads = k_ref.shape[0]
    features = parts * width
    chunks = length // BLOCK_Q
    scale = HD**-0.5
    all_here = say_hello(place.plane() + place.column())
    segments = seg_ref[place.col]
    for start in range(0, length, LANES):
        column_ref[start : start + LANES, :] = jnp.broadcast_to(
            segments[0:1, start : start + LANES], (LANES, LANES)
        ).T
    dk_ref[...] = jnp.zeros_like(dk_ref)
    dv_ref[...] = jnp.zeros_like(dv_ref)
    all_here()

    def window(chunk):
        return pl.ds(chunk * BLOCK_Q, BLOCK_Q)

    blocks = range(chunks - 1, -1, -1)
    gb_far, gb_pair, gb_cross = (copies.receivers(chunks) for _ in range(3))
    for chunk in blocks:
        piece = gb_ref.at[place.row, window(chunk)]
        copies.send(grad_low_hbm.at[window(chunk)], piece, gb_far + chunk, place.far)
        copies.send(grad_low_hbm.at[window(chunk)], piece, gb_pair + chunk, place.pair)
    gb_own = copies.local(grad_low_hbm, gb_ref.at[place.row])
    tab_in = copies.local(tab_hbm, tab_ref)
    mix_own = copies.local(mix_hbm, mixed_ref)
    y_pair = copies.receivers(2 * dp_count)
    y_held = []
    for turn, dp_at in enumerate((place.other_dp, place.dp)):
        for q, (here, there) in enumerate(
            ((place.row, place.pair_row), (place.far_row, place.cross_row))
        ):
            copies.send(y_hbm.at[dp_at, there], y_in_ref.at[turn, q], y_pair + 2 * turn + q, place.pair)
            y_held.append(copies.local(y_hbm.at[dp_at, here], y_own_ref.at[turn, q]))

    first = Spread(place, copies, res_all, place.col_at(-FIRST))
    first.plan_corner(True)
    own_block = place.block(place.dp, place.col)
    late_in = copies.receivers(2)
    late = (place.dp, place.row, place.col_at(LATE))
    own_cot = cot_all.at[own_block, place.row]
    copies.send(low_hbm, res_all.at[own_block, place.row], late_in, late)
    copies.send(own_cot, own_cot, late_in + 1, late)
    late_reads = [
        copies.local(*pair)
        for pair in ((normed_hbm, normed_ref), (hidden_hbm, hidden_ref), (grad_hbm, grad_ref), (resid_hbm, resid_ref))
    ]
    gb_own.wait()

    def pass_on(chunk):
        piece = gb_ref.at[place.far_row, window(chunk)]
        copies.arrived(piece, gb_far + chunk, place.far)
        copies.send(piece, piece, gb_cross + chunk, place.pair)

    y_last = copies.receivers(3)

    def y_over():
        for copy in y_held:
            copy.wait()
        for q in range(2):
            copies.arrived(y_in_ref.at[0, q], y_pair + q, place.pair)
            y_chip_ref[0, q] = (y_own_ref[0, q].astype(F32) + y_in_ref[0, q].astype(F32)).astype(LOW)
            copies.send(y_chip_ref.at[0, q], y_last_ref.at[q], y_last + q, place.over)

    def y_far():
        for q in range(2):
            copies.arrived(y_in_ref.at[1, q], y_pair + 2 + q, place.pair)
            copies.arrived(y_last_ref.at[q], y_last + q, place.over)
        y_chip_ref[1, 1] = (
            y_own_ref[1, 1].astype(F32) + y_in_ref[1, 1].astype(F32) + y_last_ref[1].astype(F32)
        ).astype(LOW)
        copies.send(y_chip_ref.at[1, 1], y_last_ref.at[2], y_last + 2, place.far)

    away_in = [copies.receivers(chunks) for _ in range(2)]
    last_in = copies.receivers(chunks)

    def far_share(chunk):
        rows = slice(chunk * BLOCK_Q, (chunk + 1) * BLOCK_Q)
        copies.arrived(pair_in_ref.at[1, window(chunk)], away_in[1] + chunk, place.pair)
        chip_ref[rows, :] = (own_ref[1, rows, :] + pair_in_ref[1, rows, :].astype(F32)).astype(LOW)
        copies.send(chip_ref.at[window(chunk)], last_ref.at[window(chunk)], last_in + chunk, place.far)

    lane = lax.broadcasted_iota(jnp.int32, (BLOCK_Q, LANES), 1)
    y_over()
    first.begin(True)
    pass_on(chunks - 1)
    for block in blocks:
        q_start = block * BLOCK_Q
        k_start = max(0, q_start - WINDOW)
        q_rows, k_rows = slice(q_start, q_start + BLOCK_Q), slice(k_start, q_start + BLOCK_Q)
        copies.arrived(gb_ref.at[place.pair_row, window(block)], gb_pair + block, place.pair)
        copies.arrived(gb_ref.at[place.cross_row, window(block)], gb_cross + block, place.pair)
        total = dot_nt(gb_ref[0, q_rows, :], wo_ref[0])
        for part in range(1, parts):
            total = total + dot_nt(gb_ref[part, q_rows, :], wo_ref[part])
        gm_ref[...] = total.astype(LOW)
        mask = window_mask(column_ref[q_rows, 0:1], segments[0:1, k_rows], q_start, k_start)

        @pl.loop(0, kv_heads)
        def _(kv):
            keys, vals = k_ref[kv, k_rows, :], v_ref[kv, k_rows, :]
            lanes = pl.ds(pl.multiple_of(kv * LANES, LANES), LANES)
            both, logs, queried = gm_ref[:, lanes], lse_ref[q_rows, :], []
            for half in range(2):
                head = 2 * kv + half
                queries, grad = q_ref[head, q_rows, :], both[:, half * HD : (half + 1) * HD]
                scores = dot_nt(queries, keys) * scale
                log = jnp.sum(jnp.where(lane == head, logs, 0.0), axis=1, keepdims=True)
                weights = jnp.where(mask, jnp.exp(scores - log), 0.0)
                grad_weights = dot_nt(grad, vals)
                inner = jnp.sum(weights * grad_weights, axis=1, keepdims=True)
                grad_scores = (weights * (grad_weights - inner)).astype(LOW)
                dv_ref[kv, k_rows, :] += dot_tn(weights.astype(LOW), grad)
                dk_ref[kv, k_rows, :] += dot_tn(grad_scores, queries)
                queried.append(dot_nn(grad_scores, keys) * scale)
            dq_ref[:, lanes] = jnp.concatenate(queried, axis=1)

        if block > 0:
            pass_on(block - 1)
        if block == chunks - 1:
            tab_in.wait()
        for kv in range(kv_heads):
            base = kv * 4 * HD
            queries = dq_ref[:, kv * LANES : (kv + 1) * LANES]
            queries = queries * tab_ref[0, q_rows, :] - swap_halves(queries) * tab_ref[1, q_rows, :]
            others = jnp.concatenate([dk_ref[kv, q_rows, :] * scale, dv_ref[kv, q_rows, :]], axis=1)
            others = others * tab_ref[2, q_rows, :] - swap_halves(others) * tab_ref[3, q_rows, :]
            turn_ref[q_rows, base : base + LANES] = queries.astype(LOW)
            turn_ref[q_rows, base + LANES : base + 2 * LANES] = others.astype(LOW)
        for q, row_at in ((1, place.cross_row), (0, place.pair_row)):
            away_ref[q, q_rows, :] = dot_nt(turn_ref[q_rows, :], wq_ref[row_at]).astype(LOW)
            copies.send(
                away_ref.at[q, window(block)], pair_in_ref.at[q, window(block)], away_in[q] + block, place.pair
            )
        for q, row_at in ((1, place.far_row), (0, place.row)):
            own_ref[q, q_rows, :] = dot_nt(turn_ref[q_rows, :], wq_ref[row_at])
        if block < chunks - 1:
            far_share(block + 1)
        if block == chunks - 2:
            y_far()
        if block == 0:
            first.pass_far(True)
            first.pass_over(False)

    columns = turn_ref.shape[1]
    mix_own.wait()
    for copy in late_reads:
        copy.wait()
    far_share(0)

    @pl.loop(0, parts)
    def _(part):
        features_here = pl.ds(pl.multiple_of(part * width, width), width)
        grads_ref[part, :, :columns] = dot_tn(normed_ref[:, features_here], turn_ref[...]).astype(LOW)
        grads_ref[part, :, columns:] = dot_tn(mixed_ref[...], gb_ref[part]).astype(LOW)

    gain = small_ref[place.row, GAIN_ONE : GAIN_ONE + 1, :].astype(F32)
    inner_in = copies.receivers(row_count)
    gain_sum = jnp.zeros((1, width), F32)
    for chunk in blocks:
        rows = slice(chunk * BLOCK_Q, (chunk + 1) * BLOCK_Q)
        copies.arrived(pair_in_ref.at[0, window(chunk)], away_in[0] + chunk, place.pair)
        copies.arrived(last_ref.at[window(chunk)], last_in + chunk, place.far)
        grad_normed = own_ref[0, rows, :] + pair_in_ref[0, rows, :].astype(F32) + last_ref[rows, :].astype(F32)
        own_ref[0, rows, :] = grad_normed
        along = grad_normed * hidden_ref[rows, :].astype(F32)
        gain_sum = gain_sum + jnp.sum(along * lse_ref[rows, RSTD_LANE : RSTD_LANE + 1], axis=0, keepdims=True)
        inner_ref[place.row, 0:1, rows] = row_of(jnp.sum(along * gain, axis=1, keepdims=True))
    sums_ref[...] = part_ref[...]
    sums_ref[GAIN_ONE : GAIN_ONE + 1, :] = gain_sum
    for k in range(1, row_count):
        copies.send(
            inner_ref.at[place.row], inner_ref.at[place.row], inner_in + k, (place.dp, place.row_at(k), place.col)
        )
    copies.arrived(y_last_ref.at[2], y_last + 2, place.far)
    for chunk in range(chunks):
        rows = slice(chunk * BLOCK_Q, (chunk + 1) * BLOCK_Q)
        mixture = y_own_ref[1, 0, rows, :].astype(F32) + y_in_ref[1, 0, rows, :].astype(F32)
        for slot in (0, 2):
            mixture = mixture + y_last_ref[slot, rows, :].astype(F32)
        out_ref[rows, :] = (resid_ref[rows, :] + mixture).astype(LOW)

    for k in range(1, row_count):
        copies.arrived(inner_ref.at[place.row_at(-k)], inner_in + k, place.here)
    inner = inner_ref[0, 0:1, :]
    for part in range(1, row_count):
        inner = inner + inner_ref[part, 0:1, :]
    for chunk in range(chunks):
        rows = slice(chunk * BLOCK_Q, (chunk + 1) * BLOCK_Q)
        rstd = lse_ref[rows, RSTD_LANE : RSTD_LANE + 1]
        cube = rstd * rstd * rstd * column_of(inner[:, rows]) / features
        grad_in_ref[rows, :] = (
            grad_ref[rows, :] + rstd * (own_ref[0, rows, :] * gain) - hidden_ref[rows, :].astype(F32) * cube
        )
    first.pass_corner()
    first.complete()
    z_shard = (place.block(place.dp, place.col_at(-LATE)), place.row)
    copies.arrived(res_all.at[z_shard], late_in, place.here)
    copies.arrived(cot_all.at[z_shard], late_in + 1, place.here)
    copies.finish()


def expert_grads(gate_pre, up_pre, grad_hidden):
    sig = 1.0 / (1.0 + jnp.exp(-gate_pre))
    silu = gate_pre * sig
    grad_gate = grad_hidden * up_pre * (sig * (1.0 + gate_pre * (1.0 - sig)))
    return (silu * up_pre).astype(LOW), grad_gate.astype(LOW), (grad_hidden * silu).astype(LOW)


def slot_picks(rank_row, capacity):
    at = lax.broadcasted_iota(jnp.int32, (capacity, rank_row.shape[1]), 0).astype(F32)
    return at == rank_row


def column_of(row):
    return jnp.broadcast_to(row, (LANES, row.shape[1])).T[:, 0:1]


def row_of(column):
    return jnp.broadcast_to(column, (column.shape[0], LANES)).T[0:1, :]


def experts_kernel(
    counts, low_hbm, resid_ref, cot_own_ref, packed_hbm, cot_given, small_ref, zo_hbm, wg_hbm, wu_hbm, wd_hbm,
    y_hbm, grad_ref, grad_low_ref, table_ref, part_ref, wo_hbm, cot_all, res_all, slots_x, slots_g, slots_mid,
    wg_ref, wu_ref, wd_ref, res_ref, cot_ref, x_ref, packed_ref, rank_ref, gate_ref, g_ref, pick_ref, eo_ref, back_ref,
    away_ref, pair_in_ref, own_ref, chip_ref, last_ref, stage_ref, gg_ref, gg_in_ref, rstd_ref, inner_ref, nx_ref,
    keep_x_ref, keep_g_ref, keep_mid_ref, keep_sems,
    send_sems, recv_sems,
):
    place = Place(counts)
    copies = Copies(send_sems, recv_sems)
    dp_count, row_count, col_count = counts
    _, parts, length, width = res_ref.shape
    experts, features, hidden_width = wg_ref.shape
    capacity = pick_ref.shape[0] // experts
    chunks = length // BLOCK_Q
    total_experts = dp_count * row_count * experts
    pair_count = length * TOP
    first_expert = (place.dp * row_count + place.row) * experts
    order = (place.other_dp, place.dp)
    all_here = say_hello(place.plane() + place.column())
    packed_own = copies.local(packed_hbm, packed_ref.at[place.dp])
    cot_in = [
        copies.local(cot_all.at[place.block(dp_at, place.col)], cot_ref.at[dp_at])
        for dp_at in (place.dp, place.other_dp)
    ]

    weights_in = [copies.local(*pair) for pair in ((wg_hbm, wg_ref), (wu_hbm, wu_ref), (wd_hbm, wd_ref))]

    def ranks_of(dp_at):
        ids = packed_ref[dp_at] // pair_count
        orders = (packed_ref[dp_at] - ids * pair_count).astype(F32)
        rows = []
        for e in range(experts):
            match = ids == first_expert + e
            known = jnp.max(jnp.where(match, 1.0, 0.0), axis=0, keepdims=True)
            at = jnp.sum(jnp.where(match, orders, 0.0), axis=0, keepdims=True)
            rows.append(jnp.where(known > 0.0, at, float(pair_count)))
        stacked = jnp.concatenate(rows + [jnp.zeros((LANES - experts, length), F32)], axis=0)
        columns = stacked.T
        for e in range(experts):
            count = jnp.zeros((1, length), F32)
            for start in range(0, length, BLOCK_Q):
                before = columns[start : start + BLOCK_Q, e : e + 1] < rows[e]
                count = count + jnp.sum(jnp.where(before, 1.0, 0.0), axis=0, keepdims=True)
            rank_ref[dp_at, e : e + 1, :] = jnp.where(rows[e] < float(pair_count), count, -1.0)

    def gather_grads(dp_at):
        @pl.loop(0, experts)
        def _(e):
            pick = slot_picks(rank_ref[dp_at, pl.ds(e, 1), :], capacity).astype(F32).astype(LOW)
            slots = pl.ds(pl.multiple_of(e * capacity, capacity), capacity)
            for part in range(parts):
                g_ref[dp_at, part, slots, :] = dot_nn(pick, cot_ref[dp_at, part]).astype(LOW)

    packed_own.wait()
    ranks_of(place.dp)
    cot_in[0].wait()
    gather_grads(place.dp)
    all_here()

    own_low = res_ref.at[place.dp, place.row]
    packed_over = copies.receivers()
    copies.send(packed_hbm, packed_ref.at[place.dp], packed_over, place.over)
    low_own = copies.local(low_hbm, own_low)
    halves = 2
    half_rows = length // halves
    res_at = copies.receivers(7 * halves)

    def halved(ref, half):
        return ref.at[pl.ds(half * half_rows, half_rows)]

    far_low = res_ref.at[place.dp, place.far_row]
    over_low = res_ref.at[place.other_dp, place.row]
    corner_low = res_ref.at[place.other_dp, place.far_row]
    for half in range(halves):
        source, target = halved(low_hbm, half), halved(own_low, half)
        copies.send(source, target, res_at + half, place.far)
        copies.send(source, target, res_at + halves + half, place.over)
    copies.send(low_hbm, own_low, res_at + 2 * halves, place.pair)
    own_block = place.block(place.dp, place.col)
    res_z, cot_z = copies.receivers(col_count), copies.receivers(col_count)
    for k, on_cot in ((SECOND, True), (FIRST, False), (SECOND, False)):
        peer = (place.dp, place.row, place.col_at(k))
        if on_cot:
            own_cot = cot_all.at[own_block, place.row]
            copies.send(own_cot, own_cot, cot_z + k, peer)
        else:
            copies.send(low_hbm, res_all.at[own_block, place.row], res_z + k, peer)

    def pass_side(half):
        copies.arrived(halved(far_low, half), res_at + half, place.far)
        copies.arrived(halved(over_low, half), res_at + halves + half, place.over)
        corner, peer = (far_low, place.over) if half == 0 else (over_low, place.far)
        copies.send(halved(corner, half), halved(corner, half), res_at + 3 * halves + half, peer)
        for k, ref in ((4, far_low), (5, over_low)):
            copies.send(halved(ref, half), halved(ref, half), res_at + k * halves + half, place.pair)

    def pass_corner(half):
        copies.arrived(halved(corner_low, half), res_at + 3 * halves + half, place.here)
        copies.send(
            halved(corner_low, half), halved(corner_low, half), res_at + 6 * halves + half, place.pair
        )

    copies.arrived(packed_ref.at[place.other_dp], packed_over, place.over)
    ranks_of(place.other_dp)
    pass_side(0)
    cot_in[1].wait()
    gather_grads(place.other_dp)
    pass_side(1)
    pass_corner(0)
    pass_corner(1)

    wo_in = copies.receivers(row_count)
    own_wo = copies.local(zo_hbm.at[place.row], stage_ref.at[0, pl.ds(0, zo_hbm.shape[1])])

    low_own.wait()
    copies.arrived(res_ref.at[place.dp, place.pair_row], res_at + 2 * halves, place.pair)
    for half in range(halves):
        for k, dp_at, row_at in (
            (4, place.dp, place.cross_row), (5, place.other_dp, place.pair_row), (6, place.other_dp, place.cross_row)
        ):
            copies.arrived(halved(res_ref.at[dp_at, row_at], half), res_at + k * halves + half, place.pair)
    for copy in weights_in:
        copy.wait()
    own_wo.wait()
    kept_wo = copies.local(stage_ref.at[0, pl.ds(0, zo_hbm.shape[1])], wo_hbm.at[place.row])
    kept_wo.wait()
    res_kept = [
        copies.local(res_ref.at[dp_at], res_all.at[place.block(dp_at, place.col)])
        for dp_at in (place.dp, place.other_dp)
    ]
    first, second = (Spread(place, copies, cot_all, place.col_at(-k)) for k in (FIRST, SECOND))
    first.plan_corner(False)
    second.plan_corner(True)
    first.begin(True)
    copies.arrived(
        cot_all.at[place.block(place.dp, place.col_at(-SECOND)), place.row], cot_z + SECOND, place.here
    )
    second.begin(True)

    own_scaled = place.row
    gg_same, gg_other = copies.receivers(row_count), copies.receivers(row_count)
    pair_in = copies.receivers(2 * dp_count)
    last_over, last_across, last_far = (copies.receivers() for _ in range(3))
    table_in = copies.receivers(col_count)

    kept_pairs = ((keep_x_ref, slots_x), (keep_g_ref, slots_g), (keep_mid_ref, slots_mid))
    for turn, dp_at in enumerate(order):
        last = turn == dp_count - 1

        @pl.loop(0, chunks)
        def _(chunk):
            rows = pl.ds(pl.multiple_of(chunk * BLOCK_Q, BLOCK_Q), BLOCK_Q)
            total = jnp.zeros((BLOCK_Q, 1), F32)
            for part in range(parts):
                piece = res_ref[dp_at, part, rows, :].astype(F32)
                total = total + jnp.sum(piece * piece, axis=1, keepdims=True)
            rstd = lax.rsqrt(total / features + EPSILON)
            for part in range(parts):
                piece = res_ref[dp_at, part, rows, :].astype(F32)
                gain = small_ref[part, GAIN_TWO : GAIN_TWO + 1, :].astype(F32)
                x_ref[rows, part * width : (part + 1) * width] = (piece * rstd * gain).astype(LOW)
            table_ref[place.col, dp_at, RSTD_ROW : RSTD_ROW + 1, rows] = row_of(rstd)
            if last:
                rstd_ref[rows, :] = jnp.broadcast_to(rstd, (BLOCK_Q, LANES))
                piece = res_ref[dp_at, own_scaled, rows, :].astype(F32)
                gain = small_ref[own_scaled, GAIN_TWO : GAIN_TWO + 1, :].astype(F32)
                nx_ref[rows, :] = (piece * rstd * gain).astype(LOW)

        logits = jnp.zeros((total_experts, length), F32)
        for part in range(parts):
            logits = logits + dot_nt(
                small_ref[part, :total_experts, :], x_ref[:, part * width : (part + 1) * width]
            )
        ids = packed_ref[dp_at] // pair_count
        expert_at = lax.broadcasted_iota(jnp.int32, (total_experts, length), 0)
        chosen = expert_at == ids[0:1, :]
        for k in range(1, TOP):
            chosen = chosen | (expert_at == ids[k : k + 1, :])
        shown = jnp.where(chosen, logits, NEG_LARGE)
        weights = jnp.where(chosen, jnp.exp(shown - jnp.max(shown, axis=0, keepdims=True)), 0.0)
        gate_ref[...] = weights / jnp.sum(weights, axis=0, keepdims=True)
        table_ref[place.col, dp_at, 0:experts, :] = rank_ref[dp_at, 0:experts, :]
        for e in range(experts):
            table_ref[place.col, dp_at, experts + e : experts + e + 1, :] = gate_ref[pl.ds(first_expert + e, 1), :]

        @pl.loop(0, experts)
        def _(e):
            if last:

                @pl.when(e == 1)
                def _():
                    second.pass_far(True)
                    second.pass_over(False)

                pl.when(e == experts - 1)(first.pass_corner)


            keep = lax.rem(e, 2)
            kept = [
                pltpu.make_async_copy(held.at[keep], target.at[turn, e], keep_sems.at[k, keep])
                for k, (held, target) in enumerate(kept_pairs)
            ]

            @pl.when(e + turn * experts >= 2)
            def _():
                for copy in kept:
                    copy.wait()

            here = slot_picks(rank_ref[dp_at, pl.ds(e, 1), :], capacity)
            pick = here.astype(F32).astype(LOW)
            slots = pl.ds(pl.multiple_of(e * capacity, capacity), capacity)
            pick_ref[slots, :] = pick
            gate_slot = jnp.sum(
                jnp.where(here, gate_ref[pl.ds(first_expert + e, 1), :], 0.0), axis=1, keepdims=True
            )
            x = dot_nn(pick, x_ref[...]).astype(LOW)
            keep_x_ref[keep] = x
            grad_hidden = jnp.zeros((capacity, hidden_width), F32)
            for part in range(parts):
                pair_grad = (g_ref[dp_at, part, slots, :].astype(F32) * gate_slot).astype(LOW)
                keep_g_ref[keep, :, part * width : (part + 1) * width] = pair_grad
                grad_hidden = grad_hidden + dot_nt(
                    pair_grad, wd_ref[e, :, part * width : (part + 1) * width]
                )
            hidden, grad_gate, grad_up = expert_grads(dot_nn(x, wg_ref[e]), dot_nn(x, wu_ref[e]), grad_hidden)
            keep_mid_ref[keep, 0] = hidden
            keep_mid_ref[keep, 1] = grad_gate
            keep_mid_ref[keep, 2] = grad_up
            for copy in kept:
                copy.start()
            along = jnp.zeros((capacity, 1), F32)
            for part in range(parts):
                cols = slice(part * width, (part + 1) * width)
                out = dot_nn(hidden, wd_ref[e, :, cols]).astype(LOW).astype(F32)
                along = along + jnp.sum(g_ref[dp_at, part, slots, :].astype(F32) * out, axis=1, keepdims=True)
                eo_ref[part, slots, :] = (out * gate_slot).astype(LOW)
                back_ref[part, slots, :] = (
                    dot_nt(grad_gate, wg_ref[e, cols, :]) + dot_nt(grad_up, wu_ref[e, cols, :])
                ).astype(LOW)
            gg_ref[dp_at, pl.ds(e, 1), :] = jnp.sum(jnp.where(here, along, 0.0), axis=0, keepdims=True)

        if not last:
            first.pass_far(False)
            first.pass_over(True)
        owner = place.dp * row_count + place.row
        if last:
            for k in range(1, row_count):
                copies.send(gg_ref.at[dp_at], gg_in_ref.at[owner], gg_same + k, (dp_at, place.row_at(k), place.col))
            gg_in_ref[owner] = gg_ref[dp_at]
        else:
            for k in range(row_count):
                copies.send(gg_ref.at[dp_at], gg_in_ref.at[owner], gg_other + k, (dp_at, place.row_at(k), place.col))

        for q, row_at in enumerate((place.pair_row, place.cross_row)):
            away_ref[turn, q] = dot_tn(pick_ref[...], back_ref[row_at]).astype(LOW)
            copies.send(away_ref.at[turn, q], pair_in_ref.at[turn, q], pair_in + 2 * turn + q, place.pair)
        for q, row_at in enumerate((place.far_row, place.row)):
            own_ref[q] = dot_tn(pick_ref[...], back_ref[row_at])
        copies.arrived(pair_in_ref.at[turn, 1], pair_in + 2 * turn + 1, place.pair)
        far_sum = own_ref[0] + pair_in_ref[turn, 1].astype(F32)
        if last:
            copies.arrived(last_ref.at[1], last_across, place.over)
            chip_ref[turn, 1] = (far_sum + last_ref[1].astype(F32)).astype(LOW)
            copies.send(chip_ref.at[turn, 1], last_ref.at[2], last_far, place.far)
        else:
            chip_ref[turn, 1] = far_sum.astype(LOW)
            copies.send(chip_ref.at[turn, 1], last_ref.at[1], last_across, place.over)
        copies.arrived(pair_in_ref.at[turn, 0], pair_in + 2 * turn, place.pair)
        if last:
            own_ref[1] = own_ref[1] + pair_in_ref[turn, 0].astype(F32)
        else:
            chip_ref[turn, 0] = (own_ref[1] + pair_in_ref[turn, 0].astype(F32)).astype(LOW)
            copies.send(chip_ref.at[turn, 0], last_ref.at[0], last_over, place.over)
            for k in range(col_count):
                source = place.col_at(k)
                mine = source == place.row
                step = lax.rem(source - place.row + row_count, row_count)
                copies.send(
                    zo_hbm.at[source], wo_hbm.at[place.row], wo_in + step, (place.dp, source, place.col), jnp.logical_not(mine)
                )

        for part in range(parts):
            stage_ref[part] = dot_tn(pick_ref[...], eo_ref[part]).astype(LOW)
        kept = copies.local(stage_ref, y_hbm.at[dp_at])
        kept.wait()

    for k in range(1, col_count):
        copies.send(table_ref.at[place.col], table_ref.at[place.col], table_in + k, (place.dp, place.row, place.col_at(k)))

    for k in range(1, row_count):
        copies.arrived(gg_in_ref.at[place.dp * row_count + place.row_at(-k)], gg_same + k, place.here)
    for k in range(row_count):
        copies.arrived(gg_in_ref.at[place.other_dp * row_count + place.row_at(-k)], gg_other + k, place.here)
    along = jnp.concatenate([gg_in_ref[owner, :experts, :] for owner in range(dp_count * row_count)], axis=0)
    gates = gate_ref[...]
    grad_logits = (gates * (along - jnp.sum(gates * along, axis=0, keepdims=True))).astype(LOW)
    router = small_ref[place.row, :total_experts, :]
    gain = small_ref[place.row, GAIN_TWO : GAIN_TWO + 1, :].astype(F32)
    part_ref[...] = jnp.zeros_like(part_ref)
    part_ref[:total_experts, :] = dot_nn(grad_logits, nx_ref[...])
    own_ref[1] = own_ref[1] + dot_tn(grad_logits, router)

    copies.arrived(last_ref.at[0], last_over, place.over)
    copies.arrived(last_ref.at[2], last_far, place.far)
    inner_in = copies.receivers(row_count)
    gain_sum = jnp.zeros((1, width), F32)
    for chunk in range(chunks):
        rows = slice(chunk * BLOCK_Q, (chunk + 1) * BLOCK_Q)
        grad_normed = own_ref[1, rows, :]
        for k in (0, 2):
            grad_normed = grad_normed + last_ref[k, rows, :].astype(F32)
        own_ref[0, rows, :] = grad_normed
        along = grad_normed * resid_ref[rows, :]
        gain_sum = gain_sum + jnp.sum(along * rstd_ref[rows, 0:1], axis=0, keepdims=True)
        inner_ref[place.row, 0:1, rows] = row_of(jnp.sum(along * gain, axis=1, keepdims=True))
    part_ref[GAIN_TWO : GAIN_TWO + 1, :] = gain_sum
    for k in range(1, row_count):
        copies.send(
            inner_ref.at[place.row], inner_ref.at[place.row], inner_in + k, (place.dp, place.row_at(k), place.col)
        )
    for k in range(1, row_count):
        copies.arrived(inner_ref.at[place.row_at(-k)], inner_in + k, place.here)
    inner = inner_ref[0, 0:1, :]
    for part in range(1, row_count):
        inner = inner + inner_ref[part, 0:1, :]
    for chunk in range(chunks):
        rows = slice(chunk * BLOCK_Q, (chunk + 1) * BLOCK_Q)
        rstd = rstd_ref[rows, 0:1]
        cube = rstd * rstd * rstd * column_of(inner[:, rows]) / features
        grad = (
            cot_own_ref[rows, :].astype(F32) + rstd * (own_ref[0, rows, :] * gain) - resid_ref[rows, :] * cube
        )
        grad_ref[rows, :] = grad
        grad_low_ref[rows, :] = grad.astype(LOW)

    for copy in res_kept:
        copy.wait()
    for keep in range(2):
        for k, (held, target) in enumerate(kept_pairs):
            pltpu.make_async_copy(held.at[keep], target.at[0, 0], keep_sems.at[k, keep]).wait()
    second.pass_corner()
    first.complete()
    second.complete()
    for k in (FIRST, SECOND):
        z_shard = (place.block(place.dp, place.col_at(-k)), place.row)
        copies.arrived(res_all.at[z_shard], res_z + k, place.here)
    for k in range(1, row_count):
        copies.arrived(wo_hbm.at[place.row_at(-k)], wo_in + k, place.here)
    for k in range(1, col_count):
        copies.arrived(table_ref.at[place.col_at(-k)], table_in + k, place.here)
    copies.finish()


def slot_grads(picked, rank_row, gate_row, rstd_row, res, cot, small_ref, wg, wu, wd):
    here = slot_picks(rank_row, picked)
    pick = here.astype(F32).astype(LOW)
    gate_slot = jnp.sum(jnp.where(here, gate_row, 0.0), axis=1, keepdims=True)
    rstd_slot = jnp.sum(jnp.where(here, rstd_row, 0.0), axis=1, keepdims=True)
    parts = res.shape[0]
    x = jnp.concatenate(
        [
            (
                dot_nn(pick, res[part]) * rstd_slot * small_ref[part, GAIN_TWO : GAIN_TWO + 1, :].astype(F32)
            ).astype(LOW)
            for part in range(parts)
        ],
        axis=1,
    )
    pair_grad = jnp.concatenate(
        [(dot_nn(pick, cot[part]) * gate_slot).astype(LOW) for part in range(parts)], axis=1
    )
    hidden, grad_gate, grad_up = expert_grads(dot_nn(x, wg), dot_nn(x, wu), dot_nt(pair_grad, wd))
    return x, pair_grad, hidden, grad_gate, grad_up


def weight_grads_kernel(
    counts, res_given, cot_given, grads_hbm, slots_x, slots_g, slots_mid, part_ref, table_ref, small_ref,
    wg_hbm, wu_hbm, wd_hbm,
    res_all, cot_all, dg_hbm, du_hbm, dd_hbm, own_ref, sums_ref,
    wg_ref, wu_ref, wd_ref, parts_ref, dg_ref, du_ref, dd_ref, res_ref, cot_ref, x_ref, g_ref, mid_ref, grads_in_ref, sum_ref,
    sems, keep_sems, out_sems, send_sems, recv_sems,
):
    place = Place(counts)
    copies = Copies(send_sems, recv_sems)
    dp_count, row_count, col_count = counts
    experts = wg_ref.shape[0]
    _, parts, length, width = res_all.shape
    capacity = length * TOP // (dp_count * row_count * experts)
    far_side = [(place.other_dp, place.row, place.col_at(k)) for k in range(1, col_count)]
    all_here = say_hello(
        place.plane()
        + place.column()
        + [
            (place.dp, place.row_at(j), place.col_at(k))
            for j in range(1, row_count)
            for k in range(1, col_count)
        ]
        + far_side
    )
    steps = 5
    before_late = 4 * experts

    def fetch(step):
        back = jnp.where(step < 2, FIRST, jnp.where(step < 4, SECOND, LATE))
        dp_at = lax.rem(place.dp + lax.rem(step, 2), dp_count)
        col_at = place.col_at(-back)
        b, slot = place.block(dp_at, col_at), lax.rem(step, 2)
        return dp_at, col_at, slot, (
            pltpu.make_async_copy(res_all.at[b], res_ref.at[slot], sems.at[slot]),
            pltpu.make_async_copy(cot_all.at[b], cot_ref.at[slot], sems.at[2 + slot]),
        )

    def kept_slots(turn):
        at, e, slot = turn // experts, lax.rem(turn, experts), lax.rem(turn, 2)
        pairs = ((slots_x, x_ref), (slots_g, g_ref), (slots_mid, mid_ref))
        return [
            pltpu.make_async_copy(source.at[at, e], target.at[slot], keep_sems.at[k, slot])
            for k, (source, target) in enumerate(pairs)
        ]

    for copy in fetch(0)[3]:
        copy.start()
    weights_in = [copies.local(*pair) for pair in ((wg_hbm, wg_ref), (wu_hbm, wu_ref), (wd_hbm, wd_ref))]
    for copy in kept_slots(0):
        copy.start()
    parts_ref[0] = part_ref[...]
    others = place.column() + [place.over] + far_side
    sums_in = copies.receivers(len(others) + 1)
    sum_sends = [
        copies.plan(parts_ref.at[0], parts_ref.at[k + 1], sums_in + k + 1, peer) for k, peer in enumerate(others)
    ]

    grads_in = copies.receivers(col_count)
    grads_kept = copies.local(grads_hbm.at[place.col], grads_in_ref.at[place.col])
    mine = place.row == place.col
    over_in, swap_in = copies.receivers(), copies.receivers()
    to_over = copies.plan(sum_ref.at[0], sum_ref.at[1], over_in, place.over)
    to_swap = remote(
        sum_ref.at[2], sum_ref.at[3], copies.send_sems.at[copies.sends], copies.recv_sems.at[swap_in],
        (place.dp, place.col, place.row),
    )
    copies.sends += 1
    copies.open.append((to_swap, jnp.logical_not(mine)))
    two_res, three_res, three_cot = (
        Spread(place, copies, array, place.col_at(-k))
        for k, array in ((SECOND, res_all), (LATE, res_all), (LATE, cot_all))
    )
    for spread, by_over in ((two_res, True), (three_res, True), (three_cot, False)):
        spread.plan_corner(by_over)
    grad_sends = [
        copies.plan(
            grads_hbm.at[place.col_at(k)], grads_in_ref.at[place.col], grads_in + k,
            (place.dp, place.row, place.col_at(k)),
        )
        for k in range(1, col_count)
    ]

    def begin():
        all_here()
        two_res.begin(True)
        three_res.begin(True)
        three_cot.begin(False)
        for copy in grad_sends + sum_sends:
            copy.start()

    def sum_columns():
        grads_kept.wait()
        for k in range(1, col_count):
            copies.arrived(grads_in_ref.at[place.col_at(-k)], grads_in + k, place.here)
        total = grads_in_ref[0].astype(F32)
        for col_at in range(1, col_count):
            total = total + grads_in_ref[col_at].astype(F32)
        sum_ref[0] = total.astype(LOW)
        to_over.start()

    def sum_over():
        copies.arrived(sum_ref.at[1], over_in, place.over)
        total = sum_ref[0].astype(F32) + sum_ref[1].astype(F32)
        sum_ref[2] = total.astype(LOW)
        own_ref[...] = total
        pl.when(jnp.logical_not(mine))(to_swap.start)

    def sum_parts():
        total = parts_ref[0]
        for k in range(len(others)):
            copies.arrived(parts_ref.at[k + 1], sums_in + k + 1, place.here)
            total = total + parts_ref[k + 1]
        sums_ref[...] = total

    def take_swapped():
        @pl.when(jnp.logical_not(mine))
        def _():
            copies.arrived(sum_ref.at[3], swap_in, place.here)
            own_ref[...] = sum_ref[3].astype(F32)

    events = {
        1: [begin],
        5: [lambda: two_res.pass_far(True), lambda: two_res.pass_over(False), three_cot.send_over],
        7: [two_res.complete_same],
        10: [lambda: three_res.pass_far(True), lambda: three_res.pass_over(False)],
        12: [two_res.pass_corner, lambda: three_cot.pass_far(False), two_res.complete_other, sum_columns],
        15: [lambda: three_cot.pass_over(True), three_res.complete_same, three_cot.complete_same],
        16: [three_res.pass_corner, sum_over],
        18: [three_cot.pass_corner],
        19: [sum_parts],
    }
    dg_ref[...] = jnp.zeros_like(dg_ref)
    du_ref[...] = jnp.zeros_like(du_ref)
    dd_ref[...] = jnp.zeros_like(dd_ref)
    for copy in weights_in:
        copy.wait()

    def other_blocks(turn):
        step, e = turn // experts, lax.rem(turn, experts)
        for at, actions in events.items():

            @pl.when(turn == at)
            def _(actions=actions):
                for action in actions:
                    action()

        dp_at, col_at, slot, arriving = fetch(step)

        @pl.when(e == 0)
        def _():
            @pl.when(step == 3)
            def _():
                for copy in arriving:
                    copy.start()

            for copy in arriving:
                copy.wait()

        @pl.when((e == experts - 1) & (step != 2) & (step + 1 < steps))
        def _():
            for copy in fetch(step + 1)[3]:
                copy.start()

        x, pair_grad, hidden, grad_gate, grad_up = slot_grads(
            capacity,
            table_ref[col_at, dp_at, pl.ds(e, 1), :],
            table_ref[col_at, dp_at, pl.ds(experts + e, 1), :],
            table_ref[col_at, dp_at, RSTD_ROW : RSTD_ROW + 1, :],
            res_ref.at[slot], cot_ref.at[slot], small_ref, wg_ref[e], wu_ref[e], wd_ref[e],
        )
        dd_ref[e] += dot_tn(hidden, pair_grad)
        dg_ref[e] += dot_tn(x, grad_gate)
        du_ref[e] += dot_tn(x, grad_up)

        @pl.when(step == steps - 1)
        def _():
            for k, (source, target) in enumerate(((dg_ref, dg_hbm), (du_ref, du_hbm), (dd_ref, dd_hbm))):
                pltpu.make_async_copy(source.at[e], target.at[e], out_sems.at[k, e]).start()

    pl.loop(0, before_late)(other_blocks)

    @pl.loop(0, dp_count * experts)
    def _(turn):
        e, slot = lax.rem(turn, experts), lax.rem(turn, 2)
        for copy in kept_slots(turn):
            copy.wait()

        @pl.when(turn + 1 < dp_count * experts)
        def _():
            for copy in kept_slots(turn + 1):
                copy.start()

        dd_ref[e] += dot_tn(mid_ref[slot, 0], g_ref[slot])
        dg_ref[e] += dot_tn(x_ref[slot], mid_ref[slot, 1])
        du_ref[e] += dot_tn(x_ref[slot], mid_ref[slot, 2])

    pl.loop(before_late, steps * experts)(other_blocks)
    take_swapped()
    three_res.complete_other()
    three_cot.complete_other()
    for e in range(experts):
        for k, (source, target) in enumerate(((dg_ref, dg_hbm), (du_ref, du_hbm), (dd_ref, dd_hbm))):
            pltpu.make_async_copy(source.at[e], target.at[e], out_sems.at[k, e]).wait()
    copies.finish()


def last_grads_kernel(
    counts, res_all, cot_all, table_ref, small_ref, wg_ref, wu_ref, wd_ref, dg_in, du_in, dd_in,
    out_in, grad_in_in, attn_in, sums_in,
    dg_ref, du_ref, dd_ref, out_ref, grad_in_ref, qkv_ref, wo_ref, router_ref, one_ref, two_ref,
    res_ref, cot_ref, sems,
):
    dp_count, row_count, col_count = counts
    e = pl.program_id(0)
    experts = pl.num_programs(0)
    _, parts, length, width = res_all.shape
    capacity = length * TOP // (dp_count * row_count * experts)
    col_at = lax.rem(lax.axis_index("col") + col_count - LATE, col_count)

    dp_at = dp_count - 1 - lax.axis_index("dp")
    b = dp_at * col_count + col_at
    arriving = (
        pltpu.make_async_copy(res_all.at[b], res_ref, sems.at[0]),
        pltpu.make_async_copy(cot_all.at[b], cot_ref, sems.at[1]),
    )

    @pl.when(e == 0)
    def _():
        for copy in arriving:
            copy.start()

    out_ref[...] = out_in[...]
    grad_in_ref[...] = grad_in_in[...]
    group, columns = qkv_ref.shape[1:]
    for head in range(group):
        qkv_ref[:, head, :] = attn_in[:, head * columns : (head + 1) * columns]
    wo_ref[...] = attn_in[:, group * columns :]

    @pl.when(e == experts - 1)
    def _():
        router_ref[...] = sums_in[:GAIN_ONE, :]
        one_ref[...] = sums_in[GAIN_ONE : GAIN_ONE + 1, :]
        two_ref[...] = sums_in[GAIN_TWO : GAIN_TWO + 1, :]

    @pl.when(e == 0)
    def _():
        for copy in arriving:
            copy.wait()

    x, pair_grad, hidden, grad_gate, grad_up = slot_grads(
        capacity,
        table_ref[col_at, dp_at, pl.ds(e, 1), :],
        table_ref[col_at, dp_at, pl.ds(experts + e, 1), :],
        table_ref[col_at, dp_at, RSTD_ROW : RSTD_ROW + 1, :],
        res_ref, cot_ref, small_ref, wg_ref[0], wu_ref[0], wd_ref[0],
    )
    dd_ref[0] = dd_in[0] + dot_tn(hidden, pair_grad)
    dg_ref[0] = dg_in[0] + dot_tn(x, grad_gate)
    du_ref[0] = du_in[0] + dot_tn(x, grad_up)


def fast_device(
    hidden_in, norm_gain, w_qkv, w_out, ffn_gain, router, w_gate, w_up, w_down, cotangent,
    segment_ids, expert_ids, pair_order,
):
    dp_count, row_count, col_count = (lax.axis_size(name) for name in ("dp", "row", "col"))
    my_dp, my_row, my_col = (lax.axis_index(name) for name in ("dp", "row", "col"))
    length, width = hidden_in.shape
    kv_local = w_qkv.shape[1]
    head_width = kv_local * (HQ // HK) * HD
    qkv_width = kv_local * (HQ // HK + 2) * HD
    exp_local, _, hidden_width = w_gate.shape
    capacity = length * TOP // EXPERTS
    blocks = dp_count * col_count
    vmem = pl.BlockSpec(memory_space=pltpu.VMEM)
    hbm = pl.BlockSpec(memory_space=pl.ANY)
    params = pltpu.CompilerParams(vmem_limit_bytes=VMEM_BYTES)

    packed = (expert_ids * (length * TOP) + pair_order).T
    own_q = w_qkv.reshape(width, qkv_width)
    own_o = w_out.reshape(head_width, width)
    small = jnp.concatenate(
        [router.T, norm_gain[None], ffn_gain[None], jnp.zeros((SMALL_ROWS - 2 - EXPERTS, width), LOW)], axis=0
    )
    seg_rows = jnp.broadcast_to(segment_ids, (8, length)).astype(F32)
    tables = jnp.asarray(rope_lanes(length))
    counts = (dp_count, row_count, col_count)
    (
        resid_mid, resid_low, mixed, normed_one, query_rot, key_rot, value_low, logs,
        wq_rows, wo_cols, small_all, seg_all, cot_all,
    ) = pl.pallas_call(
        functools.partial(attend_forward_kernel, counts),
        out_shape=(
            jax.ShapeDtypeStruct((length, width), F32),
            jax.ShapeDtypeStruct((length, width), LOW),
            jax.ShapeDtypeStruct((length, head_width), LOW),
            jax.ShapeDtypeStruct((length, D), LOW),
            jax.ShapeDtypeStruct((2 * kv_local, length, HD), LOW),
            jax.ShapeDtypeStruct((kv_local, length, HD), LOW),
            jax.ShapeDtypeStruct((kv_local, length, HD), LOW),
            jax.ShapeDtypeStruct((length, LANES), F32),
            jax.ShapeDtypeStruct((row_count, width, qkv_width), LOW),
            jax.ShapeDtypeStruct((col_count, head_width, width), LOW),
            jax.ShapeDtypeStruct((row_count, SMALL_ROWS, width), LOW),
            jax.ShapeDtypeStruct((row_count, 8, length), F32),
            jax.ShapeDtypeStruct((blocks, row_count, length, width), LOW),
        ),
        in_specs=[hbm] * 7,
        out_specs=[vmem] * 2 + [hbm] * 2 + [vmem] * 4 + [hbm] + [vmem] * 3 + [hbm],
        scratch_shapes=[
            pltpu.VMEM((row_count, length, head_width), LOW),
            pltpu.VMEM((length, D), LOW),
            pltpu.VMEM((row_count, width, qkv_width), LOW),
            pltpu.VMEM(tables.shape, F32),
            pltpu.VMEM((row_count, length, width), LOW),
            pltpu.VMEM((col_count, width, qkv_width), LOW),
            pltpu.VMEM((length, width), LOW),
            pltpu.VMEM((length, LANES), F32),
            pltpu.SemaphoreType.DMA((80,)),
            pltpu.SemaphoreType.DMA((80,)),
        ],
        compiler_params=pltpu.CompilerParams(
            vmem_limit_bytes=VMEM_BYTES, collective_id=1, has_side_effects=True
        ),
        cost_estimate=pl.CostEstimate(flops=50_000_000_000, bytes_accessed=30_000_000, transcendentals=0),
        name="attend_forward",
    )(hidden_in, own_q, own_o, small, seg_rows, cotangent, tables)
    block_low = jax.ShapeDtypeStruct((length, width), LOW)
    block_float = jax.ShapeDtypeStruct((length, width), F32)
    slots = exp_local * capacity
    plane = (dp_count, row_count, length, width)
    every = jax.ShapeDtypeStruct((blocks, row_count, length, width), LOW)
    y_part, grad_resid, grad_low, table, small_part, wo_rows, cot_all, res_all, *kept_slots = pl.pallas_call(
        functools.partial(experts_kernel, counts),
        out_shape=(
            jax.ShapeDtypeStruct(plane, LOW),
            block_float,
            block_low,
            jax.ShapeDtypeStruct((col_count, dp_count, 16, length), F32),
            jax.ShapeDtypeStruct((SMALL_ROWS, width), F32),
            jax.ShapeDtypeStruct((row_count, head_width, width), LOW),
            every,
            every,
            jax.ShapeDtypeStruct((dp_count, exp_local, capacity, D), LOW),
            jax.ShapeDtypeStruct((dp_count, exp_local, capacity, D), LOW),
            jax.ShapeDtypeStruct((dp_count, exp_local, 3, capacity, hidden_width), LOW),
        ),
        input_output_aliases={4: 6},
        in_specs=[hbm, vmem, vmem, hbm, hbm, vmem, hbm, hbm, hbm, hbm],
        out_specs=[hbm] + [vmem] * 4 + [hbm] * 6,
        scratch_shapes=[
            pltpu.VMEM(w_gate.shape, LOW),
            pltpu.VMEM(w_up.shape, LOW),
            pltpu.VMEM(w_down.shape, LOW),
            pltpu.VMEM(plane, LOW),
            pltpu.VMEM(plane, LOW),
            pltpu.VMEM((length, D), LOW),
            pltpu.VMEM((dp_count, TOP, length), jnp.int32),
            pltpu.VMEM((dp_count, 8, length), F32),
            pltpu.VMEM((EXPERTS, length), F32),
            pltpu.VMEM((dp_count, row_count, slots, width), LOW),
            pltpu.VMEM((slots, length), LOW),
            pltpu.VMEM((row_count, slots, width), LOW),
            pltpu.VMEM((row_count, slots, width), LOW),
            pltpu.VMEM((dp_count, 2, length, width), LOW),
            pltpu.VMEM((dp_count, 2, length, width), LOW),
            pltpu.VMEM((2, length, width), F32),
            pltpu.VMEM((dp_count, 2, length, width), LOW),
            pltpu.VMEM((3, length, width), LOW),
            pltpu.VMEM((row_count, length, width), LOW),
            pltpu.VMEM((dp_count, 8, length), F32),
            pltpu.VMEM((dp_count * row_count, 8, length), F32),
            pltpu.VMEM((length, LANES), F32),
            pltpu.VMEM((row_count, 8, length), F32),
            pltpu.VMEM((length, width), LOW),
            pltpu.VMEM((2, capacity, D), LOW),
            pltpu.VMEM((2, capacity, D), LOW),
            pltpu.VMEM((2, 3, capacity, hidden_width), LOW),
            pltpu.SemaphoreType.DMA((3, 2)),
            pltpu.SemaphoreType.DMA((80,)),
            pltpu.SemaphoreType.DMA((80,)),
        ],
        compiler_params=pltpu.CompilerParams(
            vmem_limit_bytes=VMEM_BYTES, collective_id=2, has_side_effects=True
        ),
        cost_estimate=pl.CostEstimate(flops=80_000_000_000, bytes_accessed=50_000_000, transcendentals=0),
        name="experts",
    )(resid_low, resid_mid, cotangent, packed, cot_all, small_all, wo_cols, w_gate, w_up, w_down)

    halves = (dp_count, 2, length, width)
    half = (2, length, width)
    layer_out, grad_in, grads_part, small_part, res_all, cot_all = pl.pallas_call(
        functools.partial(attend_backward_kernel, counts),
        out_shape=(
            block_low,
            block_float,
            jax.ShapeDtypeStruct((row_count, width, qkv_width + width), LOW),
            jax.ShapeDtypeStruct((SMALL_ROWS, width), F32),
            every,
            every,
        ),
        input_output_aliases={17: 4, 18: 5},
        in_specs=[hbm] * 4 + [vmem] * 2 + [hbm] * 2 + [vmem] * 7 + [hbm] * 5,
        out_specs=[vmem] * 4 + [hbm] * 2,
        scratch_shapes=[
            pltpu.VMEM((length, width), F32),
            pltpu.VMEM((length, width), LOW),
            pltpu.VMEM((length, width), F32),
            pltpu.VMEM((length, D), LOW),
            pltpu.VMEM(tables.shape, F32),
            pltpu.VMEM((row_count, length, width), LOW),
            pltpu.VMEM((length, head_width), LOW),
            pltpu.VMEM((BLOCK_Q, head_width), LOW),
            pltpu.VMEM((BLOCK_Q, head_width), F32),
            pltpu.VMEM((kv_local, length, HD), F32),
            pltpu.VMEM((kv_local, length, HD), F32),
            pltpu.VMEM((length, qkv_width), LOW),
            pltpu.VMEM((length, LANES), F32),
            pltpu.VMEM(halves, LOW),
            pltpu.VMEM(halves, LOW),
            pltpu.VMEM(halves, LOW),
            pltpu.VMEM((3, length, width), LOW),
            pltpu.VMEM(half, LOW),
            pltpu.VMEM(half, LOW),
            pltpu.VMEM(half, F32),
            pltpu.VMEM((length, width), LOW),
            pltpu.VMEM((length, width), LOW),
            pltpu.VMEM((row_count, 8, length), F32),
            pltpu.SemaphoreType.DMA((80,)),
            pltpu.SemaphoreType.DMA((80,)),
        ],
        compiler_params=pltpu.CompilerParams(
            vmem_limit_bytes=VMEM_BYTES, collective_id=3, has_side_effects=True
        ),
        cost_estimate=pl.CostEstimate(flops=40_000_000_000, bytes_accessed=30_000_000, transcendentals=0),
        name="attend_backward",
    )(
        grad_low, grad_resid, hidden_in, resid_mid, wo_rows, wq_rows, normed_one, mixed, query_rot, key_rot,
        value_low, logs, seg_all, small_all, small_part, tables, y_part, res_all,
        cot_all, resid_low,
    )

    gate_shape, down_shape = (jax.ShapeDtypeStruct(w.shape, F32) for w in (w_gate, w_down))
    one_gate = pl.BlockSpec((1,) + w_gate.shape[1:], lambda e: (e, 0, 0))
    one_down = pl.BlockSpec((1,) + w_down.shape[1:], lambda e: (e, 0, 0))
    token_pair = (2, row_count, length, width)
    res_all, cot_all, grad_gate, grad_up, grad_down, grads_own, small = pl.pallas_call(
        functools.partial(weight_grads_kernel, counts),
        out_shape=(
            every, every, gate_shape, gate_shape, down_shape,
            jax.ShapeDtypeStruct((width, qkv_width + width), F32),
            jax.ShapeDtypeStruct((SMALL_ROWS, width), F32),
        ),
        input_output_aliases={0: 0, 1: 1},
        in_specs=[hbm] * 6 + [vmem] * 3 + [hbm] * 3,
        out_specs=[hbm] * 5 + [vmem] * 2,
        scratch_shapes=[
            pltpu.VMEM(w_gate.shape, LOW),
            pltpu.VMEM(w_up.shape, LOW),
            pltpu.VMEM(w_down.shape, LOW),
            pltpu.VMEM((dp_count * col_count, SMALL_ROWS, width), F32),
            pltpu.VMEM(w_gate.shape, F32),
            pltpu.VMEM(w_up.shape, F32),
            pltpu.VMEM(w_down.shape, F32),
            pltpu.VMEM(token_pair, LOW),
            pltpu.VMEM(token_pair, LOW),
            pltpu.VMEM((2, capacity, D), LOW),
            pltpu.VMEM((2, capacity, D), LOW),
            pltpu.VMEM((2, 3, capacity, hidden_width), LOW),
            pltpu.VMEM((col_count, width, qkv_width + width), LOW),
            pltpu.VMEM((4, width, qkv_width + width), LOW),
            pltpu.SemaphoreType.DMA((4,)),
            pltpu.SemaphoreType.DMA((3, 2)),
            pltpu.SemaphoreType.DMA((3, exp_local)),
            pltpu.SemaphoreType.DMA((64,)),
            pltpu.SemaphoreType.DMA((64,)),
        ],
        compiler_params=pltpu.CompilerParams(
            vmem_limit_bytes=VMEM_BYTES, collective_id=4, has_side_effects=True
        ),
        name="weight_grads",
    )(res_all, cot_all, grads_part, *kept_slots, small_part, table, small_all, w_gate, w_up, w_down)
    def strips(rows, columns):
        return pl.BlockSpec((rows // exp_local, columns), lambda e: (e, 0))

    tokens, attn = strips(length, width), strips(width, qkv_width + width)
    whole = [pl.BlockSpec((EXPERTS, width), lambda e: (0, 0))] + [pl.BlockSpec((1, width), lambda e: (0, 0))] * 2
    gain_row = jax.ShapeDtypeStruct((1, width), F32)
    grad_gate, grad_up, grad_down, layer_out, grad_in, grad_qkv, grad_out, grad_router, *grad_gains = pl.pallas_call(
        functools.partial(last_grads_kernel, counts),
        grid=(exp_local,),
        out_shape=(
            gate_shape, gate_shape, down_shape, block_low, block_float,
            jax.ShapeDtypeStruct(w_qkv.shape, F32),
            jax.ShapeDtypeStruct((head_width, width), F32),
            jax.ShapeDtypeStruct((EXPERTS, width), F32),
            gain_row,
            gain_row,
        ),
        in_specs=[hbm, hbm, vmem, vmem] + [one_gate, one_gate, one_down] * 2 + [tokens, tokens, attn, vmem],
        out_specs=[
            one_gate, one_gate, one_down, tokens, tokens,
            pl.BlockSpec((width // exp_local,) + w_qkv.shape[1:], lambda e: (e, 0, 0)), strips(head_width, width),
        ]
        + whole,
        scratch_shapes=[
            pltpu.VMEM((row_count, length, width), LOW),
            pltpu.VMEM((row_count, length, width), LOW),
            pltpu.SemaphoreType.DMA((2,)),
        ],
        compiler_params=params,
        name="last_grads",
    )(
        res_all, cot_all, table, small_all, w_gate, w_up, w_down, grad_gate, grad_up, grad_down,
        layer_out, grad_in, grads_own, small,
    )
    return (
        layer_out,
        grad_in,
        grad_gains[0].reshape(width),
        grad_qkv,
        grad_out.reshape(w_out.shape),
        grad_gains[1].reshape(width),
        grad_router.T,
        grad_gate,
        grad_up,
        grad_down,
    )


def solution(mesh):
    token = P(("dp", "col"), "row")
    routed = P(("dp", "col"), None)
    expert = P(("dp", "row"), None, None)
    wide, tall = P("row", "col", None), P("col", None, "row")
    row = P("row")
    square = P("row", None)

    def step(*arrays):
        length = arrays[10].shape[1]
        tokens_here = arrays[0].shape[0] // (mesh.shape["dp"] * mesh.shape["col"])
        whole_sequence = tokens_here == length and mesh.shape["row"] == mesh.shape["col"]
        return jax.shard_map(
            fast_device if whole_sequence else on_device,
            mesh=mesh,
            in_specs=(
                token, row, wide, tall, row, square, expert, expert, expert, token,
                P(("dp", "row"), None), routed, routed,
            ),
            out_specs=(token, token, row, wide, tall, row, square, expert, expert, expert),
            check_vma=False,
        )(*arrays)

    return step
```

```python
import functools

import jax
import jax.numpy as jnp
import numpy as np
from jax import lax
from jax.experimental import pallas as pl
from jax.experimental.pallas import tpu as pltpu
from jax.sharding import PartitionSpec as P

D = 1024
HQ = 16
HK = 8
HD = 64
EXPERTS = 32
TOP = 8


EPSILON = 1e-06
ROPE_BASE = 10000.0
NEG_LARGE = -1e30
HIGHEST = lax.Precision.HIGHEST


def rotate(values, cosine, sine_table):
    half_size = values.shape[-1] // 2
    lower_half = values[..., :half_size]
    upper_half = values[..., half_size:]
    return jnp.concatenate(
        [
            lower_half * cosine - upper_half * sine_table,
            upper_half * cosine + lower_half * sine_table,
        ],
        axis=-1,
    )


def rotate_back(values, cosine, sine_table):
    half_size = values.shape[-1] // 2
    lower_half = values[..., :half_size]
    upper_half = values[..., half_size:]
    return jnp.concatenate(
        [
            lower_half * cosine + upper_half * sine_table,
            upper_half * cosine - lower_half * sine_table,
        ],
        axis=-1,
    )


def rope_tables(length, head_size):
    positions = jnp.arange(length, dtype=jnp.float32)
    frequency = ROPE_BASE ** (-2.0 * jnp.arange(head_size // 2, dtype=jnp.float32) / head_size)
    angles = positions[:, None] * frequency[None, :]
    return (jnp.cos(angles), jnp.sin(angles))


def visible(segment_row):
    positions = jnp.arange(segment_row.shape[-1], dtype=jnp.int32)
    causal = positions[:, None] >= positions[None, :]
    return causal & (segment_row[..., :, None] == segment_row[..., None, :])


def pair_ranks(expert_ids, pair_order, block_rows):
    experts_flat = expert_ids.reshape(-1, block_rows * TOP)
    order_flat = pair_order.reshape(-1, block_rows * TOP)

    def one_block(experts_row, order_row):
        pair_count = experts_row.shape[0]
        by_order = (
            jnp.zeros((pair_count,), jnp.int32)
            .at[order_row]
            .set(jnp.arange(pair_count, dtype=jnp.int32))
        )
        sorted_experts = experts_row[by_order]
        onehot = (sorted_experts[:, None] == jnp.arange(EXPERTS, dtype=jnp.int32)[None, :]).astype(
            jnp.int32
        )
        before = jnp.cumsum(onehot, axis=0) - onehot
        sorted_rank = jnp.sum(before * onehot, axis=1)
        return sorted_rank[order_row]

    return jax.vmap(one_block)(experts_flat, order_flat).reshape(expert_ids.shape)


def feature_total(values):
    return lax.psum(values, "row")


def tokens_by_col(values):
    return lax.all_gather(values, "col", axis=0, tiled=True)


def tokens_by_row(values):
    return lax.all_gather(values, "row", axis=0, tiled=True)


def col_scatter(term_fn, keep_rows):
    return lax.psum_scatter(
        term_fn(jnp.int32(0), keep_rows * lax.axis_size("col")),
        "col",
        scatter_dimension=0,
        tiled=True,
    )


def to_experts(outgoing):
    arrived = lax.all_to_all(outgoing, ("dp", "row"), split_axis=0, concat_axis=0, tiled=True)
    return arrived


def from_experts(outgoing):
    arrived = lax.all_to_all(outgoing, ("dp", "row"), split_axis=0, concat_axis=0, tiled=True)
    return arrived


def owner_layout(incoming, dp_count, row_count, exp_local):
    capacity = incoming.shape[1] // exp_local
    part_width = incoming.shape[2]
    sectioned = incoming.reshape(dp_count, row_count, exp_local, capacity, part_width)
    return sectioned.transpose(2, 0, 3, 1, 4).reshape(
        exp_local, dp_count * capacity, row_count * part_width
    )


def source_layout(owner_rows, dp_count, row_count):
    exp_local, slot_rows, full_width = owner_rows.shape
    capacity = slot_rows // dp_count
    part_width = full_width // row_count
    sectioned = owner_rows.reshape(exp_local, dp_count, capacity, row_count, part_width)
    return sectioned.transpose(1, 3, 0, 2, 4).reshape(
        dp_count * row_count, exp_local * capacity, part_width
    )


def attend_forward(pack):
    query_seq, key_seq, value_seq, segment_seq = pack
    score_scale = query_seq.shape[-1] ** (-0.5)
    scores = (
        jnp.einsum("qhgd,khd->hgqk", query_seq, key_seq, preferred_element_type=jnp.float32)
        * score_scale
    )
    scores = jnp.where(visible(segment_seq), scores, NEG_LARGE)
    row_max = jnp.max(scores, axis=-1, keepdims=True)
    weights = jnp.exp(scores - row_max)
    row_total = jnp.sum(weights, axis=-1, keepdims=True)
    weights_low = (weights / row_total).astype(jnp.bfloat16)
    mixed_seq = jnp.einsum(
        "hgqk,khd->qhgd", weights_low, value_seq, preferred_element_type=jnp.float32
    )
    return (mixed_seq.astype(jnp.bfloat16), row_max + jnp.log(row_total))


def attend_backward(pack):
    query_seq, key_seq, value_seq, segment_seq, log_total, grad_seq = pack
    score_scale = query_seq.shape[-1] ** (-0.5)
    scores = (
        jnp.einsum("qhgd,khd->hgqk", query_seq, key_seq, preferred_element_type=jnp.float32)
        * score_scale
    )
    scores = jnp.where(visible(segment_seq), scores, NEG_LARGE)
    weights = jnp.exp(scores - log_total)
    grad_weights = jnp.einsum(
        "qhgd,khd->hgqk", grad_seq, value_seq, preferred_element_type=jnp.float32
    )
    inner_sum = jnp.sum(weights * grad_weights, axis=-1, keepdims=True)
    grad_scores = (weights * (grad_weights - inner_sum)).astype(jnp.bfloat16)
    grad_values = jnp.einsum(
        "hgqk,qhgd->khd", weights.astype(jnp.bfloat16), grad_seq, preferred_element_type=jnp.float32
    )
    grad_query = (
        jnp.einsum("hgqk,khd->qhgd", grad_scores, key_seq, preferred_element_type=jnp.float32)
        * score_scale
    )
    grad_key = (
        jnp.einsum("hgqk,qhgd->khd", grad_scores, query_seq, preferred_element_type=jnp.float32)
        * score_scale
    )
    return (grad_query, grad_key, grad_values)


def on_device(
    hidden_in,
    norm_gain,
    w_qkv,
    w_out,
    ffn_gain,
    router,
    w_gate,
    w_up,
    w_down,
    cotangent,
    segment_ids,
    expert_ids,
    pair_order,
):
    dp_count = lax.axis_size("dp")
    row_count = lax.axis_size("row")
    owners = dp_count * row_count
    tok_rows, part_width = hidden_in.shape
    seq_count, length = segment_ids.shape
    att_rows = seq_count * length
    kv_local = w_qkv.shape[1]
    group_size = HQ // HK
    exp_local = w_gate.shape[0]
    capacity = tok_rows * TOP // EXPERTS
    total_slots = EXPERTS * capacity
    resid_in = hidden_in.astype(jnp.float32)
    gain_one = norm_gain.astype(jnp.float32)
    rstd_one = lax.rsqrt(feature_total(jnp.sum(resid_in * resid_in, axis=1)) / D + EPSILON)
    normed_one = (resid_in * rstd_one[:, None] * gain_one).astype(jnp.bfloat16)
    group_rows = tokens_by_col(normed_one)
    qkv_flat = w_qkv.reshape(part_width, -1)
    picked = group_rows
    qkv_local = lax.psum_scatter(
        jnp.dot(picked, qkv_flat, preferred_element_type=jnp.float32),
        "row",
        scatter_dimension=0,
        tiled=True,
    )
    qkv_local = qkv_local.reshape(seq_count, length, kv_local, -1)
    cosine, sine_table = rope_tables(length, HD)
    queries = qkv_local[..., : group_size * HD].reshape(seq_count, length, kv_local, group_size, HD)
    query_rot = rotate(
        queries, cosine[None, :, None, None, :], sine_table[None, :, None, None, :]
    ).astype(jnp.bfloat16)
    key_rot = rotate(
        qkv_local[..., group_size * HD : (group_size + 1) * HD],
        cosine[None, :, None, :],
        sine_table[None, :, None, :],
    ).astype(jnp.bfloat16)
    value_low = qkv_local[..., (group_size + 1) * HD :].astype(jnp.bfloat16)
    mixed_heads, log_total = lax.map(attend_forward, (query_rot, key_rot, value_low, segment_ids))
    mixed_rows = tokens_by_row(mixed_heads.reshape(att_rows, -1))
    out_flat = w_out.reshape(-1, part_width)

    def out_term(first_row, block_rows):
        return jnp.dot(mixed_rows, out_flat, preferred_element_type=jnp.float32)

    resid_mid = resid_in + col_scatter(out_term, tok_rows)
    gain_two = ffn_gain.astype(jnp.float32)
    router_float = router.astype(jnp.float32)
    square_two, logit_part = (
        lax.psum(jnp.sum(resid_mid * resid_mid, axis=1).astype(jnp.bfloat16), "row").astype(
            jnp.float32
        ),
        lax.psum(
            jnp.dot(resid_mid * gain_two, router_float, precision=HIGHEST).astype(jnp.bfloat16),
            "row",
        ).astype(jnp.float32),
    )
    rstd_two = lax.rsqrt(square_two / D + EPSILON)
    logits = logit_part * rstd_two[:, None]
    normed_float = resid_mid * rstd_two[:, None] * gain_two
    normed_two = normed_float.astype(jnp.bfloat16)
    choose = (expert_ids[:, :, None] == jnp.arange(EXPERTS, dtype=jnp.int32)[None, None, :]).astype(
        jnp.float32
    )
    gate_weights = jax.nn.softmax(jnp.sum(choose * logits[:, None, :], axis=2), axis=1)
    pair_rank = pair_ranks(expert_ids, pair_order, tok_rows)
    pair_slot = jnp.where(pair_rank < capacity, expert_ids * capacity + pair_rank, total_slots)
    pair_index = jnp.arange(tok_rows * TOP, dtype=jnp.int32)
    slot_pair = (
        jnp.full((total_slots + 1,), tok_rows * TOP, jnp.int32)
        .at[pair_slot.reshape(-1)]
        .set(pair_index)[:total_slots]
    )
    padded_two = jnp.concatenate([normed_two, jnp.zeros((1, part_width), jnp.bfloat16)], axis=0)
    outgoing = padded_two[slot_pair // TOP].reshape(owners, exp_local * capacity, part_width)
    expert_rows = owner_layout(to_experts(outgoing), dp_count, row_count, exp_local)
    gate_pre = jnp.einsum("erd,edf->erf", expert_rows, w_gate, preferred_element_type=jnp.float32)
    up_pre = jnp.einsum("erd,edf->erf", expert_rows, w_up, preferred_element_type=jnp.float32)
    hidden = (jax.nn.silu(gate_pre) * up_pre).astype(jnp.bfloat16)
    expert_out = jnp.einsum(
        "erf,efd->erd", hidden, w_down, preferred_element_type=jnp.float32
    ).astype(jnp.bfloat16)
    returned = from_experts(source_layout(expert_out, dp_count, row_count))
    slot_table = jnp.concatenate(
        [returned.reshape(total_slots, part_width), jnp.zeros((1, part_width), jnp.bfloat16)],
        axis=0,
    )
    pair_rows = slot_table[pair_slot].astype(jnp.float32)
    layer_sum = resid_mid + jnp.einsum("tk,tkd->td", gate_weights, pair_rows, precision=HIGHEST)
    grad_top = cotangent.astype(jnp.float32)
    grad_gates = lax.psum(jnp.einsum("td,tkd->tk", grad_top, pair_rows, precision=HIGHEST), "row")
    pair_grad = (gate_weights[:, :, None] * grad_top[:, None, :]).astype(jnp.bfloat16)
    grad_padded = jnp.concatenate(
        [pair_grad.reshape(tok_rows * TOP, part_width), jnp.zeros((1, part_width), jnp.bfloat16)],
        axis=0,
    )
    outgoing_grad = grad_padded[slot_pair].reshape(owners, exp_local * capacity, part_width)
    grad_rows = owner_layout(to_experts(outgoing_grad), dp_count, row_count, exp_local)
    grad_hidden = jnp.einsum("erd,efd->erf", grad_rows, w_down, preferred_element_type=jnp.float32)
    sigmoid_gate = jax.nn.sigmoid(gate_pre)
    grad_gate_pre = (
        grad_hidden * up_pre * sigmoid_gate * (1.0 + gate_pre * (1.0 - sigmoid_gate))
    ).astype(jnp.bfloat16)
    grad_up_pre = (grad_hidden * gate_pre * sigmoid_gate).astype(jnp.bfloat16)
    grad_down_local = jnp.einsum(
        "erf,erd->efd", hidden, grad_rows, preferred_element_type=jnp.float32
    )
    grad_gate_local = jnp.einsum(
        "erd,erf->edf", expert_rows, grad_gate_pre, preferred_element_type=jnp.float32
    )
    grad_up_local = jnp.einsum(
        "erd,erf->edf", expert_rows, grad_up_pre, preferred_element_type=jnp.float32
    )
    rows_back = jnp.einsum(
        "erf,edf->erd", grad_gate_pre, w_gate, preferred_element_type=jnp.float32
    )
    rows_back = (
        rows_back
        + jnp.einsum("erf,edf->erd", grad_up_pre, w_up, preferred_element_type=jnp.float32)
    ).astype(jnp.bfloat16)
    returned_grad = from_experts(source_layout(rows_back, dp_count, row_count))
    grad_table = jnp.concatenate(
        [returned_grad.reshape(total_slots, part_width), jnp.zeros((1, part_width), jnp.bfloat16)],
        axis=0,
    )
    inner_gate = jnp.sum(gate_weights * grad_gates, axis=1, keepdims=True)
    grad_chosen = gate_weights * (grad_gates - inner_gate)
    grad_logits = jnp.einsum("tk,tke->te", grad_chosen, choose, precision=HIGHEST)
    grad_router_part = jnp.einsum("td,te->de", normed_float, grad_logits, precision=HIGHEST)
    grad_normed = jnp.sum(grad_table[pair_slot].astype(jnp.float32), axis=1)
    grad_normed = grad_normed + jnp.einsum(
        "te,de->td", grad_logits, router_float, precision=HIGHEST
    )
    grad_gain_two_part = jnp.sum(grad_normed * resid_mid * rstd_two[:, None], axis=0)
    scaled_two = grad_normed * gain_two
    inner_two = feature_total(jnp.sum(scaled_two * resid_mid, axis=1))
    grad_resid = (
        grad_top
        + rstd_two[:, None] * scaled_two
        - resid_mid * (rstd_two * rstd_two * rstd_two * inner_two / D)[:, None]
    )
    branch_rows = tokens_by_col(grad_resid.astype(jnp.bfloat16))
    grad_out_local = jnp.einsum(
        "tc,td->cd", mixed_rows, branch_rows, preferred_element_type=jnp.float32
    ).reshape(w_out.shape)
    picked = branch_rows
    grad_mixed = lax.psum_scatter(
        jnp.einsum("td,cd->tc", picked, out_flat, preferred_element_type=jnp.float32).astype(
            jnp.bfloat16
        ),
        "row",
        scatter_dimension=0,
        tiled=True,
    ).astype(jnp.float32)
    grad_mixed = grad_mixed.astype(jnp.bfloat16).reshape(
        seq_count, length, kv_local, group_size, HD
    )
    grad_query, grad_key, grad_values = lax.map(
        attend_backward, (query_rot, key_rot, value_low, segment_ids, log_total, grad_mixed)
    )
    grad_query = rotate_back(
        grad_query, cosine[None, :, None, None, :], sine_table[None, :, None, None, :]
    )
    grad_key = rotate_back(grad_key, cosine[None, :, None, :], sine_table[None, :, None, :])
    grad_qkv_pre = jnp.concatenate(
        [grad_query.reshape(seq_count, length, kv_local, group_size * HD), grad_key, grad_values],
        axis=-1,
    )
    grad_qkv_pre = grad_qkv_pre.astype(jnp.bfloat16).reshape(att_rows, -1)
    qkv_rows = tokens_by_row(grad_qkv_pre)
    grad_qkv_local = jnp.einsum(
        "td,tc->dc", group_rows, qkv_rows, preferred_element_type=jnp.float32
    ).reshape(w_qkv.shape)

    def normed_term(first_row, block_rows):
        return jnp.einsum("tc,dc->td", qkv_rows, qkv_flat, preferred_element_type=jnp.float32)

    grad_normed_one = col_scatter(normed_term, tok_rows)
    grad_gain_one_part = jnp.sum(grad_normed_one * resid_in * rstd_one[:, None], axis=0)
    scaled_one = grad_normed_one * gain_one
    inner_one = feature_total(jnp.sum(scaled_one * resid_in, axis=1))
    grad_in = (
        grad_resid
        + rstd_one[:, None] * scaled_one
        - resid_in * (rstd_one * rstd_one * rstd_one * inner_one / D)[:, None]
    )
    col_sums = (
        lax.psum(grad_gate_local.astype(jnp.bfloat16), "col").astype(jnp.float32),
        lax.psum(grad_up_local.astype(jnp.bfloat16), "col").astype(jnp.float32),
        lax.psum(grad_down_local.astype(jnp.bfloat16), "col").astype(jnp.float32),
        lax.psum(grad_router_part.astype(jnp.bfloat16), "col").astype(jnp.float32),
        lax.psum(grad_gain_one_part.astype(jnp.bfloat16), "col").astype(jnp.float32),
        lax.psum(grad_gain_two_part.astype(jnp.bfloat16), "col").astype(jnp.float32),
    )
    dp_sums = (
        lax.psum(grad_qkv_local.astype(jnp.bfloat16), "dp").astype(jnp.float32),
        lax.psum(grad_out_local.astype(jnp.bfloat16), "dp").astype(jnp.float32),
        lax.psum(col_sums[3].astype(jnp.bfloat16), "dp").astype(jnp.float32),
        lax.psum(col_sums[4].astype(jnp.bfloat16), "dp").astype(jnp.float32),
        lax.psum(col_sums[5].astype(jnp.bfloat16), "dp").astype(jnp.float32),
    )
    return (
        layer_sum.astype(jnp.bfloat16),
        grad_in,
        dp_sums[3],
        dp_sums[0],
        dp_sums[1],
        dp_sums[4],
        dp_sums[2],
        col_sums[0],
        col_sums[1],
        col_sums[2],
    )

WINDOW = 512
BLOCK_Q = 256
LANES = 128
SMALL_ROWS = 48
GAIN_ONE = EXPERTS
GAIN_TWO = EXPERTS + 1
RSTD_LANE = LANES - 1
RSTD_ROW = 8
FIRST, SECOND, LATE = 1, 3, 2
F32 = jnp.float32
LOW = jnp.bfloat16
VMEM_BYTES = 67_000_000


def dot_nn(a, b):
    return jnp.dot(a, b, preferred_element_type=F32)


def dot_nt(a, b):
    return lax.dot_general(a, b, (((1,), (1,)), ((), ())), preferred_element_type=F32)


def dot_tn(a, b):
    return lax.dot_general(a, b, (((0,), (0,)), ((), ())), preferred_element_type=F32)


def rope_lanes(length):
    positions = np.arange(length, dtype=np.float32)
    frequency = (ROPE_BASE ** (-2.0 * np.arange(HD // 2, dtype=np.float32) / HD)).astype(np.float32)
    angles = (positions[:, None] * frequency[None, :]).astype(np.float32)
    cosine, sine = np.cos(angles), np.sin(angles)
    signed = np.concatenate([-sine, sine], axis=1)
    double = np.concatenate([cosine, cosine], axis=1)
    ones, zeros = np.ones_like(double), np.zeros_like(double)
    return np.stack(
        [
            np.concatenate([double, double], axis=1),
            np.concatenate([signed, signed], axis=1),
            np.concatenate([double, ones], axis=1),
            np.concatenate([signed, zeros], axis=1),
        ]
    ).astype(np.float32)


def swap_halves(values):
    half = HD // 2
    lane = lax.broadcasted_iota(jnp.int32, values.shape, 1)
    ahead = pltpu.roll(values, LANES - half, 1)
    behind = pltpu.roll(values, half, 1)
    return jnp.where(lane % HD < half, ahead, behind)


def window_mask(seg_col, seg_row, q_start, k_start):
    shape = (seg_col.shape[0], seg_row.shape[1])
    q_at = lax.broadcasted_iota(jnp.int32, shape, 0) + q_start
    k_at = lax.broadcasted_iota(jnp.int32, shape, 1) + k_start
    return (q_at >= k_at) & (seg_col == seg_row)


def remote(src, dst, send_sem, recv_sem, where):
    return pltpu.make_async_remote_copy(
        src_ref=src, dst_ref=dst, send_sem=send_sem, recv_sem=recv_sem,
        device_id=where, device_id_type=pl.DeviceIdType.MESH,
    )


class Copies:
    def __init__(self, send_sems, recv_sems):
        self.send_sems, self.recv_sems = send_sems, recv_sems
        self.sends = self.recvs = 0
        self.open = []

    def receivers(self, number=1):
        first = self.recvs
        self.recvs += number
        return first

    def send(self, src, dst, receiver, where, when=None):
        at = self.sends
        self.sends += 1
        copy = remote(src, dst, self.send_sems.at[at], self.recv_sems.at[receiver], where)
        if when is None:
            copy.start()
        else:
            pl.when(when)(copy.start)
        self.open.append((copy, when))

    def plan(self, src, dst, receiver, where):
        at = self.sends
        self.sends += 1
        copy = remote(src, dst, self.send_sems.at[at], self.recv_sems.at[receiver], where)
        self.open.append((copy, None))
        return copy

    def local(self, src, dst, when=None):
        at = self.sends
        self.sends += 1
        copy = pltpu.make_async_copy(src, dst, self.send_sems.at[at])
        if when is None:
            copy.start()
        else:
            pl.when(when)(copy.start)
        return copy

    def arrived(self, dst, receiver, where):
        remote(dst, dst, self.recv_sems.at[receiver], self.recv_sems.at[receiver], where).wait_recv()

    def finish(self):
        for copy, when in self.open:
            if when is None:
                copy.wait_send()
            else:
                pl.when(when)(copy.wait_send)


class Place:
    def __init__(self, counts):
        self.dp_count, self.row_count, self.col_count = counts
        self.dp, self.row, self.col = (lax.axis_index(name) for name in ("dp", "row", "col"))
        self.pair_row = self.row + 1 - 2 * lax.rem(self.row, 2)
        self.far_row = lax.rem(self.row + 2, self.row_count)
        self.cross_row = lax.rem(self.pair_row + 2, self.row_count)
        self.other_dp = self.dp_count - 1 - self.dp
        self.here = (self.dp, self.row, self.col)
        self.pair = (self.dp, self.pair_row, self.col)
        self.far = (self.dp, self.far_row, self.col)
        self.over = (self.other_dp, self.row, self.col)
        self.over_far = (self.other_dp, self.far_row, self.col)

    def row_at(self, step):
        return lax.rem(self.row + step + self.row_count, self.row_count)

    def col_at(self, step):
        return lax.rem(self.col + step + self.col_count, self.col_count)

    def block(self, dp_at, col_at):
        return dp_at * self.col_count + col_at

    def plane(self):
        peers = [(self.dp, self.row_at(k), self.col) for k in range(1, self.row_count)]
        return peers + [(self.other_dp, self.row_at(k), self.col) for k in range(self.row_count)]

    def column(self):
        return [(self.dp, self.row, self.col_at(k)) for k in range(1, self.col_count)]


class Spread:
    def __init__(self, place, copies, blocks, col_at):
        self.place, self.copies = place, copies
        dp, row, far_row = place.dp, place.row, place.far_row
        same, other = place.block(dp, col_at), place.block(place.other_dp, col_at)
        self.own, self.far = blocks.at[same, row], blocks.at[same, far_row]
        self.over, self.corner = blocks.at[other, row], blocks.at[other, far_row]
        self.pairs_same = (blocks.at[same, place.pair_row], blocks.at[same, place.cross_row])
        self.pairs_other = (blocks.at[other, place.pair_row], blocks.at[other, place.cross_row])
        self.at = copies.receivers(7)
        self.to_pair = copies.plan(self.own, self.own, self.at, place.pair)
        self.to_far = copies.plan(self.own, self.own, self.at + 1, place.far)
        self.to_over = copies.plan(self.own, self.own, self.at + 2, place.over)
        self.far_pair = copies.plan(self.far, self.far, self.at + 4, place.pair)
        self.over_pair = copies.plan(self.over, self.over, self.at + 5, place.pair)
        self.corner_pair = copies.plan(self.corner, self.corner, self.at + 6, place.pair)
        self.turn = None

    def begin(self, with_over):
        self.to_far.start()
        if with_over:
            self.to_over.start()
        self.to_pair.start()

    def send_over(self):
        self.to_over.start()

    def plan_corner(self, by_over):
        if by_over:
            self.turn = self.copies.plan(self.far, self.far, self.at + 3, self.place.over)
        else:
            self.turn = self.copies.plan(self.over, self.over, self.at + 3, self.place.far)

    def pass_far(self, corner):
        self.copies.arrived(self.far, self.at + 1, self.place.far)
        if corner:
            if self.turn is None:
                self.plan_corner(True)
            self.turn.start()
        self.far_pair.start()

    def pass_over(self, corner):
        self.copies.arrived(self.over, self.at + 2, self.place.over)
        if corner:
            if self.turn is None:
                self.plan_corner(False)
            self.turn.start()
        self.over_pair.start()

    def pass_corner(self):
        self.copies.arrived(self.corner, self.at + 3, self.place.here)
        self.corner_pair.start()

    def complete_same(self):
        for k, piece in zip((0, 4), self.pairs_same):
            self.copies.arrived(piece, self.at + k, self.place.pair)

    def complete_other(self):
        for k, piece in zip((5, 6), self.pairs_other):
            self.copies.arrived(piece, self.at + k, self.place.pair)

    def complete(self):
        self.complete_same()
        self.complete_other()


def say_hello(peers):
    barrier = pltpu.get_barrier_semaphore()
    for peer in peers:
        pl.semaphore_signal(barrier, inc=1, device_id=peer, device_id_type=pl.DeviceIdType.MESH)
    return functools.partial(pl.semaphore_wait, barrier, len(peers))


def greet(peers):
    say_hello(peers)()


def attend_forward_kernel(
    counts, hidden_hbm, own_q_hbm, own_o_hbm, small_hbm, seg_hbm, cot_hbm, tab_hbm,
    resid_ref, low_ref, mix_hbm, normed_hbm, q_ref, k_ref, v_ref, lse_ref, wq_hbm, zo_ref, small_ref, seg_ref, cot_all,
    mix_ref, normed_ref, wq_ref, tab_ref, h_ref, zq_ref, own_ref, column_ref, send_sems, recv_sems,
):
    place = Place(counts)
    row_count, col_count = place.row_count, place.col_count
    copies = Copies(send_sems, recv_sems)
    parts, length, width = h_ref.shape
    kv_heads = k_ref.shape[0]
    features = parts * width
    chunks = length // BLOCK_Q
    greet(place.plane() + place.column())

    h_pair, h_far, h_cross = (copies.receivers() for _ in range(3))
    copies.send(hidden_hbm, h_ref.at[place.row], h_far, place.far)
    copies.send(hidden_hbm, h_ref.at[place.row], h_pair, place.pair)
    h_own = copies.local(hidden_hbm, h_ref.at[place.row])
    tab_in = copies.local(tab_hbm, tab_ref)
    zq_own = copies.local(own_q_hbm, zq_ref.at[place.col])
    zo_own = copies.local(own_o_hbm, zo_ref.at[place.col])
    small_own = copies.local(small_hbm, small_ref.at[place.row])
    seg_own = copies.local(seg_hbm, seg_ref.at[place.row])
    half_width = width // 2
    half, other_half = (
        pl.ds(pl.multiple_of(dp_at * half_width, half_width), half_width) for dp_at in (place.dp, place.other_dp)
    )
    mine = place.row == place.col
    zq_in = copies.receivers(col_count)
    zo_in = copies.receivers(col_count)
    for k in range(1, col_count):
        copies.send(
            own_q_hbm.at[half], zq_ref.at[place.col, half], zq_in + k, (place.dp, place.row, place.col_at(k))
        )
    small_in, seg_in = copies.receivers(row_count), copies.receivers(row_count)
    for k in range(1, row_count):
        copies.send(small_hbm, small_ref.at[place.row], small_in + k, (place.dp, place.row_at(k), place.col))
        copies.send(seg_hbm, seg_ref.at[place.row], seg_in + k, (place.dp, place.row_at(k), place.col))
    cot_own = copies.local(cot_hbm, own_ref)
    cot_pair, cot_over, cot_back = copies.receivers(), copies.receivers(), copies.receivers(3)
    cot_far, cot_corner = copies.receivers(2), copies.receivers(2)
    own_cot = cot_all.at[place.block(place.dp, place.col), place.row]
    far_cot = cot_all.at[place.block(place.dp, place.col), place.far_row]
    half_rows = length // 2

    def send_cot_far(half):
        window = pl.ds(half * half_rows, half_rows)
        copies.send(cot_hbm.at[window], own_cot.at[window], cot_far + half, place.far)

    def pass_cot_far(half):
        piece = far_cot.at[pl.ds(half * half_rows, half_rows)]
        copies.arrived(piece, cot_far + half, place.far)
        copies.send(piece, piece, cot_corner + half, place.over)

    copies.send(cot_hbm, own_cot, cot_over, place.over)
    copies.send(cot_hbm, own_cot, cot_pair, place.pair)

    copies.arrived(h_ref.at[place.far_row], h_far, place.far)
    copies.send(h_ref.at[place.far_row], h_ref.at[place.far_row], h_cross, place.pair)
    wq_in, wq_over = copies.receivers(row_count), copies.receivers(row_count)
    zq_own.wait()
    copies.send(
        zq_ref.at[place.col], wq_ref.at[place.row], wq_in + lax.rem(place.col - place.row + row_count, row_count),
        (place.dp, place.col, place.col), jnp.logical_not(mine),
    )
    wq_kept = [(copies.local(zq_ref.at[place.col], wq_ref.at[place.row], mine), mine)]
    for k in range(1, col_count):
        source = place.col_at(-k)
        piece, target = zq_ref.at[source, half], wq_ref.at[place.row, half]
        copies.arrived(piece, zq_in + k, place.here)
        step = lax.rem(source - place.row + row_count, row_count)
        copies.send(piece, target, wq_in + step, (place.dp, source, place.col), source != place.row)
        copies.send(piece, target, wq_over + step, (place.other_dp, source, place.col))
        wq_kept.append((copies.local(piece, target, source == place.row), source == place.row))

    for k in range(1, col_count):
        copies.send(own_o_hbm, zo_ref.at[place.col], zo_in + k, (place.dp, place.row, place.col_at(k)))
    send_cot_far(0)
    send_cot_far(1)
    cot_z = copies.receivers(col_count)
    for k in (FIRST,):
        copies.send(cot_hbm, own_cot, cot_z + k, (place.dp, place.row, place.col_at(k)))
    h_own.wait()
    copies.arrived(h_ref.at[place.pair_row], h_pair, place.pair)
    copies.arrived(h_ref.at[place.cross_row], h_cross, place.pair)
    small_own.wait()
    for k in range(1, row_count):
        copies.arrived(small_ref.at[place.row_at(-k)], small_in + k, place.here)

    @pl.loop(0, chunks)
    def _(chunk):
        rows = pl.ds(pl.multiple_of(chunk * BLOCK_Q, BLOCK_Q), BLOCK_Q)
        total = jnp.zeros((BLOCK_Q, 1), F32)
        for part in range(parts):
            piece = h_ref[part, rows, :].astype(F32)
            total = total + jnp.sum(piece * piece, axis=1, keepdims=True)
        rstd = lax.rsqrt(total / features + EPSILON)
        lse_ref[rows, :] = jnp.broadcast_to(rstd, (BLOCK_Q, LANES))
        for part in range(parts):
            piece = h_ref[part, rows, :].astype(F32)
            gain = small_ref[part, GAIN_ONE : GAIN_ONE + 1, :].astype(F32)
            normed_ref[rows, part * width : (part + 1) * width] = (piece * rstd * gain).astype(LOW)

    written = [copies.local(normed_ref, normed_hbm)]
    seg_own.wait()
    for k in range(1, row_count):
        copies.arrived(seg_ref.at[place.row_at(-k)], seg_in + k, place.here)
    segments = seg_ref[place.col]
    for start in range(0, length, LANES):
        column_ref[start : start + LANES, :] = jnp.broadcast_to(
            segments[0:1, start : start + LANES], (LANES, LANES)
        ).T

    cot_own.wait()
    cot_kept = copies.local(own_ref, own_cot)

    for copy, here in wq_kept:
        pl.when(here)(copy.wait)

    @pl.when(mine)
    def _():
        for k in range(1, row_count):
            copies.arrived(wq_ref.at[place.row_at(-k)], wq_in + k, place.here)

    @pl.when(jnp.logical_not(mine))
    def _():
        for k in range(row_count):
            if k > 0:
                copies.arrived(wq_ref.at[place.row_at(-k), half], wq_in + k, place.here)
            copies.arrived(wq_ref.at[place.row_at(-k), other_half], wq_over + k, place.here)

    written.append(copies.local(wq_ref, wq_hbm))
    tab_in.wait()

    @pl.loop(0, chunks)
    def _(chunk):
        rows = pl.ds(pl.multiple_of(chunk * BLOCK_Q, BLOCK_Q), BLOCK_Q)
        qkv = dot_nn(normed_ref[rows, :], wq_ref[...].reshape(features, -1))
        for head in range(kv_heads):
            base = head * 4 * HD
            queries = qkv[:, base : base + LANES]
            queries = queries * tab_ref[0, rows, :] + swap_halves(queries) * tab_ref[1, rows, :]
            others = qkv[:, base + LANES : base + 2 * LANES]
            others = others * tab_ref[2, rows, :] + swap_halves(others) * tab_ref[3, rows, :]
            q_ref[2 * head, rows, :] = queries[:, :HD].astype(LOW)
            q_ref[2 * head + 1, rows, :] = queries[:, HD:].astype(LOW)
            k_ref[head, rows, :] = others[:, :HD].astype(LOW)
            v_ref[head, rows, :] = others[:, HD:].astype(LOW)

    scale = HD**-0.5
    lane = lax.broadcasted_iota(jnp.int32, (BLOCK_Q, LANES), 1)
    mix_pair, mix_far, mix_cross = (copies.receivers(chunks) for _ in range(3))

    def pass_on(block):
        piece = mix_ref.at[place.far_row, pl.ds(block * BLOCK_Q, BLOCK_Q)]
        copies.arrived(piece, mix_far + block, place.far)
        copies.send(piece, piece, mix_cross + block, place.pair)

    for block in range(chunks):
        q_start = block * BLOCK_Q
        k_start = max(0, q_start - WINDOW)
        q_rows, k_rows = slice(q_start, q_start + BLOCK_Q), slice(k_start, q_start + BLOCK_Q)
        mask = window_mask(column_ref[q_rows, 0:1], segments[0:1, k_rows], q_start, k_start)

        @pl.loop(0, kv_heads)
        def _(kv):
            keys, vals = k_ref[kv, k_rows, :], v_ref[kv, k_rows, :]
            logs, outs = lse_ref[q_rows, :], []
            for half in range(2):
                head = 2 * kv + half
                scores = dot_nt(q_ref[head, q_rows, :], keys) * scale
                scores = jnp.where(mask, scores, NEG_LARGE)
                top = jnp.max(scores, axis=1, keepdims=True)
                weights = jnp.exp(scores - top)
                total = jnp.sum(weights, axis=1, keepdims=True)
                outs.append((dot_nn(weights.astype(LOW), vals) / total).astype(LOW))
                logs = jnp.where(lane == head, top + jnp.log(total), logs)
            lse_ref[q_rows, :] = logs
            mix_ref[place.row, q_rows, pl.ds(pl.multiple_of(kv * LANES, LANES), LANES)] = jnp.concatenate(
                outs, axis=1
            )

        piece = mix_ref.at[place.row, pl.ds(q_start, BLOCK_Q)]
        copies.send(piece, piece, mix_far + block, place.far)
        copies.send(piece, piece, mix_pair + block, place.pair)
        if block > 0:
            pass_on(block - 1)
        if block == 1:
            pass_cot_far(0)
        if block == 2:
            pass_cot_far(1)
            copies.send(far_cot, far_cot, cot_back, place.pair)
            over_cot = cot_all.at[place.block(place.other_dp, place.col), place.row]
            copies.arrived(over_cot, cot_over, place.over)
            copies.send(over_cot, over_cot, cot_back + 1, place.pair)
    written.append(copies.local(mix_ref.at[place.row], mix_hbm))
    pass_on(chunks - 1)
    corner_cot = cot_all.at[place.block(place.other_dp, place.col), place.far_row]
    for half in range(2):
        copies.arrived(
            corner_cot.at[pl.ds(half * half_rows, half_rows)], cot_corner + half, place.over
        )
    copies.send(corner_cot, corner_cot, cot_back + 2, place.pair)
    zo_own.wait()
    for k in range(1, col_count):
        copies.arrived(zo_ref.at[place.col_at(-k)], zo_in + k, place.here)
    for block in range(chunks):
        rows = slice(block * BLOCK_Q, (block + 1) * BLOCK_Q)
        window = pl.ds(block * BLOCK_Q, BLOCK_Q)
        copies.arrived(mix_ref.at[place.pair_row, window], mix_pair + block, place.pair)
        copies.arrived(mix_ref.at[place.cross_row, window], mix_cross + block, place.pair)
        branch = dot_nn(mix_ref[0, rows, :], zo_ref[0])
        for part in range(1, parts):
            branch = branch + dot_nn(mix_ref[part, rows, :], zo_ref[part])
        resid = h_ref[place.row, rows, :].astype(F32) + branch
        resid_ref[rows, :] = resid
        low_ref[rows, :] = resid.astype(LOW)

    for copy in written:
        copy.wait()
    cot_kept.wait()
    copies.arrived(cot_all.at[place.block(place.dp, place.col), place.pair_row], cot_pair, place.pair)
    for k, (dp_at, row_at) in enumerate(
        ((place.dp, place.cross_row), (place.other_dp, place.pair_row), (place.other_dp, place.cross_row))
    ):
        copies.arrived(cot_all.at[place.block(dp_at, place.col), row_at], cot_back + k, place.pair)
    for k in (FIRST,):
        copies.arrived(
            cot_all.at[place.block(place.dp, place.col_at(-k)), place.row], cot_z + k, place.here
        )
    copies.finish()


def attend_backward_kernel(
    counts, grad_low_hbm, grad_hbm, hidden_hbm, resid_hbm, wo_ref, wq_ref, normed_hbm, mix_hbm, q_ref, k_ref, v_ref, lse_ref,
    seg_ref, small_ref, part_ref, tab_hbm, y_hbm, res_given, cot_given, low_hbm,
    out_ref, grad_in_ref, grads_ref, sums_ref, res_all, cot_all,
    grad_ref, hidden_ref, resid_ref, normed_ref, tab_ref, gb_ref, mixed_ref, gm_ref, dq_ref, dk_ref, dv_ref, turn_ref, column_ref, y_own_ref, y_in_ref, y_chip_ref, y_last_ref,
    away_ref, pair_in_ref, own_ref, chip_ref, last_ref, inner_ref,
    send_sems, recv_sems,
):
    place = Place(counts)
    copies = Copies(send_sems, recv_sems)
    dp_count, row_count, col_count = counts
    parts, length, width = gb_ref.shape
    kv_heads = k_ref.shape[0]
    features = parts * width
    chunks = length // BLOCK_Q
    scale = HD**-0.5
    all_here = say_hello(place.plane() + place.column())
    segments = seg_ref[place.col]
    for start in range(0, length, LANES):
        column_ref[start : start + LANES, :] = jnp.broadcast_to(
            segments[0:1, start : start + LANES], (LANES, LANES)
        ).T
    dk_ref[...] = jnp.zeros_like(dk_ref)
    dv_ref[...] = jnp.zeros_like(dv_ref)
    all_here()

    def window(chunk):
        return pl.ds(chunk * BLOCK_Q, BLOCK_Q)

    blocks = range(chunks - 1, -1, -1)
    gb_far, gb_pair, gb_cross = (copies.receivers(chunks) for _ in range(3))
    for chunk in blocks:
        piece = gb_ref.at[place.row, window(chunk)]
        copies.send(grad_low_hbm.at[window(chunk)], piece, gb_far + chunk, place.far)
        copies.send(grad_low_hbm.at[window(chunk)], piece, gb_pair + chunk, place.pair)
    gb_own = copies.local(grad_low_hbm, gb_ref.at[place.row])
    tab_in = copies.local(tab_hbm, tab_ref)
    mix_own = copies.local(mix_hbm, mixed_ref)
    y_pair = copies.receivers(2 * dp_count)
    y_held = []
    for turn, dp_at in enumerate((place.other_dp, place.dp)):
        for q, (here, there) in enumerate(
            ((place.row, place.pair_row), (place.far_row, place.cross_row))
        ):
            copies.send(y_hbm.at[dp_at, there], y_in_ref.at[turn, q], y_pair + 2 * turn + q, place.pair)
            y_held.append(copies.local(y_hbm.at[dp_at, here], y_own_ref.at[turn, q]))

    first = Spread(place, copies, res_all, place.col_at(-FIRST))
    first.plan_corner(True)
    own_block = place.block(place.dp, place.col)
    late_in = copies.receivers(2)
    late = (place.dp, place.row, place.col_at(LATE))
    own_cot = cot_all.at[own_block, place.row]
    copies.send(low_hbm, res_all.at[own_block, place.row], late_in, late)
    copies.send(own_cot, own_cot, late_in + 1, late)
    late_reads = [
        copies.local(*pair)
        for pair in ((normed_hbm, normed_ref), (hidden_hbm, hidden_ref), (grad_hbm, grad_ref), (resid_hbm, resid_ref))
    ]
    gb_own.wait()

    def pass_on(chunk):
        piece = gb_ref.at[place.far_row, window(chunk)]
        copies.arrived(piece, gb_far + chunk, place.far)
        copies.send(piece, piece, gb_cross + chunk, place.pair)

    y_last = copies.receivers(3)

    def y_over():
        for copy in y_held:
            copy.wait()
        for q in range(2):
            copies.arrived(y_in_ref.at[0, q], y_pair + q, place.pair)
            y_chip_ref[0, q] = (y_own_ref[0, q].astype(F32) + y_in_ref[0, q].astype(F32)).astype(LOW)
            copies.send(y_chip_ref.at[0, q], y_last_ref.at[q], y_last + q, place.over)

    def y_far():
        for q in range(2):
            copies.arrived(y_in_ref.at[1, q], y_pair + 2 + q, place.pair)
            copies.arrived(y_last_ref.at[q], y_last + q, place.over)
        y_chip_ref[1, 1] = (
            y_own_ref[1, 1].astype(F32) + y_in_ref[1, 1].astype(F32) + y_last_ref[1].astype(F32)
        ).astype(LOW)
        copies.send(y_chip_ref.at[1, 1], y_last_ref.at[2], y_last + 2, place.far)

    away_in = [copies.receivers(chunks) for _ in range(2)]
    last_in = copies.receivers(chunks)

    def far_share(chunk):
        rows = slice(chunk * BLOCK_Q, (chunk + 1) * BLOCK_Q)
        copies.arrived(pair_in_ref.at[1, window(chunk)], away_in[1] + chunk, place.pair)
        chip_ref[rows, :] = (own_ref[1, rows, :] + pair_in_ref[1, rows, :].astype(F32)).astype(LOW)
        copies.send(chip_ref.at[window(chunk)], last_ref.at[window(chunk)], last_in + chunk, place.far)

    lane = lax.broadcasted_iota(jnp.int32, (BLOCK_Q, LANES), 1)
    y_over()
    first.begin(True)
    pass_on(chunks - 1)
    for block in blocks:
        q_start = block * BLOCK_Q
        k_start = max(0, q_start - WINDOW)
        q_rows, k_rows = slice(q_start, q_start + BLOCK_Q), slice(k_start, q_start + BLOCK_Q)
        copies.arrived(gb_ref.at[place.pair_row, window(block)], gb_pair + block, place.pair)
        copies.arrived(gb_ref.at[place.cross_row, window(block)], gb_cross + block, place.pair)
        total = dot_nt(gb_ref[0, q_rows, :], wo_ref[0])
        for part in range(1, parts):
            total = total + dot_nt(gb_ref[part, q_rows, :], wo_ref[part])
        gm_ref[...] = total.astype(LOW)
        mask = window_mask(column_ref[q_rows, 0:1], segments[0:1, k_rows], q_start, k_start)

        @pl.loop(0, kv_heads)
        def _(kv):
            keys, vals = k_ref[kv, k_rows, :], v_ref[kv, k_rows, :]
            lanes = pl.ds(pl.multiple_of(kv * LANES, LANES), LANES)
            both, logs, queried = gm_ref[:, lanes], lse_ref[q_rows, :], []
            for half in range(2):
                head = 2 * kv + half
                queries, grad = q_ref[head, q_rows, :], both[:, half * HD : (half + 1) * HD]
                scores = dot_nt(queries, keys) * scale
                log = jnp.sum(jnp.where(lane == head, logs, 0.0), axis=1, keepdims=True)
                weights = jnp.where(mask, jnp.exp(scores - log), 0.0)
                grad_weights = dot_nt(grad, vals)
                inner = jnp.sum(weights * grad_weights, axis=1, keepdims=True)
                grad_scores = (weights * (grad_weights - inner)).astype(LOW)
                dv_ref[kv, k_rows, :] += dot_tn(weights.astype(LOW), grad)
                dk_ref[kv, k_rows, :] += dot_tn(grad_scores, queries)
                queried.append(dot_nn(grad_scores, keys) * scale)
            dq_ref[:, lanes] = jnp.concatenate(queried, axis=1)

        if block > 0:
            pass_on(block - 1)
        if block == chunks - 1:
            tab_in.wait()
        for kv in range(kv_heads):
            base = kv * 4 * HD
            queries = dq_ref[:, kv * LANES : (kv + 1) * LANES]
            queries = queries * tab_ref[0, q_rows, :] - swap_halves(queries) * tab_ref[1, q_rows, :]
            others = jnp.concatenate([dk_ref[kv, q_rows, :] * scale, dv_ref[kv, q_rows, :]], axis=1)
            others = others * tab_ref[2, q_rows, :] - swap_halves(others) * tab_ref[3, q_rows, :]
            turn_ref[q_rows, base : base + LANES] = queries.astype(LOW)
            turn_ref[q_rows, base + LANES : base + 2 * LANES] = others.astype(LOW)
        for q, row_at in ((1, place.cross_row), (0, place.pair_row)):
            away_ref[q, q_rows, :] = dot_nt(turn_ref[q_rows, :], wq_ref[row_at]).astype(LOW)
            copies.send(
                away_ref.at[q, window(block)], pair_in_ref.at[q, window(block)], away_in[q] + block, place.pair
            )
        for q, row_at in ((1, place.far_row), (0, place.row)):
            own_ref[q, q_rows, :] = dot_nt(turn_ref[q_rows, :], wq_ref[row_at])
        if block < chunks - 1:
            far_share(block + 1)
        if block == chunks - 2:
            y_far()
        if block == 0:
            first.pass_far(True)
            first.pass_over(False)

    columns = turn_ref.shape[1]
    mix_own.wait()
    for copy in late_reads:
        copy.wait()
    far_share(0)

    @pl.loop(0, parts)
    def _(part):
        features_here = pl.ds(pl.multiple_of(part * width, width), width)
        grads_ref[part, :, :columns] = dot_tn(normed_ref[:, features_here], turn_ref[...]).astype(LOW)
        grads_ref[part, :, columns:] = dot_tn(mixed_ref[...], gb_ref[part]).astype(LOW)

    gain = small_ref[place.row, GAIN_ONE : GAIN_ONE + 1, :].astype(F32)
    inner_in = copies.receivers(row_count)
    gain_sum = jnp.zeros((1, width), F32)
    for chunk in blocks:
        rows = slice(chunk * BLOCK_Q, (chunk + 1) * BLOCK_Q)
        copies.arrived(pair_in_ref.at[0, window(chunk)], away_in[0] + chunk, place.pair)
        copies.arrived(last_ref.at[window(chunk)], last_in + chunk, place.far)
        grad_normed = own_ref[0, rows, :] + pair_in_ref[0, rows, :].astype(F32) + last_ref[rows, :].astype(F32)
        own_ref[0, rows, :] = grad_normed
        along = grad_normed * hidden_ref[rows, :].astype(F32)
        gain_sum = gain_sum + jnp.sum(along * lse_ref[rows, RSTD_LANE : RSTD_LANE + 1], axis=0, keepdims=True)
        inner_ref[place.row, 0:1, rows] = row_of(jnp.sum(along * gain, axis=1, keepdims=True))
    sums_ref[...] = part_ref[...]
    sums_ref[GAIN_ONE : GAIN_ONE + 1, :] = gain_sum
    for k in range(1, row_count):
        copies.send(
            inner_ref.at[place.row], inner_ref.at[place.row], inner_in + k, (place.dp, place.row_at(k), place.col)
        )
    copies.arrived(y_last_ref.at[2], y_last + 2, place.far)
    for chunk in range(chunks):
        rows = slice(chunk * BLOCK_Q, (chunk + 1) * BLOCK_Q)
        mixture = y_own_ref[1, 0, rows, :].astype(F32) + y_in_ref[1, 0, rows, :].astype(F32)
        for slot in (0, 2):
            mixture = mixture + y_last_ref[slot, rows, :].astype(F32)
        out_ref[rows, :] = (resid_ref[rows, :] + mixture).astype(LOW)

    for k in range(1, row_count):
        copies.arrived(inner_ref.at[place.row_at(-k)], inner_in + k, place.here)
    inner = inner_ref[0, 0:1, :]
    for part in range(1, row_count):
        inner = inner + inner_ref[part, 0:1, :]
    for chunk in range(chunks):
        rows = slice(chunk * BLOCK_Q, (chunk + 1) * BLOCK_Q)
        rstd = lse_ref[rows, RSTD_LANE : RSTD_LANE + 1]
        cube = rstd * rstd * rstd * column_of(inner[:, rows]) / features
        grad_in_ref[rows, :] = (
            grad_ref[rows, :] + rstd * (own_ref[0, rows, :] * gain) - hidden_ref[rows, :].astype(F32) * cube
        )
    first.pass_corner()
    first.complete()
    z_shard = (place.block(place.dp, place.col_at(-LATE)), place.row)
    copies.arrived(res_all.at[z_shard], late_in, place.here)
    copies.arrived(cot_all.at[z_shard], late_in + 1, place.here)
    copies.finish()


def expert_grads(gate_pre, up_pre, grad_hidden):
    sig = 1.0 / (1.0 + jnp.exp(-gate_pre))
    silu = gate_pre * sig
    grad_gate = grad_hidden * up_pre * (sig * (1.0 + gate_pre * (1.0 - sig)))
    return (silu * up_pre).astype(LOW), grad_gate.astype(LOW), (grad_hidden * silu).astype(LOW)


def slot_picks(rank_row, capacity):
    at = lax.broadcasted_iota(jnp.int32, (capacity, rank_row.shape[1]), 0).astype(F32)
    return at == rank_row


def column_of(row):
    return jnp.broadcast_to(row, (LANES, row.shape[1])).T[:, 0:1]


def row_of(column):
    return jnp.broadcast_to(column, (column.shape[0], LANES)).T[0:1, :]


def experts_kernel(
    counts, low_hbm, resid_ref, cot_own_ref, packed_hbm, cot_given, small_ref, zo_hbm, wg_hbm, wu_hbm, wd_hbm,
    y_hbm, grad_ref, grad_low_ref, table_ref, part_ref, wo_hbm, cot_all, res_all, slots_x, slots_g, slots_mid,
    wg_ref, wu_ref, wd_ref, res_ref, cot_ref, x_ref, packed_ref, rank_ref, gate_ref, g_ref, pick_ref, eo_ref, back_ref,
    away_ref, pair_in_ref, own_ref, chip_ref, last_ref, stage_ref, gg_ref, gg_in_ref, rstd_ref, inner_ref, nx_ref,
    keep_x_ref, keep_g_ref, keep_mid_ref, keep_sems,
    send_sems, recv_sems,
):
    place = Place(counts)
    copies = Copies(send_sems, recv_sems)
    dp_count, row_count, col_count = counts
    _, parts, length, width = res_ref.shape
    experts, features, hidden_width = wg_ref.shape
    capacity = pick_ref.shape[0] // experts
    chunks = length // BLOCK_Q
    total_experts = dp_count * row_count * experts
    pair_count = length * TOP
    first_expert = (place.dp * row_count + place.row) * experts
    order = (place.other_dp, place.dp)
    all_here = say_hello(place.plane() + place.column())
    packed_own = copies.local(packed_hbm, packed_ref.at[place.dp])
    cot_in = [
        copies.local(cot_all.at[place.block(dp_at, place.col)], cot_ref.at[dp_at])
        for dp_at in (place.dp, place.other_dp)
    ]

    weights_in = [copies.local(*pair) for pair in ((wg_hbm, wg_ref), (wu_hbm, wu_ref), (wd_hbm, wd_ref))]

    def ranks_of(dp_at):
        ids = packed_ref[dp_at] // pair_count
        orders = (packed_ref[dp_at] - ids * pair_count).astype(F32)
        rows = []
        for e in range(experts):
            match = ids == first_expert + e
            known = jnp.max(jnp.where(match, 1.0, 0.0), axis=0, keepdims=True)
            at = jnp.sum(jnp.where(match, orders, 0.0), axis=0, keepdims=True)
            rows.append(jnp.where(known > 0.0, at, float(pair_count)))
        stacked = jnp.concatenate(rows + [jnp.zeros((LANES - experts, length), F32)], axis=0)
        columns = stacked.T
        for e in range(experts):
            count = jnp.zeros((1, length), F32)
            for start in range(0, length, BLOCK_Q):
                before = columns[start : start + BLOCK_Q, e : e + 1] < rows[e]
                count = count + jnp.sum(jnp.where(before, 1.0, 0.0), axis=0, keepdims=True)
            rank_ref[dp_at, e : e + 1, :] = jnp.where(rows[e] < float(pair_count), count, -1.0)

    def gather_grads(dp_at):
        @pl.loop(0, experts)
        def _(e):
            pick = slot_picks(rank_ref[dp_at, pl.ds(e, 1), :], capacity).astype(F32).astype(LOW)
            slots = pl.ds(pl.multiple_of(e * capacity, capacity), capacity)
            for part in range(parts):
                g_ref[dp_at, part, slots, :] = dot_nn(pick, cot_ref[dp_at, part]).astype(LOW)

    packed_own.wait()
    ranks_of(place.dp)
    cot_in[0].wait()
    gather_grads(place.dp)
    all_here()

    own_low = res_ref.at[place.dp, place.row]
    packed_over = copies.receivers()
    copies.send(packed_hbm, packed_ref.at[place.dp], packed_over, place.over)
    low_own = copies.local(low_hbm, own_low)
    halves = 2
    half_rows = length // halves
    res_at = copies.receivers(7 * halves)

    def halved(ref, half):
        return ref.at[pl.ds(half * half_rows, half_rows)]

    far_low = res_ref.at[place.dp, place.far_row]
    over_low = res_ref.at[place.other_dp, place.row]
    corner_low = res_ref.at[place.other_dp, place.far_row]
    for half in range(halves):
        source, target = halved(low_hbm, half), halved(own_low, half)
        copies.send(source, target, res_at + half, place.far)
        copies.send(source, target, res_at + halves + half, place.over)
    copies.send(low_hbm, own_low, res_at + 2 * halves, place.pair)
    own_block = place.block(place.dp, place.col)
    res_z, cot_z = copies.receivers(col_count), copies.receivers(col_count)
    for k, on_cot in ((SECOND, True), (FIRST, False), (SECOND, False)):
        peer = (place.dp, place.row, place.col_at(k))
        if on_cot:
            own_cot = cot_all.at[own_block, place.row]
            copies.send(own_cot, own_cot, cot_z + k, peer)
        else:
            copies.send(low_hbm, res_all.at[own_block, place.row], res_z + k, peer)

    def pass_side(half):
        copies.arrived(halved(far_low, half), res_at + half, place.far)
        copies.arrived(halved(over_low, half), res_at + halves + half, place.over)
        corner, peer = (far_low, place.over) if half == 0 else (over_low, place.far)
        copies.send(halved(corner, half), halved(corner, half), res_at + 3 * halves + half, peer)
        for k, ref in ((4, far_low), (5, over_low)):
            copies.send(halved(ref, half), halved(ref, half), res_at + k * halves + half, place.pair)

    def pass_corner(half):
        copies.arrived(halved(corner_low, half), res_at + 3 * halves + half, place.here)
        copies.send(
            halved(corner_low, half), halved(corner_low, half), res_at + 6 * halves + half, place.pair
        )

    copies.arrived(packed_ref.at[place.other_dp], packed_over, place.over)
    ranks_of(place.other_dp)
    pass_side(0)
    cot_in[1].wait()
    gather_grads(place.other_dp)
    pass_side(1)
    pass_corner(0)
    pass_corner(1)

    wo_in = copies.receivers(row_count)
    own_wo = copies.local(zo_hbm.at[place.row], stage_ref.at[0, pl.ds(0, zo_hbm.shape[1])])

    low_own.wait()
    copies.arrived(res_ref.at[place.dp, place.pair_row], res_at + 2 * halves, place.pair)
    for half in range(halves):
        for k, dp_at, row_at in (
            (4, place.dp, place.cross_row), (5, place.other_dp, place.pair_row), (6, place.other_dp, place.cross_row)
        ):
            copies.arrived(halved(res_ref.at[dp_at, row_at], half), res_at + k * halves + half, place.pair)
    for copy in weights_in:
        copy.wait()
    own_wo.wait()
    kept_wo = copies.local(stage_ref.at[0, pl.ds(0, zo_hbm.shape[1])], wo_hbm.at[place.row])
    kept_wo.wait()
    res_kept = [
        copies.local(res_ref.at[dp_at], res_all.at[place.block(dp_at, place.col)])
        for dp_at in (place.dp, place.other_dp)
    ]
    first, second = (Spread(place, copies, cot_all, place.col_at(-k)) for k in (FIRST, SECOND))
    first.plan_corner(False)
    second.plan_corner(True)
    first.begin(True)
    copies.arrived(
        cot_all.at[place.block(place.dp, place.col_at(-SECOND)), place.row], cot_z + SECOND, place.here
    )
    second.begin(True)

    own_scaled = place.row
    gg_same, gg_other = copies.receivers(row_count), copies.receivers(row_count)
    pair_in = copies.receivers(2 * dp_count)
    last_over, last_across, last_far = (copies.receivers() for _ in range(3))
    table_in = copies.receivers(col_count)

    kept_pairs = ((keep_x_ref, slots_x), (keep_g_ref, slots_g), (keep_mid_ref, slots_mid))
    for turn, dp_at in enumerate(order):
        last = turn == dp_count - 1

        @pl.loop(0, chunks)
        def _(chunk):
            rows = pl.ds(pl.multiple_of(chunk * BLOCK_Q, BLOCK_Q), BLOCK_Q)
            total = jnp.zeros((BLOCK_Q, 1), F32)
            for part in range(parts):
                piece = res_ref[dp_at, part, rows, :].astype(F32)
                total = total + jnp.sum(piece * piece, axis=1, keepdims=True)
            rstd = lax.rsqrt(total / features + EPSILON)
            for part in range(parts):
                piece = res_ref[dp_at, part, rows, :].astype(F32)
                gain = small_ref[part, GAIN_TWO : GAIN_TWO + 1, :].astype(F32)
                x_ref[rows, part * width : (part + 1) * width] = (piece * rstd * gain).astype(LOW)
            table_ref[place.col, dp_at, RSTD_ROW : RSTD_ROW + 1, rows] = row_of(rstd)
            if last:
                rstd_ref[rows, :] = jnp.broadcast_to(rstd, (BLOCK_Q, LANES))
                piece = res_ref[dp_at, own_scaled, rows, :].astype(F32)
                gain = small_ref[own_scaled, GAIN_TWO : GAIN_TWO + 1, :].astype(F32)
                nx_ref[rows, :] = (piece * rstd * gain).astype(LOW)

        logits = jnp.zeros((total_experts, length), F32)
        for part in range(parts):
            logits = logits + dot_nt(
                small_ref[part, :total_experts, :], x_ref[:, part * width : (part + 1) * width]
            )
        ids = packed_ref[dp_at] // pair_count
        expert_at = lax.broadcasted_iota(jnp.int32, (total_experts, length), 0)
        chosen = expert_at == ids[0:1, :]
        for k in range(1, TOP):
            chosen = chosen | (expert_at == ids[k : k + 1, :])
        shown = jnp.where(chosen, logits, NEG_LARGE)
        weights = jnp.where(chosen, jnp.exp(shown - jnp.max(shown, axis=0, keepdims=True)), 0.0)
        gate_ref[...] = weights / jnp.sum(weights, axis=0, keepdims=True)
        table_ref[place.col, dp_at, 0:experts, :] = rank_ref[dp_at, 0:experts, :]
        for e in range(experts):
            table_ref[place.col, dp_at, experts + e : experts + e + 1, :] = gate_ref[pl.ds(first_expert + e, 1), :]

        @pl.loop(0, experts)
        def _(e):
            if last:

                @pl.when(e == 1)
                def _():
                    second.pass_far(True)
                    second.pass_over(False)

                pl.when(e == experts - 1)(first.pass_corner)


            keep = lax.rem(e, 2)
            kept = [
                pltpu.make_async_copy(held.at[keep], target.at[turn, e], keep_sems.at[k, keep])
                for k, (held, target) in enumerate(kept_pairs)
            ]

            @pl.when(e + turn * experts >= 2)
            def _():
                for copy in kept:
                    copy.wait()

            here = slot_picks(rank_ref[dp_at, pl.ds(e, 1), :], capacity)
            pick = here.astype(F32).astype(LOW)
            slots = pl.ds(pl.multiple_of(e * capacity, capacity), capacity)
            pick_ref[slots, :] = pick
            gate_slot = jnp.sum(
                jnp.where(here, gate_ref[pl.ds(first_expert + e, 1), :], 0.0), axis=1, keepdims=True
            )
            x = dot_nn(pick, x_ref[...]).astype(LOW)
            keep_x_ref[keep] = x
            grad_hidden = jnp.zeros((capacity, hidden_width), F32)
            for part in range(parts):
                pair_grad = (g_ref[dp_at, part, slots, :].astype(F32) * gate_slot).astype(LOW)
                keep_g_ref[keep, :, part * width : (part + 1) * width] = pair_grad
                grad_hidden = grad_hidden + dot_nt(
                    pair_grad, wd_ref[e, :, part * width : (part + 1) * width]
                )
            hidden, grad_gate, grad_up = expert_grads(dot_nn(x, wg_ref[e]), dot_nn(x, wu_ref[e]), grad_hidden)
            keep_mid_ref[keep, 0] = hidden
            keep_mid_ref[keep, 1] = grad_gate
            keep_mid_ref[keep, 2] = grad_up
            for copy in kept:
                copy.start()
            along = jnp.zeros((capacity, 1), F32)
            for part in range(parts):
                cols = slice(part * width, (part + 1) * width)
                out = dot_nn(hidden, wd_ref[e, :, cols]).astype(LOW).astype(F32)
                along = along + jnp.sum(g_ref[dp_at, part, slots, :].astype(F32) * out, axis=1, keepdims=True)
                eo_ref[part, slots, :] = (out * gate_slot).astype(LOW)
                back_ref[part, slots, :] = (
                    dot_nt(grad_gate, wg_ref[e, cols, :]) + dot_nt(grad_up, wu_ref[e, cols, :])
                ).astype(LOW)
            gg_ref[dp_at, pl.ds(e, 1), :] = jnp.sum(jnp.where(here, along, 0.0), axis=0, keepdims=True)

        if not last:
            first.pass_far(False)
            first.pass_over(True)
        owner = place.dp * row_count + place.row
        if last:
            for k in range(1, row_count):
                copies.send(gg_ref.at[dp_at], gg_in_ref.at[owner], gg_same + k, (dp_at, place.row_at(k), place.col))
            gg_in_ref[owner] = gg_ref[dp_at]
        else:
            for k in range(row_count):
                copies.send(gg_ref.at[dp_at], gg_in_ref.at[owner], gg_other + k, (dp_at, place.row_at(k), place.col))

        for q, row_at in enumerate((place.pair_row, place.cross_row)):
            away_ref[turn, q] = dot_tn(pick_ref[...], back_ref[row_at]).astype(LOW)
            copies.send(away_ref.at[turn, q], pair_in_ref.at[turn, q], pair_in + 2 * turn + q, place.pair)
        for q, row_at in enumerate((place.far_row, place.row)):
            own_ref[q] = dot_tn(pick_ref[...], back_ref[row_at])
        copies.arrived(pair_in_ref.at[turn, 1], pair_in + 2 * turn + 1, place.pair)
        far_sum = own_ref[0] + pair_in_ref[turn, 1].astype(F32)
        if last:
            copies.arrived(last_ref.at[1], last_across, place.over)
            chip_ref[turn, 1] = (far_sum + last_ref[1].astype(F32)).astype(LOW)
            copies.send(chip_ref.at[turn, 1], last_ref.at[2], last_far, place.far)
        else:
            chip_ref[turn, 1] = far_sum.astype(LOW)
            copies.send(chip_ref.at[turn, 1], last_ref.at[1], last_across, place.over)
        copies.arrived(pair_in_ref.at[turn, 0], pair_in + 2 * turn, place.pair)
        if last:
            own_ref[1] = own_ref[1] + pair_in_ref[turn, 0].astype(F32)
        else:
            chip_ref[turn, 0] = (own_ref[1] + pair_in_ref[turn, 0].astype(F32)).astype(LOW)
            copies.send(chip_ref.at[turn, 0], last_ref.at[0], last_over, place.over)
            for k in range(col_count):
                source = place.col_at(k)
                mine = source == place.row
                step = lax.rem(source - place.row + row_count, row_count)
                copies.send(
                    zo_hbm.at[source], wo_hbm.at[place.row], wo_in + step, (place.dp, source, place.col), jnp.logical_not(mine)
                )

        for part in range(parts):
            stage_ref[part] = dot_tn(pick_ref[...], eo_ref[part]).astype(LOW)
        kept = copies.local(stage_ref, y_hbm.at[dp_at])
        kept.wait()

    for k in range(1, col_count):
        copies.send(table_ref.at[place.col], table_ref.at[place.col], table_in + k, (place.dp, place.row, place.col_at(k)))

    for k in range(1, row_count):
        copies.arrived(gg_in_ref.at[place.dp * row_count + place.row_at(-k)], gg_same + k, place.here)
    for k in range(row_count):
        copies.arrived(gg_in_ref.at[place.other_dp * row_count + place.row_at(-k)], gg_other + k, place.here)
    along = jnp.concatenate([gg_in_ref[owner, :experts, :] for owner in range(dp_count * row_count)], axis=0)
    gates = gate_ref[...]
    grad_logits = (gates * (along - jnp.sum(gates * along, axis=0, keepdims=True))).astype(LOW)
    router = small_ref[place.row, :total_experts, :]
    gain = small_ref[place.row, GAIN_TWO : GAIN_TWO + 1, :].astype(F32)
    part_ref[...] = jnp.zeros_like(part_ref)
    part_ref[:total_experts, :] = dot_nn(grad_logits, nx_ref[...])
    own_ref[1] = own_ref[1] + dot_tn(grad_logits, router)

    copies.arrived(last_ref.at[0], last_over, place.over)
    copies.arrived(last_ref.at[2], last_far, place.far)
    inner_in = copies.receivers(row_count)
    gain_sum = jnp.zeros((1, width), F32)
    for chunk in range(chunks):
        rows = slice(chunk * BLOCK_Q, (chunk + 1) * BLOCK_Q)
        grad_normed = own_ref[1, rows, :]
        for k in (0, 2):
            grad_normed = grad_normed + last_ref[k, rows, :].astype(F32)
        own_ref[0, rows, :] = grad_normed
        along = grad_normed * resid_ref[rows, :]
        gain_sum = gain_sum + jnp.sum(along * rstd_ref[rows, 0:1], axis=0, keepdims=True)
        inner_ref[place.row, 0:1, rows] = row_of(jnp.sum(along * gain, axis=1, keepdims=True))
    part_ref[GAIN_TWO : GAIN_TWO + 1, :] = gain_sum
    for k in range(1, row_count):
        copies.send(
            inner_ref.at[place.row], inner_ref.at[place.row], inner_in + k, (place.dp, place.row_at(k), place.col)
        )
    for k in range(1, row_count):
        copies.arrived(inner_ref.at[place.row_at(-k)], inner_in + k, place.here)
    inner = inner_ref[0, 0:1, :]
    for part in range(1, row_count):
        inner = inner + inner_ref[part, 0:1, :]
    for chunk in range(chunks):
        rows = slice(chunk * BLOCK_Q, (chunk + 1) * BLOCK_Q)
        rstd = rstd_ref[rows, 0:1]
        cube = rstd * rstd * rstd * column_of(inner[:, rows]) / features
        grad = (
            cot_own_ref[rows, :].astype(F32) + rstd * (own_ref[0, rows, :] * gain) - resid_ref[rows, :] * cube
        )
        grad_ref[rows, :] = grad
        grad_low_ref[rows, :] = grad.astype(LOW)

    for copy in res_kept:
        copy.wait()
    for keep in range(2):
        for k, (held, target) in enumerate(kept_pairs):
            pltpu.make_async_copy(held.at[keep], target.at[0, 0], keep_sems.at[k, keep]).wait()
    second.pass_corner()
    first.complete()
    second.complete()
    for k in (FIRST, SECOND):
        z_shard = (place.block(place.dp, place.col_at(-k)), place.row)
        copies.arrived(res_all.at[z_shard], res_z + k, place.here)
    for k in range(1, row_count):
        copies.arrived(wo_hbm.at[place.row_at(-k)], wo_in + k, place.here)
    for k in range(1, col_count):
        copies.arrived(table_ref.at[place.col_at(-k)], table_in + k, place.here)
    copies.finish()


def slot_grads(picked, rank_row, gate_row, rstd_row, res, cot, small_ref, wg, wu, wd):
    here = slot_picks(rank_row, picked)
    pick = here.astype(F32).astype(LOW)
    gate_slot = jnp.sum(jnp.where(here, gate_row, 0.0), axis=1, keepdims=True)
    rstd_slot = jnp.sum(jnp.where(here, rstd_row, 0.0), axis=1, keepdims=True)
    parts = res.shape[0]
    x = jnp.concatenate(
        [
            (
                dot_nn(pick, res[part]) * rstd_slot * small_ref[part, GAIN_TWO : GAIN_TWO + 1, :].astype(F32)
            ).astype(LOW)
            for part in range(parts)
        ],
        axis=1,
    )
    pair_grad = jnp.concatenate(
        [(dot_nn(pick, cot[part]) * gate_slot).astype(LOW) for part in range(parts)], axis=1
    )
    hidden, grad_gate, grad_up = expert_grads(dot_nn(x, wg), dot_nn(x, wu), dot_nt(pair_grad, wd))
    return x, pair_grad, hidden, grad_gate, grad_up


def weight_grads_kernel(
    counts, res_given, cot_given, grads_hbm, slots_x, slots_g, slots_mid, part_ref, table_ref, small_ref,
    wg_hbm, wu_hbm, wd_hbm,
    res_all, cot_all, dg_hbm, du_hbm, dd_hbm, own_ref, sums_ref,
    wg_ref, wu_ref, wd_ref, parts_ref, dg_ref, du_ref, dd_ref, res_ref, cot_ref, x_ref, g_ref, mid_ref, grads_in_ref, sum_ref,
    sems, keep_sems, out_sems, send_sems, recv_sems,
):
    place = Place(counts)
    copies = Copies(send_sems, recv_sems)
    dp_count, row_count, col_count = counts
    experts = wg_ref.shape[0]
    _, parts, length, width = res_all.shape
    capacity = length * TOP // (dp_count * row_count * experts)
    far_side = [(place.other_dp, place.row, place.col_at(k)) for k in range(1, col_count)]
    all_here = say_hello(
        place.plane()
        + place.column()
        + [
            (place.dp, place.row_at(j), place.col_at(k))
            for j in range(1, row_count)
            for k in range(1, col_count)
        ]
        + far_side
    )
    steps = 5
    before_late = 4 * experts

    def fetch(step):
        back = jnp.where(step < 2, FIRST, jnp.where(step < 4, SECOND, LATE))
        dp_at = lax.rem(place.dp + lax.rem(step, 2), dp_count)
        col_at = place.col_at(-back)
        b, slot = place.block(dp_at, col_at), lax.rem(step, 2)
        return dp_at, col_at, slot, (
            pltpu.make_async_copy(res_all.at[b], res_ref.at[slot], sems.at[slot]),
            pltpu.make_async_copy(cot_all.at[b], cot_ref.at[slot], sems.at[2 + slot]),
        )

    def kept_slots(turn):
        at, e, slot = turn // experts, lax.rem(turn, experts), lax.rem(turn, 2)
        pairs = ((slots_x, x_ref), (slots_g, g_ref), (slots_mid, mid_ref))
        return [
            pltpu.make_async_copy(source.at[at, e], target.at[slot], keep_sems.at[k, slot])
            for k, (source, target) in enumerate(pairs)
        ]

    for copy in fetch(0)[3]:
        copy.start()
    weights_in = [copies.local(*pair) for pair in ((wg_hbm, wg_ref), (wu_hbm, wu_ref), (wd_hbm, wd_ref))]
    for copy in kept_slots(0):
        copy.start()
    parts_ref[0] = part_ref[...]
    others = place.column() + [place.over] + far_side
    sums_in = copies.receivers(len(others) + 1)
    sum_sends = [
        copies.plan(parts_ref.at[0], parts_ref.at[k + 1], sums_in + k + 1, peer) for k, peer in enumerate(others)
    ]

    grads_in = copies.receivers(col_count)
    grads_kept = copies.local(grads_hbm.at[place.col], grads_in_ref.at[place.col])
    mine = place.row == place.col
    over_in, swap_in = copies.receivers(), copies.receivers()
    to_over = copies.plan(sum_ref.at[0], sum_ref.at[1], over_in, place.over)
    to_swap = remote(
        sum_ref.at[2], sum_ref.at[3], copies.send_sems.at[copies.sends], copies.recv_sems.at[swap_in],
        (place.dp, place.col, place.row),
    )
    copies.sends += 1
    copies.open.append((to_swap, jnp.logical_not(mine)))
    two_res, three_res, three_cot = (
        Spread(place, copies, array, place.col_at(-k))
        for k, array in ((SECOND, res_all), (LATE, res_all), (LATE, cot_all))
    )
    for spread, by_over in ((two_res, True), (three_res, True), (three_cot, False)):
        spread.plan_corner(by_over)
    grad_sends = [
        copies.plan(
            grads_hbm.at[place.col_at(k)], grads_in_ref.at[place.col], grads_in + k,
            (place.dp, place.row, place.col_at(k)),
        )
        for k in range(1, col_count)
    ]

    def begin():
        all_here()
        two_res.begin(True)
        three_res.begin(True)
        three_cot.begin(False)
        for copy in grad_sends + sum_sends:
            copy.start()

    def sum_columns():
        grads_kept.wait()
        for k in range(1, col_count):
            copies.arrived(grads_in_ref.at[place.col_at(-k)], grads_in + k, place.here)
        total = grads_in_ref[0].astype(F32)
        for col_at in range(1, col_count):
            total = total + grads_in_ref[col_at].astype(F32)
        sum_ref[0] = total.astype(LOW)
        to_over.start()

    def sum_over():
        copies.arrived(sum_ref.at[1], over_in, place.over)
        total = sum_ref[0].astype(F32) + sum_ref[1].astype(F32)
        sum_ref[2] = total.astype(LOW)
        own_ref[...] = total
        pl.when(jnp.logical_not(mine))(to_swap.start)

    def sum_parts():
        total = parts_ref[0]
        for k in range(len(others)):
            copies.arrived(parts_ref.at[k + 1], sums_in + k + 1, place.here)
            total = total + parts_ref[k + 1]
        sums_ref[...] = total

    def take_swapped():
        @pl.when(jnp.logical_not(mine))
        def _():
            copies.arrived(sum_ref.at[3], swap_in, place.here)
            own_ref[...] = sum_ref[3].astype(F32)

    events = {
        1: [begin],
        5: [lambda: two_res.pass_far(True), lambda: two_res.pass_over(False), three_cot.send_over],
        7: [two_res.complete_same],
        10: [lambda: three_res.pass_far(True), lambda: three_res.pass_over(False)],
        11: [two_res.pass_corner, two_res.complete_other],
        12: [lambda: three_cot.pass_far(False), sum_columns],
        15: [lambda: three_cot.pass_over(True), three_res.complete_same, three_cot.complete_same],
        16: [three_res.pass_corner, sum_over],
        18: [three_cot.pass_corner],
        19: [sum_parts],
    }
    dg_ref[...] = jnp.zeros_like(dg_ref)
    du_ref[...] = jnp.zeros_like(du_ref)
    dd_ref[...] = jnp.zeros_like(dd_ref)
    for copy in weights_in:
        copy.wait()

    def other_blocks(turn):
        step, e = turn // experts, lax.rem(turn, experts)
        for at, actions in events.items():

            @pl.when(turn == at)
            def _(actions=actions):
                for action in actions:
                    action()

        dp_at, col_at, slot, arriving = fetch(step)

        @pl.when(e == 0)
        def _():
            for copy in arriving:
                copy.wait()

        @pl.when((e == experts - 1) & (step + 1 < steps))
        def _():
            for copy in fetch(step + 1)[3]:
                copy.start()

        x, pair_grad, hidden, grad_gate, grad_up = slot_grads(
            capacity,
            table_ref[col_at, dp_at, pl.ds(e, 1), :],
            table_ref[col_at, dp_at, pl.ds(experts + e, 1), :],
            table_ref[col_at, dp_at, RSTD_ROW : RSTD_ROW + 1, :],
            res_ref.at[slot], cot_ref.at[slot], small_ref, wg_ref[e], wu_ref[e], wd_ref[e],
        )
        dd_ref[e] += dot_tn(hidden, pair_grad)
        dg_ref[e] += dot_tn(x, grad_gate)
        du_ref[e] += dot_tn(x, grad_up)

        @pl.when(step == steps - 1)
        def _():
            for k, (source, target) in enumerate(((dg_ref, dg_hbm), (du_ref, du_hbm), (dd_ref, dd_hbm))):
                pltpu.make_async_copy(source.at[e], target.at[e], out_sems.at[k, e]).start()

    pl.loop(0, before_late)(other_blocks)

    @pl.loop(0, dp_count * experts)
    def _(turn):
        e, slot = lax.rem(turn, experts), lax.rem(turn, 2)
        for copy in kept_slots(turn):
            copy.wait()

        @pl.when(turn + 1 < dp_count * experts)
        def _():
            for copy in kept_slots(turn + 1):
                copy.start()

        dd_ref[e] += dot_tn(mid_ref[slot, 0], g_ref[slot])
        dg_ref[e] += dot_tn(x_ref[slot], mid_ref[slot, 1])
        du_ref[e] += dot_tn(x_ref[slot], mid_ref[slot, 2])

    pl.loop(before_late, steps * experts)(other_blocks)
    take_swapped()
    three_res.complete_other()
    three_cot.complete_other()
    for e in range(experts):
        for k, (source, target) in enumerate(((dg_ref, dg_hbm), (du_ref, du_hbm), (dd_ref, dd_hbm))):
            pltpu.make_async_copy(source.at[e], target.at[e], out_sems.at[k, e]).wait()
    copies.finish()


def last_grads_kernel(
    counts, res_all, cot_all, table_ref, small_ref, wg_ref, wu_ref, wd_ref, dg_in, du_in, dd_in,
    out_in, grad_in_in, attn_in, sums_in,
    dg_ref, du_ref, dd_ref, out_ref, grad_in_ref, qkv_ref, wo_ref, router_ref, one_ref, two_ref,
    res_ref, cot_ref, sems,
):
    dp_count, row_count, col_count = counts
    e = pl.program_id(0)
    experts = pl.num_programs(0)
    _, parts, length, width = res_all.shape
    capacity = length * TOP // (dp_count * row_count * experts)
    col_at = lax.rem(lax.axis_index("col") + col_count - LATE, col_count)

    dp_at = dp_count - 1 - lax.axis_index("dp")
    b = dp_at * col_count + col_at
    arriving = (
        pltpu.make_async_copy(res_all.at[b], res_ref, sems.at[0]),
        pltpu.make_async_copy(cot_all.at[b], cot_ref, sems.at[1]),
    )

    @pl.when(e == 0)
    def _():
        for copy in arriving:
            copy.start()

    out_ref[...] = out_in[...]
    grad_in_ref[...] = grad_in_in[...]
    group, columns = qkv_ref.shape[1:]
    for head in range(group):
        qkv_ref[:, head, :] = attn_in[:, head * columns : (head + 1) * columns]
    wo_ref[...] = attn_in[:, group * columns :]

    @pl.when(e == experts - 1)
    def _():
        router_ref[...] = sums_in[:GAIN_ONE, :]
        one_ref[...] = sums_in[GAIN_ONE : GAIN_ONE + 1, :]
        two_ref[...] = sums_in[GAIN_TWO : GAIN_TWO + 1, :]

    @pl.when(e == 0)
    def _():
        for copy in arriving:
            copy.wait()

    x, pair_grad, hidden, grad_gate, grad_up = slot_grads(
        capacity,
        table_ref[col_at, dp_at, pl.ds(e, 1), :],
        table_ref[col_at, dp_at, pl.ds(experts + e, 1), :],
        table_ref[col_at, dp_at, RSTD_ROW : RSTD_ROW + 1, :],
        res_ref, cot_ref, small_ref, wg_ref[0], wu_ref[0], wd_ref[0],
    )
    dd_ref[0] = dd_in[0] + dot_tn(hidden, pair_grad)
    dg_ref[0] = dg_in[0] + dot_tn(x, grad_gate)
    du_ref[0] = du_in[0] + dot_tn(x, grad_up)


def fast_device(
    hidden_in, norm_gain, w_qkv, w_out, ffn_gain, router, w_gate, w_up, w_down, cotangent,
    segment_ids, expert_ids, pair_order,
):
    dp_count, row_count, col_count = (lax.axis_size(name) for name in ("dp", "row", "col"))
    my_dp, my_row, my_col = (lax.axis_index(name) for name in ("dp", "row", "col"))
    length, width = hidden_in.shape
    kv_local = w_qkv.shape[1]
    head_width = kv_local * (HQ // HK) * HD
    qkv_width = kv_local * (HQ // HK + 2) * HD
    exp_local, _, hidden_width = w_gate.shape
    capacity = length * TOP // EXPERTS
    blocks = dp_count * col_count
    vmem = pl.BlockSpec(memory_space=pltpu.VMEM)
    hbm = pl.BlockSpec(memory_space=pl.ANY)
    params = pltpu.CompilerParams(vmem_limit_bytes=VMEM_BYTES)

    packed = (expert_ids * (length * TOP) + pair_order).T
    own_q = w_qkv.reshape(width, qkv_width)
    own_o = w_out.reshape(head_width, width)
    small = jnp.concatenate(
        [router.T, norm_gain[None], ffn_gain[None], jnp.zeros((SMALL_ROWS - 2 - EXPERTS, width), LOW)], axis=0
    )
    seg_rows = jnp.broadcast_to(segment_ids, (8, length)).astype(F32)
    tables = jnp.asarray(rope_lanes(length))
    counts = (dp_count, row_count, col_count)
    (
        resid_mid, resid_low, mixed, normed_one, query_rot, key_rot, value_low, logs,
        wq_rows, wo_cols, small_all, seg_all, cot_all,
    ) = pl.pallas_call(
        functools.partial(attend_forward_kernel, counts),
        out_shape=(
            jax.ShapeDtypeStruct((length, width), F32),
            jax.ShapeDtypeStruct((length, width), LOW),
            jax.ShapeDtypeStruct((length, head_width), LOW),
            jax.ShapeDtypeStruct((length, D), LOW),
            jax.ShapeDtypeStruct((2 * kv_local, length, HD), LOW),
            jax.ShapeDtypeStruct((kv_local, length, HD), LOW),
            jax.ShapeDtypeStruct((kv_local, length, HD), LOW),
            jax.ShapeDtypeStruct((length, LANES), F32),
            jax.ShapeDtypeStruct((row_count, width, qkv_width), LOW),
            jax.ShapeDtypeStruct((col_count, head_width, width), LOW),
            jax.ShapeDtypeStruct((row_count, SMALL_ROWS, width), LOW),
            jax.ShapeDtypeStruct((row_count, 8, length), F32),
            jax.ShapeDtypeStruct((blocks, row_count, length, width), LOW),
        ),
        in_specs=[hbm] * 7,
        out_specs=[vmem] * 2 + [hbm] * 2 + [vmem] * 4 + [hbm] + [vmem] * 3 + [hbm],
        scratch_shapes=[
            pltpu.VMEM((row_count, length, head_width), LOW),
            pltpu.VMEM((length, D), LOW),
            pltpu.VMEM((row_count, width, qkv_width), LOW),
            pltpu.VMEM(tables.shape, F32),
            pltpu.VMEM((row_count, length, width), LOW),
            pltpu.VMEM((col_count, width, qkv_width), LOW),
            pltpu.VMEM((length, width), LOW),
            pltpu.VMEM((length, LANES), F32),
            pltpu.SemaphoreType.DMA((80,)),
            pltpu.SemaphoreType.DMA((80,)),
        ],
        compiler_params=pltpu.CompilerParams(
            vmem_limit_bytes=VMEM_BYTES, collective_id=1, has_side_effects=True
        ),
        cost_estimate=pl.CostEstimate(flops=50_000_000_000, bytes_accessed=30_000_000, transcendentals=0),
        name="attend_forward",
    )(hidden_in, own_q, own_o, small, seg_rows, cotangent, tables)
    block_low = jax.ShapeDtypeStruct((length, width), LOW)
    block_float = jax.ShapeDtypeStruct((length, width), F32)
    slots = exp_local * capacity
    plane = (dp_count, row_count, length, width)
    every = jax.ShapeDtypeStruct((blocks, row_count, length, width), LOW)
    y_part, grad_resid, grad_low, table, small_part, wo_rows, cot_all, res_all, *kept_slots = pl.pallas_call(
        functools.partial(experts_kernel, counts),
        out_shape=(
            jax.ShapeDtypeStruct(plane, LOW),
            block_float,
            block_low,
            jax.ShapeDtypeStruct((col_count, dp_count, 16, length), F32),
            jax.ShapeDtypeStruct((SMALL_ROWS, width), F32),
            jax.ShapeDtypeStruct((row_count, head_width, width), LOW),
            every,
            every,
            jax.ShapeDtypeStruct((dp_count, exp_local, capacity, D), LOW),
            jax.ShapeDtypeStruct((dp_count, exp_local, capacity, D), LOW),
            jax.ShapeDtypeStruct((dp_count, exp_local, 3, capacity, hidden_width), LOW),
        ),
        input_output_aliases={4: 6},
        in_specs=[hbm, vmem, vmem, hbm, hbm, vmem, hbm, hbm, hbm, hbm],
        out_specs=[hbm] + [vmem] * 4 + [hbm] * 6,
        scratch_shapes=[
            pltpu.VMEM(w_gate.shape, LOW),
            pltpu.VMEM(w_up.shape, LOW),
            pltpu.VMEM(w_down.shape, LOW),
            pltpu.VMEM(plane, LOW),
            pltpu.VMEM(plane, LOW),
            pltpu.VMEM((length, D), LOW),
            pltpu.VMEM((dp_count, TOP, length), jnp.int32),
            pltpu.VMEM((dp_count, 8, length), F32),
            pltpu.VMEM((EXPERTS, length), F32),
            pltpu.VMEM((dp_count, row_count, slots, width), LOW),
            pltpu.VMEM((slots, length), LOW),
            pltpu.VMEM((row_count, slots, width), LOW),
            pltpu.VMEM((row_count, slots, width), LOW),
            pltpu.VMEM((dp_count, 2, length, width), LOW),
            pltpu.VMEM((dp_count, 2, length, width), LOW),
            pltpu.VMEM((2, length, width), F32),
            pltpu.VMEM((dp_count, 2, length, width), LOW),
            pltpu.VMEM((3, length, width), LOW),
            pltpu.VMEM((row_count, length, width), LOW),
            pltpu.VMEM((dp_count, 8, length), F32),
            pltpu.VMEM((dp_count * row_count, 8, length), F32),
            pltpu.VMEM((length, LANES), F32),
            pltpu.VMEM((row_count, 8, length), F32),
            pltpu.VMEM((length, width), LOW),
            pltpu.VMEM((2, capacity, D), LOW),
            pltpu.VMEM((2, capacity, D), LOW),
            pltpu.VMEM((2, 3, capacity, hidden_width), LOW),
            pltpu.SemaphoreType.DMA((3, 2)),
            pltpu.SemaphoreType.DMA((80,)),
            pltpu.SemaphoreType.DMA((80,)),
        ],
        compiler_params=pltpu.CompilerParams(
            vmem_limit_bytes=VMEM_BYTES, collective_id=2, has_side_effects=True
        ),
        cost_estimate=pl.CostEstimate(flops=80_000_000_000, bytes_accessed=50_000_000, transcendentals=0),
        name="experts",
    )(resid_low, resid_mid, cotangent, packed, cot_all, small_all, wo_cols, w_gate, w_up, w_down)

    halves = (dp_count, 2, length, width)
    half = (2, length, width)
    layer_out, grad_in, grads_part, small_part, res_all, cot_all = pl.pallas_call(
        functools.partial(attend_backward_kernel, counts),
        out_shape=(
            block_low,
            block_float,
            jax.ShapeDtypeStruct((row_count, width, qkv_width + width), LOW),
            jax.ShapeDtypeStruct((SMALL_ROWS, width), F32),
            every,
            every,
        ),
        input_output_aliases={17: 4, 18: 5},
        in_specs=[hbm] * 4 + [vmem] * 2 + [hbm] * 2 + [vmem] * 7 + [hbm] * 5,
        out_specs=[vmem] * 4 + [hbm] * 2,
        scratch_shapes=[
            pltpu.VMEM((length, width), F32),
            pltpu.VMEM((length, width), LOW),
            pltpu.VMEM((length, width), F32),
            pltpu.VMEM((length, D), LOW),
            pltpu.VMEM(tables.shape, F32),
            pltpu.VMEM((row_count, length, width), LOW),
            pltpu.VMEM((length, head_width), LOW),
            pltpu.VMEM((BLOCK_Q, head_width), LOW),
            pltpu.VMEM((BLOCK_Q, head_width), F32),
            pltpu.VMEM((kv_local, length, HD), F32),
            pltpu.VMEM((kv_local, length, HD), F32),
            pltpu.VMEM((length, qkv_width), LOW),
            pltpu.VMEM((length, LANES), F32),
            pltpu.VMEM(halves, LOW),
            pltpu.VMEM(halves, LOW),
            pltpu.VMEM(halves, LOW),
            pltpu.VMEM((3, length, width), LOW),
            pltpu.VMEM(half, LOW),
            pltpu.VMEM(half, LOW),
            pltpu.VMEM(half, F32),
            pltpu.VMEM((length, width), LOW),
            pltpu.VMEM((length, width), LOW),
            pltpu.VMEM((row_count, 8, length), F32),
            pltpu.SemaphoreType.DMA((80,)),
            pltpu.SemaphoreType.DMA((80,)),
        ],
        compiler_params=pltpu.CompilerParams(
            vmem_limit_bytes=VMEM_BYTES, collective_id=3, has_side_effects=True
        ),
        cost_estimate=pl.CostEstimate(flops=40_000_000_000, bytes_accessed=30_000_000, transcendentals=0),
        name="attend_backward",
    )(
        grad_low, grad_resid, hidden_in, resid_mid, wo_rows, wq_rows, normed_one, mixed, query_rot, key_rot,
        value_low, logs, seg_all, small_all, small_part, tables, y_part, res_all,
        cot_all, resid_low,
    )

    gate_shape, down_shape = (jax.ShapeDtypeStruct(w.shape, F32) for w in (w_gate, w_down))
    one_gate = pl.BlockSpec((1,) + w_gate.shape[1:], lambda e: (e, 0, 0))
    one_down = pl.BlockSpec((1,) + w_down.shape[1:], lambda e: (e, 0, 0))
    token_pair = (2, row_count, length, width)
    res_all, cot_all, grad_gate, grad_up, grad_down, grads_own, small = pl.pallas_call(
        functools.partial(weight_grads_kernel, counts),
        out_shape=(
            every, every, gate_shape, gate_shape, down_shape,
            jax.ShapeDtypeStruct((width, qkv_width + width), F32),
            jax.ShapeDtypeStruct((SMALL_ROWS, width), F32),
        ),
        input_output_aliases={0: 0, 1: 1},
        in_specs=[hbm] * 6 + [vmem] * 3 + [hbm] * 3,
        out_specs=[hbm] * 5 + [vmem] * 2,
        scratch_shapes=[
            pltpu.VMEM(w_gate.shape, LOW),
            pltpu.VMEM(w_up.shape, LOW),
            pltpu.VMEM(w_down.shape, LOW),
            pltpu.VMEM((dp_count * col_count, SMALL_ROWS, width), F32),
            pltpu.VMEM(w_gate.shape, F32),
            pltpu.VMEM(w_up.shape, F32),
            pltpu.VMEM(w_down.shape, F32),
            pltpu.VMEM(token_pair, LOW),
            pltpu.VMEM(token_pair, LOW),
            pltpu.VMEM((2, capacity, D), LOW),
            pltpu.VMEM((2, capacity, D), LOW),
            pltpu.VMEM((2, 3, capacity, hidden_width), LOW),
            pltpu.VMEM((col_count, width, qkv_width + width), LOW),
            pltpu.VMEM((4, width, qkv_width + width), LOW),
            pltpu.SemaphoreType.DMA((4,)),
            pltpu.SemaphoreType.DMA((3, 2)),
            pltpu.SemaphoreType.DMA((3, exp_local)),
            pltpu.SemaphoreType.DMA((64,)),
            pltpu.SemaphoreType.DMA((64,)),
        ],
        compiler_params=pltpu.CompilerParams(
            vmem_limit_bytes=VMEM_BYTES, collective_id=4, has_side_effects=True
        ),
        name="weight_grads",
    )(res_all, cot_all, grads_part, *kept_slots, small_part, table, small_all, w_gate, w_up, w_down)
    def strips(rows, columns):
        return pl.BlockSpec((rows // exp_local, columns), lambda e: (e, 0))

    tokens, attn = strips(length, width), strips(width, qkv_width + width)
    whole = [pl.BlockSpec((EXPERTS, width), lambda e: (0, 0))] + [pl.BlockSpec((1, width), lambda e: (0, 0))] * 2
    gain_row = jax.ShapeDtypeStruct((1, width), F32)
    grad_gate, grad_up, grad_down, layer_out, grad_in, grad_qkv, grad_out, grad_router, *grad_gains = pl.pallas_call(
        functools.partial(last_grads_kernel, counts),
        grid=(exp_local,),
        out_shape=(
            gate_shape, gate_shape, down_shape, block_low, block_float,
            jax.ShapeDtypeStruct(w_qkv.shape, F32),
            jax.ShapeDtypeStruct((head_width, width), F32),
            jax.ShapeDtypeStruct((EXPERTS, width), F32),
            gain_row,
            gain_row,
        ),
        in_specs=[hbm, hbm, vmem, vmem] + [one_gate, one_gate, one_down] * 2 + [tokens, tokens, attn, vmem],
        out_specs=[
            one_gate, one_gate, one_down, tokens, tokens,
            pl.BlockSpec((width // exp_local,) + w_qkv.shape[1:], lambda e: (e, 0, 0)), strips(head_width, width),
        ]
        + whole,
        scratch_shapes=[
            pltpu.VMEM((row_count, length, width), LOW),
            pltpu.VMEM((row_count, length, width), LOW),
            pltpu.SemaphoreType.DMA((2,)),
        ],
        compiler_params=params,
        name="last_grads",
    )(
        res_all, cot_all, table, small_all, w_gate, w_up, w_down, grad_gate, grad_up, grad_down,
        layer_out, grad_in, grads_own, small,
    )
    return (
        layer_out,
        grad_in,
        grad_gains[0].reshape(width),
        grad_qkv,
        grad_out.reshape(w_out.shape),
        grad_gains[1].reshape(width),
        grad_router.T,
        grad_gate,
        grad_up,
        grad_down,
    )


def solution(mesh):
    token = P(("dp", "col"), "row")
    routed = P(("dp", "col"), None)
    expert = P(("dp", "row"), None, None)
    wide, tall = P("row", "col", None), P("col", None, "row")
    row = P("row")
    square = P("row", None)

    def step(*arrays):
        length = arrays[10].shape[1]
        tokens_here = arrays[0].shape[0] // (mesh.shape["dp"] * mesh.shape["col"])
        whole_sequence = tokens_here == length and mesh.shape["row"] == mesh.shape["col"]
        return jax.shard_map(
            fast_device if whole_sequence else on_device,
            mesh=mesh,
            in_specs=(
                token, row, wide, tall, row, square, expert, expert, expert, token,
                P(("dp", "row"), None), routed, routed,
            ),
            out_specs=(token, token, row, wide, tall, row, square, expert, expert, expert),
            check_vma=False,
        )(*arrays)

    return step
```
